32 devices in a mesh: dp: 8 (over z, core), tp: 4 (over y, x).
Axes of the slice: x: 2, y: 2, z: 4, core: 2. Of those that a mesh axis runs over, the one named last changes fastest.
Arguments:
- x_in: bfloat16 [8192, 2048], P(('dp', 'tp')), may hold values from -6 to 6
- norm_gain: float32 [2048], replicated, may hold values from 0.5 to 1.5
- w_z: bfloat16 [2048, 4096], P(None, 'tp'), may hold values from -0.125 to 0.125
- w_x: bfloat16 [2048, 4096], P(None, 'tp'), may hold values from -0.125 to 0.125
- w_b: bfloat16 [2048, 128], P(None, 'tp'), may hold values from -0.125 to 0.125
- w_c: bfloat16 [2048, 128], P(None, 'tp'), may hold values from -0.125 to 0.125
- w_dt: bfloat16 [2048, 64], P(None, 'tp'), may hold values from -0.125 to 0.125
- conv_w: float32 [4352, 4], replicated, may hold values from -3 to 3
- conv_b: float32 [4352], replicated, may hold values from -3 to 3
- dt_bias: float32 [64], replicated, may hold values from -6 to -2
- a_log: float32 [64], replicated, may hold values from -2.5 to 0.5
- d_skip: float32 [64], replicated, may hold values from 0.5 to 1.5
- gate_gain: float32 [4096], replicated, may hold values from 0.5 to 1.5
- w_out: bfloat16 [4096, 2048], P('tp'), may hold values from -0.09375 to 0.09375
- doc_lens: int32 [8, 8], P('dp'), may hold values from 1 to 512, 1024 in all within a row
- d_out: bfloat16 [8192, 2048], P(('dp', 'tp')), may hold values from -6 to 6
Outputs:
- block_out: bfloat16 [8192, 2048], P(('dp', 'tp'))
- grad_x: float32 [8192, 2048], P(('dp', 'tp'))
- grad_norm_gain: float32 [2048], replicated
- grad_w_z: float32 [2048, 4096], P('dp', 'tp')
- grad_w_x: float32 [2048, 4096], P('dp', 'tp')
- grad_w_b: float32 [2048, 128], P('dp', 'tp')
- grad_w_c: float32 [2048, 128], P('dp', 'tp')
- grad_w_dt: float32 [2048, 64], P('dp', 'tp')
- grad_conv_w: float32 [4352, 4], replicated
- grad_conv_b: float32 [4352], replicated
- grad_dt_bias: float32 [64], replicated
- grad_a_log: float32 [64], replicated
- grad_d_skip: float32 [64], replicated
- grad_gate_gain: float32 [4096], replicated
- grad_w_out: float32 [4096, 2048], P('tp', 'dp')
The draws below stay inside these ranges and needn't reach their ends.
Inputs may be any that keep to these rules, and one draw needn't show every extreme that they name: `doc_lens`: each row gives, in order, the lengths of the 8 documents packed into one sequence of 1024 tokens; a row sums to 1024 and its longest document has exactly 512 tokens.
All inputs are finite; a program needn't handle non-finite values.
Results may differ from the reference program's by a relative error of at most 0.012.
Values may be sent and summed in bfloat16 or wider, within the bound.
A program may use at most 256 MiB of HBM per device.

```python
import math
import jax
import jax.numpy as jnp
import numpy as np
from jax import lax

D = 2048
HEADS = 64
HDIM = 64
NSTATE = 128
CONV = 4
SPAN = 256
DOCS = 8
INNER = 4096
SEQ = 1024
MOST = 512
TOKENS = 8192
N_DP = 8


def draw_a_log(key, part):
    key_slow = jax.random.fold_in(key, 11)
    return jax.random.uniform(key_slow, (HEADS,), jnp.float32, -2.5, 0.5)


def levels(own_key, shape, shards, least, high):
    def one(position, shards_of):
        draws = jax.random.uniform(jax.random.fold_in(jax.random.fold_in(own_key, 6), position), (shards_of,), jnp.float32, least / len(shards), high / len(shards))
        return jnp.repeat(jnp.exp(draws), shape[position] // shards_of).reshape((-1,) + (1,) * (len(shape) - position - 1))

    loudness = one(*shards[0])
    for cut in shards[1:]:
        loudness = loudness * one(*cut)
    return loudness


def length_profile(amount, total, limit, slope):
    weights = [(1 << 20) // math.isqrt(standing ** slope) + 1 for standing in range(2, amount + 1)]
    spare, holding = total - limit - (amount - 1), [1] * (amount - 1)
    while spare > 0:
        free = [i for i in range(amount - 1) if holding[i] < limit]
        mass, budget = sum([weights[i] for i in free]), spare
        for i in free:
            extra = min(limit - holding[i], max(1, budget * weights[i] // mass), spare)
            holding[i] = holding[i] + extra
            spare = spare - extra
    return np.array([limit] + holding)


def uneven_parts(key, amount, total, limit, slope):
    if amount == 2:
        one = jax.random.randint(key, (), max(1, total - limit), min(limit, total - 1) + 1)
        return jnp.stack([one, total - one])
    lengths = jnp.asarray(length_profile(amount, total, limit, slope), jnp.int32)
    twos = (amount - 1) // 2
    donor, receiver = lengths[1:1 + 2 * twos:2], lengths[2:2 + 2 * twos:2]
    margin = jnp.minimum(donor - 1, limit - receiver)
    shifted = jax.random.randint(jax.random.fold_in(key, 1), (twos,), 0, 1 << 20) % (margin + 1)
    lengths = lengths.at[1:1 + 2 * twos:2].set(donor - shifted).at[2:2 + 2 * twos:2].set(receiver + shifted)
    return lengths[jax.random.permutation(jax.random.fold_in(key, 2), amount)]


def centred(key, extent, scale, most, pieces=(), kind=jnp.bfloat16):
    values = scale * jax.random.normal(key, extent, jnp.float32)
    if pieces:
        values = values * levels(key, extent, pieces, -0.22, 0.18)
    return jnp.clip(values, -most, most).astype(kind)


def setup_inputs(seed: int = 0) -> dict:
    seeds = jax.random.split(jax.random.key(seed), 17)
    x_in = centred(seeds[0], (TOKENS, D), 1.0, 6.0, ((0, 32),))
    norm_gain = jnp.clip(1.0 + 0.1 * jax.random.normal(seeds[1], (D,), jnp.float32), 0.5, 1.5)
    w_z = centred(seeds[2], (D, INNER), D ** -0.5, 0.125, ((1, 4),))
    w_x = centred(seeds[3], (D, INNER), D ** -0.5, 0.125, ((1, 4),))
    w_b = centred(seeds[4], (D, NSTATE), D ** -0.5, 0.125, ((1, 4),))
    w_c = centred(seeds[5], (D, NSTATE), D ** -0.5, 0.125, ((1, 4),))
    w_dt = centred(seeds[6], (D, HEADS), D ** -0.5, 0.125, ((1, 4),))
    conv_w = centred(seeds[7], (INNER + 2 * NSTATE, CONV), CONV ** -0.5, 3.0, (), jnp.float32)
    conv_b = centred(seeds[8], (INNER + 2 * NSTATE,), 0.5, 3.0, (), jnp.float32)
    dt_bias = jnp.clip(jax.random.uniform(seeds[9], (HEADS,), jnp.float32, -6.0, -2.0), -6.0, -2.0)
    a_log = draw_a_log(jax.random.fold_in(seeds[16], 71), 0)
    d_skip = jnp.clip(jax.random.uniform(seeds[11], (HEADS,), jnp.float32, 0.5, 1.5), 0.5, 1.5)
    gate_gain = jnp.clip(1.0 + 0.1 * jax.random.normal(seeds[12], (INNER,), jnp.float32), 0.5, 1.5)
    w_out = centred(seeds[13], (INNER, D), INNER ** -0.5, 0.09375, ((0, 4),))
    doc_lens = jax.vmap(lambda own: uneven_parts(own, DOCS, SEQ, MOST, 2))(jax.random.split(seeds[14], N_DP)).reshape((N_DP, DOCS)).astype(jnp.int32)
    d_out = centred(seeds[15], (TOKENS, D), 1.0, 6.0, ((0, 32),))
    return dict(x_in=x_in, norm_gain=norm_gain, w_z=w_z, w_x=w_x, w_b=w_b, w_c=w_c, w_dt=w_dt, conv_w=conv_w, conv_b=conv_b, dt_bias=dt_bias, a_log=a_log, d_skip=d_skip, gate_gain=gate_gain, w_out=w_out, doc_lens=doc_lens, d_out=d_out)


EPSILON = 1e-05
HIGHEST = lax.Precision.HIGHEST

@jax.custom_vjp
def low(v):
    return lax.optimization_barrier(v.astype(jnp.bfloat16)).astype(jnp.float32)

@jax.custom_vjp
def low_back(v):
    return v

def low_keep(v):
    return (low(v), None)

def low_pass(kept, grad):
    return (grad,)

def back_keep(v):
    return (v, None)

def back_low(kept, grad):
    return (low(grad),)
low.defvjp(low_keep, low_pass)
low_back.defvjp(back_keep, back_low)

def span_pass(state, values, b_rows, c_rows, log_decay, steps_dt, segments, segment_prev):
    cumulative = jnp.cumsum(log_decay, axis=0)
    inward = jnp.exp(cumulative) * (segments == segment_prev).astype(jnp.float32)[:, None]
    carried = jnp.exp(cumulative[-1]) * (segments[-1] == segment_prev).astype(jnp.float32)
    length = segments.shape[0]
    order = jnp.arange(length, dtype=jnp.int32)
    same = (segments[:, None] == segments[None, :]) & (order[:, None] >= order[None, :])
    spread = cumulative[:, None, :] - cumulative[None, :, :]
    decays = jnp.exp(jnp.where(same[:, :, None], spread, -1e+30))
    scores = jnp.dot(c_rows, b_rows.T, precision=HIGHEST)
    mixing = decays * scores[:, :, None] * steps_dt[None, :, :]
    output = jnp.einsum('tsh,shp->thp', mixing, values, precision=HIGHEST)
    output = output + jnp.einsum('tn,hpn->thp', c_rows, state, precision=HIGHEST) * inward[:, :, None]
    tail_same = segments == segments[-1]
    tail = jnp.exp(jnp.where(tail_same[:, None], cumulative[-1][None, :] - cumulative, -1e+30)) * steps_dt
    weighted = tail[:, :, None] * values
    state_out = carried[:, None, None] * state + jnp.einsum('shp,sn->hpn', weighted, b_rows, precision=HIGHEST)
    return (output, state_out, carried)

def block_forward(segments, x_val, norm_gain, w_z, w_x, w_b, w_c, w_dt, conv_w, conv_b, dt_bias, a_log, d_skip, gate_gain, w_out):
    total_rows = x_val.shape[0]
    normed = low(x_val * lax.rsqrt(lax.optimization_barrier(jnp.mean(x_val * x_val, axis=-1, keepdims=True)) + EPSILON) * norm_gain[None, :])

    def project(matrix):
        return low(low_back(jnp.dot(normed, matrix, precision=HIGHEST)))
    gate_in = project(w_z)
    conv_in = jnp.concatenate([project(w_x), project(w_b), project(w_c)], axis=1)
    dt_in = project(w_dt)
    channels = conv_in.shape[1]
    seg_pad = jnp.concatenate([jnp.zeros((CONV - 1,), jnp.int32), segments])
    padded = jnp.concatenate([jnp.zeros((CONV - 1, channels), jnp.float32), conv_in], axis=0)
    summed = jnp.zeros((total_rows, channels), jnp.float32) + conv_b[None, :]
    for kernel_tap in range(CONV):
        match = (seg_pad[kernel_tap:kernel_tap + total_rows] == segments).astype(jnp.float32)
        summed = summed + conv_w[:, kernel_tap][None, :] * padded[kernel_tap:kernel_tap + total_rows] * match[:, None]
    active = jax.nn.silu(summed)
    values = active[:, :INNER].reshape(total_rows, HEADS, HDIM)
    b_rows = active[:, INNER:INNER + NSTATE]
    c_rows = active[:, INNER + NSTATE:]
    steps_dt = jax.nn.softplus(dt_in + dt_bias[None, :])
    log_decay = -steps_dt * jnp.exp(a_log)[None, :]
    span_count = total_rows // SPAN
    seq_count = total_rows // SEQ
    per_seq = SEQ // SPAN
    seg_prev = jnp.concatenate([jnp.zeros((1,), jnp.int32), segments[:-1]]).reshape(span_count, SPAN)[:, 0]

    def one_span(state, item):
        values_c, b_c, c_c, decay_c, dt_c, seg_c, prev_c = item
        output, state, carried = span_pass(state, values_c, b_c, c_c, decay_c, dt_c, seg_c, prev_c)
        return (state, output)

    def one_sequence(seq_items):
        _, outputs = lax.scan(jax.checkpoint(one_span), jnp.zeros((HEADS, HDIM, NSTATE), jnp.float32), seq_items)
        return outputs
    items = (values.reshape(seq_count, per_seq, SPAN, HEADS, HDIM), b_rows.reshape(seq_count, per_seq, SPAN, NSTATE), c_rows.reshape(seq_count, per_seq, SPAN, NSTATE), log_decay.reshape(seq_count, per_seq, SPAN, HEADS), steps_dt.reshape(seq_count, per_seq, SPAN, HEADS), segments.reshape(seq_count, per_seq, SPAN), seg_prev.reshape(seq_count, per_seq))
    outputs = lax.map(one_sequence, items)
    ssd_out = outputs.reshape(total_rows, HEADS, HDIM)
    mixed = (ssd_out + d_skip[None, :, None] * values).reshape(total_rows, INNER)
    gated_rows = mixed * jax.nn.silu(gate_in)
    scale = lax.rsqrt(lax.optimization_barrier(jnp.mean(gated_rows * gated_rows, axis=-1, keepdims=True)) + EPSILON)
    normal_out = low(low_back(gated_rows * scale * gate_gain[None, :]))
    return x_val + jnp.dot(normal_out, w_out, precision=HIGHEST)

def reference(x_in, norm_gain, w_z, w_x, w_b, w_c, w_dt, conv_w, conv_b, dt_bias, a_log, d_skip, gate_gain, w_out, doc_lens, d_out):
    total_rows = x_in.shape[0]
    seq_count = doc_lens.shape[0]
    offsets = (jnp.arange(seq_count, dtype=jnp.int32) * SEQ)[:, None]
    doc_starts = (jnp.cumsum(doc_lens, axis=1) - doc_lens + offsets).reshape(-1).astype(jnp.int32)
    positions = jnp.arange(total_rows, dtype=jnp.int32)
    segments = lax.optimization_barrier(jnp.sum((positions[:, None] >= doc_starts[None, :]).astype(jnp.int32), axis=1)).astype(jnp.int32)
    floats = [array.astype(jnp.float32) for array in (x_in, norm_gain, w_z, w_x, w_b, w_c, w_dt, conv_w, conv_b, dt_bias, a_log, d_skip, gate_gain, w_out)]

    def forward_only(*params):
        return block_forward(segments, *params)
    result, backward = jax.vjp(forward_only, *floats)
    grads = backward(d_out.astype(jnp.float32))
    return (result.astype(jnp.bfloat16), grads[0], grads[1], grads[2], grads[3], grads[4], grads[5], grads[6], grads[7], grads[8], grads[9], grads[10], grads[11], grads[12], grads[13])
```

```python
import functools

import jax
import jax.numpy as jnp
from jax import lax
from jax.experimental import pallas as pl
from jax.experimental.pallas import tpu as pltpu
from jax.sharding import PartitionSpec as P

EPSILON = 1e-05
HIGHEST = lax.Precision.HIGHEST
F32 = jnp.float32
BF16 = jnp.bfloat16
CHUNK = 128
LANES = 128
CONTRACT_FIRST = (((0,), (0,)), ((), ()))
CONTRACT_LAST = (((1,), (1,)), ((), ()))


def dot(a, b, dims=(((1,), (0,)), ((), ()))):
    return lax.dot_general(a, b, dims, preferred_element_type=F32)


def two_parts(v):
    high = v.astype(BF16)
    return jnp.concatenate([high, (v - high.astype(F32)).astype(BF16)], axis=1)


def prepare_chunk(width, x_ref, bc_ref, dt_ref, halo_x_ref, halo_bc_ref, pos_ref, prm_ref, head_ref, expand_ref, ext):
    rows = x_ref.shape[0]
    ext[8:, :width] = x_ref[...].astype(F32)
    ext[8:, width:] = bc_ref[...].astype(F32)
    ext[:8, :width] = halo_x_ref[...].astype(F32)[8:, :]
    ext[:8, width:] = halo_bc_ref[...].astype(F32)[8:, :]
    pos = pos_ref[...]
    pre = prm_ref[3:4, :] * ext[8:, :] + prm_ref[4:5, :]
    for back in (1, 2, 3):
        here = (pos >= back).astype(F32)
        pre = pre + prm_ref[3 - back : 4 - back, :] * (ext[8 - back : 8 - back + rows, :] * here)
    sig = jax.nn.sigmoid(pre)
    act = pre * sig
    xc = act[:, :width]
    state_size = (act.shape[1] - width) // 2
    b_rows = act[:, width : width + state_size].astype(BF16)
    c_rows = act[:, width + state_size :].astype(BF16)
    raw = dt_ref[...].astype(F32) + head_ref[0:1, :]
    dt = jnp.maximum(raw, 0.0) + jnp.log1p(jnp.exp(-jnp.abs(raw)))
    log_decay = -dt * head_ref[1:2, :]
    t_idx = lax.broadcasted_iota(jnp.int32, (rows, rows), 0)
    s_idx = lax.broadcasted_iota(jnp.int32, (rows, rows), 1)
    lower = (s_idx <= t_idx).astype(F32)
    cum = lax.dot_general(
        lower, log_decay, (((1,), (0,)), ((), ())), precision=HIGHEST, preferred_element_type=F32
    )
    same = (s_idx <= t_idx) & (s_idx >= t_idx - pos)
    scores = jnp.where(same, dot(c_rows, b_rows, CONTRACT_LAST), 0.0)
    t_col = lax.broadcasted_iota(jnp.int32, (rows, 1), 0)
    pos_last = pos[rows - 1 : rows, :]
    cum_last = cum[rows - 1 : rows, :]
    inward = jnp.exp(cum) * (pos > t_col).astype(F32)
    tail = jnp.exp(cum_last - cum) * (t_col >= rows - 1 - pos_last).astype(F32)
    carried = jnp.exp(cum_last) * (pos_last >= rows).astype(F32)
    wide = dot(
        two_parts(jnp.concatenate([dt, inward, tail, jnp.broadcast_to(carried, (8, LANES))], axis=0)),
        expand_ref[...],
    )
    return dict(
        pos=pos,
        pre=pre,
        sig=sig,
        xc=xc,
        b=b_rows,
        c=c_rows,
        raw=raw,
        dt=dt,
        log_decay=log_decay,
        cum=cum,
        cum_t=cum.T,
        same=same,
        scores=scores,
        carried=carried,
        t_idx=t_idx,
        s_idx=s_idx,
        dt_w=wide[:rows],
        in_w=wide[rows : 2 * rows],
        tail_w=wide[2 * rows : 3 * rows],
        carried_w=wide[3 * rows : 3 * rows + 1],
    )


def decay_of(k, head):
    return jnp.exp(jnp.minimum(k["cum"][:, head : head + 1] - k["cum_t"][head : head + 1, :], 0.0))


def halves(pair):
    lane = lax.broadcasted_iota(jnp.int32, pair.shape, 1)
    zero = jnp.zeros_like(pair)
    return jnp.concatenate(
        [jnp.where(lane < LANES // 2, pair, zero), jnp.where(lane < LANES // 2, zero, pair)], axis=0
    )


def forward_kernel(
    width, order, z_ref, x_ref, bc_ref, dt_ref, halo_x_ref, halo_bc_ref, pos_ref, prm_ref, head_ref,
    expand_ref, y_ref, g_ref, sum_ref, state_ref, ext, state,
):
    @pl.when(pl.program_id(0) == 0)
    def _():
        state[...] = jnp.zeros_like(state)

    k = prepare_chunk(
        width, x_ref, bc_ref, dt_ref, halo_x_ref, halo_bc_ref, pos_ref, prm_ref, head_ref, expand_ref, ext
    )
    rows = x_ref.shape[0]
    stepped = (k["xc"] * k["dt_w"]).astype(BF16)
    held = state[...]
    held_low = held.astype(BF16)
    state_ref[0] = held_low
    reached = dot(k["c"], held_low) * k["in_w"]
    weighted = (stepped.astype(F32) * k["tail_w"]).astype(BF16)
    state[...] = k["carried_w"] * held + dot(k["b"], weighted, CONTRACT_FIRST)
    for pair in range(width // LANES):
        lanes = slice(pair * LANES, (pair + 1) * LANES)
        mixing = jnp.concatenate(
            [
                (decay_of(k, 2 * pair) * k["scores"]).astype(BF16),
                (decay_of(k, 2 * pair + 1) * k["scores"]).astype(BF16),
            ],
            axis=1,
        )
        y_ref[:, lanes] = dot(mixing, halves(stepped[:, lanes])) + reached[:, lanes]
    z = z_ref[...].astype(F32)
    g = (y_ref[...] + prm_ref[6:7, :width] * k["xc"]) * (z * jax.nn.sigmoid(z))
    g_ref[...] = g
    total = jnp.sum(g * g, axis=1, keepdims=True)
    sum_ref[...] = jnp.broadcast_to(total, (rows, LANES)).T[:8, :]


def backward_kernel(
    width, chunks, order, z_ref, x_ref, bc_ref, dt_ref, halo_x_ref, halo_bc_ref, pos_ref, prm_ref, head_ref,
    expand_ref, y_ref, g_ref, state_ref, dyo_ref, coef_ref, grad_ref, small_ref, ext, d_state, later, later_pos,
):
    first = pl.program_id(0) == 0

    @pl.when(first)
    def _():
        d_state[...] = jnp.zeros_like(d_state)
        later[...] = jnp.zeros_like(later)
        later_pos[...] = jnp.zeros_like(later_pos)
        small_ref[...] = jnp.zeros_like(small_ref)

    k = prepare_chunk(
        width, x_ref, bc_ref, dt_ref, halo_x_ref, halo_bc_ref, pos_ref, prm_ref, head_ref, expand_ref, ext
    )
    rows = x_ref.shape[0]
    xc = k["xc"]
    z = z_ref[...].astype(F32)
    sig_z = jax.nn.sigmoid(z)
    r_col = coef_ref[:, 0:1]
    back_col = coef_ref[:, 1:2]
    g = g_ref[...]
    y = y_ref[...]
    dyo = dyo_ref[...].astype(F32)
    skip = prm_ref[6:7, :width]
    dg = r_col * (dyo * prm_ref[5:6, :width]) - g * back_col
    dy = dg * (z * sig_z)
    grad_ref[:, :width] = (dg * (y + skip * xc) * (sig_z * (1.0 + z * (1.0 - sig_z)))).astype(BF16)
    small_ref[5:6, :width] += jnp.sum(dyo * g * r_col, axis=0, keepdims=True)
    small_ref[6:7, :width] += jnp.sum(dy * xc, axis=0, keepdims=True)

    stepped = (xc * k["dt_w"]).astype(BF16)
    dy_low = dy.astype(BF16)
    d_held = d_state[...]
    d_held_low = d_held.astype(BF16)
    held_low = state_ref[0]
    weighted = (stepped.astype(F32) * k["tail_w"]).astype(BF16)
    dy_in = (dy * k["in_w"]).astype(BF16)
    from_state = dot(k["b"], d_held_low) * k["tail_w"]
    dc = dot(dy_in, held_low, CONTRACT_LAST)
    db = dot(weighted, d_held_low, CONTRACT_LAST)
    d_state[...] = k["carried_w"] * d_held + dot(k["c"], dy_in, CONTRACT_FIRST)
    d_scores = jnp.zeros((rows, rows), F32)
    d_stepped = []
    for pair in range(width // LANES):
        lanes = slice(pair * LANES, (pair + 1) * LANES)
        decay_a = decay_of(k, 2 * pair)
        decay_b = decay_of(k, 2 * pair + 1)
        mixing = jnp.concatenate(
            [(decay_a * k["scores"]).astype(BF16), (decay_b * k["scores"]).astype(BF16)], axis=0
        )
        d_mixing = dot(dy_low[:, lanes], halves(stepped[:, lanes]), CONTRACT_LAST)
        d_scores = d_scores + decay_a * d_mixing[:, :rows] + decay_b * d_mixing[:, rows:]
        d_stepped.append(dot(mixing, halves(dy_low[:, lanes]), CONTRACT_FIRST))
    d_stepped = jnp.concatenate(d_stepped, axis=1) + from_state
    d_scores = jnp.where(k["same"], d_scores, 0.0).astype(BF16)
    dc = dc + dot(d_scores, k["b"])
    db = db + dot(d_scores, k["c"], CONTRACT_FIRST)
    dxc = skip * dy + d_stepped * k["dt_w"]

    stepped_f = stepped.astype(F32)
    tail_term = jnp.sum(stepped_f * from_state, axis=0, keepdims=True) + k["carried_w"] * jnp.sum(
        held_low.astype(F32) * d_held, axis=0, keepdims=True
    )
    gathered = two_parts(
        jnp.concatenate(
            [
                d_stepped * xc,
                dy_low.astype(F32) * y - stepped_f * d_stepped,
                jnp.broadcast_to(tail_term, (8, width)),
            ],
            axis=0,
        )
    )
    expand = expand_ref[:LANES, :]
    narrow = dot(gathered[:, :width], expand, CONTRACT_LAST) + dot(gathered[:, width:], expand, CONTRACT_LAST)
    d_dt = narrow[:rows]
    d_cum = narrow[rows : 2 * rows]
    upper = (k["s_idx"] >= k["t_idx"]).astype(F32)
    d_decay = (
        lax.dot_general(
            upper, d_cum, (((1,), (0,)), ((), ())), precision=HIGHEST, preferred_element_type=F32
        )
        + narrow[2 * rows : 2 * rows + 1]
    )
    d_raw = (d_dt - d_decay * head_ref[1:2, :]) * jax.nn.sigmoid(k["raw"])
    small_ref[7:8, :LANES] += jnp.sum(d_raw, axis=0, keepdims=True)
    small_ref[7:8, LANES : 2 * LANES] += jnp.sum(d_decay * k["log_decay"], axis=0, keepdims=True)
    conv_end = grad_ref.shape[1] - LANES
    grad_ref[:, conv_end:] = d_raw.astype(BF16)

    pre, sig, pos = k["pre"], k["sig"], k["pos"]
    d_pre = jnp.concatenate([dxc, db, dc], axis=1) * (sig * (1.0 + pre * (1.0 - sig)))
    small_ref[4:5, :] += jnp.sum(d_pre, axis=0, keepdims=True)
    later[:rows, :] = d_pre
    later_pos[:rows, :] = jnp.broadcast_to(pos, (rows, LANES))
    d_in = prm_ref[3:4, :] * d_pre
    small_ref[3:4, :] += jnp.sum(d_pre * ext[8:, :], axis=0, keepdims=True)
    for back in (1, 2, 3):
        here = (pos >= back).astype(F32)
        small_ref[3 - back : 4 - back, :] += jnp.sum(
            d_pre * (ext[8 - back : 8 - back + rows, :] * here), axis=0, keepdims=True
        )
        there = (later_pos[back : back + rows, 0:1] >= back).astype(F32)
        d_in = d_in + prm_ref[3 - back : 4 - back, :] * (later[back : back + rows, :] * there)
    grad_ref[:, width:conv_end] = d_in.astype(BF16)
    later[rows:, :] = later[:8, :]
    later_pos[rows:, :] = later_pos[:8, :]


def token_specs(width, chunks, per_block, reverse):
    def at(step):
        return chunks - 1 - step if reverse else step

    def place(step, order):
        chunk = at(step)
        return order[chunk // per_block] * per_block + chunk % per_block

    def before(step, order):
        tile = jnp.maximum(at(step) * (CHUNK // 16) - 1, 0)
        tiles = per_block * (CHUNK // 16)
        return order[tile // tiles] * tiles + tile % tiles

    bc = 2 * LANES
    specs = [
        pl.BlockSpec((CHUNK, width), lambda i, o: (place(i, o), 0)),
        pl.BlockSpec((CHUNK, width), lambda i, o: (place(i, o), 1)),
        pl.BlockSpec((CHUNK, bc), lambda i, o: (place(i, o), 2 * width // bc)),
        pl.BlockSpec((CHUNK, LANES), lambda i, o: (place(i, o), (2 * width + bc) // LANES)),
        pl.BlockSpec((16, width), lambda i, o: (before(i, o), 1)),
        pl.BlockSpec((16, bc), lambda i, o: (before(i, o), 2 * width // bc)),
        pl.BlockSpec((CHUNK, 1), lambda i, o: (at(i), 0)),
        pl.BlockSpec((8, width + bc), lambda i, o: (0, 0)),
        pl.BlockSpec((8, LANES), lambda i, o: (0, 0)),
        pl.BlockSpec((2 * LANES, width), lambda i, o: (0, 0)),
    ]
    return specs, place, at


def mixer_forward(width, order, projected, pos, prm, head_prm, expand):
    rows = projected.shape[0]
    chunks = rows // CHUNK
    per_block = chunks // order.shape[0]
    specs, place, at = token_specs(width, chunks, per_block, False)
    return pl.pallas_call(
        functools.partial(forward_kernel, width),
        out_shape=(
            jax.ShapeDtypeStruct((rows, width), F32),
            jax.ShapeDtypeStruct((rows, width), F32),
            jax.ShapeDtypeStruct((8, rows), F32),
            jax.ShapeDtypeStruct((chunks, LANES, width), BF16),
        ),
        grid_spec=pltpu.PrefetchScalarGridSpec(
            num_scalar_prefetch=1,
            grid=(chunks,),
            in_specs=specs,
            out_specs=(
                pl.BlockSpec((CHUNK, width), lambda i, o: (place(i, o), 0)),
                pl.BlockSpec((CHUNK, width), lambda i, o: (place(i, o), 0)),
                pl.BlockSpec((8, CHUNK), lambda i, o: (0, place(i, o))),
                pl.BlockSpec((1, LANES, width), lambda i, o: (i, 0, 0)),
            ),
            scratch_shapes=[
                pltpu.VMEM((CHUNK + 8, width + 2 * LANES), F32),
                pltpu.VMEM((LANES, width), F32),
            ],
        ),
        compiler_params=pltpu.CompilerParams(
            dimension_semantics=("arbitrary",), vmem_limit_bytes=40 * 1024 * 1024
        ),
        cost_estimate=pl.CostEstimate(flops=rows * width * 1024, bytes_accessed=rows * width * 14, transcendentals=0),
    )(order, projected, projected, projected, projected, projected, projected, pos, prm, head_prm, expand)


def mixer_backward(width, order, projected, pos, prm, head_prm, expand, y, g, states, dyo, coef):
    rows, columns = projected.shape
    chunks = rows // CHUNK
    per_block = chunks // order.shape[0]
    specs, place, at = token_specs(width, chunks, per_block, True)
    wide = pl.BlockSpec((CHUNK, width), lambda i, o: (place(i, o), 0))
    return pl.pallas_call(
        functools.partial(backward_kernel, width, chunks),
        out_shape=(
            jax.ShapeDtypeStruct((rows, columns), BF16),
            jax.ShapeDtypeStruct((8, width + 2 * LANES), F32),
        ),
        grid_spec=pltpu.PrefetchScalarGridSpec(
            num_scalar_prefetch=1,
            grid=(chunks,),
            in_specs=specs
            + [
                wide,
                wide,
                pl.BlockSpec((1, LANES, width), lambda i, o: (at(i), 0, 0)),
                wide,
                pl.BlockSpec((CHUNK, 8), lambda i, o: (place(i, o), 0)),
            ],
            out_specs=(
                pl.BlockSpec((CHUNK, columns), lambda i, o: (place(i, o), 0)),
                pl.BlockSpec((8, width + 2 * LANES), lambda i, o: (0, 0)),
            ),
            scratch_shapes=[
                pltpu.VMEM((CHUNK + 8, width + 2 * LANES), F32),
                pltpu.VMEM((LANES, width), F32),
                pltpu.VMEM((CHUNK + 8, width + 2 * LANES), F32),
                pltpu.VMEM((CHUNK + 8, LANES), jnp.int32),
            ],
        ),
        compiler_params=pltpu.CompilerParams(
            dimension_semantics=("arbitrary",), vmem_limit_bytes=48 * 1024 * 1024
        ),
        cost_estimate=pl.CostEstimate(flops=rows * width * 2048, bytes_accessed=rows * width * 20, transcendentals=0),
    )(order, projected, projected, projected, projected, projected, projected, pos, prm, head_prm, expand,
      y, g, states, dyo, coef)


def swap(array, axis, bits):
    return lax.ppermute(array, axis, [(i, i ^ bits) for i in range(lax.axis_size(axis))])


def gather_tp(block):
    if lax.axis_size("tp") != 4:
        return lax.all_gather(block, "tp", axis=0, tiled=True)
    half = block.shape[0] // 2
    a = swap(block, "tp", 1)
    b = swap(block, "tp", 2)
    c = swap(a[:half], "tp", 2)
    d = swap(b[half:], "tp", 1)
    return jnp.concatenate([block, a, b, c, d], axis=0)


def scatter_tp(blocks):
    if lax.axis_size("tp") != 4:
        return lax.psum_scatter(jnp.concatenate(blocks, axis=0), "tp", scatter_dimension=0, tiled=True).astype(F32)
    half = blocks[0].shape[0] // 2
    a = swap(blocks[3][:half], "tp", 1)
    b = swap(blocks[3][half:], "tp", 2)
    to_1 = jnp.concatenate([blocks[1][:half], blocks[1][half:] + b], axis=0)
    to_2 = jnp.concatenate([blocks[2][:half] + a, blocks[2][half:]], axis=0)
    c = swap(to_1, "tp", 1)
    d = swap(to_2, "tp", 2)
    return blocks[0].astype(F32) + c.astype(F32) + d.astype(F32)


def sum_tp(array):
    if lax.axis_size("tp") != 4:
        return lax.psum(array, "tp")
    parts = jnp.split(array, 4, axis=-1)
    total = array
    for bits in (1, 2, 3):
        total = total + swap(jnp.concatenate([parts[k ^ bits] for k in range(4)], axis=-1), "tp", bits)
    return total


def in_norm_scale(values):
    return lax.rsqrt(jnp.mean(values * values, axis=-1, keepdims=True) + EPSILON)


def body(
    x_in, norm_gain, w_z, w_x, w_b, w_c, w_dt, conv_w, conv_b, dt_bias, a_log, d_skip, gate_gain, w_out,
    doc_lens, d_out,
):
    tp_count = lax.axis_size("tp")
    rank = lax.axis_index("tp")
    dev_rows, model = x_in.shape
    rows = dev_rows * tp_count
    inner = gate_gain.shape[0]
    width = w_z.shape[1]
    heads = w_dt.shape[1]
    state_size = (conv_w.shape[0] - inner) // 2
    head_size = width // heads
    own_cols = w_b.shape[1]
    order = jnp.arange(tp_count, dtype=jnp.int32)
    if tp_count == 4:
        order = order ^ rank.astype(jnp.int32)

    x_float = x_in.astype(F32)
    r_in = in_norm_scale(x_float)
    normed = (x_float * r_in * norm_gain[None, :]).astype(BF16)

    w_bc_own = jnp.concatenate([w_b, w_c], axis=1).T
    w_bc_all = lax.all_gather(w_bc_own, "tp", axis=0) if tp_count != 4 else None
    if tp_count == 4:
        parts = jnp.stack([w_bc_own] + [swap(w_bc_own, "tp", bits) for bits in (1, 2, 3)])
        w_bc_all = jnp.stack([lax.dynamic_index_in_dim(parts, order[j], 0, False) for j in range(4)])
    w_bc_all = w_bc_all.reshape(tp_count, 2, own_cols, model)
    w_bc = jnp.swapaxes(w_bc_all, 0, 1).reshape(2 * state_size, model).T
    w_joined = jnp.concatenate(
        [w_z, w_x, w_bc, w_dt, jnp.zeros((model, LANES - heads), BF16)], axis=1
    )
    gathered = gather_tp(normed)
    projected = dot(gathered, w_joined).astype(BF16)

    lengths = doc_lens[0]
    doc_starts = jnp.cumsum(lengths) - lengths
    positions = jnp.arange(rows, dtype=jnp.int32)
    started = jnp.where(positions[:, None] >= doc_starts[None, :], doc_starts[None, :], 0)
    pos = (positions - jnp.max(started, axis=1))[:, None]

    def own(array, count):
        return lax.dynamic_slice_in_dim(array, rank * count, count, axis=0)

    taps = jnp.concatenate([own(conv_w[:inner], width), conv_w[inner:]], axis=0).T
    bias = jnp.concatenate([own(conv_b[:inner], width), conv_b[inner:]])
    pad_bc = jnp.zeros((2 * state_size,), F32)
    gain_own = own(gate_gain, width)
    skip_own = jnp.repeat(own(d_skip, heads), head_size)
    prm = jnp.concatenate(
        [
            taps,
            bias[None],
            jnp.concatenate([gain_own, pad_bc])[None],
            jnp.concatenate([skip_own, pad_bc])[None],
            jnp.zeros((1, width + 2 * state_size), F32),
        ],
        axis=0,
    )
    pad_heads = jnp.zeros((LANES - heads,), F32)
    head_prm = jnp.concatenate(
        [
            jnp.concatenate([own(dt_bias, heads), pad_heads])[None],
            jnp.concatenate([jnp.exp(own(a_log, heads)), pad_heads])[None],
            jnp.zeros((6, LANES), F32),
        ],
        axis=0,
    )
    expand = (
        (jnp.arange(2 * LANES) % LANES)[:, None] == (jnp.arange(width) // head_size)[None, :]
    ).astype(BF16)

    y, g, g_sum, states = mixer_forward(width, order, projected, pos, prm, head_prm, expand)
    d_held, _ = lax.optimization_barrier((d_out, gathered))
    grad_gathered = gather_tp(d_held)
    g_total = sum_tp(g_sum)[0]
    r_gate = lax.rsqrt(g_total / inner + EPSILON)
    dyo = dot(grad_gathered, w_out, CONTRACT_LAST).astype(BF16)
    eg_sum = jnp.sum(dyo.astype(F32) * gain_own[None, :] * g, axis=1)
    eg_total = sum_tp(eg_sum)
    coef = jnp.stack([r_gate, r_gate**3 * (eg_total / inner)] + [jnp.zeros_like(r_gate)] * 6, axis=1)
    yo = (g * r_gate[:, None] * gain_own[None, :]).astype(BF16)
    yo = lax.optimization_barrier(yo)

    def block(array, k):
        return array[k * dev_rows : (k + 1) * dev_rows]

    out_parts = [dot(block(yo, k), w_out).astype(BF16) for k in range(tp_count)]
    block_out = (x_float + scatter_tp(out_parts)).astype(BF16)

    grad_projected, small = mixer_backward(
        width, order, projected, pos, prm, head_prm, expand, y, g, states, dyo, coef
    )

    def scatter_dp(partial):
        return lax.psum_scatter(partial.astype(BF16), "dp", scatter_dimension=0, tiled=True).astype(F32)

    grad_w_out = scatter_dp(dot(grad_gathered, yo, CONTRACT_FIRST)).T
    grad_w_z = scatter_dp(dot(gathered, grad_projected[:, :width], CONTRACT_FIRST))

    d_bc = grad_projected[:, 2 * width : 2 * width + 2 * state_size]
    d_dt = grad_projected[:, 2 * width + 2 * state_size : 2 * width + 2 * state_size + heads]
    by_owner = jnp.moveaxis(d_bc.reshape(rows, 2, tp_count, own_cols), 2, 0).reshape(tp_count, rows, 2 * own_cols)
    if tp_count == 4:
        d_bc_own = lax.dynamic_index_in_dim(by_owner, rank, 0, False).astype(F32)
        for bits in (1, 2, 3):
            sent = lax.dynamic_index_in_dim(by_owner, order[bits], 0, False)
            sent = sent.reshape(tp_count, dev_rows, -1)
            sent = jnp.stack([sent[k ^ bits] for k in range(tp_count)]).reshape(rows, -1)
            d_bc_own = d_bc_own + swap(sent, "tp", bits).astype(F32)
    else:
        d_bc_own = lax.psum_scatter(by_owner.astype(F32), "tp", scatter_dimension=0, tiled=False)
    last = jnp.concatenate(
        [
            grad_projected[:, width : 2 * width],
            d_bc_own.astype(BF16),
            d_dt,
            jnp.zeros((rows, (-2 * own_cols - heads) % LANES), BF16),
        ],
        axis=1,
    )
    grad_last = scatter_dp(dot(gathered, last, CONTRACT_FIRST))

    du_parts = [dot(block(grad_projected, k), w_joined, CONTRACT_LAST) for k in range(tp_count)]
    gain_part = sum(
        jnp.sum(du_parts[k] * block(gathered, k).astype(F32), axis=0) for k in range(tp_count)
    ) / norm_gain
    du = scatter_tp([part.astype(BF16) for part in du_parts])
    e_in = du * norm_gain[None, :]
    grad_x = d_out.astype(F32) + r_in * e_in - x_float * (
        r_in**3 * jnp.mean(e_in * x_float, axis=-1, keepdims=True)
    )

    per_head = small[6, :width].reshape(heads, head_size).sum(axis=1)
    own_small = jnp.concatenate(
        [small[:6, :width].reshape(-1), small[7, :heads], small[7, LANES : LANES + heads], per_head]
    )
    shared_small = jnp.concatenate([small[:5, width:].reshape(-1), gain_part])
    own_small = lax.psum(own_small, "dp")
    shared_small = lax.psum(shared_small, ("dp", "tp"))
    all_small = lax.all_gather(own_small, "tp")
    channels = all_small[:, : 6 * width].reshape(tp_count, 6, width)
    channels = jnp.swapaxes(channels, 0, 1).reshape(6, inner)
    rest = all_small[:, 6 * width :].reshape(tp_count, 3, heads)
    rest = jnp.swapaxes(rest, 0, 1).reshape(3, heads * tp_count)
    shared = shared_small[: 5 * 2 * state_size].reshape(5, 2 * state_size)
    grad_conv = jnp.concatenate([channels[:5], shared], axis=1)
    return (
        block_out,
        grad_x,
        shared_small[5 * 2 * state_size :],
        grad_w_z,
        grad_last[:, :width],
        grad_last[:, width : width + own_cols],
        grad_last[:, width + own_cols : width + 2 * own_cols],
        grad_last[:, width + 2 * own_cols : width + 2 * own_cols + heads],
        grad_conv[:4].T,
        grad_conv[4],
        rest[0],
        rest[1],
        rest[2],
        channels[5],
        grad_w_out,
    )


def solution(mesh):
    rows = P(("dp", "tp"), None)
    columns = P(None, "tp")
    both = P("dp", "tp")
    none = P()
    return jax.shard_map(
        body,
        mesh=mesh,
        in_specs=(
            rows, none, columns, columns, columns, columns, columns, none, none, none, none, none, none,
            P("tp", None), P("dp", None), rows,
        ),
        out_specs=(
            rows, rows, none, both, both, both, both, both, none, none, none, none, none, none, P("tp", "dp"),
        ),
        check_vma=False,
    )
```

```python
import functools

import jax
import jax.numpy as jnp
from jax import lax
from jax.experimental import pallas as pl
from jax.experimental.pallas import tpu as pltpu
from jax.sharding import PartitionSpec as P

EPSILON = 1e-05
HIGHEST = lax.Precision.HIGHEST
F32 = jnp.float32
BF16 = jnp.bfloat16
CHUNK = 128
LANES = 128
CONTRACT_FIRST = (((0,), (0,)), ((), ()))
CONTRACT_LAST = (((1,), (1,)), ((), ()))


def dot(a, b, dims=(((1,), (0,)), ((), ()))):
    return lax.dot_general(a, b, dims, preferred_element_type=F32)


def two_parts(v):
    high = v.astype(BF16)
    return jnp.concatenate([high, (v - high.astype(F32)).astype(BF16)], axis=1)


def prepare_chunk(width, x, bc, raw_dt, pos, prm_ref, head_ref, expand_ref, ext):
    rows = CHUNK
    ext[8:, :width] = x.astype(F32)
    ext[8:, width:] = bc.astype(F32)
    pre = prm_ref[3:4, :] * ext[8:, :] + prm_ref[4:5, :]
    for back in (1, 2, 3):
        here = (pos >= back).astype(F32)
        pre = pre + prm_ref[3 - back : 4 - back, :] * (ext[8 - back : 8 - back + rows, :] * here)
    sig = jax.nn.sigmoid(pre)
    act = pre * sig
    xc = act[:, :width]
    state_size = (act.shape[1] - width) // 2
    b_rows = act[:, width : width + state_size].astype(BF16)
    c_rows = act[:, width + state_size :].astype(BF16)
    raw = raw_dt.astype(F32) + head_ref[0:1, :]
    dt = jnp.maximum(raw, 0.0) + jnp.log1p(jnp.exp(-jnp.abs(raw)))
    log_decay = -dt * head_ref[1:2, :]
    t_idx = lax.broadcasted_iota(jnp.int32, (rows, rows), 0)
    s_idx = lax.broadcasted_iota(jnp.int32, (rows, rows), 1)
    lower = (s_idx <= t_idx).astype(F32)
    cum = lax.dot_general(
        lower, log_decay, (((1,), (0,)), ((), ())), precision=HIGHEST, preferred_element_type=F32
    )
    same = (s_idx <= t_idx) & (s_idx >= t_idx - pos)
    scores = jnp.where(same, dot(c_rows, b_rows, CONTRACT_LAST), 0.0)
    t_col = lax.broadcasted_iota(jnp.int32, (rows, 1), 0)
    pos_last = pos[rows - 1 : rows, :]
    cum_last = cum[rows - 1 : rows, :]
    inward = jnp.exp(cum) * (pos > t_col).astype(F32)
    tail = jnp.exp(cum_last - cum) * (t_col >= rows - 1 - pos_last).astype(F32)
    carried = jnp.exp(cum_last) * (pos_last >= rows).astype(F32)
    wide = dot(
        two_parts(jnp.concatenate([dt, inward, tail, jnp.broadcast_to(carried, (8, LANES))], axis=0)),
        expand_ref[...],
    )
    return dict(
        pre=pre,
        sig=sig,
        xc=xc,
        b=b_rows,
        c=c_rows,
        raw=raw,
        log_decay=log_decay,
        cum=cum,
        cum_t=cum.T,
        same=same,
        scores=scores,
        t_idx=t_idx,
        s_idx=s_idx,
        dt_w=wide[:rows],
        in_w=wide[rows : 2 * rows],
        tail_w=wide[2 * rows : 3 * rows],
        carried_w=wide[3 * rows : 3 * rows + 1],
    )


def decay_of(k, head):
    return jnp.exp(jnp.minimum(k["cum"][:, head : head + 1] - k["cum_t"][head : head + 1, :], 0.0))


def halves(pair):
    lane = lax.broadcasted_iota(jnp.int32, pair.shape, 1)
    zero = jnp.zeros_like(pair)
    return jnp.concatenate(
        [jnp.where(lane < LANES // 2, pair, zero), jnp.where(lane < LANES // 2, zero, pair)], axis=0
    )


def forward_chunk(
    width, at, zx_ref, bcdt_ref, pos_ref, prm_ref, head_ref, expand_ref, mixed_ref, g_ref, sum_ref, state_ref, ext,
    state,
):
    if isinstance(at, int):
        rows = slice(at * CHUNK, (at + 1) * CHUNK)
    else:
        rows = pl.ds(pl.multiple_of(at * CHUNK, CHUNK), CHUNK)
    ext[:8, :] = ext[CHUNK:, :]
    k = prepare_chunk(
        width,
        zx_ref[rows, width:],
        bcdt_ref[rows, : 2 * LANES],
        bcdt_ref[rows, 2 * LANES :],
        pos_ref[rows, :],
        prm_ref,
        head_ref,
        expand_ref,
        ext,
    )
    stepped = (k["xc"] * k["dt_w"]).astype(BF16)
    held = state[...]
    held_low = held.astype(BF16)
    state_ref[at] = held_low
    reached = dot(k["c"], held_low) * k["in_w"] + prm_ref[6:7, :width] * k["xc"]
    weighted = (stepped.astype(F32) * k["tail_w"]).astype(BF16)
    state[...] = k["carried_w"] * held + dot(k["b"], weighted, CONTRACT_FIRST)
    for pair in range(width // LANES):
        lanes = slice(pair * LANES, (pair + 1) * LANES)
        mixing = jnp.concatenate(
            [
                (decay_of(k, 2 * pair) * k["scores"]).astype(BF16),
                (decay_of(k, 2 * pair + 1) * k["scores"]).astype(BF16),
            ],
            axis=1,
        )
        mixed_ref[rows, lanes] = dot(mixing, halves(stepped[:, lanes])) + reached[:, lanes]
    z = zx_ref[rows, :width].astype(F32)
    g = mixed_ref[rows, :] * (z * jax.nn.sigmoid(z))
    g_ref[rows, :] = g
    total = jnp.sum(g * g, axis=1, keepdims=True)
    sum_ref[:, rows] = jnp.broadcast_to(total, (CHUNK, LANES)).T[:8, :]


def forward_kernel(
    width, zx_ref, bcdt_ref, pos_ref, prm_ref, head_ref, expand_ref, mixed_ref, g_ref, sum_ref, state_ref, ext, state
):
    @pl.when(pl.program_id(0) == 0)
    def _():
        state[...] = jnp.zeros_like(state)
        ext[...] = jnp.zeros_like(ext)

    forward_chunk(
        width, 0, zx_ref, bcdt_ref, pos_ref, prm_ref, head_ref, expand_ref, mixed_ref, g_ref, sum_ref, state_ref, ext,
        state,
    )


def backward_kernel(
    width, zx_ref, bcdt_ref, halo_x_ref, halo_bc_ref, pos_ref, prm_ref, head_ref,
    expand_ref, mixed_ref, g_ref, state_ref, dyo_ref, coef_ref, grad_x_ref, grad_bcdt_ref, small_ref, ext, d_state,
    later, later_pos,
):
    @pl.when(pl.program_id(0) == 0)
    def _():
        d_state[...] = jnp.zeros_like(d_state)
        later[...] = jnp.zeros_like(later)
        later_pos[...] = jnp.zeros_like(later_pos)
        small_ref[...] = jnp.zeros_like(small_ref)

    rows = CHUNK
    ext[:8, :width] = halo_x_ref[...].astype(F32)[8:, :]
    ext[:8, width:] = halo_bc_ref[...].astype(F32)[8:, : 2 * LANES]
    pos = pos_ref[...]
    k = prepare_chunk(
        width,
        zx_ref[:, width:],
        bcdt_ref[:, : 2 * LANES],
        bcdt_ref[:, 2 * LANES :],
        pos,
        prm_ref,
        head_ref,
        expand_ref,
        ext,
    )
    xc = k["xc"]
    z = zx_ref[:, :width].astype(F32)
    r_col = coef_ref[:, 0:1]
    back_col = coef_ref[:, 8:9]
    g = g_ref[...]
    dyo = dyo_ref[...].astype(F32)
    skip = prm_ref[6:7, :width]
    y = mixed_ref[...] - skip * xc
    dg = r_col * (dyo * prm_ref[5:6, :width]) - g * back_col
    dy = dg * (z * jax.nn.sigmoid(z))
    small_ref[5:6, :width] += jnp.sum(dyo * g * r_col, axis=0, keepdims=True)
    small_ref[6:7, :width] += jnp.sum(dy * xc, axis=0, keepdims=True)

    stepped = (xc * k["dt_w"]).astype(BF16)
    dy_low = dy.astype(BF16)
    d_held = d_state[...]
    d_held_low = d_held.astype(BF16)
    held_low = state_ref[0]
    weighted = (stepped.astype(F32) * k["tail_w"]).astype(BF16)
    dy_in = (dy * k["in_w"]).astype(BF16)
    from_state = dot(k["b"], d_held_low) * k["tail_w"]
    dc = dot(dy_in, held_low, CONTRACT_LAST)
    db = dot(weighted, d_held_low, CONTRACT_LAST)
    d_state[...] = k["carried_w"] * d_held + dot(k["c"], dy_in, CONTRACT_FIRST)
    d_scores = jnp.zeros((rows, rows), F32)
    d_stepped = []
    for pair in range(width // LANES):
        lanes = slice(pair * LANES, (pair + 1) * LANES)
        decay_a = decay_of(k, 2 * pair)
        decay_b = decay_of(k, 2 * pair + 1)
        mixing = jnp.concatenate(
            [(decay_a * k["scores"]).astype(BF16), (decay_b * k["scores"]).astype(BF16)], axis=0
        )
        d_mixing = dot(dy_low[:, lanes], halves(stepped[:, lanes]), CONTRACT_LAST)
        d_scores = d_scores + decay_a * d_mixing[:, :rows] + decay_b * d_mixing[:, rows:]
        d_stepped.append(dot(mixing, halves(dy_low[:, lanes]), CONTRACT_FIRST))
    d_stepped = jnp.concatenate(d_stepped, axis=1) + from_state
    d_scores = jnp.where(k["same"], d_scores, 0.0).astype(BF16)
    dc = dc + dot(d_scores, k["b"])
    db = db + dot(d_scores, k["c"], CONTRACT_FIRST)
    dxc = skip * dy + d_stepped * k["dt_w"]

    stepped_f = stepped.astype(F32)
    tail_term = jnp.sum(stepped_f * from_state, axis=0, keepdims=True) + k["carried_w"] * jnp.sum(
        held_low.astype(F32) * d_held, axis=0, keepdims=True
    )
    gathered = two_parts(
        jnp.concatenate(
            [
                d_stepped * xc,
                dy_low.astype(F32) * y - stepped_f * d_stepped,
                jnp.broadcast_to(tail_term, (8, width)),
            ],
            axis=0,
        )
    )
    expand = expand_ref[:LANES, :]
    narrow = dot(gathered[:, :width], expand, CONTRACT_LAST) + dot(gathered[:, width:], expand, CONTRACT_LAST)
    d_dt = narrow[:rows]
    d_cum = narrow[rows : 2 * rows]
    upper = (k["s_idx"] >= k["t_idx"]).astype(F32)
    d_decay = (
        lax.dot_general(
            upper, d_cum, (((1,), (0,)), ((), ())), precision=HIGHEST, preferred_element_type=F32
        )
        + narrow[2 * rows : 2 * rows + 1]
    )
    d_raw = (d_dt - d_decay * head_ref[1:2, :]) * jax.nn.sigmoid(k["raw"])
    small_ref[7:8, :LANES] += jnp.sum(d_raw, axis=0, keepdims=True)
    small_ref[7:8, LANES : 2 * LANES] += jnp.sum(d_decay * k["log_decay"], axis=0, keepdims=True)
    grad_bcdt_ref[:, 2 * LANES :] = d_raw.astype(BF16)

    pre, sig = k["pre"], k["sig"]
    d_pre = jnp.concatenate([dxc, db, dc], axis=1) * (sig * (1.0 + pre * (1.0 - sig)))
    small_ref[4:5, :] += jnp.sum(d_pre, axis=0, keepdims=True)
    later[:rows, :] = d_pre
    later_pos[:rows, :] = jnp.broadcast_to(pos, (rows, LANES))
    d_in = prm_ref[3:4, :] * d_pre
    small_ref[3:4, :] += jnp.sum(d_pre * ext[8:, :], axis=0, keepdims=True)
    for back in (1, 2, 3):
        here = (pos >= back).astype(F32)
        small_ref[3 - back : 4 - back, :] += jnp.sum(
            d_pre * (ext[8 - back : 8 - back + rows, :] * here), axis=0, keepdims=True
        )
        there = (later_pos[back : back + rows, 0:1] >= back).astype(F32)
        d_in = d_in + prm_ref[3 - back : 4 - back, :] * (later[back : back + rows, :] * there)
    grad_x_ref[...] = d_in[:, :width].astype(BF16)
    grad_bcdt_ref[:, : 2 * LANES] = d_in[:, width:].astype(BF16)
    later[rows:, :] = later[:8, :]
    later_pos[rows:, :] = later_pos[:8, :]


def mixer_forward(width, zx, bcdt, pos, prm, head_prm, expand):
    rows = zx.shape[0]
    chunks = rows // CHUNK

    def tokens(columns):
        return pl.BlockSpec((CHUNK, columns), lambda i: (i, 0))

    def whole(array):
        return pl.BlockSpec(array.shape, lambda i: (0, 0))

    return pl.pallas_call(
        functools.partial(forward_kernel, width),
        out_shape=(
            jax.ShapeDtypeStruct((rows, width), F32),
            jax.ShapeDtypeStruct((rows, width), F32),
            jax.ShapeDtypeStruct((8, rows), F32),
            jax.ShapeDtypeStruct((chunks, LANES, width), BF16),
        ),
        grid=(chunks,),
        in_specs=[tokens(2 * width), tokens(3 * LANES), tokens(1), whole(prm), whole(head_prm), whole(expand)],
        out_specs=(
            tokens(width),
            tokens(width),
            pl.BlockSpec((8, CHUNK), lambda i: (0, i)),
            pl.BlockSpec((1, LANES, width), lambda i: (i, 0, 0)),
        ),
        scratch_shapes=[
            pltpu.VMEM((CHUNK + 8, width + 2 * LANES), F32),
            pltpu.VMEM((LANES, width), F32),
        ],
        compiler_params=pltpu.CompilerParams(
            dimension_semantics=("arbitrary",), vmem_limit_bytes=40 * 1024 * 1024
        ),
    )(zx, bcdt, pos, prm, head_prm, expand)


def mixer_backward(width, zx, bcdt, pos, prm, head_prm, expand, mixed, g, states, dyo, coef):
    rows = zx.shape[0]
    chunks = rows // CHUNK

    def tokens(columns):
        return pl.BlockSpec((CHUNK, columns), lambda i: (chunks - 1 - i, 0))

    def before(columns, place):
        return pl.BlockSpec(
            (16, columns), lambda i: (jnp.maximum((chunks - 1 - i) * (CHUNK // 16) - 1, 0), place)
        )

    def whole(array):
        return pl.BlockSpec(array.shape, lambda i: (0, 0))

    return pl.pallas_call(
        functools.partial(backward_kernel, width),
        out_shape=(
            jax.ShapeDtypeStruct((rows, width), BF16),
            jax.ShapeDtypeStruct((rows, 3 * LANES), BF16),
            jax.ShapeDtypeStruct((8, width + 2 * LANES), F32),
        ),
        grid=(chunks,),
        in_specs=[
            tokens(2 * width),
            tokens(3 * LANES),
            before(width, 1),
            before(3 * LANES, 0),
            tokens(1),
            whole(prm),
            whole(head_prm),
            whole(expand),
            tokens(width),
            tokens(width),
            pl.BlockSpec((1, LANES, width), lambda i: (chunks - 1 - i, 0, 0)),
            tokens(width),
            tokens(LANES),
        ],
        out_specs=(
            tokens(width),
            tokens(3 * LANES),
            pl.BlockSpec((8, width + 2 * LANES), lambda i: (0, 0)),
        ),
        scratch_shapes=[
            pltpu.VMEM((CHUNK + 8, width + 2 * LANES), F32),
            pltpu.VMEM((LANES, width), F32),
            pltpu.VMEM((CHUNK + 8, width + 2 * LANES), F32),
            pltpu.VMEM((CHUNK + 8, LANES), jnp.int32),
        ],
        compiler_params=pltpu.CompilerParams(
            dimension_semantics=("arbitrary",), vmem_limit_bytes=48 * 1024 * 1024
        ),
        cost_estimate=pl.CostEstimate(flops=rows * width * 2048, bytes_accessed=rows * width * 20, transcendentals=0),
    )(zx, bcdt, zx, bcdt, pos, prm, head_prm, expand, mixed, g, states, dyo, coef)


MESH = pl.DeviceIdType.MESH


def tp_places():
    me = lax.axis_index("tp")
    return me, me + 1 - 2 * lax.rem(me, 2), lax.rem(me + 2, 4), 3 - me


def greet(peers):
    barrier = pltpu.get_barrier_semaphore()
    for peer in peers:
        pl.semaphore_signal(barrier, inc=1, device_id=peer, device_id_type=MESH)
    pl.semaphore_wait(barrier, len(peers))


def send(src, dst, send_sem, recv_sem, peer):
    return pltpu.make_async_remote_copy(
        src_ref=src, dst_ref=dst, send_sem=send_sem, recv_sem=recv_sem, device_id=peer, device_id_type=MESH
    )


class Gather:
    def __init__(self, whole, rows, send_sems, recv_sems, own=None):
        me, side, up, _ = tp_places()
        half = rows // 2

        def part(place, start, count):
            return whole.at[pl.ds(pl.multiple_of(place * rows + start, half), count)]

        own = part(me, 0, rows) if own is None else own
        self.to_side = send(own, part(me, 0, rows), send_sems.at[0], recv_sems.at[0], {"tp": side})
        self.to_up = send(own, part(me, 0, rows), send_sems.at[1], recv_sems.at[1], {"tp": up})
        self.pass_up = send(
            part(side, 0, half), part(side, 0, half), send_sems.at[2], recv_sems.at[2], {"tp": up}
        )
        self.pass_side = send(
            part(up, half, half), part(up, half, half), send_sems.at[3], recv_sems.at[3], {"tp": side}
        )

    def start(self):
        self.to_side.start()
        self.to_up.start()

    def forward(self):
        self.to_side.wait_recv()
        self.pass_up.start()
        self.to_up.wait_recv()
        self.pass_side.start()

    def finish(self):
        self.pass_up.wait_recv()
        self.pass_side.wait_recv()

    def end(self):
        for copy in (self.to_side, self.to_up, self.pass_up, self.pass_side):
            copy.wait_send()


def project_kernel(
    own_cols, x_ref, gain_ref, small_ref, wz_ref, wx_ref, u_ref, zx_ref, bcdt_ref, wbc_ref, weights, parts, sems,
    local_sems,
):
    rows, model = x_ref.shape
    width = wz_ref.shape[1]
    me, side, up, far = tp_places()
    load_z = pltpu.make_async_copy(wz_ref, weights.at[:, :width], local_sems.at[0])
    load_x = pltpu.make_async_copy(wx_ref, weights.at[:, width:], local_sems.at[1])
    load_z.start()
    load_x.start()
    parts[pl.ds(pl.multiple_of(me * 2 * own_cols, own_cols), 2 * own_cols)] = small_ref[: 2 * own_cols, :]
    greet([{"tp": side}, {"tp": up}])
    small_gather = Gather(parts, 2 * own_cols, sems.at[0], sems.at[1])
    small_gather.start()

    def norm(i, carry):
        piece = pl.ds(pl.multiple_of(i * 32, 32), 32)
        x = x_ref[piece, :].astype(F32)
        scale = lax.rsqrt(jnp.mean(x * x, axis=-1, keepdims=True) + EPSILON)
        u_ref[pl.ds(pl.multiple_of(me * rows + i * 32, 32), 32), :] = (x * scale * gain_ref[...]).astype(BF16)
        return carry

    lax.fori_loop(0, rows // 32, norm, 0)
    gather = Gather(u_ref, rows, sems.at[2], sems.at[3])
    gather.start()
    wbc_ref[2 * LANES :, :] = jnp.zeros((LANES, model), BF16)
    wbc_ref[2 * LANES : 2 * LANES + small_ref.shape[0] - 2 * own_cols, :] = small_ref[2 * own_cols :, :]
    load_z.wait()
    load_x.wait()

    def project(place):
        piece = pl.ds(pl.multiple_of(place * rows, rows), rows)

        def tile(n, carry):
            columns = pl.ds(pl.multiple_of(n * 256, 256), 256)
            zx_ref[piece, columns] = dot(u_ref[piece, :], weights[:, columns]).astype(BF16)
            return carry

        lax.fori_loop(0, 2 * width // 256, tile, 0)

    def project_small(place):
        piece = pl.ds(pl.multiple_of(place * rows, rows), rows)
        bcdt_ref[piece, :] = dot(u_ref[piece, :], wbc_ref[...], CONTRACT_LAST).astype(BF16)

    project(me)
    small_gather.forward()
    gather.forward()
    small_gather.finish()
    for place in range(4):
        wbc_ref[place * own_cols : (place + 1) * own_cols, :] = parts[
            2 * place * own_cols : (2 * place + 1) * own_cols, :
        ]
        wbc_ref[LANES + place * own_cols : LANES + (place + 1) * own_cols, :] = parts[
            (2 * place + 1) * own_cols : (2 * place + 2) * own_cols, :
        ]

    project(side)
    project(up)
    project_small(me)
    project_small(side)
    project_small(up)
    gather.finish()
    project(far)
    project_small(far)
    small_gather.end()
    gather.end()


def gather_project(x_in, gain, small, w_z, w_x, own_cols):
    rows, model = x_in.shape
    total = 4 * rows
    width = w_z.shape[1]
    vmem = pl.BlockSpec(memory_space=pltpu.VMEM)
    return pl.pallas_call(
        functools.partial(project_kernel, own_cols),
        out_shape=(
            jax.ShapeDtypeStruct((total, model), BF16),
            jax.ShapeDtypeStruct((total, 2 * width), BF16),
            jax.ShapeDtypeStruct((total, 3 * LANES), BF16),
            jax.ShapeDtypeStruct((3 * LANES, model), BF16),
        ),
        in_specs=[vmem, vmem, vmem, pl.BlockSpec(memory_space=pl.ANY), pl.BlockSpec(memory_space=pl.ANY)],
        out_specs=(vmem, vmem, vmem, vmem),
        scratch_shapes=[
            pltpu.VMEM((model, 2 * width), BF16),
            pltpu.VMEM((8 * own_cols, model), BF16),
            pltpu.SemaphoreType.DMA((4, 4)),
            pltpu.SemaphoreType.DMA((2,)),
        ],
        compiler_params=pltpu.CompilerParams(
            collective_id=0, has_side_effects=True, vmem_limit_bytes=56 * 1024 * 1024
        ),
    )(x_in, gain, small, w_z, w_x)


def mix_kernel(
    inner, zx_ref, bcdt_ref, pos_ref, prm_ref, head_ref, expand_ref, d_own_ref, w_out_ref, mixed_ref, g_ref, yo_ref,
    state_ref, d_ref, dyo_ref, coef_ref, ext, state, sums, acc, sems, sum_sems, local_sem,
):
    total, width = mixed_ref.shape
    rows = d_own_ref.shape[0]
    chunks = total // CHUNK
    me, side, up, far = tp_places()
    keep = pltpu.make_async_copy(d_own_ref, d_ref.at[pl.ds(pl.multiple_of(me * rows, rows), rows)], local_sem)
    keep.start()
    greet([{"tp": side}, {"tp": up}, {"tp": far}])
    gather = Gather(d_ref, rows, sems.at[0], sems.at[1], own=d_own_ref)
    gather.start()
    state[...] = jnp.zeros_like(state)
    ext[...] = jnp.zeros_like(ext)

    def chunk(i, carry):
        forward_chunk(
            width, i, zx_ref, bcdt_ref, pos_ref, prm_ref, head_ref, expand_ref, mixed_ref, g_ref, sums.at[0, 0],
            state_ref, ext, state,
        )
        return carry

    lax.fori_loop(0, chunks, chunk, 0)

    def exchange(which):
        copies = [
            send(
                sums.at[which, 0], sums.at[which, 1 + n], sum_sems.at[which, 0, n], sum_sems.at[which, 1, n], {"tp": peer}
            )
            for n, peer in enumerate((side, up, far))
        ]
        for copy in copies:
            copy.start()
        return copies

    copies = exchange(0)
    keep.wait()

    def back_to_heads(place):
        piece = pl.ds(pl.multiple_of(place * rows, rows), rows)
        acc[...] = jnp.zeros_like(acc)

        def tile(n, carry):
            columns = pl.ds(pl.multiple_of(n * 256, 256), 256)
            low = dot(d_ref[piece, :], w_out_ref[columns, :], CONTRACT_LAST).astype(BF16)
            dyo_ref[piece, columns] = low
            both = low.astype(F32) * prm_ref[5:6, columns] * g_ref[piece, columns]
            acc[...] += both[:, :LANES] + both[:, LANES:]
            return carry

        lax.fori_loop(0, width // 256, tile, 0)
        column = jnp.sum(acc[...], axis=1, keepdims=True)
        sums[1, 0, :, piece] = jnp.broadcast_to(column, (rows, LANES)).T[:8, :]

    back_to_heads(me)
    for copy in copies:
        copy.wait()

    def gate(i, carry):
        piece = pl.ds(pl.multiple_of(i * CHUNK, CHUNK), CHUNK)
        squares = sums[0, 0, :, piece] + sums[0, 1, :, piece] + sums[0, 2, :, piece] + sums[0, 3, :, piece]
        scale = lax.rsqrt(squares / inner + EPSILON)
        columns = jnp.concatenate([scale, jnp.zeros((LANES - 8, LANES), F32)], axis=0).T
        coef_ref[piece, :] = columns
        yo_ref[piece, :] = (g_ref[piece, :] * columns[:, 0:1] * prm_ref[5:6, :width]).astype(BF16)
        return carry

    lax.fori_loop(0, chunks, gate, 0)
    gather.forward()
    back_to_heads(side)
    back_to_heads(up)
    gather.finish()
    back_to_heads(far)
    copies = exchange(1)
    gather.end()
    for copy in copies:
        copy.wait()

    def weigh(i, carry):
        piece = pl.ds(pl.multiple_of(i * CHUNK, CHUNK), CHUNK)
        squares = sums[0, 0, :, piece] + sums[0, 1, :, piece] + sums[0, 2, :, piece] + sums[0, 3, :, piece]
        cross = sums[1, 0, :, piece] + sums[1, 1, :, piece] + sums[1, 2, :, piece] + sums[1, 3, :, piece]
        scale = lax.rsqrt(squares / inner + EPSILON)
        back = scale * scale * scale * (cross / inner)
        coef_ref[piece, :] = jnp.concatenate([scale, back, jnp.zeros((LANES - 16, LANES), F32)], axis=0).T
        return carry

    lax.fori_loop(0, chunks, weigh, 0)


def gather_mix(inner, zx, bcdt, pos, prm, head_prm, expand, d_out, w_out):
    total = zx.shape[0]
    width, model = w_out.shape
    rows = d_out.shape[0]
    vmem = pl.BlockSpec(memory_space=pltpu.VMEM)
    return pl.pallas_call(
        functools.partial(mix_kernel, inner),
        out_shape=(
            jax.ShapeDtypeStruct((total, width), F32),
            jax.ShapeDtypeStruct((total, width), F32),
            jax.ShapeDtypeStruct((total, width), BF16),
            jax.ShapeDtypeStruct((total // CHUNK, LANES, width), BF16),
            jax.ShapeDtypeStruct((total, model), BF16),
            jax.ShapeDtypeStruct((total, width), BF16),
            jax.ShapeDtypeStruct((total, LANES), F32),
        ),
        in_specs=[vmem] * 8,
        out_specs=(vmem,) * 7,
        scratch_shapes=[
            pltpu.VMEM((CHUNK + 8, width + 2 * LANES), F32),
            pltpu.VMEM((LANES, width), F32),
            pltpu.VMEM((2, 4, 8, total), F32),
            pltpu.VMEM((rows, LANES), F32),
            pltpu.SemaphoreType.DMA((2, 4)),
            pltpu.SemaphoreType.DMA((2, 2, 3)),
            pltpu.SemaphoreType.DMA,
        ],
        compiler_params=pltpu.CompilerParams(
            collective_id=1, has_side_effects=True, vmem_limit_bytes=58 * 1024 * 1024
        ),
    )(zx, bcdt, pos, prm, head_prm, expand, d_out, w_out)


def add_up_kernel(own_ref, out_ref, over_dp, dp_sems, tp_sems, local_sem):
    dp_count = over_dp.shape[0]
    tp_count = out_ref.shape[0]
    d = lax.axis_index("dp")
    t = lax.axis_index("tp")
    greet(
        [{"dp": lax.rem(d + n, dp_count)} for n in range(1, dp_count)]
        + [{"tp": lax.rem(t + n, tp_count)} for n in range(1, tp_count)]
    )
    copies = [
        send(own_ref, over_dp.at[n], dp_sems.at[0, n], dp_sems.at[1, n], {"dp": lax.rem(d + n, dp_count)})
        for n in range(1, dp_count)
    ]
    for copy in copies:
        copy.start()
    for copy in copies:
        copy.wait()
    total = own_ref[...]
    for n in range(1, dp_count):
        total = total + over_dp[n]
    over_dp[0] = total
    keep = pltpu.make_async_copy(over_dp.at[0], out_ref.at[t], local_sem)
    keep.start()
    copies = [
        send(over_dp.at[0], out_ref.at[t], tp_sems.at[0, n], tp_sems.at[1, n], {"tp": lax.rem(t + n, tp_count)})
        for n in range(1, tp_count)
    ]
    for copy in copies:
        copy.start()
    for copy in copies:
        copy.wait()
    keep.wait()


def add_up(own):
    dp_count, tp_count = lax.axis_size("dp"), lax.axis_size("tp")
    vmem = pl.BlockSpec(memory_space=pltpu.VMEM)
    return pl.pallas_call(
        add_up_kernel,
        out_shape=jax.ShapeDtypeStruct((tp_count,) + own.shape, F32),
        in_specs=[vmem],
        out_specs=vmem,
        scratch_shapes=[
            pltpu.VMEM((dp_count,) + own.shape, F32),
            pltpu.SemaphoreType.DMA((2, dp_count)),
            pltpu.SemaphoreType.DMA((2, tp_count)),
            pltpu.SemaphoreType.DMA,
        ],
        compiler_params=pltpu.CompilerParams(collective_id=2, has_side_effects=True),
    )(own)


def swap(array, axis, bits):
    return lax.ppermute(array, axis, [(i, i ^ bits) for i in range(lax.axis_size(axis))])


def scatter_tp(parts):
    count = lax.axis_size("tp")
    rank = lax.axis_index("tp")
    if count != 4:
        blocks = jnp.concatenate([parts(k) for k in range(count)], axis=0)
        return lax.psum_scatter(blocks, "tp", scatter_dimension=0, tiled=True).astype(F32)
    far = parts(rank ^ 3)
    half = far.shape[0] // 2
    a = swap(far[:half], "tp", 1)
    b = swap(far[half:], "tp", 2)
    side = parts(rank ^ 1)
    up = parts(rank ^ 2)
    to_side = jnp.concatenate([side[:half], side[half:] + b], axis=0)
    to_up = jnp.concatenate([up[:half] + a, up[half:]], axis=0)
    c = swap(to_side, "tp", 1)
    d = swap(to_up, "tp", 2)
    return parts(rank).astype(F32) + c.astype(F32) + d.astype(F32)


def in_norm_scale(values):
    return lax.rsqrt(jnp.mean(values * values, axis=-1, keepdims=True) + EPSILON)


def body(
    x_in, norm_gain, w_z, w_x, w_b, w_c, w_dt, conv_w, conv_b, dt_bias, a_log, d_skip, gate_gain, w_out,
    doc_lens, d_out,
):
    tp_count = lax.axis_size("tp")
    rank = lax.axis_index("tp")
    dev_rows, model = x_in.shape
    rows = dev_rows * tp_count
    inner = gate_gain.shape[0]
    width = w_z.shape[1]
    heads = w_dt.shape[1]
    state_size = (conv_w.shape[0] - inner) // 2
    head_size = width // heads
    own_cols = w_b.shape[1]

    x_float = x_in.astype(F32)
    r_in = in_norm_scale(x_float)
    small_weights = jnp.concatenate([w_b, w_c, w_dt], axis=1).T
    if tp_count == 4:
        gathered, zx, bcdt, w_bcdt = gather_project(x_in, norm_gain[None, :], small_weights, w_z, w_x, own_cols)
    else:
        normed = (x_float * r_in * norm_gain[None, :]).astype(BF16)
        gathered = lax.all_gather(normed, "tp", axis=0, tiled=True)
        w_bc = lax.all_gather(small_weights[: 2 * own_cols], "tp", axis=0).reshape(tp_count, 2, own_cols, model)
        w_bcdt = jnp.concatenate(
            [
                jnp.swapaxes(w_bc, 0, 1).reshape(2 * state_size, model),
                small_weights[2 * own_cols :],
                jnp.zeros((LANES - heads, model), BF16),
            ],
            axis=0,
        )
        zx = dot(gathered, jnp.concatenate([w_z, w_x], axis=1)).astype(BF16)
        bcdt = dot(gathered, w_bcdt, CONTRACT_LAST).astype(BF16)

    lengths = doc_lens[0]
    doc_starts = jnp.cumsum(lengths) - lengths
    positions = jnp.arange(rows, dtype=jnp.int32)
    started = jnp.where(positions[:, None] >= doc_starts[None, :], doc_starts[None, :], 0)
    pos = (positions - jnp.max(started, axis=1))[:, None]

    def own(array, count):
        return lax.dynamic_slice_in_dim(array, rank * count, count, axis=0)

    taps = jnp.concatenate([own(conv_w[:inner], width), conv_w[inner:]], axis=0).T
    bias = jnp.concatenate([own(conv_b[:inner], width), conv_b[inner:]])
    pad_bc = jnp.zeros((2 * state_size,), F32)
    gain_own = own(gate_gain, width)
    skip_own = jnp.repeat(own(d_skip, heads), head_size)
    prm = jnp.concatenate(
        [
            taps,
            bias[None],
            jnp.concatenate([gain_own, pad_bc])[None],
            jnp.concatenate([skip_own, pad_bc])[None],
            jnp.zeros((1, width + 2 * state_size), F32),
        ],
        axis=0,
    )
    pad_heads = jnp.zeros((LANES - heads,), F32)
    head_prm = jnp.concatenate(
        [
            jnp.concatenate([own(dt_bias, heads), pad_heads])[None],
            jnp.concatenate([jnp.exp(own(a_log, heads)), pad_heads])[None],
            jnp.zeros((6, LANES), F32),
        ],
        axis=0,
    )
    expand = (
        (jnp.arange(2 * LANES) % LANES)[:, None] == (jnp.arange(width) // head_size)[None, :]
    ).astype(BF16)

    if tp_count == 4:
        mixed, g, yo, states, grad_gathered, dyo, coef = gather_mix(
            inner, zx, bcdt, pos, prm, head_prm, expand, d_out, w_out
        )
    else:
        mixed, g, g_sum, states = mixer_forward(width, zx, bcdt, pos, prm, head_prm, expand)
        grad_gathered = lax.all_gather(d_out, "tp", axis=0, tiled=True)
        dyo = dot(grad_gathered, w_out, CONTRACT_LAST).astype(BF16)
        eg_sum = jnp.sum(dyo.astype(F32) * gain_own[None, :] * g, axis=1)
        g_total, eg_total = lax.psum((g_sum[0], eg_sum), "tp")
        r_gate = lax.rsqrt(g_total / inner + EPSILON)
        zeros = jnp.zeros_like(r_gate)
        coef = jnp.stack([r_gate] + [zeros] * 7 + [r_gate**3 * (eg_total / inner)] + [zeros] * (LANES - 9), axis=1)
        yo = (g * r_gate[:, None] * gain_own[None, :]).astype(BF16)

    def scatter_dp(partial):
        return lax.psum_scatter(partial.astype(BF16), "dp", scatter_dimension=0, tiled=True).astype(F32)

    grad_w_out = scatter_dp(dot(grad_gathered, yo, CONTRACT_FIRST)).T
    z = zx[:, :width].astype(F32)
    sig_z = jax.nn.sigmoid(z)
    dg = coef[:, 0:1] * (dyo.astype(F32) * gain_own[None, :]) - g * coef[:, 8:9]
    dz = (dg * mixed * (sig_z * (1.0 + z * (1.0 - sig_z)))).astype(BF16)
    grad_w_z = scatter_dp(dot(gathered, dz, CONTRACT_FIRST))

    def block(array, k):
        return lax.dynamic_slice_in_dim(array, k * dev_rows, dev_rows, axis=0)

    block_out = (x_float + scatter_tp(lambda k: dot(block(yo, k), w_out).astype(BF16))).astype(BF16)

    grad_xs, grad_bcdt, small = mixer_backward(
        width, zx, bcdt, pos, prm, head_prm, expand, mixed, g, states, dyo, coef
    )

    d_bc = grad_bcdt[:, : 2 * state_size]
    by_owner = jnp.moveaxis(d_bc.reshape(rows, 2, tp_count, own_cols), 2, 0).reshape(tp_count, rows, 2 * own_cols)
    if tp_count == 4:
        d_bc_own = lax.dynamic_index_in_dim(by_owner, rank, 0, False).astype(F32)
        for bits in (1, 2, 3):
            sent = lax.dynamic_index_in_dim(by_owner, rank ^ bits, 0, False)
            d_bc_own = d_bc_own + swap(sent, "tp", bits).astype(F32)
    else:
        d_bc_own = lax.psum_scatter(by_owner.astype(F32), "tp", scatter_dimension=0, tiled=False)
    last = jnp.concatenate(
        [
            grad_xs,
            d_bc_own.astype(BF16),
            grad_bcdt[:, 2 * state_size : 2 * state_size + heads],
            jnp.zeros((rows, (-2 * own_cols - heads) % LANES), BF16),
        ],
        axis=1,
    )
    grad_last = scatter_dp(dot(gathered, last, CONTRACT_FIRST))

    def du_part(k):
        return (
            dot(block(dz, k), w_z, CONTRACT_LAST)
            + dot(block(grad_xs, k), w_x, CONTRACT_LAST)
            + dot(block(grad_bcdt, k), w_bcdt)
        )

    gain_parts = []

    def du_low(k):
        part = du_part(k)
        gain_parts.append(jnp.sum(part * block(gathered, k).astype(F32), axis=0))
        return part.astype(BF16)

    du = scatter_tp(du_low)
    gain_part = sum(gain_parts) / norm_gain
    e_in = du * norm_gain[None, :]
    grad_x = d_out.astype(F32) + r_in * e_in - x_float * (
        r_in**3 * jnp.mean(e_in * x_float, axis=-1, keepdims=True)
    )

    packed = jnp.concatenate([small, gain_part.reshape(8, model // 8)], axis=1)
    sums = add_up(packed)
    channels = jnp.swapaxes(sums[:, :7, :width], 0, 1).reshape(7, inner)
    shared = jnp.sum(sums[:, :5, width : width + 2 * state_size], axis=0)
    grad_conv = jnp.concatenate([channels[:5], shared], axis=1)
    grad_norm_gain = jnp.sum(sums[:, :, width + 2 * state_size :], axis=0).reshape(model)
    return (
        block_out,
        grad_x,
        grad_norm_gain,
        grad_w_z,
        grad_last[:, :width],
        grad_last[:, width : width + own_cols],
        grad_last[:, width + own_cols : width + 2 * own_cols],
        grad_last[:, width + 2 * own_cols : width + 2 * own_cols + heads],
        grad_conv[:4].T,
        grad_conv[4],
        sums[:, 7, :heads].reshape(-1),
        sums[:, 7, LANES : LANES + heads].reshape(-1),
        channels[6].reshape(heads * tp_count, head_size).sum(axis=1),
        channels[5],
        grad_w_out,
    )


def solution(mesh):
    rows = P(("dp", "tp"), None)
    columns = P(None, "tp")
    both = P("dp", "tp")
    none = P()
    return jax.shard_map(
        body,
        mesh=mesh,
        in_specs=(
            rows, none, columns, columns, columns, columns, columns, none, none, none, none, none, none,
            P("tp", None), P("dp", None), rows,
        ),
        out_specs=(
            rows, rows, none, both, both, both, both, both, none, none, none, none, none, none, P("tp", "dp"),
        ),
        check_vma=False,
    )
```

```python
import functools

import jax
import jax.numpy as jnp
from jax import lax
from jax.experimental import pallas as pl
from jax.experimental.pallas import tpu as pltpu
from jax.sharding import PartitionSpec as P

EPSILON = 1e-05
HIGHEST = lax.Precision.HIGHEST
F32 = jnp.float32
BF16 = jnp.bfloat16
CHUNK = 128
LANES = 128
CONTRACT_FIRST = (((0,), (0,)), ((), ()))
CONTRACT_LAST = (((1,), (1,)), ((), ()))


def dot(a, b, dims=(((1,), (0,)), ((), ()))):
    return lax.dot_general(a, b, dims, preferred_element_type=F32)


def two_parts(v):
    high = v.astype(BF16)
    return jnp.concatenate([high, (v - high.astype(F32)).astype(BF16)], axis=1)


def prepare_chunk(width, x, bc, raw_dt, pos, prm_ref, head_ref, expand_ref, ext):
    rows = CHUNK
    ext[8:, :width] = x.astype(F32)
    ext[8:, width:] = bc.astype(F32)
    pre = prm_ref[3:4, :] * ext[8:, :] + prm_ref[4:5, :]
    for back in (1, 2, 3):
        here = (pos >= back).astype(F32)
        pre = pre + prm_ref[3 - back : 4 - back, :] * (ext[8 - back : 8 - back + rows, :] * here)
    sig = jax.nn.sigmoid(pre)
    act = pre * sig
    xc = act[:, :width]
    state_size = (act.shape[1] - width) // 2
    b_rows = act[:, width : width + state_size].astype(BF16)
    c_rows = act[:, width + state_size :].astype(BF16)
    raw = raw_dt.astype(F32) + head_ref[0:1, :]
    dt = jnp.maximum(raw, 0.0) + jnp.log1p(jnp.exp(-jnp.abs(raw)))
    log_decay = -dt * head_ref[1:2, :]
    t_idx = lax.broadcasted_iota(jnp.int32, (rows, rows), 0)
    s_idx = lax.broadcasted_iota(jnp.int32, (rows, rows), 1)
    lower = (s_idx <= t_idx).astype(F32)
    cum = lax.dot_general(
        lower, log_decay, (((1,), (0,)), ((), ())), precision=HIGHEST, preferred_element_type=F32
    )
    same = (s_idx <= t_idx) & (s_idx >= t_idx - pos)
    scores = jnp.where(same, dot(c_rows, b_rows, CONTRACT_LAST), 0.0)
    t_col = lax.broadcasted_iota(jnp.int32, (rows, 1), 0)
    pos_last = pos[rows - 1 : rows, :]
    cum_last = cum[rows - 1 : rows, :]
    inward = jnp.exp(cum) * (pos > t_col).astype(F32)
    tail = jnp.exp(cum_last - cum) * (t_col >= rows - 1 - pos_last).astype(F32)
    carried = jnp.exp(cum_last) * (pos_last >= rows).astype(F32)
    wide = dot(
        two_parts(jnp.concatenate([dt, inward, tail, jnp.broadcast_to(carried, (8, LANES))], axis=0)),
        expand_ref[...],
    )
    return dict(
        pre=pre,
        sig=sig,
        xc=xc,
        b=b_rows,
        c=c_rows,
        raw=raw,
        log_decay=log_decay,
        cum=cum,
        cum_t=cum.T,
        same=same,
        scores=scores,
        t_idx=t_idx,
        s_idx=s_idx,
        dt_w=wide[:rows],
        in_w=wide[rows : 2 * rows],
        tail_w=wide[2 * rows : 3 * rows],
        carried_w=wide[3 * rows : 3 * rows + 1],
    )


def decay_of(k, head):
    return jnp.exp(jnp.minimum(k["cum"][:, head : head + 1] - k["cum_t"][head : head + 1, :], 0.0))


def halves(pair):
    lane = lax.broadcasted_iota(jnp.int32, pair.shape, 1)
    zero = jnp.zeros_like(pair)
    return jnp.concatenate(
        [jnp.where(lane < LANES // 2, pair, zero), jnp.where(lane < LANES // 2, zero, pair)], axis=0
    )


def forward_chunk(
    width, at, zx_ref, bcdt_ref, pos_ref, prm_ref, head_ref, expand_ref, mixed_ref, g_ref, sum_ref, state_ref, ext,
    state,
):
    if isinstance(at, int):
        rows = slice(at * CHUNK, (at + 1) * CHUNK)
    else:
        rows = pl.ds(pl.multiple_of(at * CHUNK, CHUNK), CHUNK)
    ext[:8, :] = ext[CHUNK:, :]
    k = prepare_chunk(
        width,
        zx_ref[rows, width:],
        bcdt_ref[rows, : 2 * LANES],
        bcdt_ref[rows, 2 * LANES :],
        pos_ref[rows, :],
        prm_ref,
        head_ref,
        expand_ref,
        ext,
    )
    stepped = (k["xc"] * k["dt_w"]).astype(BF16)
    held = state[...]
    held_low = held.astype(BF16)
    state_ref[at] = held_low
    reached = dot(k["c"], held_low) * k["in_w"] + prm_ref[6:7, :width] * k["xc"]
    weighted = (stepped.astype(F32) * k["tail_w"]).astype(BF16)
    state[...] = k["carried_w"] * held + dot(k["b"], weighted, CONTRACT_FIRST)
    for pair in range(width // LANES):
        lanes = slice(pair * LANES, (pair + 1) * LANES)
        mixing = jnp.concatenate(
            [
                (decay_of(k, 2 * pair) * k["scores"]).astype(BF16),
                (decay_of(k, 2 * pair + 1) * k["scores"]).astype(BF16),
            ],
            axis=1,
        )
        mixed_ref[rows, lanes] = dot(mixing, halves(stepped[:, lanes])) + reached[:, lanes]
    z = zx_ref[rows, :width].astype(F32)
    g = mixed_ref[rows, :] * (z * jax.nn.sigmoid(z))
    g_ref[rows, :] = g
    total = jnp.sum(g * g, axis=1, keepdims=True)
    sum_ref[:, rows] = jnp.broadcast_to(total, (CHUNK, LANES)).T[:8, :]


def forward_kernel(
    width, zx_ref, bcdt_ref, pos_ref, prm_ref, head_ref, expand_ref, mixed_ref, g_ref, sum_ref, state_ref, ext, state
):
    @pl.when(pl.program_id(0) == 0)
    def _():
        state[...] = jnp.zeros_like(state)
        ext[...] = jnp.zeros_like(ext)

    forward_chunk(
        width, 0, zx_ref, bcdt_ref, pos_ref, prm_ref, head_ref, expand_ref, mixed_ref, g_ref, sum_ref, state_ref, ext,
        state,
    )


def backward_kernel(
    width, zx_ref, bcdt_ref, halo_x_ref, halo_bc_ref, pos_ref, prm_ref, head_ref,
    expand_ref, mixed_ref, g_ref, state_ref, dyo_ref, coef_ref, grad_x_ref, grad_bcdt_ref, small_ref, ext, d_state,
    later, later_pos,
):
    @pl.when(pl.program_id(0) == 0)
    def _():
        d_state[...] = jnp.zeros_like(d_state)
        later[...] = jnp.zeros_like(later)
        later_pos[...] = jnp.zeros_like(later_pos)
        small_ref[...] = jnp.zeros_like(small_ref)

    rows = CHUNK
    ext[:8, :width] = halo_x_ref[...].astype(F32)[8:, :]
    ext[:8, width:] = halo_bc_ref[...].astype(F32)[8:, : 2 * LANES]
    pos = pos_ref[...]
    k = prepare_chunk(
        width,
        zx_ref[:, width:],
        bcdt_ref[:, : 2 * LANES],
        bcdt_ref[:, 2 * LANES :],
        pos,
        prm_ref,
        head_ref,
        expand_ref,
        ext,
    )
    xc = k["xc"]
    z = zx_ref[:, :width].astype(F32)
    r_col = coef_ref[:, 0:1]
    back_col = coef_ref[:, 8:9]
    g = g_ref[...]
    dyo = dyo_ref[...].astype(F32)
    skip = prm_ref[6:7, :width]
    y = mixed_ref[...] - skip * xc
    dg = r_col * (dyo * prm_ref[5:6, :width]) - g * back_col
    dy = dg * (z * jax.nn.sigmoid(z))
    small_ref[5:6, :width] += jnp.sum(dyo * g * r_col, axis=0, keepdims=True)
    small_ref[6:7, :width] += jnp.sum(dy * xc, axis=0, keepdims=True)

    stepped = (xc * k["dt_w"]).astype(BF16)
    dy_low = dy.astype(BF16)
    d_held = d_state[...]
    d_held_low = d_held.astype(BF16)
    held_low = state_ref[0]
    weighted = (stepped.astype(F32) * k["tail_w"]).astype(BF16)
    dy_in = (dy * k["in_w"]).astype(BF16)
    from_state = dot(k["b"], d_held_low) * k["tail_w"]
    dc = dot(dy_in, held_low, CONTRACT_LAST)
    db = dot(weighted, d_held_low, CONTRACT_LAST)
    d_state[...] = k["carried_w"] * d_held + dot(k["c"], dy_in, CONTRACT_FIRST)
    d_scores = jnp.zeros((rows, rows), F32)
    d_stepped = []
    for pair in range(width // LANES):
        lanes = slice(pair * LANES, (pair + 1) * LANES)
        decay_a = decay_of(k, 2 * pair)
        decay_b = decay_of(k, 2 * pair + 1)
        mixing = jnp.concatenate(
            [(decay_a * k["scores"]).astype(BF16), (decay_b * k["scores"]).astype(BF16)], axis=0
        )
        d_mixing = dot(dy_low[:, lanes], halves(stepped[:, lanes]), CONTRACT_LAST)
        d_scores = d_scores + decay_a * d_mixing[:, :rows] + decay_b * d_mixing[:, rows:]
        d_stepped.append(dot(mixing, halves(dy_low[:, lanes]), CONTRACT_FIRST))
    d_stepped = jnp.concatenate(d_stepped, axis=1) + from_state
    d_scores = jnp.where(k["same"], d_scores, 0.0).astype(BF16)
    dc = dc + dot(d_scores, k["b"])
    db = db + dot(d_scores, k["c"], CONTRACT_FIRST)
    dxc = skip * dy + d_stepped * k["dt_w"]

    stepped_f = stepped.astype(F32)
    tail_term = jnp.sum(stepped_f * from_state, axis=0, keepdims=True) + k["carried_w"] * jnp.sum(
        held_low.astype(F32) * d_held, axis=0, keepdims=True
    )
    gathered = two_parts(
        jnp.concatenate(
            [
                d_stepped * xc,
                dy_low.astype(F32) * y - stepped_f * d_stepped,
                jnp.broadcast_to(tail_term, (8, width)),
            ],
            axis=0,
        )
    )
    expand = expand_ref[:LANES, :]
    narrow = dot(gathered[:, :width], expand, CONTRACT_LAST) + dot(gathered[:, width:], expand, CONTRACT_LAST)
    d_dt = narrow[:rows]
    d_cum = narrow[rows : 2 * rows]
    upper = (k["s_idx"] >= k["t_idx"]).astype(F32)
    d_decay = (
        lax.dot_general(
            upper, d_cum, (((1,), (0,)), ((), ())), precision=HIGHEST, preferred_element_type=F32
        )
        + narrow[2 * rows : 2 * rows + 1]
    )
    d_raw = (d_dt - d_decay * head_ref[1:2, :]) * jax.nn.sigmoid(k["raw"])
    small_ref[7:8, :LANES] += jnp.sum(d_raw, axis=0, keepdims=True)
    small_ref[7:8, LANES : 2 * LANES] += jnp.sum(d_decay * k["log_decay"], axis=0, keepdims=True)
    grad_bcdt_ref[:, 2 * LANES :] = d_raw.astype(BF16)

    pre, sig = k["pre"], k["sig"]
    d_pre = jnp.concatenate([dxc, db, dc], axis=1) * (sig * (1.0 + pre * (1.0 - sig)))
    small_ref[4:5, :] += jnp.sum(d_pre, axis=0, keepdims=True)
    later[:rows, :] = d_pre
    later_pos[:rows, :] = jnp.broadcast_to(pos, (rows, LANES))
    d_in = prm_ref[3:4, :] * d_pre
    small_ref[3:4, :] += jnp.sum(d_pre * ext[8:, :], axis=0, keepdims=True)
    for back in (1, 2, 3):
        here = (pos >= back).astype(F32)
        small_ref[3 - back : 4 - back, :] += jnp.sum(
            d_pre * (ext[8 - back : 8 - back + rows, :] * here), axis=0, keepdims=True
        )
        there = (later_pos[back : back + rows, 0:1] >= back).astype(F32)
        d_in = d_in + prm_ref[3 - back : 4 - back, :] * (later[back : back + rows, :] * there)
    grad_x_ref[...] = d_in[:, :width].astype(BF16)
    grad_bcdt_ref[:, : 2 * LANES] = d_in[:, width:].astype(BF16)
    later[rows:, :] = later[:8, :]
    later_pos[rows:, :] = later_pos[:8, :]


def mixer_forward(width, zx, bcdt, pos, prm, head_prm, expand):
    rows = zx.shape[0]
    chunks = rows // CHUNK

    def tokens(columns):
        return pl.BlockSpec((CHUNK, columns), lambda i: (i, 0))

    def whole(array):
        return pl.BlockSpec(array.shape, lambda i: (0, 0))

    return pl.pallas_call(
        functools.partial(forward_kernel, width),
        out_shape=(
            jax.ShapeDtypeStruct((rows, width), F32),
            jax.ShapeDtypeStruct((rows, width), F32),
            jax.ShapeDtypeStruct((8, rows), F32),
            jax.ShapeDtypeStruct((chunks, LANES, width), BF16),
        ),
        grid=(chunks,),
        in_specs=[tokens(2 * width), tokens(3 * LANES), tokens(1), whole(prm), whole(head_prm), whole(expand)],
        out_specs=(
            tokens(width),
            tokens(width),
            pl.BlockSpec((8, CHUNK), lambda i: (0, i)),
            pl.BlockSpec((1, LANES, width), lambda i: (i, 0, 0)),
        ),
        scratch_shapes=[
            pltpu.VMEM((CHUNK + 8, width + 2 * LANES), F32),
            pltpu.VMEM((LANES, width), F32),
        ],
        compiler_params=pltpu.CompilerParams(
            dimension_semantics=("arbitrary",), vmem_limit_bytes=40 * 1024 * 1024
        ),
    )(zx, bcdt, pos, prm, head_prm, expand)


def mixer_backward(width, zx, bcdt, pos, prm, head_prm, expand, mixed, g, states, dyo, coef):
    rows = zx.shape[0]
    chunks = rows // CHUNK

    def tokens(columns):
        return pl.BlockSpec((CHUNK, columns), lambda i: (chunks - 1 - i, 0))

    def before(columns, place):
        return pl.BlockSpec(
            (16, columns), lambda i: (jnp.maximum((chunks - 1 - i) * (CHUNK // 16) - 1, 0), place)
        )

    def whole(array):
        return pl.BlockSpec(array.shape, lambda i: (0, 0))

    return pl.pallas_call(
        functools.partial(backward_kernel, width),
        out_shape=(
            jax.ShapeDtypeStruct((rows, width), BF16),
            jax.ShapeDtypeStruct((rows, 3 * LANES), BF16),
            jax.ShapeDtypeStruct((8, width + 2 * LANES), F32),
        ),
        grid=(chunks,),
        in_specs=[
            tokens(2 * width),
            tokens(3 * LANES),
            before(width, 1),
            before(3 * LANES, 0),
            tokens(1),
            whole(prm),
            whole(head_prm),
            whole(expand),
            tokens(width),
            tokens(width),
            pl.BlockSpec((1, LANES, width), lambda i: (chunks - 1 - i, 0, 0)),
            tokens(width),
            tokens(LANES),
        ],
        out_specs=(
            tokens(width),
            tokens(3 * LANES),
            pl.BlockSpec((8, width + 2 * LANES), lambda i: (0, 0)),
        ),
        scratch_shapes=[
            pltpu.VMEM((CHUNK + 8, width + 2 * LANES), F32),
            pltpu.VMEM((LANES, width), F32),
            pltpu.VMEM((CHUNK + 8, width + 2 * LANES), F32),
            pltpu.VMEM((CHUNK + 8, LANES), jnp.int32),
        ],
        compiler_params=pltpu.CompilerParams(
            dimension_semantics=("arbitrary",), vmem_limit_bytes=48 * 1024 * 1024
        ),
        cost_estimate=pl.CostEstimate(flops=rows * width * 2048, bytes_accessed=rows * width * 20, transcendentals=0),
    )(zx, bcdt, zx, bcdt, pos, prm, head_prm, expand, mixed, g, states, dyo, coef)


MESH = pl.DeviceIdType.MESH


def tp_places():
    me = lax.axis_index("tp")
    return me, me + 1 - 2 * lax.rem(me, 2), lax.rem(me + 2, 4), 3 - me


def greet(peers):
    barrier = pltpu.get_barrier_semaphore()
    for peer in peers:
        pl.semaphore_signal(barrier, inc=1, device_id=peer, device_id_type=MESH)
    pl.semaphore_wait(barrier, len(peers))


def send(src, dst, send_sem, recv_sem, peer):
    return pltpu.make_async_remote_copy(
        src_ref=src, dst_ref=dst, send_sem=send_sem, recv_sem=recv_sem, device_id=peer, device_id_type=MESH
    )


class Gather:
    def __init__(self, whole, rows, send_sems, recv_sems, own=None):
        me, side, up, _ = tp_places()
        half = rows // 2

        def part(place, start, count):
            return whole.at[pl.ds(pl.multiple_of(place * rows + start, half), count)]

        own = part(me, 0, rows) if own is None else own
        self.to_side = send(own, part(me, 0, rows), send_sems.at[0], recv_sems.at[0], {"tp": side})
        self.to_up = send(own, part(me, 0, rows), send_sems.at[1], recv_sems.at[1], {"tp": up})
        self.pass_up = send(
            part(side, 0, half), part(side, 0, half), send_sems.at[2], recv_sems.at[2], {"tp": up}
        )
        self.pass_side = send(
            part(up, half, half), part(up, half, half), send_sems.at[3], recv_sems.at[3], {"tp": side}
        )

    def start(self):
        self.to_side.start()
        self.to_up.start()

    def forward(self):
        self.to_side.wait_recv()
        self.pass_up.start()
        self.to_up.wait_recv()
        self.pass_side.start()

    def finish(self):
        self.pass_up.wait_recv()
        self.pass_side.wait_recv()

    def end(self):
        for copy in (self.to_side, self.to_up, self.pass_up, self.pass_side):
            copy.wait_send()


def set_up(width, heads, inner, taps_ref, flat_ref, lens_ref, prm, head, expand, pos):
    rank = lax.axis_index("tp")
    channels = taps_ref.shape[1]
    own = pl.ds(pl.multiple_of(rank * width, LANES), width)
    own_gain = pl.ds(pl.multiple_of(channels + rank * width, LANES), width)
    prm[...] = jnp.zeros_like(prm)
    prm[0:4, :width] = taps_ref[:, own]
    prm[0:4, width:] = taps_ref[:, inner:]
    prm[4:5, :width] = flat_ref[:, own]
    prm[4:5, width:] = flat_ref[:, inner:channels]
    prm[5:6, :width] = flat_ref[:, own_gain]
    lane = lax.broadcasted_iota(jnp.int32, (LANES, LANES), 1)
    pick = ((lax.broadcasted_iota(jnp.int32, (LANES, LANES), 0) == lane + rank * heads) & (lane < heads)).astype(F32)
    start = channels + inner
    tiles = [jnp.broadcast_to(flat_ref[:, start + n * LANES : start + (n + 1) * LANES], (8, LANES)) for n in range(3)]
    tiles[1] = jnp.exp(tiles[1])
    picked = lax.dot_general(
        jnp.concatenate(tiles, axis=0), pick, (((1,), (0,)), ((), ())), precision=HIGHEST, preferred_element_type=F32
    )
    head[...] = jnp.concatenate([picked[0:1], picked[8:9], jnp.zeros((6, LANES), F32)], axis=0)
    row = lax.broadcasted_iota(jnp.int32, (2 * LANES, width), 0)
    column = lax.broadcasted_iota(jnp.int32, (2 * LANES, width), 1)
    expand[...] = (lax.rem(row, LANES) == column // (width // heads)).astype(F32).astype(BF16)
    prm[6:7, :width] = dot(two_parts(picked[16:24]), expand[...])[0:1]
    starts = [jnp.int32(0)]
    for n in range(lens_ref.shape[1] - 1):
        starts.append(starts[-1] + lens_ref[0, n])

    def place(i, carry):
        token = lax.broadcasted_iota(jnp.int32, (CHUNK, 1), 0) + i * CHUNK
        begun = jnp.zeros((CHUNK, 1), jnp.int32)
        for first in starts[1:]:
            begun = jnp.where(token >= first, first, begun)
        pos[pl.ds(pl.multiple_of(i * CHUNK, CHUNK), CHUNK), :] = token - begun
        return carry

    lax.fori_loop(0, pos.shape[0] // CHUNK, place, 0)


def first_kernel(
    inner, heads, own_cols, x_ref, gain_ref, small_ref, taps_ref, flat_ref, lens_ref, wz_ref, wx_ref, w_out_ref, d_own_ref,
    u_out, zx_out, bcdt_out, wbc_out, mixed_out, g_out, yo_out, yo_t_out, state_out, d_out, dyo_out, coef_out, pos_out,
    prm_out, head_out, expand_out,
    weights, w_out, u, zx, bcdt, wbc, mixed, g, yo, yo_t, states, d, dyo, coef, pos, prm, head, expand, ext, state, sums,
    acc, sems, sum_sems, load_sems, store_sems,
):
    rows, model = x_ref.shape
    total, width = mixed.shape
    chunks = total // CHUNK
    me, side, up, far = tp_places()
    dp = lax.axis_index("dp")
    parity = lax.rem(dp, 2)
    partner = {"dp": dp + 1 - 2 * parity}

    def block(place):
        return pl.ds(pl.multiple_of(place * rows, rows), rows)

    loads = [
        pltpu.make_async_copy(wz_ref, weights.at[:, :width], load_sems.at[0]),
        pltpu.make_async_copy(wx_ref, weights.at[:, width:], load_sems.at[1]),
        pltpu.make_async_copy(w_out_ref, w_out, load_sems.at[2]),
        pltpu.make_async_copy(d_own_ref, d.at[block(me)], load_sems.at[3]),
    ]
    for copy in loads:
        copy.start()
    stores = []

    def keep(source, target):
        copy = pltpu.make_async_copy(source, target, store_sems.at[len(stores)])
        copy.start()
        stores.append(copy)

    bc_own = pl.ds(pl.multiple_of(parity * LANES, LANES), LANES)
    wbc[pl.ds(pl.multiple_of(parity * LANES + me * own_cols, own_cols), own_cols), :] = small_ref[
        pl.ds(pl.multiple_of(parity * own_cols, own_cols), own_cols), :
    ]
    greet([{"tp": side}, {"tp": up}, {"tp": far}, partner])
    small_gather = Gather(wbc.at[bc_own], own_cols, sems.at[0], sems.at[1])
    small_gather.start()

    def norm(i, carry):
        piece = pl.ds(pl.multiple_of(i * 32, 32), 32)
        x = x_ref[piece, :].astype(F32)
        scale = lax.rsqrt(jnp.mean(x * x, axis=-1, keepdims=True) + EPSILON)
        u[pl.ds(pl.multiple_of(me * rows + i * 32, 32), 32), :] = (x * scale * gain_ref[...]).astype(BF16)
        return carry

    lax.fori_loop(0, rows // 32, norm, 0)
    gather = Gather(u, rows, sems.at[2], sems.at[3])
    gather.start()
    wbc[2 * LANES :, :] = jnp.zeros((LANES, model), BF16)
    wbc[2 * LANES : 2 * LANES + heads, :] = small_ref[2 * own_cols :, :]
    set_up(width, heads, inner, taps_ref, flat_ref, lens_ref, prm, head, expand, pos)
    keep(pos, pos_out)
    keep(prm, prm_out)
    keep(head, head_out)
    keep(expand, expand_out)
    loads[0].wait()
    loads[1].wait()

    def project(place):
        piece = block(place)

        def tile(n, carry):
            columns = pl.ds(pl.multiple_of(n * 256, 256), 256)
            zx[piece, columns] = dot(u[piece, :], weights[:, columns]).astype(BF16)
            return carry

        lax.fori_loop(0, 2 * width // 256, tile, 0)

    def project_small(place):
        bcdt[block(place), :] = dot(u[block(place), :], wbc[...], CONTRACT_LAST).astype(BF16)

    small_gather.forward()
    project(me)
    small_gather.finish()
    trade = send(wbc.at[bc_own], wbc.at[bc_own], sems.at[6, 0], sems.at[6, 1], partner)
    trade.start()
    gather.forward()
    project(side)
    project(up)
    trade.wait()
    keep(wbc, wbc_out)
    project_small(me)
    project_small(side)
    project_small(up)
    gather.finish()
    loads[3].wait()
    d_gather = Gather(d, rows, sems.at[4], sems.at[5])
    d_gather.start()
    keep(u, u_out)
    project(far)
    project_small(far)
    keep(zx, zx_out)
    keep(bcdt, bcdt_out)

    state[...] = jnp.zeros_like(state)
    ext[...] = jnp.zeros_like(ext)

    def chunk(i, carry):
        forward_chunk(
            width, i, zx, bcdt, pos, prm, head, expand, mixed, g, sums.at[0, 0], states, ext, state
        )
        return carry

    lax.fori_loop(0, chunks, chunk, 0)

    def exchange(which):
        copies = [
            send(
                sums.at[which, 0], sums.at[which, 1 + n], sum_sems.at[which, 0, n], sum_sems.at[which, 1, n], {"tp": peer}
            )
            for n, peer in enumerate((side, up, far))
        ]
        for copy in copies:
            copy.start()
        return copies

    copies = exchange(0)
    keep(mixed, mixed_out)
    keep(g, g_out)
    keep(states, state_out)
    loads[2].wait()

    def back_to_heads(place):
        piece = block(place)
        acc[...] = jnp.zeros_like(acc)

        def tile(n, carry):
            columns = pl.ds(pl.multiple_of(n * 256, 256), 256)
            low = dot(d[piece, :], w_out[columns, :], CONTRACT_LAST).astype(BF16)
            dyo[piece, columns] = low
            both = low.astype(F32) * prm[5:6, columns] * g[piece, columns]
            acc[...] += both[:, :LANES] + both[:, LANES:]
            return carry

        lax.fori_loop(0, width // 256, tile, 0)
        column = jnp.sum(acc[...], axis=1, keepdims=True)
        sums[1, 0, :, piece] = jnp.broadcast_to(column, (rows, LANES)).T[:8, :]
        keep(dyo.at[piece], dyo_out.at[piece])

    d_gather.forward()
    back_to_heads(me)
    for copy in copies:
        copy.wait()

    def gate(i, carry):
        piece = pl.ds(pl.multiple_of(i * CHUNK, CHUNK), CHUNK)
        squares = sums[0, 0, :, piece] + sums[0, 1, :, piece] + sums[0, 2, :, piece] + sums[0, 3, :, piece]
        scale = lax.rsqrt(squares / inner + EPSILON)
        columns = jnp.concatenate([scale, jnp.zeros((LANES - 8, LANES), F32)], axis=0).T
        gated = g[piece, :] * columns[:, 0:1] * prm[5:6, :width]
        yo[piece, :] = gated.astype(BF16)
        yo_t[:, piece] = gated.T.astype(BF16)
        return carry

    lax.fori_loop(0, chunks, gate, 0)
    keep(yo, yo_out)
    keep(yo_t, yo_t_out)
    back_to_heads(side)
    back_to_heads(up)
    d_gather.finish()
    keep(d, d_out)
    back_to_heads(far)
    copies = exchange(1)
    for copy in copies:
        copy.wait()

    def weigh(i, carry):
        piece = pl.ds(pl.multiple_of(i * CHUNK, CHUNK), CHUNK)
        squares = sums[0, 0, :, piece] + sums[0, 1, :, piece] + sums[0, 2, :, piece] + sums[0, 3, :, piece]
        cross = sums[1, 0, :, piece] + sums[1, 1, :, piece] + sums[1, 2, :, piece] + sums[1, 3, :, piece]
        scale = lax.rsqrt(squares / inner + EPSILON)
        back = scale * scale * scale * (cross / inner)
        coef[piece, :] = jnp.concatenate([scale, back, jnp.zeros((LANES - 16, LANES), F32)], axis=0).T
        return carry

    lax.fori_loop(0, chunks, weigh, 0)
    keep(coef, coef_out)
    small_gather.end()
    gather.end()
    d_gather.end()
    for copy in stores:
        copy.wait()


def first_part(inner, heads, own_cols, x_in, gain, small, taps, flat, lens, w_z, w_x, w_out, d_out):
    rows, model = x_in.shape
    total = 4 * rows
    width = w_z.shape[1]
    chunks = total // CHUNK
    vmem = pl.BlockSpec(memory_space=pltpu.VMEM)
    anywhere = pl.BlockSpec(memory_space=pl.ANY)
    results = [
        ((total, model), BF16),
        ((total, 2 * width), BF16),
        ((total, 3 * LANES), BF16),
        ((3 * LANES, model), BF16),
        ((total, width), F32),
        ((total, width), F32),
        ((total, width), BF16),
        ((width, total), BF16),
        ((chunks, LANES, width), BF16),
        ((total, model), BF16),
        ((total, width), BF16),
        ((total, LANES), F32),
        ((total, 1), jnp.int32),
        ((8, width + 2 * LANES), F32),
        ((8, LANES), F32),
        ((2 * LANES, width), BF16),
    ]
    return pl.pallas_call(
        functools.partial(first_kernel, inner, heads, own_cols),
        out_shape=[jax.ShapeDtypeStruct(*result) for result in results],
        in_specs=[vmem] * 5 + [pl.BlockSpec(memory_space=pltpu.SMEM)] + [anywhere] * 4,
        out_specs=[anywhere] * len(results),
        scratch_shapes=[pltpu.VMEM((model, 2 * width), BF16), pltpu.VMEM((width, model), BF16)]
        + [pltpu.VMEM(*result) for result in results]
        + [
            pltpu.VMEM((CHUNK + 8, width + 2 * LANES), F32),
            pltpu.VMEM((LANES, width), F32),
            pltpu.VMEM((2, 4, 8, total), F32),
            pltpu.VMEM((rows, LANES), F32),
            pltpu.SemaphoreType.DMA((7, 4)),
            pltpu.SemaphoreType.DMA((2, 2, 3)),
            pltpu.SemaphoreType.DMA((4,)),
            pltpu.SemaphoreType.DMA((24,)),
        ],
        compiler_params=pltpu.CompilerParams(
            collective_id=0, has_side_effects=True, vmem_limit_bytes=60 * 1024 * 1024
        ),
    )(x_in, gain, small, taps, flat, lens, w_z, w_x, w_out, d_out)


def add_up_kernel(own_ref, out_ref, over_dp, dp_sems, tp_sems, local_sem):
    dp_count = over_dp.shape[0]
    tp_count = out_ref.shape[0]
    d = lax.axis_index("dp")
    t = lax.axis_index("tp")
    greet(
        [{"dp": lax.rem(d + n, dp_count)} for n in range(1, dp_count)]
        + [{"tp": lax.rem(t + n, tp_count)} for n in range(1, tp_count)]
    )
    copies = [
        send(own_ref, over_dp.at[n], dp_sems.at[0, n], dp_sems.at[1, n], {"dp": lax.rem(d + n, dp_count)})
        for n in range(1, dp_count)
    ]
    for copy in copies:
        copy.start()
    for copy in copies:
        copy.wait()
    total = own_ref[...]
    for n in range(1, dp_count):
        total = total + over_dp[n]
    over_dp[0] = total
    keep = pltpu.make_async_copy(over_dp.at[0], out_ref.at[t], local_sem)
    keep.start()
    copies = [
        send(over_dp.at[0], out_ref.at[t], tp_sems.at[0, n], tp_sems.at[1, n], {"tp": lax.rem(t + n, tp_count)})
        for n in range(1, tp_count)
    ]
    for copy in copies:
        copy.start()
    for copy in copies:
        copy.wait()
    keep.wait()


def add_up(own):
    dp_count, tp_count = lax.axis_size("dp"), lax.axis_size("tp")
    vmem = pl.BlockSpec(memory_space=pltpu.VMEM)
    return pl.pallas_call(
        add_up_kernel,
        out_shape=jax.ShapeDtypeStruct((tp_count,) + own.shape, F32),
        in_specs=[vmem],
        out_specs=vmem,
        scratch_shapes=[
            pltpu.VMEM((dp_count,) + own.shape, F32),
            pltpu.SemaphoreType.DMA((2, dp_count)),
            pltpu.SemaphoreType.DMA((2, tp_count)),
            pltpu.SemaphoreType.DMA,
        ],
        compiler_params=pltpu.CompilerParams(collective_id=2, has_side_effects=True),
    )(own)


def swap(array, axis, bits):
    return lax.ppermute(array, axis, [(i, i ^ bits) for i in range(lax.axis_size(axis))])


def scatter_tp(parts):
    count = lax.axis_size("tp")
    rank = lax.axis_index("tp")
    if count != 4:
        blocks = jnp.concatenate([parts(k) for k in range(count)], axis=0)
        return lax.psum_scatter(blocks, "tp", scatter_dimension=0, tiled=True).astype(F32)
    far = parts(rank ^ 3)
    half = far.shape[0] // 2
    a = swap(far[:half], "tp", 1)
    b = swap(far[half:], "tp", 2)
    side = parts(rank ^ 1)
    up = parts(rank ^ 2)
    to_side = jnp.concatenate([side[:half], side[half:] + b], axis=0)
    to_up = jnp.concatenate([up[:half] + a, up[half:]], axis=0)
    c = swap(to_side, "tp", 1)
    d = swap(to_up, "tp", 2)
    return parts(rank).astype(F32) + c.astype(F32) + d.astype(F32)


def in_norm_scale(values):
    return lax.rsqrt(jnp.mean(values * values, axis=-1, keepdims=True) + EPSILON)


def body(
    x_in, norm_gain, w_z, w_x, w_b, w_c, w_dt, conv_w, conv_b, dt_bias, a_log, d_skip, gate_gain, w_out,
    doc_lens, d_out,
):
    tp_count = lax.axis_size("tp")
    rank = lax.axis_index("tp")
    dev_rows, model = x_in.shape
    rows = dev_rows * tp_count
    inner = gate_gain.shape[0]
    width = w_z.shape[1]
    heads = w_dt.shape[1]
    state_size = (conv_w.shape[0] - inner) // 2
    head_size = width // heads
    own_cols = w_b.shape[1]

    x_float = x_in.astype(F32)
    r_in = in_norm_scale(x_float)
    small_weights = jnp.concatenate([w_b, w_c, w_dt], axis=1).T
    if tp_count == 4:
        lanes = jnp.zeros((LANES - d_skip.shape[0],), F32)
        flat = jnp.concatenate([conv_b, gate_gain, dt_bias, lanes, a_log, lanes, d_skip, lanes])[None, :]
        (
            gathered, zx, bcdt, w_bcdt, mixed, g, yo, yo_t, states, grad_gathered, dyo, coef, pos, prm, head_prm, expand
        ) = first_part(
            inner, heads, own_cols, x_in, norm_gain[None, :], small_weights, conv_w.T, flat, doc_lens, w_z, w_x, w_out,
            d_out,
        )
        gain_own = prm[5, :width]
    else:
        normed = (x_float * r_in * norm_gain[None, :]).astype(BF16)
        gathered = lax.all_gather(normed, "tp", axis=0, tiled=True)
        w_bc = lax.all_gather(small_weights[: 2 * own_cols], "tp", axis=0).reshape(tp_count, 2, own_cols, model)
        w_bcdt = jnp.concatenate(
            [
                jnp.swapaxes(w_bc, 0, 1).reshape(2 * state_size, model),
                small_weights[2 * own_cols :],
                jnp.zeros((LANES - heads, model), BF16),
            ],
            axis=0,
        )
        zx = dot(gathered, jnp.concatenate([w_z, w_x], axis=1)).astype(BF16)
        bcdt = dot(gathered, w_bcdt, CONTRACT_LAST).astype(BF16)
        lengths = doc_lens[0]
        doc_starts = jnp.cumsum(lengths) - lengths
        positions = jnp.arange(rows, dtype=jnp.int32)
        started = jnp.where(positions[:, None] >= doc_starts[None, :], doc_starts[None, :], 0)
        pos = (positions - jnp.max(started, axis=1))[:, None]

        def own(array, count):
            return lax.dynamic_slice_in_dim(array, rank * count, count, axis=0)

        taps = jnp.concatenate([own(conv_w[:inner], width), conv_w[inner:]], axis=0).T
        bias = jnp.concatenate([own(conv_b[:inner], width), conv_b[inner:]])
        pad_bc = jnp.zeros((2 * state_size,), F32)
        gain_own = own(gate_gain, width)
        skip_own = jnp.repeat(own(d_skip, heads), head_size)
        prm = jnp.concatenate(
            [
                taps,
                bias[None],
                jnp.concatenate([gain_own, pad_bc])[None],
                jnp.concatenate([skip_own, pad_bc])[None],
                jnp.zeros((1, width + 2 * state_size), F32),
            ],
            axis=0,
        )
        pad_heads = jnp.zeros((LANES - heads,), F32)
        head_prm = jnp.concatenate(
            [
                jnp.concatenate([own(dt_bias, heads), pad_heads])[None],
                jnp.concatenate([jnp.exp(own(a_log, heads)), pad_heads])[None],
                jnp.zeros((6, LANES), F32),
            ],
            axis=0,
        )
        expand = (
            (jnp.arange(2 * LANES) % LANES)[:, None] == (jnp.arange(width) // head_size)[None, :]
        ).astype(BF16)
        mixed, g, g_sum, states = mixer_forward(width, zx, bcdt, pos, prm, head_prm, expand)
        grad_gathered = lax.all_gather(d_out, "tp", axis=0, tiled=True)
        dyo = dot(grad_gathered, w_out, CONTRACT_LAST).astype(BF16)
        eg_sum = jnp.sum(dyo.astype(F32) * gain_own[None, :] * g, axis=1)
        g_total, eg_total = lax.psum((g_sum[0], eg_sum), "tp")
        r_gate = lax.rsqrt(g_total / inner + EPSILON)
        zeros = jnp.zeros_like(r_gate)
        coef = jnp.stack([r_gate] + [zeros] * 7 + [r_gate**3 * (eg_total / inner)] + [zeros] * (LANES - 9), axis=1)
        yo = (g * r_gate[:, None] * gain_own[None, :]).astype(BF16)

    def scatter_dp(partial):
        return lax.psum_scatter(partial.astype(BF16), "dp", scatter_dimension=0, tiled=True).astype(F32)

    grad_w_out = scatter_dp(dot(grad_gathered, yo, CONTRACT_FIRST)).T
    z = zx[:, :width].astype(F32)
    sig_z = jax.nn.sigmoid(z)
    dg = coef[:, 0:1] * (dyo.astype(F32) * gain_own[None, :]) - g * coef[:, 8:9]
    dz = (dg * mixed * (sig_z * (1.0 + z * (1.0 - sig_z)))).astype(BF16)
    grad_w_z = scatter_dp(dot(gathered, dz, CONTRACT_FIRST))

    def block(array, k):
        return lax.dynamic_slice_in_dim(array, k * dev_rows, dev_rows, axis=0)

    block_out = (x_float + scatter_tp(lambda k: dot(block(yo, k), w_out).astype(BF16))).astype(BF16)

    grad_xs, grad_bcdt, small = mixer_backward(
        width, zx, bcdt, pos, prm, head_prm, expand, mixed, g, states, dyo, coef
    )

    d_bc = grad_bcdt[:, : 2 * state_size]
    by_owner = jnp.moveaxis(d_bc.reshape(rows, 2, tp_count, own_cols), 2, 0).reshape(tp_count, rows, 2 * own_cols)
    if tp_count == 4:
        d_bc_own = lax.dynamic_index_in_dim(by_owner, rank, 0, False).astype(F32)
        for bits in (1, 2, 3):
            sent = lax.dynamic_index_in_dim(by_owner, rank ^ bits, 0, False)
            d_bc_own = d_bc_own + swap(sent, "tp", bits).astype(F32)
    else:
        d_bc_own = lax.psum_scatter(by_owner.astype(F32), "tp", scatter_dimension=0, tiled=False)
    last = jnp.concatenate(
        [
            grad_xs,
            d_bc_own.astype(BF16),
            grad_bcdt[:, 2 * state_size : 2 * state_size + heads],
            jnp.zeros((rows, (-2 * own_cols - heads) % LANES), BF16),
        ],
        axis=1,
    )
    grad_last = scatter_dp(dot(gathered, last, CONTRACT_FIRST))

    def du_part(k):
        return (
            dot(block(dz, k), w_z, CONTRACT_LAST)
            + dot(block(grad_xs, k), w_x, CONTRACT_LAST)
            + dot(block(grad_bcdt, k), w_bcdt)
        )

    gain_parts = []

    def du_low(k):
        part = du_part(k)
        gain_parts.append(jnp.sum(part * block(gathered, k).astype(F32), axis=0))
        return part.astype(BF16)

    du = scatter_tp(du_low)
    gain_part = sum(gain_parts) / norm_gain
    e_in = du * norm_gain[None, :]
    grad_x = d_out.astype(F32) + r_in * e_in - x_float * (
        r_in**3 * jnp.mean(e_in * x_float, axis=-1, keepdims=True)
    )

    packed = jnp.concatenate([small, gain_part.reshape(8, model // 8)], axis=1)
    sums = add_up(packed)
    channels = jnp.swapaxes(sums[:, :7, :width], 0, 1).reshape(7, inner)
    shared = jnp.sum(sums[:, :5, width : width + 2 * state_size], axis=0)
    grad_conv = jnp.concatenate([channels[:5], shared], axis=1)
    grad_norm_gain = jnp.sum(sums[:, :, width + 2 * state_size :], axis=0).reshape(model)
    return (
        block_out,
        grad_x,
        grad_norm_gain,
        grad_w_z,
        grad_last[:, :width],
        grad_last[:, width : width + own_cols],
        grad_last[:, width + own_cols : width + 2 * own_cols],
        grad_last[:, width + 2 * own_cols : width + 2 * own_cols + heads],
        grad_conv[:4].T,
        grad_conv[4],
        sums[:, 7, :heads].reshape(-1),
        sums[:, 7, LANES : LANES + heads].reshape(-1),
        channels[6].reshape(heads * tp_count, head_size).sum(axis=1),
        channels[5],
        grad_w_out,
    )


def solution(mesh):
    rows = P(("dp", "tp"), None)
    columns = P(None, "tp")
    both = P("dp", "tp")
    none = P()
    return jax.shard_map(
        body,
        mesh=mesh,
        in_specs=(
            rows, none, columns, columns, columns, columns, columns, none, none, none, none, none, none,
            P("tp", None), P("dp", None), rows,
        ),
        out_specs=(
            rows, rows, none, both, both, both, both, both, none, none, none, none, none, none, P("tp", "dp"),
        ),
        check_vma=False,
    )
```

```python
import functools

import jax
import jax.numpy as jnp
from jax import lax
from jax.experimental import pallas as pl
from jax.experimental.pallas import tpu as pltpu
from jax.sharding import PartitionSpec as P

EPSILON = 1e-05
HIGHEST = lax.Precision.HIGHEST
F32 = jnp.float32
BF16 = jnp.bfloat16
CHUNK = 128
LANES = 128
CONTRACT_FIRST = (((0,), (0,)), ((), ()))
CONTRACT_LAST = (((1,), (1,)), ((), ()))


def dot(a, b, dims=(((1,), (0,)), ((), ()))):
    return lax.dot_general(a, b, dims, preferred_element_type=F32)


def two_parts(v):
    high = v.astype(BF16)
    return jnp.concatenate([high, (v - high.astype(F32)).astype(BF16)], axis=1)


def prepare_chunk(width, x, bc, raw_dt, pos, prm_ref, head_ref, expand_ref, ext):
    rows = CHUNK
    ext[8:, :width] = x.astype(F32)
    ext[8:, width:] = bc.astype(F32)
    pre = prm_ref[3:4, :] * ext[8:, :] + prm_ref[4:5, :]
    for back in (1, 2, 3):
        here = (pos >= back).astype(F32)
        pre = pre + prm_ref[3 - back : 4 - back, :] * (ext[8 - back : 8 - back + rows, :] * here)
    sig = jax.nn.sigmoid(pre)
    act = pre * sig
    xc = act[:, :width]
    state_size = (act.shape[1] - width) // 2
    b_rows = act[:, width : width + state_size].astype(BF16)
    c_rows = act[:, width + state_size :].astype(BF16)
    raw = raw_dt.astype(F32) + head_ref[0:1, :]
    dt = jnp.maximum(raw, 0.0) + jnp.log1p(jnp.exp(-jnp.abs(raw)))
    log_decay = -dt * head_ref[1:2, :]
    t_idx = lax.broadcasted_iota(jnp.int32, (rows, rows), 0)
    s_idx = lax.broadcasted_iota(jnp.int32, (rows, rows), 1)
    lower = (s_idx <= t_idx).astype(F32)
    cum = lax.dot_general(
        lower, log_decay, (((1,), (0,)), ((), ())), precision=HIGHEST, preferred_element_type=F32
    )
    same = (s_idx <= t_idx) & (s_idx >= t_idx - pos)
    scores = jnp.where(same, dot(c_rows, b_rows, CONTRACT_LAST), 0.0)
    t_col = lax.broadcasted_iota(jnp.int32, (rows, 1), 0)
    pos_last = pos[rows - 1 : rows, :]
    cum_last = cum[rows - 1 : rows, :]
    inward = jnp.exp(cum) * (pos > t_col).astype(F32)
    tail = jnp.exp(cum_last - cum) * (t_col >= rows - 1 - pos_last).astype(F32)
    carried = jnp.exp(cum_last) * (pos_last >= rows).astype(F32)
    wide = dot(
        two_parts(jnp.concatenate([dt, inward, tail, jnp.broadcast_to(carried, (8, LANES))], axis=0)),
        expand_ref[...],
    )
    return dict(
        pre=pre,
        sig=sig,
        xc=xc,
        b=b_rows,
        c=c_rows,
        raw=raw,
        log_decay=log_decay,
        cum=cum,
        cum_t=cum.T,
        same=same,
        scores=scores,
        t_idx=t_idx,
        s_idx=s_idx,
        dt_w=wide[:rows],
        in_w=wide[rows : 2 * rows],
        tail_w=wide[2 * rows : 3 * rows],
        carried_w=wide[3 * rows : 3 * rows + 1],
    )


def decay_of(k, head):
    return jnp.exp(jnp.minimum(k["cum"][:, head : head + 1] - k["cum_t"][head : head + 1, :], 0.0))


def halves(pair):
    lane = lax.broadcasted_iota(jnp.int32, pair.shape, 1)
    zero = jnp.zeros_like(pair)
    return jnp.concatenate(
        [jnp.where(lane < LANES // 2, pair, zero), jnp.where(lane < LANES // 2, zero, pair)], axis=0
    )


def forward_chunk(
    width, at, zx_ref, bcdt_ref, pos_ref, prm_ref, head_ref, expand_ref, mixed_ref, g_ref, sum_ref, state_ref, ext,
    state,
):
    if isinstance(at, int):
        rows = slice(at * CHUNK, (at + 1) * CHUNK)
    else:
        rows = pl.ds(pl.multiple_of(at * CHUNK, CHUNK), CHUNK)
    ext[:8, :] = ext[CHUNK:, :]
    k = prepare_chunk(
        width,
        zx_ref[rows, width:],
        bcdt_ref[rows, : 2 * LANES],
        bcdt_ref[rows, 2 * LANES :],
        pos_ref[rows, :],
        prm_ref,
        head_ref,
        expand_ref,
        ext,
    )
    stepped = (k["xc"] * k["dt_w"]).astype(BF16)
    held = state[...]
    held_low = held.astype(BF16)
    state_ref[at] = held_low
    reached = dot(k["c"], held_low) * k["in_w"] + prm_ref[6:7, :width] * k["xc"]
    weighted = (stepped.astype(F32) * k["tail_w"]).astype(BF16)
    state[...] = k["carried_w"] * held + dot(k["b"], weighted, CONTRACT_FIRST)
    for pair in range(width // LANES):
        lanes = slice(pair * LANES, (pair + 1) * LANES)
        mixing = jnp.concatenate(
            [
                (decay_of(k, 2 * pair) * k["scores"]).astype(BF16),
                (decay_of(k, 2 * pair + 1) * k["scores"]).astype(BF16),
            ],
            axis=1,
        )
        mixed_ref[rows, lanes] = dot(mixing, halves(stepped[:, lanes])) + reached[:, lanes]
    z = zx_ref[rows, :width].astype(F32)
    g = mixed_ref[rows, :] * (z * jax.nn.sigmoid(z))
    g_ref[rows, :] = g
    total = jnp.sum(g * g, axis=1, keepdims=True)
    sum_ref[:, rows] = jnp.broadcast_to(total, (CHUNK, LANES)).T[:8, :]


def forward_kernel(
    width, zx_ref, bcdt_ref, pos_ref, prm_ref, head_ref, expand_ref, mixed_ref, g_ref, sum_ref, state_ref, ext, state
):
    @pl.when(pl.program_id(0) == 0)
    def _():
        state[...] = jnp.zeros_like(state)
        ext[...] = jnp.zeros_like(ext)

    forward_chunk(
        width, 0, zx_ref, bcdt_ref, pos_ref, prm_ref, head_ref, expand_ref, mixed_ref, g_ref, sum_ref, state_ref, ext,
        state,
    )


def backward_chunk(
    width, tokens, halo_x, halo_bc, held, zx_ref, bcdt_ref, pos_ref, prm_ref, head_ref, expand_ref, mixed_ref, g_ref,
    dyo_ref, coef_ref, grad_x_ref, grad_bcdt_ref, grad_t_ref, small_ref, ext, d_state, later, later_pos,
):
    rows = CHUNK
    ext[:8, :width] = halo_x.astype(F32)[8:, :]
    ext[:8, width:] = halo_bc.astype(F32)[8:, :]
    pos = pos_ref[tokens, :]
    k = prepare_chunk(
        width,
        zx_ref[tokens, width:],
        bcdt_ref[tokens, : 2 * LANES],
        bcdt_ref[tokens, 2 * LANES :],
        pos,
        prm_ref,
        head_ref,
        expand_ref,
        ext,
    )
    xc = k["xc"]
    z = zx_ref[tokens, :width].astype(F32)
    r_col = coef_ref[tokens, 0:1]
    back_col = coef_ref[tokens, 8:9]
    g = g_ref[tokens, :]
    dyo = dyo_ref[tokens, :].astype(F32)
    skip = prm_ref[6:7, :width]
    y = mixed_ref[tokens, :] - skip * xc
    dg = r_col * (dyo * prm_ref[5:6, :width]) - g * back_col
    dy = dg * (z * jax.nn.sigmoid(z))
    small_ref[5:6, :width] += jnp.sum(dyo * g * r_col, axis=0, keepdims=True)
    small_ref[6:7, :width] += jnp.sum(dy * xc, axis=0, keepdims=True)

    stepped = (xc * k["dt_w"]).astype(BF16)
    dy_low = dy.astype(BF16)
    d_held = d_state[...]
    d_held_low = d_held.astype(BF16)
    held_low = held
    weighted = (stepped.astype(F32) * k["tail_w"]).astype(BF16)
    dy_in = (dy * k["in_w"]).astype(BF16)
    from_state = dot(k["b"], d_held_low) * k["tail_w"]
    dc = dot(dy_in, held_low, CONTRACT_LAST)
    db = dot(weighted, d_held_low, CONTRACT_LAST)
    d_state[...] = k["carried_w"] * d_held + dot(k["c"], dy_in, CONTRACT_FIRST)
    d_scores = jnp.zeros((rows, rows), F32)
    d_stepped = []
    for pair in range(width // LANES):
        lanes = slice(pair * LANES, (pair + 1) * LANES)
        decay_a = decay_of(k, 2 * pair)
        decay_b = decay_of(k, 2 * pair + 1)
        mixing = jnp.concatenate(
            [(decay_a * k["scores"]).astype(BF16), (decay_b * k["scores"]).astype(BF16)], axis=0
        )
        d_mixing = dot(dy_low[:, lanes], halves(stepped[:, lanes]), CONTRACT_LAST)
        d_scores = d_scores + decay_a * d_mixing[:, :rows] + decay_b * d_mixing[:, rows:]
        d_stepped.append(dot(mixing, halves(dy_low[:, lanes]), CONTRACT_FIRST))
    d_stepped = jnp.concatenate(d_stepped, axis=1) + from_state
    d_scores = jnp.where(k["same"], d_scores, 0.0).astype(BF16)
    dc = dc + dot(d_scores, k["b"])
    db = db + dot(d_scores, k["c"], CONTRACT_FIRST)
    dxc = skip * dy + d_stepped * k["dt_w"]

    stepped_f = stepped.astype(F32)
    tail_term = jnp.sum(stepped_f * from_state, axis=0, keepdims=True) + k["carried_w"] * jnp.sum(
        held_low.astype(F32) * d_held, axis=0, keepdims=True
    )
    gathered = two_parts(
        jnp.concatenate(
            [
                d_stepped * xc,
                dy_low.astype(F32) * y - stepped_f * d_stepped,
                jnp.broadcast_to(tail_term, (8, width)),
            ],
            axis=0,
        )
    )
    expand = expand_ref[:LANES, :]
    narrow = dot(gathered[:, :width], expand, CONTRACT_LAST) + dot(gathered[:, width:], expand, CONTRACT_LAST)
    d_dt = narrow[:rows]
    d_cum = narrow[rows : 2 * rows]
    upper = (k["s_idx"] >= k["t_idx"]).astype(F32)
    d_decay = (
        lax.dot_general(
            upper, d_cum, (((1,), (0,)), ((), ())), precision=HIGHEST, preferred_element_type=F32
        )
        + narrow[2 * rows : 2 * rows + 1]
    )
    d_raw = (d_dt - d_decay * head_ref[1:2, :]) * jax.nn.sigmoid(k["raw"])
    small_ref[7:8, :LANES] += jnp.sum(d_raw, axis=0, keepdims=True)
    small_ref[7:8, LANES : 2 * LANES] += jnp.sum(d_decay * k["log_decay"], axis=0, keepdims=True)
    grad_bcdt_ref[tokens, 2 * LANES :] = d_raw.astype(BF16)

    pre, sig = k["pre"], k["sig"]
    d_pre = jnp.concatenate([dxc, db, dc], axis=1) * (sig * (1.0 + pre * (1.0 - sig)))
    small_ref[4:5, :] += jnp.sum(d_pre, axis=0, keepdims=True)
    later[:rows, :] = d_pre
    later_pos[:rows, :] = jnp.broadcast_to(pos, (rows, LANES))
    d_in = prm_ref[3:4, :] * d_pre
    small_ref[3:4, :] += jnp.sum(d_pre * ext[8:, :], axis=0, keepdims=True)
    for back in (1, 2, 3):
        here = (pos >= back).astype(F32)
        small_ref[3 - back : 4 - back, :] += jnp.sum(
            d_pre * (ext[8 - back : 8 - back + rows, :] * here), axis=0, keepdims=True
        )
        there = (later_pos[back : back + rows, 0:1] >= back).astype(F32)
        d_in = d_in + prm_ref[3 - back : 4 - back, :] * (later[back : back + rows, :] * there)
    grad_x_ref[tokens, :] = d_in[:, :width].astype(BF16)
    grad_bcdt_ref[tokens, : 2 * LANES] = d_in[:, width:].astype(BF16)
    later[rows:, :] = later[:8, :]
    later_pos[rows:, :] = later_pos[:8, :]
    if grad_t_ref is not None:
        grad_t_ref[:width, tokens] = d_in[:, :width].T.astype(BF16)


def backward_start(small_ref, d_state, later, later_pos):
    d_state[...] = jnp.zeros_like(d_state)
    later[...] = jnp.zeros_like(later)
    later_pos[...] = jnp.zeros_like(later_pos)
    small_ref[...] = jnp.zeros_like(small_ref)


def backward_kernel(
    width, zx_ref, bcdt_ref, halo_x_ref, halo_bc_ref, pos_ref, prm_ref, head_ref,
    expand_ref, mixed_ref, g_ref, state_ref, dyo_ref, coef_ref, grad_x_ref, grad_bcdt_ref, small_ref, ext, d_state,
    later, later_pos,
):
    @pl.when(pl.program_id(0) == 0)
    def _():
        backward_start(small_ref, d_state, later, later_pos)

    backward_chunk(
        width, slice(0, CHUNK), halo_x_ref[...], halo_bc_ref[:, : 2 * LANES], state_ref[0], zx_ref, bcdt_ref, pos_ref,
        prm_ref, head_ref, expand_ref, mixed_ref, g_ref, dyo_ref, coef_ref, grad_x_ref, grad_bcdt_ref, None, small_ref,
        ext, d_state, later, later_pos,
    )


def mixer_forward(width, zx, bcdt, pos, prm, head_prm, expand):
    rows = zx.shape[0]
    chunks = rows // CHUNK

    def tokens(columns):
        return pl.BlockSpec((CHUNK, columns), lambda i: (i, 0))

    def whole(array):
        return pl.BlockSpec(array.shape, lambda i: (0, 0))

    return pl.pallas_call(
        functools.partial(forward_kernel, width),
        out_shape=(
            jax.ShapeDtypeStruct((rows, width), F32),
            jax.ShapeDtypeStruct((rows, width), F32),
            jax.ShapeDtypeStruct((8, rows), F32),
            jax.ShapeDtypeStruct((chunks, LANES, width), BF16),
        ),
        grid=(chunks,),
        in_specs=[tokens(2 * width), tokens(3 * LANES), tokens(1), whole(prm), whole(head_prm), whole(expand)],
        out_specs=(
            tokens(width),
            tokens(width),
            pl.BlockSpec((8, CHUNK), lambda i: (0, i)),
            pl.BlockSpec((1, LANES, width), lambda i: (i, 0, 0)),
        ),
        scratch_shapes=[
            pltpu.VMEM((CHUNK + 8, width + 2 * LANES), F32),
            pltpu.VMEM((LANES, width), F32),
        ],
        compiler_params=pltpu.CompilerParams(
            dimension_semantics=("arbitrary",), vmem_limit_bytes=40 * 1024 * 1024
        ),
    )(zx, bcdt, pos, prm, head_prm, expand)


def mixer_backward(width, zx, bcdt, pos, prm, head_prm, expand, mixed, g, states, dyo, coef):
    rows = zx.shape[0]
    chunks = rows // CHUNK

    def tokens(columns):
        return pl.BlockSpec((CHUNK, columns), lambda i: (chunks - 1 - i, 0))

    def before(columns, place):
        return pl.BlockSpec(
            (16, columns), lambda i: (jnp.maximum((chunks - 1 - i) * (CHUNK // 16) - 1, 0), place)
        )

    def whole(array):
        return pl.BlockSpec(array.shape, lambda i: (0, 0))

    return pl.pallas_call(
        functools.partial(backward_kernel, width),
        out_shape=(
            jax.ShapeDtypeStruct((rows, width), BF16),
            jax.ShapeDtypeStruct((rows, 3 * LANES), BF16),
            jax.ShapeDtypeStruct((8, width + 2 * LANES), F32),
        ),
        grid=(chunks,),
        in_specs=[
            tokens(2 * width),
            tokens(3 * LANES),
            before(width, 1),
            before(3 * LANES, 0),
            tokens(1),
            whole(prm),
            whole(head_prm),
            whole(expand),
            tokens(width),
            tokens(width),
            pl.BlockSpec((1, LANES, width), lambda i: (chunks - 1 - i, 0, 0)),
            tokens(width),
            tokens(LANES),
        ],
        out_specs=(
            tokens(width),
            tokens(3 * LANES),
            pl.BlockSpec((8, width + 2 * LANES), lambda i: (0, 0)),
        ),
        scratch_shapes=[
            pltpu.VMEM((CHUNK + 8, width + 2 * LANES), F32),
            pltpu.VMEM((LANES, width), F32),
            pltpu.VMEM((CHUNK + 8, width + 2 * LANES), F32),
            pltpu.VMEM((CHUNK + 8, LANES), jnp.int32),
        ],
        compiler_params=pltpu.CompilerParams(
            dimension_semantics=("arbitrary",), vmem_limit_bytes=48 * 1024 * 1024
        ),
        cost_estimate=pl.CostEstimate(flops=rows * width * 2048, bytes_accessed=rows * width * 20, transcendentals=0),
    )(zx, bcdt, zx, bcdt, pos, prm, head_prm, expand, mixed, g, states, dyo, coef)


MESH = pl.DeviceIdType.MESH


def tp_places():
    me = lax.axis_index("tp")
    return me, me + 1 - 2 * lax.rem(me, 2), lax.rem(me + 2, 4), 3 - me


def greet(peers):
    barrier = pltpu.get_barrier_semaphore()
    for peer in peers:
        pl.semaphore_signal(barrier, inc=1, device_id=peer, device_id_type=MESH)
    pl.semaphore_wait(barrier, len(peers))


def send(src, dst, send_sem, recv_sem, peer):
    return pltpu.make_async_remote_copy(
        src_ref=src, dst_ref=dst, send_sem=send_sem, recv_sem=recv_sem, device_id=peer, device_id_type=MESH
    )


class Gather:
    def __init__(self, whole, rows, send_sems, recv_sems, own=None):
        me, side, up, _ = tp_places()
        half = rows // 2

        def part(place, start, count):
            return whole.at[pl.ds(pl.multiple_of(place * rows + start, half), count)]

        own = part(me, 0, rows) if own is None else own
        self.to_side = send(own, part(me, 0, rows), send_sems.at[0], recv_sems.at[0], {"tp": side})
        self.to_up = send(own, part(me, 0, rows), send_sems.at[1], recv_sems.at[1], {"tp": up})
        self.pass_up = send(
            part(side, 0, half), part(side, 0, half), send_sems.at[2], recv_sems.at[2], {"tp": up}
        )
        self.pass_side = send(
            part(up, half, half), part(up, half, half), send_sems.at[3], recv_sems.at[3], {"tp": side}
        )

    def start(self):
        self.to_side.start()
        self.to_up.start()

    def forward(self):
        self.to_side.wait_recv()
        self.pass_up.start()
        self.to_up.wait_recv()
        self.pass_side.start()

    def finish(self):
        self.pass_up.wait_recv()
        self.pass_side.wait_recv()

    def end(self):
        for copy in (self.to_side, self.to_up, self.pass_up, self.pass_side):
            copy.wait_send()


def set_up(width, heads, inner, taps_ref, flat_ref, lens_ref, prm, head, expand, pos):
    rank = lax.axis_index("tp")
    channels = taps_ref.shape[1]
    own = pl.ds(pl.multiple_of(rank * width, LANES), width)
    own_gain = pl.ds(pl.multiple_of(channels + rank * width, LANES), width)
    prm[...] = jnp.zeros_like(prm)
    prm[0:4, :width] = taps_ref[:, own]
    prm[0:4, width:] = taps_ref[:, inner:]
    prm[4:5, :width] = flat_ref[:, own]
    prm[4:5, width:] = flat_ref[:, inner:channels]
    prm[5:6, :width] = flat_ref[:, own_gain]
    lane = lax.broadcasted_iota(jnp.int32, (LANES, LANES), 1)
    pick = ((lax.broadcasted_iota(jnp.int32, (LANES, LANES), 0) == lane + rank * heads) & (lane < heads)).astype(F32)
    start = channels + inner
    tiles = [jnp.broadcast_to(flat_ref[:, start + n * LANES : start + (n + 1) * LANES], (8, LANES)) for n in range(3)]
    tiles[1] = jnp.exp(tiles[1])
    picked = lax.dot_general(
        jnp.concatenate(tiles, axis=0), pick, (((1,), (0,)), ((), ())), precision=HIGHEST, preferred_element_type=F32
    )
    head[...] = jnp.concatenate([picked[0:1], picked[8:9], jnp.zeros((6, LANES), F32)], axis=0)
    row = lax.broadcasted_iota(jnp.int32, (2 * LANES, width), 0)
    column = lax.broadcasted_iota(jnp.int32, (2 * LANES, width), 1)
    expand[...] = (lax.rem(row, LANES) == column // (width // heads)).astype(F32).astype(BF16)
    prm[6:7, :width] = dot(two_parts(picked[16:24]), expand[...])[0:1]
    starts = [jnp.int32(0)]
    for n in range(lens_ref.shape[1] - 1):
        starts.append(starts[-1] + lens_ref[0, n])

    def place(i, carry):
        token = lax.broadcasted_iota(jnp.int32, (CHUNK, 1), 0) + i * CHUNK
        begun = jnp.zeros((CHUNK, 1), jnp.int32)
        for first in starts[1:]:
            begun = jnp.where(token >= first, first, begun)
        pos[pl.ds(pl.multiple_of(i * CHUNK, CHUNK), CHUNK), :] = token - begun
        return carry

    lax.fori_loop(0, pos.shape[0] // CHUNK, place, 0)


def first_kernel(
    inner, heads, own_cols, x_ref, gain_ref, small_ref, taps_ref, flat_ref, lens_ref, wz_ref, wx_ref, w_out_ref, d_own_ref,
    u_out, zx_out, bcdt_out, wbc_out, mixed_out, g_out, yo_out, yo_t_out, state_out, d_out, dyo_out, coef_out, pos_out,
    prm_out, head_out, expand_out,
    weights, w_out, u, zx, bcdt, wbc, mixed, g, yo, yo_t, states, d, dyo, coef, pos, prm, head, expand, ext, state, sums,
    acc, sems, sum_sems, load_sems, store_sems,
):
    rows, model = x_ref.shape
    total, width = mixed.shape
    chunks = total // CHUNK
    me, side, up, far = tp_places()
    dp = lax.axis_index("dp")
    parity = lax.rem(dp, 2)
    partner = {"dp": dp + 1 - 2 * parity}

    def block(place):
        return pl.ds(pl.multiple_of(place * rows, rows), rows)

    loads = [
        pltpu.make_async_copy(wz_ref, weights.at[:, :width], load_sems.at[0]),
        pltpu.make_async_copy(wx_ref, weights.at[:, width:], load_sems.at[1]),
        pltpu.make_async_copy(w_out_ref, w_out, load_sems.at[2]),
        pltpu.make_async_copy(d_own_ref, d.at[block(me)], load_sems.at[3]),
    ]
    for copy in loads:
        copy.start()
    stores = []

    def keep(source, target):
        copy = pltpu.make_async_copy(source, target, store_sems.at[len(stores)])
        copy.start()
        stores.append(copy)

    bc_own = pl.ds(pl.multiple_of(parity * LANES, LANES), LANES)
    wbc[pl.ds(pl.multiple_of(parity * LANES + me * own_cols, own_cols), own_cols), :] = small_ref[
        pl.ds(pl.multiple_of(parity * own_cols, own_cols), own_cols), :
    ]
    greet([{"tp": side}, {"tp": up}, {"tp": far}, partner])
    small_gather = Gather(wbc.at[bc_own], own_cols, sems.at[0], sems.at[1])
    small_gather.start()

    def norm(i, carry):
        piece = pl.ds(pl.multiple_of(i * 32, 32), 32)
        x = x_ref[piece, :].astype(F32)
        scale = lax.rsqrt(jnp.mean(x * x, axis=-1, keepdims=True) + EPSILON)
        u[pl.ds(pl.multiple_of(me * rows + i * 32, 32), 32), :] = (x * scale * gain_ref[...]).astype(BF16)
        return carry

    lax.fori_loop(0, rows // 32, norm, 0)
    gather = Gather(u, rows, sems.at[2], sems.at[3])
    gather.start()
    wbc[2 * LANES :, :] = jnp.zeros((LANES, model), BF16)
    wbc[2 * LANES : 2 * LANES + heads, :] = small_ref[2 * own_cols :, :]
    set_up(width, heads, inner, taps_ref, flat_ref, lens_ref, prm, head, expand, pos)
    keep(pos, pos_out)
    keep(prm, prm_out)
    keep(head, head_out)
    keep(expand, expand_out)
    loads[0].wait()
    loads[1].wait()

    def project(place):
        piece = block(place)

        def tile(n, carry):
            columns = pl.ds(pl.multiple_of(n * 256, 256), 256)
            zx[piece, columns] = dot(u[piece, :], weights[:, columns]).astype(BF16)
            return carry

        lax.fori_loop(0, 2 * width // 256, tile, 0)

    def project_small(place):
        bcdt[block(place), :] = dot(u[block(place), :], wbc[...], CONTRACT_LAST).astype(BF16)

    small_gather.forward()
    project(me)
    small_gather.finish()
    trade = send(wbc.at[bc_own], wbc.at[bc_own], sems.at[6, 0], sems.at[6, 1], partner)
    trade.start()
    gather.forward()
    project(side)
    project(up)
    trade.wait()
    keep(wbc, wbc_out)
    project_small(me)
    project_small(side)
    project_small(up)
    gather.finish()
    loads[3].wait()
    d_gather = Gather(d, rows, sems.at[4], sems.at[5])
    d_gather.start()
    keep(u, u_out)
    project(far)
    project_small(far)
    keep(zx, zx_out)
    keep(bcdt, bcdt_out)

    state[...] = jnp.zeros_like(state)
    ext[...] = jnp.zeros_like(ext)

    def chunk(i, carry):
        forward_chunk(
            width, i, zx, bcdt, pos, prm, head, expand, mixed, g, sums.at[0, 0], states, ext, state
        )
        return carry

    lax.fori_loop(0, chunks, chunk, 0)

    def exchange(which):
        copies = [
            send(
                sums.at[which, 0], sums.at[which, 1 + n], sum_sems.at[which, 0, n], sum_sems.at[which, 1, n], {"tp": peer}
            )
            for n, peer in enumerate((side, up, far))
        ]
        for copy in copies:
            copy.start()
        return copies

    copies = exchange(0)
    keep(mixed, mixed_out)
    keep(g, g_out)
    keep(states, state_out)
    loads[2].wait()

    def back_to_heads(place):
        piece = block(place)
        acc[...] = jnp.zeros_like(acc)

        def tile(n, carry):
            columns = pl.ds(pl.multiple_of(n * 256, 256), 256)
            low = dot(d[piece, :], w_out[columns, :], CONTRACT_LAST).astype(BF16)
            dyo[piece, columns] = low
            both = low.astype(F32) * prm[5:6, columns] * g[piece, columns]
            acc[...] += both[:, :LANES] + both[:, LANES:]
            return carry

        lax.fori_loop(0, width // 256, tile, 0)
        column = jnp.sum(acc[...], axis=1, keepdims=True)
        sums[1, 0, :, piece] = jnp.broadcast_to(column, (rows, LANES)).T[:8, :]
        keep(dyo.at[piece], dyo_out.at[piece])

    d_gather.forward()
    back_to_heads(me)
    for copy in copies:
        copy.wait()

    def gate(i, carry):
        piece = pl.ds(pl.multiple_of(i * CHUNK, CHUNK), CHUNK)
        squares = sums[0, 0, :, piece] + sums[0, 1, :, piece] + sums[0, 2, :, piece] + sums[0, 3, :, piece]
        scale = lax.rsqrt(squares / inner + EPSILON)
        columns = jnp.concatenate([scale, jnp.zeros((LANES - 8, LANES), F32)], axis=0).T
        gated = g[piece, :] * columns[:, 0:1] * prm[5:6, :width]
        yo[piece, :] = gated.astype(BF16)
        yo_t[:, piece] = gated.T.astype(BF16)
        return carry

    lax.fori_loop(0, chunks, gate, 0)
    keep(yo, yo_out)
    keep(yo_t, yo_t_out)
    back_to_heads(side)
    back_to_heads(up)
    d_gather.finish()
    keep(d, d_out)
    back_to_heads(far)
    copies = exchange(1)
    for copy in copies:
        copy.wait()

    def weigh(i, carry):
        piece = pl.ds(pl.multiple_of(i * CHUNK, CHUNK), CHUNK)
        squares = sums[0, 0, :, piece] + sums[0, 1, :, piece] + sums[0, 2, :, piece] + sums[0, 3, :, piece]
        cross = sums[1, 0, :, piece] + sums[1, 1, :, piece] + sums[1, 2, :, piece] + sums[1, 3, :, piece]
        scale = lax.rsqrt(squares / inner + EPSILON)
        back = scale * scale * scale * (cross / inner)
        coef[piece, :] = jnp.concatenate([scale, back, jnp.zeros((LANES - 16, LANES), F32)], axis=0).T
        return carry

    lax.fori_loop(0, chunks, weigh, 0)
    keep(coef, coef_out)
    small_gather.end()
    gather.end()
    d_gather.end()
    for copy in stores:
        copy.wait()


def first_part(inner, heads, own_cols, x_in, gain, small, taps, flat, lens, w_z, w_x, w_out, d_out):
    rows, model = x_in.shape
    total = 4 * rows
    width = w_z.shape[1]
    chunks = total // CHUNK
    vmem = pl.BlockSpec(memory_space=pltpu.VMEM)
    anywhere = pl.BlockSpec(memory_space=pl.ANY)
    results = [
        ((total, model), BF16),
        ((total, 2 * width), BF16),
        ((total, 3 * LANES), BF16),
        ((3 * LANES, model), BF16),
        ((total, width), F32),
        ((total, width), F32),
        ((total, width), BF16),
        ((width, total), BF16),
        ((chunks, LANES, width), BF16),
        ((total, model), BF16),
        ((total, width), BF16),
        ((total, LANES), F32),
        ((total, 1), jnp.int32),
        ((8, width + 2 * LANES), F32),
        ((8, LANES), F32),
        ((2 * LANES, width), BF16),
    ]
    return pl.pallas_call(
        functools.partial(first_kernel, inner, heads, own_cols),
        out_shape=[jax.ShapeDtypeStruct(*result) for result in results],
        in_specs=[vmem] * 5 + [pl.BlockSpec(memory_space=pltpu.SMEM)] + [anywhere] * 4,
        out_specs=[anywhere] * len(results),
        scratch_shapes=[pltpu.VMEM((model, 2 * width), BF16), pltpu.VMEM((width, model), BF16)]
        + [pltpu.VMEM(*result) for result in results]
        + [
            pltpu.VMEM((CHUNK + 8, width + 2 * LANES), F32),
            pltpu.VMEM((LANES, width), F32),
            pltpu.VMEM((2, 4, 8, total), F32),
            pltpu.VMEM((rows, LANES), F32),
            pltpu.SemaphoreType.DMA((7, 4)),
            pltpu.SemaphoreType.DMA((2, 2, 3)),
            pltpu.SemaphoreType.DMA((4,)),
            pltpu.SemaphoreType.DMA((24,)),
        ],
        compiler_params=pltpu.CompilerParams(
            collective_id=0, has_side_effects=True, vmem_limit_bytes=60 * 1024 * 1024
        ),
    )(x_in, gain, small, taps, flat, lens, w_z, w_x, w_out, d_out)


def add_into(target, other):
    tile = 128

    def one(i, carry):
        piece = pl.ds(pl.multiple_of(i * tile, tile), tile)
        target[piece, :] = (target[piece, :].astype(F32) + other[piece, :].astype(F32)).astype(BF16)
        return carry

    lax.fori_loop(0, target.shape[0] // tile, one, 0)


class LineSum:
    def __init__(self, parts, pair, right, left, pair_sems, right_sems, left_sems):
        dp = lax.axis_index("dp")
        self.dp = dp
        self.count = parts.shape[0] // 2
        self.z = dp // 2
        self.parity = lax.rem(dp, 2)
        self.partner = {"dp": dp + 1 - 2 * self.parity}
        self.parts, self.pair = parts, pair
        self.lines = {1: (right, right_sems), -1: (left, left_sems)}
        self.swaps = {}
        self.pair_sems = pair_sems

    def peers(self):
        n = 2 * self.count
        return [self.partner, {"dp": lax.rem(self.dp + 2, n)}, {"dp": lax.rem(self.dp + n - 2, n)}]

    def order(self):
        low, high, out = 0, self.count - 1, []
        while low <= high:
            out += [high, low] if low < high else [low]
            low, high = low + 1, high - 1
        return out

    def swap(self, z):
        copy = send(
            self.parts.at[2 * z + 1 - self.parity], self.pair.at[z], self.pair_sems.at[0, z], self.pair_sems.at[1, z],
            self.partner,
        )
        copy.start()
        self.swaps[z] = copy

    def merge(self, z):
        self.swaps[z].wait()
        add_into(self.parts.at[2 * z + self.parity], self.pair.at[z])

    def away(self, way):
        return self.z if way == 1 else self.count - 1 - self.z

    def copy(self, way, step):
        line, line_sems = self.lines[way]
        far = self.count - step + self.away(way)
        z = far if way == 1 else self.count - 1 - far
        chunk = self.parts.at[2 * z + self.parity]
        return chunk, send(
            chunk, line.at[step - 1], line_sems.at[0, step - 1], line_sems.at[1, step - 1],
            {"dp": self.dp + 2 * way},
        )

    def arrived(self, way, step):
        line, line_sems = self.lines[way]
        return send(
            self.parts.at[self.dp], line.at[step - 1], line_sems.at[0, step - 1], line_sems.at[1, step - 1],
            self.partner,
        )

    def move(self, step):
        for way in (1, -1):
            away = self.away(way)

            @pl.when(away == 0)
            def _():
                if step > 1:
                    self.copy(way, step - 1)[1].wait_send()
                self.copy(way, step)[1].start()

            if step > 1:

                @pl.when((away >= 1) & (away <= min(step - 1, self.count - 2)))
                def _():
                    chunk, copy = self.copy(way, step)
                    self.arrived(way, step - 1).wait_recv()
                    add_into(chunk, self.lines[way][0].at[step - 2])
                    copy.start()

    def finish(self):
        last = self.count - 1
        for way in (1, -1):

            @pl.when(self.away(way) >= 1)
            def _():
                self.arrived(way, last).wait_recv()

        total = self.parts.at[self.dp]
        for way in (1, -1):

            @pl.when(self.away(way) >= 1)
            def _():
                add_into(total, self.lines[way][0].at[last - 1])

        return total

    def end(self):
        for way in (1, -1):
            away = self.away(way)
            for step in range(1, self.count):

                @pl.when((away <= step - 1) & (away <= self.count - 2) & ((away >= 1) | (step == self.count - 1)))
                def _():
                    self.copy(way, step)[1].wait_send()


class PlaneSum:
    def __init__(self, away, to_side, to_up, in_half, in_side, in_up, sems):
        _, side, up, _ = tp_places()
        side, up = {"tp": side}, {"tp": up}
        rows = to_side.shape[0]
        half = rows // 2
        self.to_side, self.to_up, self.in_half, self.half = to_side, to_up, in_half, half
        self.in_side, self.in_up = in_side, in_up
        low, high = pl.ds(0, half), pl.ds(half, half)

        def one(n, source, target, peer):
            return send(source, target, sems.at[0, n], sems.at[1, n], peer)

        self.away_side = one(0, away.at[low], in_half.at[0], side)
        self.away_up = one(1, away.at[high], in_half.at[1], up)
        self.side_low = one(2, to_side.at[low], in_side.at[low], side)
        self.side_high = one(3, to_side.at[high], in_side.at[high], side)
        self.up_low = one(4, to_up.at[low], in_up.at[low], up)
        self.up_high = one(5, to_up.at[high], in_up.at[high], up)
        self.low, self.high = low, high

    def start_far(self):
        self.away_side.start()
        self.away_up.start()

    def start_side(self):
        self.side_low.start()

    def start_up(self):
        self.up_high.start()

    def pass_on(self):
        self.away_side.wait_recv()
        add_into(self.to_up.at[self.low], self.in_half.at[0])
        self.up_low.start()
        self.away_up.wait_recv()
        add_into(self.to_side.at[self.high], self.in_half.at[1])
        self.side_high.start()

    def finish(self):
        for copy in (self.side_low, self.up_high, self.side_high, self.up_low):
            copy.wait_recv()

    def end(self):
        for copy in (self.away_side, self.away_up, self.side_low, self.side_high, self.up_low, self.up_high):
            copy.wait_send()


def plane_scratch(rows, model):
    half = rows // 2
    return [
        pltpu.VMEM((rows, model), BF16),
        pltpu.VMEM((rows, model), BF16),
        pltpu.VMEM((rows, model), BF16),
        pltpu.VMEM((2, half, model), BF16),
        pltpu.VMEM((rows, model), BF16),
        pltpu.VMEM((rows, model), BF16),
        pltpu.SemaphoreType.DMA((2, 6)),
    ]


def line_scratch(dp_count, shape):
    z = dp_count // 2
    return [
        pltpu.VMEM((dp_count,) + shape, BF16),
        pltpu.VMEM((z,) + shape, BF16),
        pltpu.VMEM((z - 1,) + shape, BF16),
        pltpu.VMEM((z - 1,) + shape, BF16),
        pltpu.SemaphoreType.DMA((2, z)),
        pltpu.SemaphoreType.DMA((2, z - 1)),
        pltpu.SemaphoreType.DMA((2, z - 1)),
    ]


class Copies:
    def __init__(self, sems):
        self.sems, self.started = sems, []

    def start(self, source, target):
        copy = pltpu.make_async_copy(source, target, self.sems.at[len(self.started)])
        copy.start()
        self.started.append(copy)
        return copy


def product_chunk(left_t, right, chunk, target, tile):
    columns = pl.ds(pl.multiple_of(chunk * target.shape[1], target.shape[1]), target.shape[1])

    def one(i, carry):
        piece = pl.ds(pl.multiple_of(i * tile, tile), tile)
        target[piece, :] = dot(left_t[piece, :], right[:, columns]).astype(BF16)
        return carry

    lax.fori_loop(0, target.shape[0] // tile, one, 0)


def second_kernel(
    x_ref, yo_ref, yo_t_ref, d_ref, w_out_ref, dyo_ref, g_ref, mixed_ref, zx_ref, coef_ref, prm_ref, u_ref,
    block_out, gw_out, dz_out, gz_out,
    yo, yo_t, d, w_out, dyo, g, mixed, z, coef, own, gz,
    parts, pair, right, left, pair_sems, right_sems, left_sems,
    away, to_side, to_up, in_half, in_side, in_up, plane_sems, load_sems, store_sems,
):
    rows, model = x_ref.shape
    total, width = yo.shape
    me, side, up, far = tp_places()
    loads, stores = Copies(load_sems), Copies(store_sems)
    load_yo = loads.start(yo_ref, yo)
    load_w = loads.start(w_out_ref, w_out)
    load_yo_t = loads.start(yo_t_ref, yo_t)
    load_d = loads.start(d_ref, d)
    rest = [
        loads.start(dyo_ref, dyo),
        loads.start(g_ref, g),
        loads.start(mixed_ref, mixed),
        loads.start(zx_ref.at[:, :width], z),
        loads.start(coef_ref, coef),
    ]
    line = LineSum(parts, pair, right, left, pair_sems, right_sems, left_sems)
    plane = PlaneSum(away, to_side, to_up, in_half, in_side, in_up, plane_sems)
    greet([{"tp": side}, {"tp": up}] + line.peers())

    def out_block(place, target):
        piece = pl.ds(pl.multiple_of(place * rows, rows), rows)

        def tile(n, carry):
            columns = pl.ds(pl.multiple_of(n * 256, 256), 256)
            target[:, columns] = dot(yo[piece, :], w_out[:, columns]).astype(target.dtype)
            return carry

        lax.fori_loop(0, model // 256, tile, 0)

    load_yo.wait()
    load_w.wait()
    out_block(far, away)
    plane.start_far()
    load_yo_t.wait()
    load_d.wait()
    for z_chunk in line.order():
        for chunk in (2 * z_chunk + 1 - line.parity, 2 * z_chunk + line.parity):
            product_chunk(yo_t, d, chunk, parts.at[chunk], width // 2)
            if z_chunk not in line.swaps:
                line.swap(z_chunk)
    load_u = loads.start(u_ref, d)
    order = line.order()
    for z_chunk in order[:2]:
        line.merge(z_chunk)
    line.move(1)
    for z_chunk in order[2:]:
        line.merge(z_chunk)
    out_block(side, to_side)
    plane.start_side()
    out_block(up, to_up)
    plane.start_up()
    out_block(me, own)
    for copy in rest:
        copy.wait()

    def gate_back(i, carry):
        piece = pl.ds(pl.multiple_of(i * CHUNK, CHUNK), CHUNK)
        z_piece = z[piece, :].astype(F32)
        sig = jax.nn.sigmoid(z_piece)
        dg = coef[piece, 0:1] * (dyo[piece, :].astype(F32) * prm_ref[5:6, :width]) - g[piece, :] * coef[piece, 8:9]
        dz = dg * mixed[piece, :] * (sig * (1.0 + z_piece * (1.0 - sig)))
        yo[piece, :] = dz.astype(BF16)
        yo_t[:, piece] = dz.T.astype(BF16)
        return carry

    chunks = total // CHUNK
    lax.fori_loop(0, chunks, gate_back, 0)
    stores.start(yo, dz_out)
    line.move(2)
    plane.pass_on()
    load_u.wait()
    dp_count = parts.shape[0]

    def gate_products(first, last):
        def one(chunk, carry):
            product_chunk(yo_t, d, chunk, gz.at[chunk], width // 2)
            return carry

        lax.fori_loop(first, last, one, 0)

    gate_products(0, dp_count)
    stores.start(gz, gz_out)
    for step in range(3, line.count):
        line.move(step)
    plane.finish()

    def add_own(i, carry):
        piece = pl.ds(pl.multiple_of(i * 32, 32), 32)
        total_out = own[piece, :] + in_side[piece, :].astype(F32) + in_up[piece, :].astype(F32)
        block_out[piece, :] = (x_ref[piece, :].astype(F32) + total_out).astype(BF16)
        return carry

    lax.fori_loop(0, rows // 32, add_own, 0)
    sum_ref = line.finish()
    gw_out[...] = sum_ref[...].astype(F32)
    line.end()
    plane.end()
    for copy in stores.started:
        copy.wait()


def second_part(x_in, yo, yo_t, d, w_out, dyo, g, mixed, zx, coef, prm, u):
    rows, model = x_in.shape
    total, width = yo.shape
    dp_count = lax.axis_size("dp")
    cut = model // dp_count
    vmem = pl.BlockSpec(memory_space=pltpu.VMEM)
    anywhere = pl.BlockSpec(memory_space=pl.ANY)
    return pl.pallas_call(
        second_kernel,
        out_shape=(
            jax.ShapeDtypeStruct((rows, model), BF16),
            jax.ShapeDtypeStruct((width, cut), F32),
            jax.ShapeDtypeStruct((total, width), BF16),
            jax.ShapeDtypeStruct((dp_count, width, cut), BF16),
        ),
        in_specs=[vmem] + [anywhere] * 9 + [vmem, anywhere],
        out_specs=(vmem, vmem, anywhere, anywhere),
        scratch_shapes=[
            pltpu.VMEM((total, width), BF16),
            pltpu.VMEM((width, total), BF16),
            pltpu.VMEM((total, model), BF16),
            pltpu.VMEM((width, model), BF16),
            pltpu.VMEM((total, width), BF16),
            pltpu.VMEM((total, width), F32),
            pltpu.VMEM((total, width), F32),
            pltpu.VMEM((total, width), BF16),
            pltpu.VMEM((total, LANES), F32),
            pltpu.VMEM((rows, model), F32),
            pltpu.VMEM((dp_count, width, cut), BF16),
        ]
        + line_scratch(dp_count, (width, cut))
        + plane_scratch(rows, model)
        + [pltpu.SemaphoreType.DMA((10,)), pltpu.SemaphoreType.DMA((2,))],
        compiler_params=pltpu.CompilerParams(
            collective_id=1, has_side_effects=True, vmem_limit_bytes=60 * 1024 * 1024
        ),
    )(x_in, yo, yo_t, d, w_out, dyo, g, mixed, zx, coef, prm, u)


def third_kernel(
    own_cols, heads, zx_ref, bcdt_ref, pos_ref, prm_ref, head_ref, expand_ref, mixed_ref, g_ref, state_ref, dyo_ref,
    coef_ref, u_ref, gz_ref,
    gw_z, dx_out, dbcdt_out, gl_out, small_out,
    zx, bcdt, mixed, g, states, dyo, u, dx, dbcdt, dx_t, gl, bc_in, ext, d_state, later, later_pos,
    parts, pair, right, left, pair_sems, right_sems, left_sems, bc_sems, load_sems, store_sems,
):
    total, width = mixed.shape
    chunks = total // CHUNK
    me, side, up, far = tp_places()
    dp_count = parts.shape[0]
    loads, stores = Copies(load_sems), Copies(store_sems)
    load_parts = loads.start(gz_ref, parts)
    first_loads = [
        loads.start(zx_ref, zx),
        loads.start(bcdt_ref, bcdt),
        loads.start(mixed_ref, mixed),
        loads.start(g_ref, g),
        loads.start(state_ref, states),
        loads.start(dyo_ref, dyo),
    ]
    load_u = loads.start(u_ref, u)
    line = LineSum(parts, pair, right, left, pair_sems, right_sems, left_sems)
    greet([{"tp": side}, {"tp": up}, {"tp": far}] + line.peers())
    load_parts.wait()
    order = line.order()
    for z_chunk in order:
        line.swap(z_chunk)
    backward_start(small_out, d_state, later, later_pos)
    for z_chunk in order[:2]:
        line.merge(z_chunk)
    line.move(1)
    for z_chunk in order[2:]:
        line.merge(z_chunk)
    for copy in first_loads:
        copy.wait()
    hooks = {3: 2, 6: 3}

    def chunk(i, carry):
        at = chunks - 1 - i
        tokens = pl.ds(pl.multiple_of(at * CHUNK, CHUNK), CHUNK)
        halo = pl.ds(pl.multiple_of(lax.rem(at * CHUNK + total - 16, total), 16), 16)
        backward_chunk(
            width, tokens, zx[halo, width:], bcdt[halo, : 2 * LANES], states[at], zx, bcdt, pos_ref, prm_ref, head_ref,
            expand_ref, mixed, g, dyo, coef_ref, dx, dbcdt, dx_t, small_out, ext, d_state, later, later_pos,
        )
        for when, step in hooks.items():

            @pl.when(i == when - 1)
            def _():
                line.move(step)

        return carry

    lax.fori_loop(0, chunks, chunk, 0)
    stores.start(dx, dx_out)
    stores.start(dbcdt, dbcdt_out)

    pick_row = lax.broadcasted_iota(jnp.int32, (2 * own_cols, 2 * LANES), 0)
    pick_col = lax.broadcasted_iota(jnp.int32, (2 * own_cols, 2 * LANES), 1)

    def columns_of(place):
        wanted = jnp.where(pick_row < own_cols, pick_row, pick_row - own_cols + LANES) + place * own_cols
        pick = (pick_col == wanted).astype(F32).astype(BF16)
        return dot(pick, dbcdt[:, : 2 * LANES], CONTRACT_LAST)

    copies = []
    for n, peer in enumerate((side, up, far)):
        bc_in[n] = columns_of(peer).astype(BF16)
        copies.append(send(bc_in.at[n], bc_in.at[3 + n], bc_sems.at[0, n], bc_sems.at[1, n], {"tp": peer}))
        copies[-1].start()
    own_bc = columns_of(me)
    dx_t[width:, :] = jnp.zeros((LANES, total), BF16)
    dx_t[width + 2 * own_cols : width + 2 * own_cols + heads, :] = dbcdt[:, 2 * LANES :].astype(F32).T[:heads, :].astype(
        BF16
    )
    load_u.wait()
    for copy in copies:
        copy.wait()
    for n in range(3):
        own_bc = own_bc + bc_in[3 + n].astype(F32)
    dx_t[width : width + 2 * own_cols, :] = own_bc.astype(BF16)

    def last_product(c, carry):
        product_chunk(dx_t, u, c, gl.at[c], (width + LANES) // 3)
        return carry

    lax.fori_loop(0, dp_count, last_product, 0)
    stores.start(gl, gl_out)
    sum_ref = line.finish()

    def turn(i, carry):
        piece = pl.ds(pl.multiple_of(i * CHUNK, CHUNK), CHUNK)
        gw_z[:, piece] = sum_ref[piece, :].astype(F32).T
        return carry

    lax.fori_loop(0, width // CHUNK, turn, 0)
    line.end()
    for copy in stores.started:
        copy.wait()


def third_part(own_cols, heads, zx, bcdt, pos, prm, head_prm, expand, mixed, g, states, dyo, coef, u, gz):
    total, width = mixed.shape
    model = u.shape[1]
    dp_count = lax.axis_size("dp")
    cut = model // dp_count
    vmem = pl.BlockSpec(memory_space=pltpu.VMEM)
    anywhere = pl.BlockSpec(memory_space=pl.ANY)
    return pl.pallas_call(
        functools.partial(third_kernel, own_cols, heads),
        out_shape=(
            jax.ShapeDtypeStruct((cut, width), F32),
            jax.ShapeDtypeStruct((total, width), BF16),
            jax.ShapeDtypeStruct((total, 3 * LANES), BF16),
            jax.ShapeDtypeStruct((dp_count, width + LANES, cut), BF16),
            jax.ShapeDtypeStruct((8, width + 2 * LANES), F32),
        ),
        in_specs=[anywhere] * 2 + [vmem] * 4 + [anywhere] * 4 + [vmem] + [anywhere] * 2,
        out_specs=(vmem, anywhere, anywhere, anywhere, vmem),
        scratch_shapes=[
            pltpu.VMEM(zx.shape, BF16),
            pltpu.VMEM(bcdt.shape, BF16),
            pltpu.VMEM((total, width), F32),
            pltpu.VMEM((total, width), F32),
            pltpu.VMEM(states.shape, BF16),
            pltpu.VMEM((total, width), BF16),
            pltpu.VMEM((total, model), BF16),
            pltpu.VMEM((total, width), BF16),
            pltpu.VMEM((total, 3 * LANES), BF16),
            pltpu.VMEM((width + LANES, total), BF16),
            pltpu.VMEM((dp_count, width + LANES, cut), BF16),
            pltpu.VMEM((6, 2 * own_cols, total), BF16),
            pltpu.VMEM((CHUNK + 8, width + 2 * LANES), F32),
            pltpu.VMEM((LANES, width), F32),
            pltpu.VMEM((CHUNK + 8, width + 2 * LANES), F32),
            pltpu.VMEM((CHUNK + 8, LANES), jnp.int32),
        ]
        + line_scratch(dp_count, (width, cut))
        + [pltpu.SemaphoreType.DMA((2, 3)), pltpu.SemaphoreType.DMA((8,)), pltpu.SemaphoreType.DMA((3,))],
        compiler_params=pltpu.CompilerParams(
            collective_id=2, has_side_effects=True, vmem_limit_bytes=60 * 1024 * 1024
        ),
    )(zx, bcdt, pos, prm, head_prm, expand, mixed, g, states, dyo, coef, u, gz)


def fourth_kernel(
    x_ref, d_own_ref, gain_ref, small_ref, dz_ref, dx_ref, dbcdt_ref, wz_ref, wx_ref, wbc_ref, u_ref, gl_ref,
    gw_x, gw_rest, grad_x, sums,
    dz, dx, dbcdt, wz, wx, wbc, u, own, gain_part, packed, over_z,
    parts, pair, right, left, pair_sems, right_sems, left_sems,
    away, to_side, to_up, in_half, in_side, in_up, plane_sems, z_sems, tp_sems, load_sems,
):
    rows, model = x_ref.shape
    width = dz.shape[1]
    me, side, up, far = tp_places()
    dp_count = parts.shape[0]
    loads = Copies(load_sems)
    load_parts = loads.start(gl_ref, parts)
    first_loads = [
        loads.start(dz_ref, dz),
        loads.start(dx_ref, dx),
        loads.start(dbcdt_ref, dbcdt),
        loads.start(wz_ref, wz),
        loads.start(wx_ref, wx),
        loads.start(wbc_ref, wbc),
        loads.start(u_ref, u),
    ]
    line = LineSum(parts, pair, right, left, pair_sems, right_sems, left_sems)
    plane = PlaneSum(away, to_side, to_up, in_half, in_side, in_up, plane_sems)
    others = [{"dp": lax.rem(line.dp + 2 * n, dp_count)} for n in range(1, dp_count // 2)]
    greet([{"tp": side}, {"tp": up}, {"tp": far}, line.partner] + others)
    load_parts.wait()
    order = line.order()
    for z_chunk in order:
        line.swap(z_chunk)
    gain_part[...] = jnp.zeros_like(gain_part)

    def du_block(place, target):
        piece = pl.ds(pl.multiple_of(place * rows, rows), rows)

        def tile(n, carry):
            columns = pl.ds(pl.multiple_of(n * 256, 256), 256)
            du = (
                dot(dz[piece, :], wz[columns, :], CONTRACT_LAST)
                + dot(dx[piece, :], wx[columns, :], CONTRACT_LAST)
                + dot(dbcdt[piece, :], wbc[:, columns])
            )
            target[:, columns] = du.astype(target.dtype)
            gain_part[0:1, columns] += jnp.sum(du * u[piece, columns].astype(F32), axis=0, keepdims=True)
            return carry

        lax.fori_loop(0, model // 256, tile, 0)

    for copy in first_loads:
        copy.wait()
    du_block(far, away)
    plane.start_far()
    for z_chunk in order[:2]:
        line.merge(z_chunk)
    line.move(1)
    for z_chunk in order[2:]:
        line.merge(z_chunk)
    du_block(side, to_side)
    plane.start_side()
    du_block(up, to_up)
    plane.start_up()
    du_block(me, own)

    wide = width + 2 * LANES
    packed[0, :, :wide] = small_ref[...]
    packed[0, :, wide:] = jnp.concatenate([gain_part[0:1, :] / gain_ref[...], jnp.zeros((7, model), F32)], axis=0)
    trade = send(packed.at[0], packed.at[1], z_sems.at[0, 0], z_sems.at[1, 0], line.partner)
    trade.start()
    plane.pass_on()
    line.move(2)
    trade.wait()
    over_z[0] = packed[0] + packed[1]
    copies = [
        send(over_z.at[0], over_z.at[n], z_sems.at[0, n], z_sems.at[1, n], others[n - 1])
        for n in range(1, dp_count // 2)
    ]
    for copy in copies:
        copy.start()
    for copy in copies:
        copy.wait()
    everything = over_z[0]
    for n in range(1, dp_count // 2):
        everything = everything + over_z[n]
    sums[me] = everything
    copies = [
        send(sums.at[me], sums.at[me], tp_sems.at[0, n], tp_sems.at[1, n], {"tp": peer})
        for n, peer in enumerate((side, up, far))
    ]
    for copy in copies:
        copy.start()
    for step in range(3, line.count):
        line.move(step)
    plane.finish()

    def norm_back(i, carry):
        piece = pl.ds(pl.multiple_of(i * 32, 32), 32)
        x = x_ref[piece, :].astype(F32)
        r_in = lax.rsqrt(jnp.mean(x * x, axis=-1, keepdims=True) + EPSILON)
        du = own[piece, :] + in_side[piece, :].astype(F32) + in_up[piece, :].astype(F32)
        e_in = du * gain_ref[...]
        back = r_in * r_in * r_in * jnp.mean(e_in * x, axis=-1, keepdims=True)
        grad_x[piece, :] = d_own_ref[piece, :].astype(F32) + r_in * e_in - x * back
        return carry

    lax.fori_loop(0, rows // 32, norm_back, 0)
    for copy in copies:
        copy.wait()
    sum_ref = line.finish()

    def turn(i, carry):
        piece = pl.ds(pl.multiple_of(i * CHUNK, CHUNK), CHUNK)
        gw_x[:, piece] = sum_ref[piece, :].astype(F32).T
        return carry

    lax.fori_loop(0, width // CHUNK, turn, 0)
    gw_rest[...] = sum_ref[width:, :].astype(F32).T
    line.end()
    plane.end()


def fourth_part(x_in, d_out, gain, small, dz, dx, dbcdt, w_z, w_x, wbc, u, gl):
    rows, model = x_in.shape
    total, width = dz.shape
    dp_count = lax.axis_size("dp")
    cut = model // dp_count
    wide = width + 2 * LANES + model
    vmem = pl.BlockSpec(memory_space=pltpu.VMEM)
    anywhere = pl.BlockSpec(memory_space=pl.ANY)
    return pl.pallas_call(
        fourth_kernel,
        out_shape=(
            jax.ShapeDtypeStruct((cut, width), F32),
            jax.ShapeDtypeStruct((cut, LANES), F32),
            jax.ShapeDtypeStruct((rows, model), F32),
            jax.ShapeDtypeStruct((4, 8, wide), F32),
        ),
        in_specs=[vmem] * 4 + [anywhere] * 8,
        out_specs=(vmem,) * 4,
        scratch_shapes=[
            pltpu.VMEM((total, width), BF16),
            pltpu.VMEM((total, width), BF16),
            pltpu.VMEM((total, 3 * LANES), BF16),
            pltpu.VMEM((model, width), BF16),
            pltpu.VMEM((model, width), BF16),
            pltpu.VMEM((3 * LANES, model), BF16),
            pltpu.VMEM((total, model), BF16),
            pltpu.VMEM((rows, model), F32),
            pltpu.VMEM((8, model), F32),
            pltpu.VMEM((2, 8, wide), F32),
            pltpu.VMEM((dp_count // 2, 8, wide), F32),
        ]
        + line_scratch(dp_count, (width + LANES, cut))
        + plane_scratch(rows, model)
        + [
            pltpu.SemaphoreType.DMA((2, dp_count // 2)),
            pltpu.SemaphoreType.DMA((2, 3)),
            pltpu.SemaphoreType.DMA((8,)),
        ],
        compiler_params=pltpu.CompilerParams(
            collective_id=3, has_side_effects=True, vmem_limit_bytes=60 * 1024 * 1024
        ),
    )(x_in, d_out, gain, small, dz, dx, dbcdt, w_z, w_x, wbc, u, gl)


def in_norm_scale(values):
    return lax.rsqrt(jnp.mean(values * values, axis=-1, keepdims=True) + EPSILON)


def body(
    x_in, norm_gain, w_z, w_x, w_b, w_c, w_dt, conv_w, conv_b, dt_bias, a_log, d_skip, gate_gain, w_out,
    doc_lens, d_out,
):
    tp_count = lax.axis_size("tp")
    rank = lax.axis_index("tp")
    dev_rows, model = x_in.shape
    rows = dev_rows * tp_count
    inner = gate_gain.shape[0]
    width = w_z.shape[1]
    heads = w_dt.shape[1]
    state_size = (conv_w.shape[0] - inner) // 2
    head_size = width // heads
    own_cols = w_b.shape[1]

    x_float = x_in.astype(F32)
    r_in = in_norm_scale(x_float)
    small_weights = jnp.concatenate([w_b, w_c, w_dt], axis=1).T
    if tp_count == 4:
        lanes = jnp.zeros((LANES - d_skip.shape[0],), F32)
        flat = jnp.concatenate([conv_b, gate_gain, dt_bias, lanes, a_log, lanes, d_skip, lanes])[None, :]
        (
            gathered, zx, bcdt, w_bcdt, mixed, g, yo, yo_t, states, grad_gathered, dyo, coef, pos, prm, head_prm, expand
        ) = first_part(
            inner, heads, own_cols, x_in, norm_gain[None, :], small_weights, conv_w.T, flat, doc_lens, w_z, w_x, w_out,
            d_out,
        )
        gain_own = prm[5, :width]
    else:
        normed = (x_float * r_in * norm_gain[None, :]).astype(BF16)
        gathered = lax.all_gather(normed, "tp", axis=0, tiled=True)
        w_bc = lax.all_gather(small_weights[: 2 * own_cols], "tp", axis=0).reshape(tp_count, 2, own_cols, model)
        w_bcdt = jnp.concatenate(
            [
                jnp.swapaxes(w_bc, 0, 1).reshape(2 * state_size, model),
                small_weights[2 * own_cols :],
                jnp.zeros((LANES - heads, model), BF16),
            ],
            axis=0,
        )
        zx = dot(gathered, jnp.concatenate([w_z, w_x], axis=1)).astype(BF16)
        bcdt = dot(gathered, w_bcdt, CONTRACT_LAST).astype(BF16)
        lengths = doc_lens[0]
        doc_starts = jnp.cumsum(lengths) - lengths
        positions = jnp.arange(rows, dtype=jnp.int32)
        started = jnp.where(positions[:, None] >= doc_starts[None, :], doc_starts[None, :], 0)
        pos = (positions - jnp.max(started, axis=1))[:, None]

        def own(array, count):
            return lax.dynamic_slice_in_dim(array, rank * count, count, axis=0)

        taps = jnp.concatenate([own(conv_w[:inner], width), conv_w[inner:]], axis=0).T
        bias = jnp.concatenate([own(conv_b[:inner], width), conv_b[inner:]])
        pad_bc = jnp.zeros((2 * state_size,), F32)
        gain_own = own(gate_gain, width)
        skip_own = jnp.repeat(own(d_skip, heads), head_size)
        prm = jnp.concatenate(
            [
                taps,
                bias[None],
                jnp.concatenate([gain_own, pad_bc])[None],
                jnp.concatenate([skip_own, pad_bc])[None],
                jnp.zeros((1, width + 2 * state_size), F32),
            ],
            axis=0,
        )
        pad_heads = jnp.zeros((LANES - heads,), F32)
        head_prm = jnp.concatenate(
            [
                jnp.concatenate([own(dt_bias, heads), pad_heads])[None],
                jnp.concatenate([jnp.exp(own(a_log, heads)), pad_heads])[None],
                jnp.zeros((6, LANES), F32),
            ],
            axis=0,
        )
        expand = (
            (jnp.arange(2 * LANES) % LANES)[:, None] == (jnp.arange(width) // head_size)[None, :]
        ).astype(BF16)
        mixed, g, g_sum, states = mixer_forward(width, zx, bcdt, pos, prm, head_prm, expand)
        grad_gathered = lax.all_gather(d_out, "tp", axis=0, tiled=True)
        dyo = dot(grad_gathered, w_out, CONTRACT_LAST).astype(BF16)
        eg_sum = jnp.sum(dyo.astype(F32) * gain_own[None, :] * g, axis=1)
        g_total, eg_total = lax.psum((g_sum[0], eg_sum), "tp")
        r_gate = lax.rsqrt(g_total / inner + EPSILON)
        zeros = jnp.zeros_like(r_gate)
        coef = jnp.stack([r_gate] + [zeros] * 7 + [r_gate**3 * (eg_total / inner)] + [zeros] * (LANES - 9), axis=1)
        yo = (g * r_gate[:, None] * gain_own[None, :]).astype(BF16)

    if tp_count == 4:
        block_out, grad_w_out, dz, gz = second_part(
            x_in, yo, yo_t, grad_gathered, w_out, dyo, g, mixed, zx, coef, prm, gathered
        )
        grad_w_z, grad_xs, grad_bcdt, gl, small = third_part(
            own_cols, heads, zx, bcdt, pos, prm, head_prm, expand, mixed, g, states, dyo, coef, gathered, gz
        )
        grad_w_x, grad_rest, grad_x, sums = fourth_part(
            x_in, d_out, norm_gain[None, :], small, dz, grad_xs, grad_bcdt, w_z, w_x, w_bcdt, gathered, gl
        )
        grad_norm_gain = jnp.sum(sums[:, 0, width + 2 * state_size :], axis=0)
    else:

        def scatter_dp(partial):
            return lax.psum_scatter(partial.astype(BF16), "dp", scatter_dimension=0, tiled=True).astype(F32)

        def scatter_tp(array):
            return lax.psum_scatter(array.astype(BF16), "tp", scatter_dimension=0, tiled=True).astype(F32)

        grad_w_out = scatter_dp(dot(grad_gathered, yo, CONTRACT_FIRST)).T
        z = zx[:, :width].astype(F32)
        sig_z = jax.nn.sigmoid(z)
        dg = coef[:, 0:1] * (dyo.astype(F32) * gain_own[None, :]) - g * coef[:, 8:9]
        dz = (dg * mixed * (sig_z * (1.0 + z * (1.0 - sig_z)))).astype(BF16)
        grad_w_z = scatter_dp(dot(gathered, dz, CONTRACT_FIRST))
        block_out = (x_float + scatter_tp(dot(yo, w_out))).astype(BF16)
        grad_xs, grad_bcdt, small = mixer_backward(
            width, zx, bcdt, pos, prm, head_prm, expand, mixed, g, states, dyo, coef
        )
        d_bc = grad_bcdt[:, : 2 * state_size]
        by_owner = jnp.moveaxis(d_bc.reshape(rows, 2, tp_count, own_cols), 2, 0)
        by_owner = by_owner.reshape(tp_count, rows, 2 * own_cols)
        d_bc_own = lax.psum_scatter(by_owner.astype(F32), "tp", scatter_dimension=0, tiled=False)
        d_rest = jnp.concatenate(
            [
                d_bc_own.astype(BF16),
                grad_bcdt[:, 2 * state_size : 2 * state_size + heads],
                jnp.zeros((rows, (-2 * own_cols - heads) % LANES), BF16),
            ],
            axis=1,
        )
        grad_w_x = scatter_dp(dot(gathered, grad_xs, CONTRACT_FIRST))
        grad_rest = scatter_dp(dot(gathered, d_rest, CONTRACT_FIRST))
        du_part = (
            dot(dz, w_z, CONTRACT_LAST) + dot(grad_xs, w_x, CONTRACT_LAST) + dot(grad_bcdt, w_bcdt)
        )
        gain_part = jnp.sum(du_part * gathered.astype(F32), axis=0) / norm_gain
        du = scatter_tp(du_part)
        e_in = du * norm_gain[None, :]
        grad_x = d_out.astype(F32) + r_in * e_in - x_float * (
            r_in**3 * jnp.mean(e_in * x_float, axis=-1, keepdims=True)
        )
        sums = lax.all_gather(lax.psum(small, "dp"), "tp")
        grad_norm_gain = lax.psum(gain_part, ("dp", "tp"))

    channels = jnp.swapaxes(sums[:, :7, :width], 0, 1).reshape(7, inner)
    shared = jnp.sum(sums[:, :5, width : width + 2 * state_size], axis=0)
    grad_conv = jnp.concatenate([channels[:5], shared], axis=1)
    return (
        block_out,
        grad_x,
        grad_norm_gain,
        grad_w_z,
        grad_w_x,
        grad_rest[:, :own_cols],
        grad_rest[:, own_cols : 2 * own_cols],
        grad_rest[:, 2 * own_cols : 2 * own_cols + heads],
        grad_conv[:4].T,
        grad_conv[4],
        sums[:, 7, :heads].reshape(-1),
        sums[:, 7, LANES : LANES + heads].reshape(-1),
        channels[6].reshape(heads * tp_count, head_size).sum(axis=1),
        channels[5],
        grad_w_out,
    )


def solution(mesh):
    rows = P(("dp", "tp"), None)
    columns = P(None, "tp")
    both = P("dp", "tp")
    none = P()
    return jax.shard_map(
        body,
        mesh=mesh,
        in_specs=(
            rows, none, columns, columns, columns, columns, columns, none, none, none, none, none, none,
            P("tp", None), P("dp", None), rows,
        ),
        out_specs=(
            rows, rows, none, both, both, both, both, both, none, none, none, none, none, none, P("tp", "dp"),
        ),
        check_vma=False,
    )
```

```python
import functools

import jax
import jax.numpy as jnp
from jax import lax
from jax.experimental import pallas as pl
from jax.experimental.pallas import tpu as pltpu
from jax.sharding import PartitionSpec as P

EPSILON = 1e-05
HIGHEST = lax.Precision.HIGHEST
F32 = jnp.float32
BF16 = jnp.bfloat16
CHUNK = 128
LANES = 128
CONTRACT_FIRST = (((0,), (0,)), ((), ()))
CONTRACT_LAST = (((1,), (1,)), ((), ()))


def dot(a, b, dims=(((1,), (0,)), ((), ()))):
    return lax.dot_general(a, b, dims, preferred_element_type=F32)


def two_parts(v):
    high = v.astype(BF16)
    return jnp.concatenate([high, (v - high.astype(F32)).astype(BF16)], axis=1)


def prepare_chunk(width, x, bc, raw_dt, pos, prm_ref, head_ref, expand_ref, ext):
    rows = CHUNK
    ext[8:, :width] = x.astype(F32)
    ext[8:, width:] = bc.astype(F32)
    pre = prm_ref[3:4, :] * ext[8:, :] + prm_ref[4:5, :]
    for back in (1, 2, 3):
        here = (pos >= back).astype(F32)
        pre = pre + prm_ref[3 - back : 4 - back, :] * (ext[8 - back : 8 - back + rows, :] * here)
    sig = jax.nn.sigmoid(pre)
    act = pre * sig
    xc = act[:, :width]
    state_size = (act.shape[1] - width) // 2
    b_rows = act[:, width : width + state_size].astype(BF16)
    c_rows = act[:, width + state_size :].astype(BF16)
    raw = raw_dt.astype(F32) + head_ref[0:1, :]
    dt = jnp.maximum(raw, 0.0) + jnp.log1p(jnp.exp(-jnp.abs(raw)))
    log_decay = -dt * head_ref[1:2, :]
    t_idx = lax.broadcasted_iota(jnp.int32, (rows, rows), 0)
    s_idx = lax.broadcasted_iota(jnp.int32, (rows, rows), 1)
    lower = (s_idx <= t_idx).astype(F32)
    cum = lax.dot_general(
        lower, log_decay, (((1,), (0,)), ((), ())), precision=HIGHEST, preferred_element_type=F32
    )
    same = (s_idx <= t_idx) & (s_idx >= t_idx - pos)
    scores = jnp.where(same, dot(c_rows, b_rows, CONTRACT_LAST), 0.0)
    t_col = lax.broadcasted_iota(jnp.int32, (rows, 1), 0)
    pos_last = pos[rows - 1 : rows, :]
    cum_last = cum[rows - 1 : rows, :]
    inward = jnp.exp(cum) * (pos > t_col).astype(F32)
    tail = jnp.exp(cum_last - cum) * (t_col >= rows - 1 - pos_last).astype(F32)
    carried = jnp.exp(cum_last) * (pos_last >= rows).astype(F32)
    wide = dot(
        two_parts(jnp.concatenate([dt, inward, tail, jnp.broadcast_to(carried, (8, LANES))], axis=0)),
        expand_ref[...],
    )
    return dict(
        pre=pre,
        sig=sig,
        xc=xc,
        b=b_rows,
        c=c_rows,
        raw=raw,
        log_decay=log_decay,
        cum=cum,
        cum_t=cum.T,
        same=same,
        scores=scores,
        t_idx=t_idx,
        s_idx=s_idx,
        dt_w=wide[:rows],
        in_w=wide[rows : 2 * rows],
        tail_w=wide[2 * rows : 3 * rows],
        carried_w=wide[3 * rows : 3 * rows + 1],
    )


def decay_of(k, head):
    return jnp.exp(jnp.minimum(k["cum"][:, head : head + 1] - k["cum_t"][head : head + 1, :], 0.0))


def halves(pair):
    lane = lax.broadcasted_iota(jnp.int32, pair.shape, 1)
    zero = jnp.zeros_like(pair)
    return jnp.concatenate(
        [jnp.where(lane < LANES // 2, pair, zero), jnp.where(lane < LANES // 2, zero, pair)], axis=0
    )


def forward_chunk(
    width, at, zx_ref, bcdt_ref, pos_ref, prm_ref, head_ref, expand_ref, mixed_ref, g_ref, sum_ref, state_ref, ext,
    state,
):
    if isinstance(at, int):
        rows = slice(at * CHUNK, (at + 1) * CHUNK)
    else:
        rows = pl.ds(pl.multiple_of(at * CHUNK, CHUNK), CHUNK)
    ext[:8, :] = ext[CHUNK:, :]
    k = prepare_chunk(
        width,
        zx_ref[rows, width:],
        bcdt_ref[rows, : 2 * LANES],
        bcdt_ref[rows, 2 * LANES :],
        pos_ref[rows, :],
        prm_ref,
        head_ref,
        expand_ref,
        ext,
    )
    stepped = (k["xc"] * k["dt_w"]).astype(BF16)
    held = state[...]
    held_low = held.astype(BF16)
    state_ref[at] = held_low
    reached = dot(k["c"], held_low) * k["in_w"] + prm_ref[6:7, :width] * k["xc"]
    weighted = (stepped.astype(F32) * k["tail_w"]).astype(BF16)
    state[...] = k["carried_w"] * held + dot(k["b"], weighted, CONTRACT_FIRST)
    for pair in range(width // LANES):
        lanes = slice(pair * LANES, (pair + 1) * LANES)
        mixing = jnp.concatenate(
            [
                (decay_of(k, 2 * pair) * k["scores"]).astype(BF16),
                (decay_of(k, 2 * pair + 1) * k["scores"]).astype(BF16),
            ],
            axis=1,
        )
        mixed_ref[rows, lanes] = dot(mixing, halves(stepped[:, lanes])) + reached[:, lanes]
    z = zx_ref[rows, :width].astype(F32)
    g = mixed_ref[rows, :] * (z * jax.nn.sigmoid(z))
    g_ref[rows, :] = g
    total = jnp.sum(g * g, axis=1, keepdims=True)
    sum_ref[:, rows] = jnp.broadcast_to(total, (CHUNK, LANES)).T[:8, :]


def forward_kernel(
    width, zx_ref, bcdt_ref, pos_ref, prm_ref, head_ref, expand_ref, mixed_ref, g_ref, sum_ref, state_ref, ext, state
):
    @pl.when(pl.program_id(0) == 0)
    def _():
        state[...] = jnp.zeros_like(state)
        ext[...] = jnp.zeros_like(ext)

    forward_chunk(
        width, 0, zx_ref, bcdt_ref, pos_ref, prm_ref, head_ref, expand_ref, mixed_ref, g_ref, sum_ref, state_ref, ext,
        state,
    )


def backward_chunk(
    width, tokens, halo_x, halo_bc, held, x_ref, bcdt_ref, pos_ref, prm_ref, head_ref, expand_ref, mixed_ref,
    dy_ref, grad_x_ref, grad_bcdt_ref, grad_t_ref, small_ref, ext, d_state, later, later_pos,
):
    rows = CHUNK
    ext[:8, :width] = halo_x.astype(F32)[8:, :]
    ext[:8, width:] = halo_bc.astype(F32)[8:, :]
    pos = pos_ref[tokens, :]
    k = prepare_chunk(
        width,
        x_ref[tokens, :],
        bcdt_ref[tokens, : 2 * LANES],
        bcdt_ref[tokens, 2 * LANES :],
        pos,
        prm_ref,
        head_ref,
        expand_ref,
        ext,
    )
    xc = k["xc"]
    skip = prm_ref[6:7, :width]
    y = mixed_ref[tokens, :] - skip * xc
    dy_low = dy_ref[tokens, :]
    dy = dy_low.astype(F32)
    small_ref[6:7, :width] += jnp.sum(dy * xc, axis=0, keepdims=True)

    stepped = (xc * k["dt_w"]).astype(BF16)
    d_held = d_state[...]
    d_held_low = d_held.astype(BF16)
    held_low = held
    weighted = (stepped.astype(F32) * k["tail_w"]).astype(BF16)
    dy_in = (dy * k["in_w"]).astype(BF16)
    from_state = dot(k["b"], d_held_low) * k["tail_w"]
    dc = dot(dy_in, held_low, CONTRACT_LAST)
    db = dot(weighted, d_held_low, CONTRACT_LAST)
    d_state[...] = k["carried_w"] * d_held + dot(k["c"], dy_in, CONTRACT_FIRST)
    d_scores = jnp.zeros((rows, rows), F32)
    d_stepped = []
    for pair in range(width // LANES):
        lanes = slice(pair * LANES, (pair + 1) * LANES)
        decay_a = decay_of(k, 2 * pair)
        decay_b = decay_of(k, 2 * pair + 1)
        mixing = jnp.concatenate(
            [(decay_a * k["scores"]).astype(BF16), (decay_b * k["scores"]).astype(BF16)], axis=0
        )
        d_mixing = dot(dy_low[:, lanes], halves(stepped[:, lanes]), CONTRACT_LAST)
        d_scores = d_scores + decay_a * d_mixing[:, :rows] + decay_b * d_mixing[:, rows:]
        d_stepped.append(dot(mixing, halves(dy_low[:, lanes]), CONTRACT_FIRST))
    d_stepped = jnp.concatenate(d_stepped, axis=1) + from_state
    d_scores = jnp.where(k["same"], d_scores, 0.0).astype(BF16)
    dc = dc + dot(d_scores, k["b"])
    db = db + dot(d_scores, k["c"], CONTRACT_FIRST)
    dxc = skip * dy + d_stepped * k["dt_w"]

    stepped_f = stepped.astype(F32)
    tail_term = jnp.sum(stepped_f * from_state, axis=0, keepdims=True) + k["carried_w"] * jnp.sum(
        held_low.astype(F32) * d_held, axis=0, keepdims=True
    )
    gathered = two_parts(
        jnp.concatenate([dy * y - stepped_f * d_stepped, jnp.broadcast_to(tail_term, (8, width))], axis=0)
    )
    expand = expand_ref[:LANES, :]
    narrow = dot(gathered[:, :width], expand, CONTRACT_LAST) + dot(gathered[:, width:], expand, CONTRACT_LAST)
    d_cum = narrow[:rows]
    d_dt = dot((d_stepped * xc).astype(BF16), expand, CONTRACT_LAST)
    upper = (k["s_idx"] >= k["t_idx"]).astype(F32)
    d_decay = (
        lax.dot_general(
            upper, d_cum, (((1,), (0,)), ((), ())), precision=HIGHEST, preferred_element_type=F32
        )
        + narrow[rows : rows + 1]
    )
    d_raw = (d_dt - d_decay * head_ref[1:2, :]) * jax.nn.sigmoid(k["raw"])
    small_ref[7:8, :LANES] += jnp.sum(d_raw, axis=0, keepdims=True)
    small_ref[7:8, LANES : 2 * LANES] += jnp.sum(d_decay * k["log_decay"], axis=0, keepdims=True)
    grad_bcdt_ref[tokens, 2 * LANES :] = d_raw.astype(BF16)

    pre, sig = k["pre"], k["sig"]
    d_pre = jnp.concatenate([dxc, db, dc], axis=1) * (sig * (1.0 + pre * (1.0 - sig)))
    small_ref[4:5, :] += jnp.sum(d_pre, axis=0, keepdims=True)
    later[:rows, :] = d_pre
    later_pos[:rows, :] = jnp.broadcast_to(pos, (rows, LANES))
    x_own = ext[8:, :]
    d_in = prm_ref[3:4, :] * d_pre
    small_ref[3:4, :] += jnp.sum(d_pre * x_own, axis=0, keepdims=True)
    for back in (1, 2, 3):
        there = (later_pos[back : back + rows, 0:1] >= back).astype(F32)
        reaching = later[back : back + rows, :] * there
        small_ref[3 - back : 4 - back, :] += jnp.sum(reaching * x_own, axis=0, keepdims=True)
        d_in = d_in + prm_ref[3 - back : 4 - back, :] * reaching
    grad_x_ref[tokens, :] = d_in[:, :width].astype(BF16)
    grad_bcdt_ref[tokens, : 2 * LANES] = d_in[:, width:].astype(BF16)
    later[rows:, :] = later[:8, :]
    later_pos[rows:, :] = later_pos[:8, :]
    if grad_t_ref is not None:
        grad_t_ref[:width, tokens] = d_in[:, :width].T.astype(BF16)


def backward_start(small_ref, d_state, later, later_pos):
    d_state[...] = jnp.zeros_like(d_state)
    later[...] = jnp.zeros_like(later)
    later_pos[...] = jnp.zeros_like(later_pos)
    small_ref[...] = jnp.zeros_like(small_ref)


def backward_kernel(
    width, x_ref, bcdt_ref, halo_x_ref, halo_bc_ref, pos_ref, prm_ref, head_ref,
    expand_ref, mixed_ref, state_ref, dy_ref, grad_x_ref, grad_bcdt_ref, small_ref, ext, d_state,
    later, later_pos,
):
    @pl.when(pl.program_id(0) == 0)
    def _():
        backward_start(small_ref, d_state, later, later_pos)

    backward_chunk(
        width, slice(0, CHUNK), halo_x_ref[...], halo_bc_ref[:, : 2 * LANES], state_ref[0], x_ref, bcdt_ref, pos_ref,
        prm_ref, head_ref, expand_ref, mixed_ref, dy_ref, grad_x_ref, grad_bcdt_ref, None, small_ref,
        ext, d_state, later, later_pos,
    )


def mixer_forward(width, zx, bcdt, pos, prm, head_prm, expand):
    rows = zx.shape[0]
    chunks = rows // CHUNK

    def tokens(columns):
        return pl.BlockSpec((CHUNK, columns), lambda i: (i, 0))

    def whole(array):
        return pl.BlockSpec(array.shape, lambda i: (0, 0))

    return pl.pallas_call(
        functools.partial(forward_kernel, width),
        out_shape=(
            jax.ShapeDtypeStruct((rows, width), F32),
            jax.ShapeDtypeStruct((rows, width), F32),
            jax.ShapeDtypeStruct((8, rows), F32),
            jax.ShapeDtypeStruct((chunks, LANES, width), BF16),
        ),
        grid=(chunks,),
        in_specs=[tokens(2 * width), tokens(3 * LANES), tokens(1), whole(prm), whole(head_prm), whole(expand)],
        out_specs=(
            tokens(width),
            tokens(width),
            pl.BlockSpec((8, CHUNK), lambda i: (0, i)),
            pl.BlockSpec((1, LANES, width), lambda i: (i, 0, 0)),
        ),
        scratch_shapes=[
            pltpu.VMEM((CHUNK + 8, width + 2 * LANES), F32),
            pltpu.VMEM((LANES, width), F32),
        ],
        compiler_params=pltpu.CompilerParams(
            dimension_semantics=("arbitrary",), vmem_limit_bytes=40 * 1024 * 1024
        ),
    )(zx, bcdt, pos, prm, head_prm, expand)


def mixer_backward(width, zx, bcdt, pos, prm, head_prm, expand, mixed, states, dy):
    rows = zx.shape[0]
    chunks = rows // CHUNK

    def tokens(columns):
        return pl.BlockSpec((CHUNK, columns), lambda i: (chunks - 1 - i, 0))

    def before(columns, place):
        return pl.BlockSpec(
            (16, columns), lambda i: (jnp.maximum((chunks - 1 - i) * (CHUNK // 16) - 1, 0), place)
        )

    def whole(array):
        return pl.BlockSpec(array.shape, lambda i: (0, 0))

    return pl.pallas_call(
        functools.partial(backward_kernel, width),
        out_shape=(
            jax.ShapeDtypeStruct((rows, width), BF16),
            jax.ShapeDtypeStruct((rows, 3 * LANES), BF16),
            jax.ShapeDtypeStruct((8, width + 2 * LANES), F32),
        ),
        grid=(chunks,),
        in_specs=[
            pl.BlockSpec((CHUNK, width), lambda i: (chunks - 1 - i, 1)),
            tokens(3 * LANES),
            before(width, 1),
            before(3 * LANES, 0),
            tokens(1),
            whole(prm),
            whole(head_prm),
            whole(expand),
            tokens(width),
            pl.BlockSpec((1, LANES, width), lambda i: (chunks - 1 - i, 0, 0)),
            tokens(width),
        ],
        out_specs=(
            tokens(width),
            tokens(3 * LANES),
            pl.BlockSpec((8, width + 2 * LANES), lambda i: (0, 0)),
        ),
        scratch_shapes=[
            pltpu.VMEM((CHUNK + 8, width + 2 * LANES), F32),
            pltpu.VMEM((LANES, width), F32),
            pltpu.VMEM((CHUNK + 8, width + 2 * LANES), F32),
            pltpu.VMEM((CHUNK + 8, LANES), jnp.int32),
        ],
        compiler_params=pltpu.CompilerParams(
            dimension_semantics=("arbitrary",), vmem_limit_bytes=48 * 1024 * 1024
        ),
        cost_estimate=pl.CostEstimate(flops=rows * width * 2048, bytes_accessed=rows * width * 20, transcendentals=0),
    )(zx, bcdt, zx, bcdt, pos, prm, head_prm, expand, mixed, states, dy)


MESH = pl.DeviceIdType.MESH


def tp_places():
    me = lax.axis_index("tp")
    return me, me + 1 - 2 * lax.rem(me, 2), lax.rem(me + 2, 4), 3 - me


def greet(peers):
    barrier = pltpu.get_barrier_semaphore()
    for peer in peers:
        pl.semaphore_signal(barrier, inc=1, device_id=peer, device_id_type=MESH)
    pl.semaphore_wait(barrier, len(peers))


def send(src, dst, send_sem, recv_sem, peer):
    return pltpu.make_async_remote_copy(
        src_ref=src, dst_ref=dst, send_sem=send_sem, recv_sem=recv_sem, device_id=peer, device_id_type=MESH
    )


class Gather:
    def __init__(self, whole, rows, send_sems, recv_sems, own=None):
        me, side, up, _ = tp_places()
        half = rows // 2

        def part(place, start, count):
            return whole.at[pl.ds(pl.multiple_of(place * rows + start, half), count)]

        own = part(me, 0, rows) if own is None else own
        self.to_side = send(own, part(me, 0, rows), send_sems.at[0], recv_sems.at[0], {"tp": side})
        self.to_up = send(own, part(me, 0, rows), send_sems.at[1], recv_sems.at[1], {"tp": up})
        self.pass_up = send(
            part(side, 0, half), part(side, 0, half), send_sems.at[2], recv_sems.at[2], {"tp": up}
        )
        self.pass_side = send(
            part(up, half, half), part(up, half, half), send_sems.at[3], recv_sems.at[3], {"tp": side}
        )

    def start(self):
        self.to_side.start()
        self.to_up.start()

    def forward(self):
        self.to_side.wait_recv()
        self.pass_up.start()
        self.to_up.wait_recv()
        self.pass_side.start()

    def finish(self):
        self.pass_up.wait_recv()
        self.pass_side.wait_recv()

    def end(self):
        for copy in (self.to_side, self.to_up, self.pass_up, self.pass_side):
            copy.wait_send()


def set_up(width, heads, inner, taps_ref, flat_ref, lens_ref, prm, head, expand, pos):
    rank = lax.axis_index("tp")
    channels = taps_ref.shape[1]
    own = pl.ds(pl.multiple_of(rank * width, LANES), width)
    own_gain = pl.ds(pl.multiple_of(channels + rank * width, LANES), width)
    prm[...] = jnp.zeros_like(prm)
    prm[0:4, :width] = taps_ref[:, own]
    prm[0:4, width:] = taps_ref[:, inner:]
    prm[4:5, :width] = flat_ref[:, own]
    prm[4:5, width:] = flat_ref[:, inner:channels]
    prm[5:6, :width] = flat_ref[:, own_gain]
    lane = lax.broadcasted_iota(jnp.int32, (LANES, LANES), 1)
    pick = ((lax.broadcasted_iota(jnp.int32, (LANES, LANES), 0) == lane + rank * heads) & (lane < heads)).astype(F32)
    start = channels + inner
    tiles = [jnp.broadcast_to(flat_ref[:, start + n * LANES : start + (n + 1) * LANES], (8, LANES)) for n in range(3)]
    tiles[1] = jnp.exp(tiles[1])
    picked = lax.dot_general(
        jnp.concatenate(tiles, axis=0), pick, (((1,), (0,)), ((), ())), precision=HIGHEST, preferred_element_type=F32
    )
    head[...] = jnp.concatenate([picked[0:1], picked[8:9], jnp.zeros((6, LANES), F32)], axis=0)
    row = lax.broadcasted_iota(jnp.int32, (2 * LANES, width), 0)
    column = lax.broadcasted_iota(jnp.int32, (2 * LANES, width), 1)
    expand[...] = (lax.rem(row, LANES) == column // (width // heads)).astype(F32).astype(BF16)
    prm[6:7, :width] = dot(two_parts(picked[16:24]), expand[...])[0:1]
    starts = [jnp.int32(0)]
    for n in range(lens_ref.shape[1] - 1):
        starts.append(starts[-1] + lens_ref[0, n])

    def place(i, carry):
        token = lax.broadcasted_iota(jnp.int32, (CHUNK, 1), 0) + i * CHUNK
        begun = jnp.zeros((CHUNK, 1), jnp.int32)
        for first in starts[1:]:
            begun = jnp.where(token >= first, first, begun)
        pos[pl.ds(pl.multiple_of(i * CHUNK, CHUNK), CHUNK), :] = token - begun
        return carry

    lax.fori_loop(0, pos.shape[0] // CHUNK, place, 0)


def first_kernel(
    inner, heads, own_cols, x_ref, gain_ref, small_ref, taps_ref, flat_ref, lens_ref, wz_ref, wx_ref, w_out_ref, d_own_ref,
    u_out, zx_out, bcdt_out, wbc_out, mixed_out, g_out, yo_out, yo_t_out, state_out, d_out, dyo_out, coef_out, pos_out,
    prm_out, head_out, expand_out,
    weights, w_out, u, zx, bcdt, wbc, mixed, g, yo, yo_t, states, d, dyo, coef, pos, prm, head, expand, ext, state, sums,
    acc, sems, sum_sems, load_sems, store_sems,
):
    rows, model = x_ref.shape
    total, width = mixed.shape
    chunks = total // CHUNK
    me, side, up, far = tp_places()
    dp = lax.axis_index("dp")
    parity = lax.rem(dp, 2)
    partner = {"dp": dp + 1 - 2 * parity}

    def block(place):
        return pl.ds(pl.multiple_of(place * rows, rows), rows)

    loads = [
        pltpu.make_async_copy(wz_ref, weights.at[:, :width], load_sems.at[0]),
        pltpu.make_async_copy(wx_ref, weights.at[:, width:], load_sems.at[1]),
        pltpu.make_async_copy(w_out_ref, w_out, load_sems.at[2]),
        pltpu.make_async_copy(d_own_ref, d.at[block(me)], load_sems.at[3]),
    ]
    for copy in loads:
        copy.start()
    stores = []

    def keep(source, target):
        copy = pltpu.make_async_copy(source, target, store_sems.at[len(stores)])
        copy.start()
        stores.append(copy)

    bc_own = pl.ds(pl.multiple_of(parity * LANES, LANES), LANES)
    wbc[pl.ds(pl.multiple_of(parity * LANES + me * own_cols, own_cols), own_cols), :] = small_ref[
        pl.ds(pl.multiple_of(parity * own_cols, own_cols), own_cols), :
    ]
    greet([{"tp": side}, {"tp": up}, {"tp": far}, partner])
    small_gather = Gather(wbc.at[bc_own], own_cols, sems.at[0], sems.at[1])
    small_gather.start()

    def norm(i, carry):
        piece = pl.ds(pl.multiple_of(i * 32, 32), 32)
        x = x_ref[piece, :].astype(F32)
        scale = lax.rsqrt(jnp.mean(x * x, axis=-1, keepdims=True) + EPSILON)
        u[pl.ds(pl.multiple_of(me * rows + i * 32, 32), 32), :] = (x * scale * gain_ref[...]).astype(BF16)
        return carry

    lax.fori_loop(0, rows // 32, norm, 0)
    gather = Gather(u, rows, sems.at[2], sems.at[3])
    gather.start()
    wbc[2 * LANES :, :] = jnp.zeros((LANES, model), BF16)
    wbc[2 * LANES : 2 * LANES + heads, :] = small_ref[2 * own_cols :, :]
    set_up(width, heads, inner, taps_ref, flat_ref, lens_ref, prm, head, expand, pos)
    keep(pos, pos_out)
    keep(prm, prm_out)
    keep(head, head_out)
    keep(expand, expand_out)
    loads[0].wait()
    loads[1].wait()

    def project(place):
        piece = block(place)

        def tile(n, carry):
            columns = pl.ds(pl.multiple_of(n * 512, 512), 512)
            zx[piece, columns] = dot(u[piece, :], weights[:, columns]).astype(BF16)
            return carry

        lax.fori_loop(0, 2 * width // 512, tile, 0)

    def project_small(place):
        bcdt[block(place), :] = dot(u[block(place), :], wbc[...], CONTRACT_LAST).astype(BF16)

    small_gather.forward()
    project(me)
    small_gather.finish()
    trade = send(wbc.at[bc_own], wbc.at[bc_own], sems.at[6, 0], sems.at[6, 1], partner)
    trade.start()
    gather.forward()
    project(side)
    project(up)
    trade.wait()
    keep(wbc, wbc_out)
    project_small(me)
    project_small(side)
    project_small(up)
    gather.finish()
    loads[3].wait()
    d_gather = Gather(d, rows, sems.at[4], sems.at[5])
    d_gather.start()
    keep(u, u_out)
    project(far)
    project_small(far)
    keep(zx, zx_out)
    keep(bcdt, bcdt_out)

    state[...] = jnp.zeros_like(state)
    ext[...] = jnp.zeros_like(ext)

    def chunk(i, carry):
        forward_chunk(
            width, i, zx, bcdt, pos, prm, head, expand, mixed, g, sums.at[0, 0], states, ext, state
        )
        return carry

    lax.fori_loop(0, chunks, chunk, 0)

    def exchange(which):
        copies = [
            send(
                sums.at[which, 0], sums.at[which, 1 + n], sum_sems.at[which, 0, n], sum_sems.at[which, 1, n], {"tp": peer}
            )
            for n, peer in enumerate((side, up, far))
        ]
        for copy in copies:
            copy.start()
        return copies

    copies = exchange(0)
    keep(mixed, mixed_out)
    keep(g, g_out)
    keep(states, state_out)
    loads[2].wait()

    def back_to_heads(place):
        piece = block(place)
        acc[...] = jnp.zeros_like(acc)

        def tile(n, carry):
            columns = pl.ds(pl.multiple_of(n * 256, 256), 256)
            low = dot(d[piece, :], w_out[columns, :], CONTRACT_LAST).astype(BF16)
            dyo[piece, columns] = low
            both = low.astype(F32) * prm[5:6, columns] * g[piece, columns]
            acc[...] += both[:, :LANES] + both[:, LANES:]
            return carry

        lax.fori_loop(0, width // 256, tile, 0)
        column = jnp.sum(acc[...], axis=1, keepdims=True)
        sums[1, 0, :, piece] = jnp.broadcast_to(column, (rows, LANES)).T[:8, :]
        keep(dyo.at[piece], dyo_out.at[piece])

    d_gather.forward()
    back_to_heads(me)
    for copy in copies:
        copy.wait()

    def gate(i, carry):
        piece = pl.ds(pl.multiple_of(i * CHUNK, CHUNK), CHUNK)
        squares = sums[0, 0, :, piece] + sums[0, 1, :, piece] + sums[0, 2, :, piece] + sums[0, 3, :, piece]
        scale = lax.rsqrt(squares / inner + EPSILON)
        columns = jnp.concatenate([scale, jnp.zeros((LANES - 8, LANES), F32)], axis=0).T
        gated = g[piece, :] * columns[:, 0:1] * prm[5:6, :width]
        yo[piece, :] = gated.astype(BF16)
        yo_t[:, piece] = gated.T.astype(BF16)
        return carry

    lax.fori_loop(0, chunks, gate, 0)
    keep(yo, yo_out)
    keep(yo_t, yo_t_out)
    back_to_heads(side)
    back_to_heads(up)
    d_gather.finish()
    keep(d, d_out)
    back_to_heads(far)
    copies = exchange(1)
    for copy in copies:
        copy.wait()

    def weigh(i, carry):
        piece = pl.ds(pl.multiple_of(i * CHUNK, CHUNK), CHUNK)
        squares = sums[0, 0, :, piece] + sums[0, 1, :, piece] + sums[0, 2, :, piece] + sums[0, 3, :, piece]
        cross = sums[1, 0, :, piece] + sums[1, 1, :, piece] + sums[1, 2, :, piece] + sums[1, 3, :, piece]
        scale = lax.rsqrt(squares / inner + EPSILON)
        back = scale * scale * scale * (cross / inner)
        coef[piece, :] = jnp.concatenate([scale, back, jnp.zeros((LANES - 16, LANES), F32)], axis=0).T
        return carry

    lax.fori_loop(0, chunks, weigh, 0)
    keep(coef, coef_out)
    small_gather.end()
    gather.end()
    d_gather.end()
    for copy in stores:
        copy.wait()


def first_part(inner, heads, own_cols, x_in, gain, small, taps, flat, lens, w_z, w_x, w_out, d_out):
    rows, model = x_in.shape
    total = 4 * rows
    width = w_z.shape[1]
    chunks = total // CHUNK
    vmem = pl.BlockSpec(memory_space=pltpu.VMEM)
    anywhere = pl.BlockSpec(memory_space=pl.ANY)
    results = [
        ((total, model), BF16),
        ((total, 2 * width), BF16),
        ((total, 3 * LANES), BF16),
        ((3 * LANES, model), BF16),
        ((total, width), F32),
        ((total, width), F32),
        ((total, width), BF16),
        ((width, total), BF16),
        ((chunks, LANES, width), BF16),
        ((total, model), BF16),
        ((total, width), BF16),
        ((total, LANES), F32),
        ((total, 1), jnp.int32),
        ((8, width + 2 * LANES), F32),
        ((8, LANES), F32),
        ((2 * LANES, width), BF16),
    ]
    return pl.pallas_call(
        functools.partial(first_kernel, inner, heads, own_cols),
        out_shape=[jax.ShapeDtypeStruct(*result) for result in results],
        in_specs=[vmem] * 5 + [pl.BlockSpec(memory_space=pltpu.SMEM)] + [anywhere] * 4,
        out_specs=[anywhere] * len(results),
        scratch_shapes=[pltpu.VMEM((model, 2 * width), BF16), pltpu.VMEM((width, model), BF16)]
        + [pltpu.VMEM(*result) for result in results]
        + [
            pltpu.VMEM((CHUNK + 8, width + 2 * LANES), F32),
            pltpu.VMEM((LANES, width), F32),
            pltpu.VMEM((2, 4, 8, total), F32),
            pltpu.VMEM((rows, LANES), F32),
            pltpu.SemaphoreType.DMA((7, 4)),
            pltpu.SemaphoreType.DMA((2, 2, 3)),
            pltpu.SemaphoreType.DMA((4,)),
            pltpu.SemaphoreType.DMA((24,)),
        ],
        compiler_params=pltpu.CompilerParams(
            collective_id=0, has_side_effects=True, vmem_limit_bytes=60 * 1024 * 1024
        ),
    )(x_in, gain, small, taps, flat, lens, w_z, w_x, w_out, d_out)


def add_into(target, other):
    tile = 128

    def one(i, carry):
        piece = pl.ds(pl.multiple_of(i * tile, tile), tile)
        target[piece, :] = (target[piece, :].astype(F32) + other[piece, :].astype(F32)).astype(BF16)
        return carry

    lax.fori_loop(0, target.shape[0] // tile, one, 0)


class LineSum:
    def __init__(self, parts, pair, right, left, pair_sems, right_sems, left_sems):
        dp = lax.axis_index("dp")
        self.dp = dp
        self.count = parts.shape[0] // 2
        self.z = dp // 2
        self.parity = lax.rem(dp, 2)
        self.partner = {"dp": dp + 1 - 2 * self.parity}
        self.parts, self.pair = parts, pair
        self.lines = {1: (right, right_sems), -1: (left, left_sems)}
        self.swaps = {}
        self.pair_sems = pair_sems

    def peers(self):
        n = 2 * self.count
        return [self.partner, {"dp": lax.rem(self.dp + 2, n)}, {"dp": lax.rem(self.dp + n - 2, n)}]

    def order(self):
        low, high, out = 0, self.count - 1, []
        while low <= high:
            out += [high, low] if low < high else [low]
            low, high = low + 1, high - 1
        return out

    def swap(self, z):
        copy = send(
            self.parts.at[2 * z + 1 - self.parity], self.pair.at[z], self.pair_sems.at[0, z], self.pair_sems.at[1, z],
            self.partner,
        )
        copy.start()
        self.swaps[z] = copy

    def merge(self, z):
        self.swaps[z].wait()
        add_into(self.parts.at[2 * z + self.parity], self.pair.at[z])

    def away(self, way):
        return self.z if way == 1 else self.count - 1 - self.z

    def copy(self, way, step):
        line, line_sems = self.lines[way]
        far = self.count - step + self.away(way)
        z = far if way == 1 else self.count - 1 - far
        chunk = self.parts.at[2 * z + self.parity]
        return chunk, send(
            chunk, line.at[step - 1], line_sems.at[0, step - 1], line_sems.at[1, step - 1],
            {"dp": self.dp + 2 * way},
        )

    def arrived(self, way, step):
        line, line_sems = self.lines[way]
        return send(
            self.parts.at[self.dp], line.at[step - 1], line_sems.at[0, step - 1], line_sems.at[1, step - 1],
            self.partner,
        )

    def move(self, step):
        for way in (1, -1):
            away = self.away(way)

            @pl.when(away == 0)
            def _():
                if step > 1:
                    self.copy(way, step - 1)[1].wait_send()
                self.copy(way, step)[1].start()

            if step > 1:

                @pl.when((away >= 1) & (away <= min(step - 1, self.count - 2)))
                def _():
                    chunk, copy = self.copy(way, step)
                    self.arrived(way, step - 1).wait_recv()
                    add_into(chunk, self.lines[way][0].at[step - 2])
                    copy.start()

    def finish(self):
        last = self.count - 1
        for way in (1, -1):

            @pl.when(self.away(way) >= 1)
            def _():
                self.arrived(way, last).wait_recv()

        total = self.parts.at[self.dp]
        for way in (1, -1):

            @pl.when(self.away(way) >= 1)
            def _():
                add_into(total, self.lines[way][0].at[last - 1])

        return total

    def end(self):
        for way in (1, -1):
            away = self.away(way)
            for step in range(1, self.count):

                @pl.when((away <= step - 1) & (away <= self.count - 2) & ((away >= 1) | (step == self.count - 1)))
                def _():
                    self.copy(way, step)[1].wait_send()


class PlaneSum:
    def __init__(self, away, to_side, to_up, in_half, in_side, in_up, sems):
        _, side, up, _ = tp_places()
        side, up = {"tp": side}, {"tp": up}
        rows = to_side.shape[0]
        half = rows // 2
        self.to_side, self.to_up, self.in_half, self.half = to_side, to_up, in_half, half
        self.in_side, self.in_up = in_side, in_up
        low, high = pl.ds(0, half), pl.ds(half, half)

        def one(n, source, target, peer):
            return send(source, target, sems.at[0, n], sems.at[1, n], peer)

        self.away_side = one(0, away.at[low], in_half.at[0], side)
        self.away_up = one(1, away.at[high], in_half.at[1], up)
        self.side_low = one(2, to_side.at[low], in_side.at[low], side)
        self.side_high = one(3, to_side.at[high], in_side.at[high], side)
        self.up_low = one(4, to_up.at[low], in_up.at[low], up)
        self.up_high = one(5, to_up.at[high], in_up.at[high], up)
        self.low, self.high = low, high

    def start_far(self):
        self.away_side.start()
        self.away_up.start()

    def start_side(self):
        self.side_low.start()

    def start_up(self):
        self.up_high.start()

    def pass_on(self):
        self.away_side.wait_recv()
        add_into(self.to_up.at[self.low], self.in_half.at[0])
        self.up_low.start()
        self.away_up.wait_recv()
        add_into(self.to_side.at[self.high], self.in_half.at[1])
        self.side_high.start()

    def finish(self):
        for copy in (self.side_low, self.up_high, self.side_high, self.up_low):
            copy.wait_recv()

    def end(self):
        for copy in (self.away_side, self.away_up, self.side_low, self.side_high, self.up_low, self.up_high):
            copy.wait_send()


def plane_scratch(rows, model):
    half = rows // 2
    return [
        pltpu.VMEM((rows, model), BF16),
        pltpu.VMEM((rows, model), BF16),
        pltpu.VMEM((rows, model), BF16),
        pltpu.VMEM((2, half, model), BF16),
        pltpu.VMEM((rows, model), BF16),
        pltpu.VMEM((rows, model), BF16),
        pltpu.SemaphoreType.DMA((2, 6)),
    ]


def line_scratch(dp_count, shape):
    z = dp_count // 2
    return [
        pltpu.VMEM((dp_count,) + shape, BF16),
        pltpu.VMEM((z,) + shape, BF16),
        pltpu.VMEM((z - 1,) + shape, BF16),
        pltpu.VMEM((z - 1,) + shape, BF16),
        pltpu.SemaphoreType.DMA((2, z)),
        pltpu.SemaphoreType.DMA((2, z - 1)),
        pltpu.SemaphoreType.DMA((2, z - 1)),
    ]


class Copies:
    def __init__(self, sems):
        self.sems, self.started = sems, []

    def start(self, source, target):
        copy = pltpu.make_async_copy(source, target, self.sems.at[len(self.started)])
        copy.start()
        self.started.append(copy)
        return copy


def product_chunk(left_t, right, chunk, target, tile):
    columns = pl.ds(pl.multiple_of(chunk * target.shape[1], target.shape[1]), target.shape[1])

    def one(i, carry):
        piece = pl.ds(pl.multiple_of(i * tile, tile), tile)
        target[piece, :] = dot(left_t[piece, :], right[:, columns]).astype(BF16)
        return carry

    lax.fori_loop(0, target.shape[0] // tile, one, 0)


def second_kernel(
    x_ref, yo_ref, yo_t_ref, d_ref, w_out_ref, dyo_ref, g_ref, mixed_ref, zx_ref, coef_ref, prm_ref, u_ref,
    block_out, gw_out, dz_out, dy_out, gz_out, gain_out,
    yo, yo_t, d, w_out, dyo, g, mixed, z, coef, own, gz,
    parts, pair, right, left, pair_sems, right_sems, left_sems,
    away, to_side, to_up, in_half, in_side, in_up, plane_sems, load_sems, store_sems,
):
    rows, model = x_ref.shape
    total, width = yo.shape
    taken = parts.shape[1]
    me, side, up, far = tp_places()
    loads, stores = Copies(load_sems), Copies(store_sems)
    load_yo = loads.start(yo_ref, yo)
    load_w = loads.start(w_out_ref, w_out)
    line = LineSum(parts, pair, right, left, pair_sems, right_sems, left_sems)
    plane = PlaneSum(away, to_side, to_up, in_half, in_side, in_up, plane_sems)
    greet([{"tp": side}, {"tp": up}] + line.peers())

    def out_block(place, target):
        piece = pl.ds(pl.multiple_of(place * rows, rows), rows)

        def tile(n, carry):
            columns = pl.ds(pl.multiple_of(n * 512, 512), 512)
            target[:, columns] = dot(yo[piece, :], w_out[:, columns]).astype(target.dtype)
            return carry

        lax.fori_loop(0, model // 512, tile, 0)

    load_yo.wait()
    load_w.wait()
    load_yo_t = loads.start(yo_t_ref, yo_t)
    load_d = loads.start(d_ref, d)
    out_block(far, away)
    plane.start_far()
    load_yo_t.wait()
    load_d.wait()
    rest = [
        loads.start(dyo_ref, dyo),
        loads.start(g_ref, g),
        loads.start(mixed_ref, mixed),
        loads.start(zx_ref.at[:, :width], z),
        loads.start(coef_ref, coef),
    ]
    order = line.order()

    def products(z_chunk):
        for chunk in (2 * z_chunk + 1 - line.parity, 2 * z_chunk + line.parity):
            product_chunk(yo_t, d, chunk, parts.at[chunk], taken // 2)
            if z_chunk not in line.swaps:
                line.swap(z_chunk)

    for z_chunk in order[:2]:
        products(z_chunk)
    for z_chunk in order[:2]:
        line.merge(z_chunk)
    line.move(1)
    for z_chunk in order[2:]:
        products(z_chunk)

    def left_over(chunk, carry):
        columns = pl.ds(pl.multiple_of(chunk * parts.shape[2], parts.shape[2]), parts.shape[2])
        gz[chunk, width:, :] = dot(yo_t[taken:, :], d[:, columns]).astype(BF16)
        return carry

    dp_count = parts.shape[0]
    for z_chunk in order[2:]:
        line.merge(z_chunk)
    out_block(side, to_side)
    plane.start_side()
    out_block(up, to_up)
    plane.start_up()
    lax.fori_loop(0, dp_count, left_over, 0)
    load_u = loads.start(u_ref, d)
    line.move(2)
    plane.pass_on()
    out_block(me, own)
    for copy in rest:
        copy.wait()
    gain_out[...] = jnp.zeros_like(gain_out)

    def gate_back(i, carry):
        piece = pl.ds(pl.multiple_of(i * CHUNK, CHUNK), CHUNK)
        z_piece = z[piece, :].astype(F32)
        sig = jax.nn.sigmoid(z_piece)
        dyo_piece = dyo[piece, :].astype(F32)
        g_piece = g[piece, :]
        scaled = coef[piece, 0:1] * dyo_piece
        dg = scaled * prm_ref[5:6, :width] - g_piece * coef[piece, 8:9]
        gain_out[0:1, :] += jnp.sum(scaled * g_piece, axis=0, keepdims=True)
        dz = dg * mixed[piece, :] * (sig * (1.0 + z_piece * (1.0 - sig)))
        yo[piece, :] = dz.astype(BF16)
        yo_t[:, piece] = dz.T.astype(BF16)
        dyo[piece, :] = (dg * (z_piece * sig)).astype(BF16)
        return carry

    chunks = total // CHUNK
    lax.fori_loop(0, chunks, gate_back, 0)
    stores.start(yo, dz_out)
    stores.start(dyo, dy_out)
    for step in range(3, line.count):
        line.move(step)
    load_u.wait()

    def gate_products(chunk, carry):
        product_chunk(yo_t, d, chunk, gz.at[chunk, :width], width // 2)
        return carry

    lax.fori_loop(0, dp_count, gate_products, 0)
    stores.start(gz, gz_out)
    sum_ref = line.finish()
    gw_out[...] = sum_ref[...].astype(F32)
    plane.finish()

    def add_own(i, carry):
        piece = pl.ds(pl.multiple_of(i * 32, 32), 32)
        total_out = own[piece, :] + in_side[piece, :].astype(F32) + in_up[piece, :].astype(F32)
        block_out[piece, :] = (x_ref[piece, :].astype(F32) + total_out).astype(BF16)
        return carry

    lax.fori_loop(0, rows // 32, add_own, 0)
    line.end()
    plane.end()
    for copy in stores.started:
        copy.wait()


def second_part(x_in, yo, yo_t, d, w_out, dyo, g, mixed, zx, coef, prm, u):
    rows, model = x_in.shape
    total, width = yo.shape
    dp_count = lax.axis_size("dp")
    cut = model // dp_count
    kept = width // 8
    vmem = pl.BlockSpec(memory_space=pltpu.VMEM)
    anywhere = pl.BlockSpec(memory_space=pl.ANY)
    return pl.pallas_call(
        second_kernel,
        out_shape=(
            jax.ShapeDtypeStruct((rows, model), BF16),
            jax.ShapeDtypeStruct((width - kept, cut), F32),
            jax.ShapeDtypeStruct((total, width), BF16),
            jax.ShapeDtypeStruct((total, width), BF16),
            jax.ShapeDtypeStruct((dp_count, width + kept, cut), BF16),
            jax.ShapeDtypeStruct((8, width), F32),
        ),
        in_specs=[vmem] + [anywhere] * 9 + [vmem, anywhere],
        out_specs=(vmem, vmem, anywhere, anywhere, anywhere, vmem),
        scratch_shapes=[
            pltpu.VMEM((total, width), BF16),
            pltpu.VMEM((width, total), BF16),
            pltpu.VMEM((total, model), BF16),
            pltpu.VMEM((width, model), BF16),
            pltpu.VMEM((total, width), BF16),
            pltpu.VMEM((total, width), F32),
            pltpu.VMEM((total, width), F32),
            pltpu.VMEM((total, width), BF16),
            pltpu.VMEM((total, LANES), F32),
            pltpu.VMEM((rows, model), F32),
            pltpu.VMEM((dp_count, width + kept, cut), BF16),
        ]
        + line_scratch(dp_count, (width - kept, cut))
        + plane_scratch(rows, model)
        + [pltpu.SemaphoreType.DMA((10,)), pltpu.SemaphoreType.DMA((3,))],
        compiler_params=pltpu.CompilerParams(
            collective_id=1, has_side_effects=True, vmem_limit_bytes=60 * 1024 * 1024
        ),
    )(x_in, yo, yo_t, d, w_out, dyo, g, mixed, zx, coef, prm, u)


def third_kernel(
    own_cols, heads, zx_ref, bcdt_ref, pos_ref, prm_ref, head_ref, expand_ref, mixed_ref, state_ref, dy_ref,
    u_ref, gz_ref,
    gw_z, gw_last, dx_out, dbcdt_out, gl_out, small_out,
    x, bcdt, mixed, states, dy, u, dx, dbcdt, dx_t, gl, bc_in, ext, d_state, later, later_pos,
    parts, pair, right, left, pair_sems, right_sems, left_sems, bc_sems, load_sems, store_sems,
):
    total, width = mixed.shape
    chunks = total // CHUNK
    me, side, up, far = tp_places()
    dp_count = parts.shape[0]
    loads, stores = Copies(load_sems), Copies(store_sems)
    load_parts = loads.start(gz_ref, parts)
    line = LineSum(parts, pair, right, left, pair_sems, right_sems, left_sems)
    greet([{"tp": side}, {"tp": up}, {"tp": far}] + line.peers())
    load_parts.wait()
    order = line.order()
    for z_chunk in order:
        line.swap(z_chunk)
    halves_of_loads = []
    for first in (total // 2, 0):
        piece = pl.ds(first, total // 2)
        pieces = pl.ds(first // CHUNK, chunks // 2)
        halves_of_loads.append(
            [
                loads.start(zx_ref.at[piece, width:], x.at[piece]),
                loads.start(bcdt_ref.at[piece], bcdt.at[piece]),
                loads.start(mixed_ref.at[piece], mixed.at[piece]),
                loads.start(state_ref.at[pieces], states.at[pieces]),
                loads.start(dy_ref.at[piece], dy.at[piece]),
            ]
        )
    load_u = loads.start(u_ref, u)
    backward_start(small_out, d_state, later, later_pos)
    for z_chunk in order[:2]:
        line.merge(z_chunk)
    line.move(1)
    for z_chunk in order[2:]:
        line.merge(z_chunk)
    for copies in halves_of_loads:
        for copy in copies:
            copy.wait()
    hooks = {3: 2, 7: 3}

    def chunk(i, carry):
        at = chunks - 1 - i
        tokens = pl.ds(pl.multiple_of(at * CHUNK, CHUNK), CHUNK)
        halo = pl.ds(pl.multiple_of(lax.rem(at * CHUNK + total - 16, total), 16), 16)
        backward_chunk(
            width, tokens, x[halo, :], bcdt[halo, : 2 * LANES], states[at], x, bcdt, pos_ref, prm_ref, head_ref,
            expand_ref, mixed, dy, dx, dbcdt, dx_t, small_out, ext, d_state, later, later_pos,
        )
        for when, step in hooks.items():

            @pl.when(i == when - 1)
            def _():
                line.move(step)

        return carry

    lax.fori_loop(0, chunks, chunk, 0)
    stores.start(dx, dx_out)
    stores.start(dbcdt, dbcdt_out)

    pick_row = lax.broadcasted_iota(jnp.int32, (2 * own_cols, 2 * LANES), 0)
    pick_col = lax.broadcasted_iota(jnp.int32, (2 * own_cols, 2 * LANES), 1)

    def columns_of(place):
        wanted = jnp.where(pick_row < own_cols, pick_row, pick_row - own_cols + LANES) + place * own_cols
        pick = (pick_col == wanted).astype(F32).astype(BF16)
        return dot(pick, dbcdt[:, : 2 * LANES], CONTRACT_LAST)

    copies = []
    for n, peer in enumerate((side, up, far)):
        bc_in[n] = columns_of(peer).astype(BF16)
        copies.append(send(bc_in.at[n], bc_in.at[3 + n], bc_sems.at[0, n], bc_sems.at[1, n], {"tp": peer}))
        copies[-1].start()
    own_bc = columns_of(me)
    dx_t[width:, :] = jnp.zeros((LANES, total), BF16)
    dx_t[width + 2 * own_cols : width + 2 * own_cols + heads, :] = dbcdt[:, 2 * LANES :].astype(F32).T[:heads, :].astype(
        BF16
    )
    load_u.wait()

    def x_product(c, carry):
        product_chunk(dx_t, u, c, gl.at[c, :width], width // 2)
        return carry

    lax.fori_loop(0, dp_count, x_product, 0)
    for copy in copies:
        copy.wait()
    for n in range(3):
        own_bc = own_bc + bc_in[3 + n].astype(F32)
    dx_t[width : width + 2 * own_cols, :] = own_bc.astype(BF16)

    def bc_product(c, carry):
        columns = pl.ds(pl.multiple_of(c * gl.shape[2], gl.shape[2]), gl.shape[2])
        gl[c, width:, :] = dot(dx_t[width:, :], u[:, columns]).astype(BF16)
        return carry

    lax.fori_loop(0, dp_count, bc_product, 0)
    stores.start(gl, gl_out)
    sum_ref = line.finish()

    def turn(i, carry):
        piece = pl.ds(pl.multiple_of(i * CHUNK, CHUNK), CHUNK)
        gw_z[:, piece] = sum_ref[piece, :].astype(F32).T
        return carry

    lax.fori_loop(0, width // CHUNK, turn, 0)
    gw_last[...] = sum_ref[width:, :].astype(F32)
    line.end()
    for copy in stores.started:
        copy.wait()


def third_part(own_cols, heads, zx, bcdt, pos, prm, head_prm, expand, mixed, states, dy, u, gz):
    total, width = mixed.shape
    model = u.shape[1]
    dp_count = lax.axis_size("dp")
    cut = model // dp_count
    vmem = pl.BlockSpec(memory_space=pltpu.VMEM)
    anywhere = pl.BlockSpec(memory_space=pl.ANY)
    return pl.pallas_call(
        functools.partial(third_kernel, own_cols, heads),
        out_shape=(
            jax.ShapeDtypeStruct((cut, width), F32),
            jax.ShapeDtypeStruct((gz.shape[1] - width, cut), F32),
            jax.ShapeDtypeStruct((total, width), BF16),
            jax.ShapeDtypeStruct((total, 3 * LANES), BF16),
            jax.ShapeDtypeStruct((dp_count, width + LANES, cut), BF16),
            jax.ShapeDtypeStruct((8, width + 2 * LANES), F32),
        ),
        in_specs=[anywhere] * 2 + [vmem] * 4 + [anywhere] * 5,
        out_specs=(vmem, vmem, anywhere, anywhere, anywhere, vmem),
        scratch_shapes=[
            pltpu.VMEM((total, width), BF16),
            pltpu.VMEM(bcdt.shape, BF16),
            pltpu.VMEM((total, width), F32),
            pltpu.VMEM(states.shape, BF16),
            pltpu.VMEM((total, width), BF16),
            pltpu.VMEM((total, model), BF16),
            pltpu.VMEM((total, width), BF16),
            pltpu.VMEM((total, 3 * LANES), BF16),
            pltpu.VMEM((width + LANES, total), BF16),
            pltpu.VMEM((dp_count, width + LANES, cut), BF16),
            pltpu.VMEM((6, 2 * own_cols, total), BF16),
            pltpu.VMEM((CHUNK + 8, width + 2 * LANES), F32),
            pltpu.VMEM((LANES, width), F32),
            pltpu.VMEM((CHUNK + 8, width + 2 * LANES), F32),
            pltpu.VMEM((CHUNK + 8, LANES), jnp.int32),
        ]
        + line_scratch(dp_count, gz.shape[1:])
        + [pltpu.SemaphoreType.DMA((2, 3)), pltpu.SemaphoreType.DMA((12,)), pltpu.SemaphoreType.DMA((3,))],
        compiler_params=pltpu.CompilerParams(
            collective_id=2, has_side_effects=True, vmem_limit_bytes=60 * 1024 * 1024
        ),
    )(zx, bcdt, pos, prm, head_prm, expand, mixed, states, dy, u, gz)


def fourth_kernel(
    heads, x_ref, d_own_ref, gain_ref, small_ref, gain_sum_ref, expand_ref, dz_ref, dx_ref, dbcdt_ref, wz_ref, wx_ref,
    wbc_ref, u_ref, gl_ref,
    gw_x, gw_rest, grad_x, sums,
    dz, dx, dbcdt, wz, wx, wbc, u, own, gain_part, packed, over_z,
    parts, pair, right, left, pair_sems, right_sems, left_sems,
    away, to_side, to_up, in_half, in_side, in_up, plane_sems, z_sems, tp_sems, load_sems,
):
    rows, model = x_ref.shape
    width = dz.shape[1]
    me, side, up, far = tp_places()
    dp_count = parts.shape[0]
    loads = Copies(load_sems)
    load_parts = loads.start(gl_ref, parts)
    line = LineSum(parts, pair, right, left, pair_sems, right_sems, left_sems)
    plane = PlaneSum(away, to_side, to_up, in_half, in_side, in_up, plane_sems)
    others = [{"dp": lax.rem(line.dp + 2 * n, dp_count)} for n in range(1, dp_count // 2)]
    greet([{"tp": side}, {"tp": up}, {"tp": far}, line.partner] + others)
    load_parts.wait()
    order = line.order()
    for z_chunk in order:
        line.swap(z_chunk)
    loads_of = {}
    weights = [loads.start(wz_ref, wz), loads.start(wx_ref, wx), loads.start(wbc_ref, wbc)]
    for name, place in (("far", far), ("side", side), ("up", up), ("me", me)):
        piece = pl.ds(pl.multiple_of(place * rows, rows), rows)
        loads_of[name] = [
            loads.start(source.at[piece], target.at[piece])
            for source, target in ((dz_ref, dz), (dx_ref, dx), (dbcdt_ref, dbcdt), (u_ref, u))
        ]
    gain_part[...] = jnp.zeros_like(gain_part)

    def du_block(name, place, target):
        for copy in loads_of[name]:
            copy.wait()
        piece = pl.ds(pl.multiple_of(place * rows, rows), rows)

        def tile(n, carry):
            columns = pl.ds(pl.multiple_of(n * 512, 512), 512)
            du = (
                dot(dz[piece, :], wz[columns, :], CONTRACT_LAST)
                + dot(dx[piece, :], wx[columns, :], CONTRACT_LAST)
                + dot(dbcdt[piece, :], wbc[:, columns])
            )
            target[:, columns] = du.astype(target.dtype)
            gain_part[0:1, columns] += jnp.sum(du * u[piece, columns].astype(F32), axis=0, keepdims=True)
            return carry

        lax.fori_loop(0, model // 512, tile, 0)

    for z_chunk in order[:2]:
        line.merge(z_chunk)
    line.move(1)
    for copy in weights:
        copy.wait()
    du_block("far", far, away)
    plane.start_far()
    for z_chunk in order[2:]:
        line.merge(z_chunk)
    du_block("side", side, to_side)
    plane.start_side()
    du_block("up", up, to_up)
    plane.start_up()
    line.move(2)
    du_block("me", me, own)
    plane.pass_on()

    wide = width + 2 * LANES
    shift = (
        lax.broadcasted_iota(jnp.int32, (LANES, LANES), 1)
        == lax.broadcasted_iota(jnp.int32, (LANES, LANES), 0) + me * heads
    ).astype(F32)
    shift = jnp.where(lax.broadcasted_iota(jnp.int32, (LANES, LANES), 0) < heads, shift, 0.0)
    skip_rows = two_parts(jnp.broadcast_to(small_ref[6:7, :width], (8, width)))
    expand = expand_ref[:LANES, :]
    per_head = dot(skip_rows[:, :width], expand, CONTRACT_LAST) + dot(skip_rows[:, width:], expand, CONTRACT_LAST)
    tiles = jnp.concatenate([small_ref[:, :LANES], small_ref[:, LANES : 2 * LANES], per_head], axis=0)
    placed = lax.dot_general(
        tiles, shift, (((1,), (0,)), ((), ())), precision=HIGHEST, preferred_element_type=F32
    )
    packed[0, :, :wide] = small_ref[...]
    packed[0, 5:6, :width] = gain_sum_ref[0:1, :]
    packed[0, 6:7, width : width + LANES] = placed[16:17]
    packed[0, 7:8, :LANES] = placed[7:8]
    packed[0, 7:8, LANES : 2 * LANES] = placed[15:16]
    packed[0, :, wide:] = jnp.concatenate([gain_part[0:1, :] / gain_ref[...], jnp.zeros((7, model), F32)], axis=0)
    trade = send(packed.at[0], packed.at[1], z_sems.at[0, 0], z_sems.at[1, 0], line.partner)
    trade.start()
    trade.wait()
    over_z[0] = packed[0] + packed[1]
    copies = [
        send(over_z.at[0], over_z.at[n], z_sems.at[0, n], z_sems.at[1, n], others[n - 1])
        for n in range(1, dp_count // 2)
    ]
    for copy in copies:
        copy.start()
    for step in range(3, line.count):
        line.move(step)
    for copy in copies:
        copy.wait()
    everything = over_z[0]
    for n in range(1, dp_count // 2):
        everything = everything + over_z[n]
    sums[me] = everything
    copies = [
        send(sums.at[me], sums.at[me], tp_sems.at[0, n], tp_sems.at[1, n], {"tp": peer})
        for n, peer in enumerate((side, up, far))
    ]
    for copy in copies:
        copy.start()
    plane.finish()

    def norm_back(i, carry):
        piece = pl.ds(pl.multiple_of(i * 32, 32), 32)
        x = x_ref[piece, :].astype(F32)
        r_in = lax.rsqrt(jnp.mean(x * x, axis=-1, keepdims=True) + EPSILON)
        du = own[piece, :] + in_side[piece, :].astype(F32) + in_up[piece, :].astype(F32)
        e_in = du * gain_ref[...]
        back = r_in * r_in * r_in * jnp.mean(e_in * x, axis=-1, keepdims=True)
        grad_x[piece, :] = d_own_ref[piece, :].astype(F32) + r_in * e_in - x * back
        return carry

    lax.fori_loop(0, rows // 32, norm_back, 0)
    for copy in copies:
        copy.wait()
    sum_ref = line.finish()

    def turn(i, carry):
        piece = pl.ds(pl.multiple_of(i * CHUNK, CHUNK), CHUNK)
        gw_x[:, piece] = sum_ref[piece, :].astype(F32).T
        return carry

    lax.fori_loop(0, width // CHUNK, turn, 0)
    gw_rest[...] = sum_ref[width:, :].astype(F32)
    line.end()
    plane.end()


def fourth_part(heads, x_in, d_out, gain, small, gain_sum, expand, dz, dx, dbcdt, w_z, w_x, wbc, u, gl):
    rows, model = x_in.shape
    total, width = dz.shape
    dp_count = lax.axis_size("dp")
    cut = model // dp_count
    wide = width + 2 * LANES + model
    vmem = pl.BlockSpec(memory_space=pltpu.VMEM)
    anywhere = pl.BlockSpec(memory_space=pl.ANY)
    return pl.pallas_call(
        functools.partial(fourth_kernel, heads),
        out_shape=(
            jax.ShapeDtypeStruct((cut, width), F32),
            jax.ShapeDtypeStruct((LANES, cut), F32),
            jax.ShapeDtypeStruct((rows, model), F32),
            jax.ShapeDtypeStruct((4, 8, wide), F32),
        ),
        in_specs=[vmem] * 6 + [anywhere] * 8,
        out_specs=(vmem,) * 4,
        scratch_shapes=[
            pltpu.VMEM((total, width), BF16),
            pltpu.VMEM((total, width), BF16),
            pltpu.VMEM((total, 3 * LANES), BF16),
            pltpu.VMEM((model, width), BF16),
            pltpu.VMEM((model, width), BF16),
            pltpu.VMEM((3 * LANES, model), BF16),
            pltpu.VMEM((total, model), BF16),
            pltpu.VMEM((rows, model), F32),
            pltpu.VMEM((8, model), F32),
            pltpu.VMEM((2, 8, wide), F32),
            pltpu.VMEM((dp_count // 2, 8, wide), F32),
        ]
        + line_scratch(dp_count, (width + LANES, cut))
        + plane_scratch(rows, model)
        + [
            pltpu.SemaphoreType.DMA((2, dp_count // 2)),
            pltpu.SemaphoreType.DMA((2, 3)),
            pltpu.SemaphoreType.DMA((20,)),
        ],
        compiler_params=pltpu.CompilerParams(
            collective_id=3, has_side_effects=True, vmem_limit_bytes=60 * 1024 * 1024
        ),
    )(x_in, d_out, gain, small, gain_sum, expand, dz, dx, dbcdt, w_z, w_x, wbc, u, gl)


def results_kernel(
    own_cols, heads, block_ref, grad_x_ref, first_ref, last_ref, z_ref, x_ref, rest_ref, sums_ref,
    block_out, grad_x, gw_z, gw_x, gw_b, gw_c, gw_dt, gw_out, conv_w, conv_b, gate, norm, dt_bias, a_log, skip,
    held_block, held_grad_x, held_z, held_x, held_first, held_last, load_sems, sems,
):
    taken = first_ref.shape[0]
    loads, copies = Copies(load_sems), Copies(sems)
    held = (held_block, held_grad_x, held_z, held_x, held_first, held_last)
    targets = (block_out, grad_x, gw_z, gw_x, gw_out.at[:taken], gw_out.at[taken:])
    for source, target in zip((block_ref, grad_x_ref, z_ref, x_ref, first_ref, last_ref), held):
        loads.start(source, target)
    for load, source, target in zip(loads.started, held, targets):
        load.wait()
        copies.start(source, target)
    width = z_ref.shape[1]
    count = sums_ref.shape[0]
    inner = gate.shape[1]
    wide = width + 2 * LANES
    gw_b[...] = rest_ref[:own_cols, :]
    gw_c[...] = rest_ref[own_cols : 2 * own_cols, :]
    gw_dt[...] = rest_ref[2 * own_cols : 2 * own_cols + heads, :]

    def over_tp(rows, columns):
        total = sums_ref[0, rows, columns]
        for n in range(1, count):
            total = total + sums_ref[n, rows, columns]
        return total

    for n in range(count):
        own = slice(n * width, (n + 1) * width)
        conv_w[:, own] = sums_ref[n, 0:4, :width]
        conv_b[:, own] = sums_ref[n, 4:5, :width]
        gate[:, own] = sums_ref[n, 5:6, :width]
    conv_w[:, inner:] = over_tp(slice(0, 4), slice(width, wide))
    conv_b[:, inner:] = over_tp(slice(4, 5), slice(width, wide))
    norm[...] = over_tp(slice(0, 1), slice(wide, None))
    total_heads = dt_bias.shape[1]
    dt_bias[...] = over_tp(slice(7, 8), slice(0, LANES))[:, :total_heads]
    a_log[...] = over_tp(slice(7, 8), slice(LANES, 2 * LANES))[:, :total_heads]
    skip[...] = over_tp(slice(6, 7), slice(width, width + LANES))[:, :total_heads]
    for copy in copies.started:
        copy.wait()


def results_part(own_cols, heads, block_out, grad_x, first, last, gw_z, gw_x, rest, sums):
    cut, width = gw_z.shape
    count = sums.shape[0]
    inner = width * count
    model = grad_x.shape[1]
    vmem = pl.BlockSpec(memory_space=pltpu.VMEM)
    anywhere = pl.BlockSpec(memory_space=pl.ANY)
    shapes = [
        ((own_cols, cut), F32),
        ((own_cols, cut), F32),
        ((heads, cut), F32),
        ((first.shape[0] + last.shape[0], cut), F32),
        ((4, inner + 2 * LANES), F32),
        ((1, inner + 2 * LANES), F32),
        ((1, inner), F32),
        ((1, model), F32),
        ((1, heads * count), F32),
        ((1, heads * count), F32),
        ((1, heads * count), F32),
    ]
    return pl.pallas_call(
        functools.partial(results_kernel, own_cols, heads),
        out_shape=[
            jax.ShapeDtypeStruct(block_out.shape, BF16),
            jax.ShapeDtypeStruct(grad_x.shape, F32),
            jax.ShapeDtypeStruct(gw_z.shape, F32),
            jax.ShapeDtypeStruct(gw_x.shape, F32),
        ]
        + [jax.ShapeDtypeStruct(*shape) for shape in shapes],
        in_specs=[anywhere] * 6 + [vmem] * 2,
        out_specs=[anywhere] * 4 + [vmem] * 3 + [anywhere] + [vmem] * 7,
        scratch_shapes=[pltpu.VMEM(large.shape, large.dtype) for large in (block_out, grad_x, gw_z, gw_x, first, last)]
        + [pltpu.SemaphoreType.DMA((6,)), pltpu.SemaphoreType.DMA((6,))],
        compiler_params=pltpu.CompilerParams(vmem_limit_bytes=60 * 1024 * 1024),
    )(block_out, grad_x, first, last, gw_z, gw_x, rest, sums)


def in_norm_scale(values):
    return lax.rsqrt(jnp.mean(values * values, axis=-1, keepdims=True) + EPSILON)


def body(
    x_in, norm_gain, w_z, w_x, w_b, w_c, w_dt, conv_w, conv_b, dt_bias, a_log, d_skip, gate_gain, w_out,
    doc_lens, d_out,
):
    tp_count = lax.axis_size("tp")
    rank = lax.axis_index("tp")
    dev_rows, model = x_in.shape
    rows = dev_rows * tp_count
    inner = gate_gain.shape[0]
    width = w_z.shape[1]
    heads = w_dt.shape[1]
    state_size = (conv_w.shape[0] - inner) // 2
    head_size = width // heads
    own_cols = w_b.shape[1]

    x_float = x_in.astype(F32)
    r_in = in_norm_scale(x_float)
    small_weights = jnp.concatenate([w_b, w_c, w_dt], axis=1).T
    if tp_count == 4:
        lanes = jnp.zeros((LANES - d_skip.shape[0],), F32)
        flat = jnp.concatenate([conv_b, gate_gain, dt_bias, lanes, a_log, lanes, d_skip, lanes])[None, :]
        (
            gathered, zx, bcdt, w_bcdt, mixed, g, yo, yo_t, states, grad_gathered, dyo, coef, pos, prm, head_prm, expand
        ) = first_part(
            inner, heads, own_cols, x_in, norm_gain[None, :], small_weights, conv_w.T, flat, doc_lens, w_z, w_x, w_out,
            d_out,
        )
        gain_own = prm[5, :width]
    else:
        normed = (x_float * r_in * norm_gain[None, :]).astype(BF16)
        gathered = lax.all_gather(normed, "tp", axis=0, tiled=True)
        w_bc = lax.all_gather(small_weights[: 2 * own_cols], "tp", axis=0).reshape(tp_count, 2, own_cols, model)
        w_bcdt = jnp.concatenate(
            [
                jnp.swapaxes(w_bc, 0, 1).reshape(2 * state_size, model),
                small_weights[2 * own_cols :],
                jnp.zeros((LANES - heads, model), BF16),
            ],
            axis=0,
        )
        zx = dot(gathered, jnp.concatenate([w_z, w_x], axis=1)).astype(BF16)
        bcdt = dot(gathered, w_bcdt, CONTRACT_LAST).astype(BF16)
        lengths = doc_lens[0]
        doc_starts = jnp.cumsum(lengths) - lengths
        positions = jnp.arange(rows, dtype=jnp.int32)
        started = jnp.where(positions[:, None] >= doc_starts[None, :], doc_starts[None, :], 0)
        pos = (positions - jnp.max(started, axis=1))[:, None]

        def own(array, count):
            return lax.dynamic_slice_in_dim(array, rank * count, count, axis=0)

        taps = jnp.concatenate([own(conv_w[:inner], width), conv_w[inner:]], axis=0).T
        bias = jnp.concatenate([own(conv_b[:inner], width), conv_b[inner:]])
        pad_bc = jnp.zeros((2 * state_size,), F32)
        gain_own = own(gate_gain, width)
        skip_own = jnp.repeat(own(d_skip, heads), head_size)
        prm = jnp.concatenate(
            [
                taps,
                bias[None],
                jnp.concatenate([gain_own, pad_bc])[None],
                jnp.concatenate([skip_own, pad_bc])[None],
                jnp.zeros((1, width + 2 * state_size), F32),
            ],
            axis=0,
        )
        pad_heads = jnp.zeros((LANES - heads,), F32)
        head_prm = jnp.concatenate(
            [
                jnp.concatenate([own(dt_bias, heads), pad_heads])[None],
                jnp.concatenate([jnp.exp(own(a_log, heads)), pad_heads])[None],
                jnp.zeros((6, LANES), F32),
            ],
            axis=0,
        )
        expand = (
            (jnp.arange(2 * LANES) % LANES)[:, None] == (jnp.arange(width) // head_size)[None, :]
        ).astype(BF16)
        mixed, g, g_sum, states = mixer_forward(width, zx, bcdt, pos, prm, head_prm, expand)
        grad_gathered = lax.all_gather(d_out, "tp", axis=0, tiled=True)
        dyo = dot(grad_gathered, w_out, CONTRACT_LAST).astype(BF16)
        eg_sum = jnp.sum(dyo.astype(F32) * gain_own[None, :] * g, axis=1)
        g_total, eg_total = lax.psum((g_sum[0], eg_sum), "tp")
        r_gate = lax.rsqrt(g_total / inner + EPSILON)
        zeros = jnp.zeros_like(r_gate)
        coef = jnp.stack([r_gate] + [zeros] * 7 + [r_gate**3 * (eg_total / inner)] + [zeros] * (LANES - 9), axis=1)
        yo = (g * r_gate[:, None] * gain_own[None, :]).astype(BF16)

    if tp_count == 4:
        block_out, gw_first, dz, dy, gz, gain_sum = second_part(
            x_in, yo, yo_t, grad_gathered, w_out, dyo, g, mixed, zx, coef, prm, gathered
        )
        gw_z, gw_last, grad_xs, grad_bcdt, gl, small = third_part(
            own_cols, heads, zx, bcdt, pos, prm, head_prm, expand, mixed, states, dy, gathered, gz
        )
        gw_x, gw_rest, grad_x, sums = fourth_part(
            heads, x_in, d_out, norm_gain[None, :], small, gain_sum, expand, dz, grad_xs, grad_bcdt, w_z, w_x, w_bcdt,
            gathered, gl
        )
        (
            block_out, grad_x, gw_z, gw_x, gw_b, gw_c, gw_dt, gw_out, g_conv_w, g_conv_b, g_gate, g_norm, g_dt_bias,
            g_a_log, g_skip
        ) = results_part(
            own_cols, heads, block_out, grad_x, gw_first, gw_last, gw_z, gw_x, gw_rest, sums
        )
        return (
            block_out, grad_x, g_norm[0], gw_z, gw_x, gw_b.T, gw_c.T, gw_dt.T, g_conv_w.T, g_conv_b[0], g_dt_bias[0],
            g_a_log[0], g_skip[0], g_gate[0], gw_out
        )
    else:

        def scatter_dp(partial):
            return lax.psum_scatter(partial.astype(BF16), "dp", scatter_dimension=0, tiled=True).astype(F32)

        def scatter_tp(array):
            return lax.psum_scatter(array.astype(BF16), "tp", scatter_dimension=0, tiled=True).astype(F32)

        grad_w_out = scatter_dp(dot(grad_gathered, yo, CONTRACT_FIRST)).T
        z = zx[:, :width].astype(F32)
        sig_z = jax.nn.sigmoid(z)
        dg = coef[:, 0:1] * (dyo.astype(F32) * gain_own[None, :]) - g * coef[:, 8:9]
        dz = (dg * mixed * (sig_z * (1.0 + z * (1.0 - sig_z)))).astype(BF16)
        dy = (dg * (z * sig_z)).astype(BF16)
        gain_sum = jnp.sum(dyo.astype(F32) * g * coef[:, 0:1], axis=0)
        grad_w_z = scatter_dp(dot(gathered, dz, CONTRACT_FIRST))
        block_out = (x_float + scatter_tp(dot(yo, w_out))).astype(BF16)
        grad_xs, grad_bcdt, small = mixer_backward(
            width, zx, bcdt, pos, prm, head_prm, expand, mixed, states, dy
        )
        small = small.at[5, :width].set(gain_sum)
        d_bc = grad_bcdt[:, : 2 * state_size]
        by_owner = jnp.moveaxis(d_bc.reshape(rows, 2, tp_count, own_cols), 2, 0)
        by_owner = by_owner.reshape(tp_count, rows, 2 * own_cols)
        d_bc_own = lax.psum_scatter(by_owner.astype(F32), "tp", scatter_dimension=0, tiled=False)
        d_rest = jnp.concatenate(
            [
                d_bc_own.astype(BF16),
                grad_bcdt[:, 2 * state_size : 2 * state_size + heads],
                jnp.zeros((rows, (-2 * own_cols - heads) % LANES), BF16),
            ],
            axis=1,
        )
        grad_w_x = scatter_dp(dot(gathered, grad_xs, CONTRACT_FIRST))
        grad_rest = scatter_dp(dot(gathered, d_rest, CONTRACT_FIRST))
        du_part = (
            dot(dz, w_z, CONTRACT_LAST) + dot(grad_xs, w_x, CONTRACT_LAST) + dot(grad_bcdt, w_bcdt)
        )
        gain_part = jnp.sum(du_part * gathered.astype(F32), axis=0) / norm_gain
        du = scatter_tp(du_part)
        e_in = du * norm_gain[None, :]
        grad_x = d_out.astype(F32) + r_in * e_in - x_float * (
            r_in**3 * jnp.mean(e_in * x_float, axis=-1, keepdims=True)
        )
        sums = lax.all_gather(lax.psum(small, "dp"), "tp")
        grad_norm_gain = lax.psum(gain_part, ("dp", "tp"))

    channels = jnp.swapaxes(sums[:, :7, :width], 0, 1).reshape(7, inner)
    shared = jnp.sum(sums[:, :5, width : width + 2 * state_size], axis=0)
    grad_conv = jnp.concatenate([channels[:5], shared], axis=1)
    return (
        block_out,
        grad_x,
        grad_norm_gain,
        grad_w_z,
        grad_w_x,
        grad_rest[:, :own_cols],
        grad_rest[:, own_cols : 2 * own_cols],
        grad_rest[:, 2 * own_cols : 2 * own_cols + heads],
        grad_conv[:4].T,
        grad_conv[4],
        sums[:, 7, :heads].reshape(-1),
        sums[:, 7, LANES : LANES + heads].reshape(-1),
        channels[6].reshape(heads * tp_count, head_size).sum(axis=1),
        channels[5],
        grad_w_out,
    )


def solution(mesh):
    rows = P(("dp", "tp"), None)
    columns = P(None, "tp")
    both = P("dp", "tp")
    none = P()
    return jax.shard_map(
        body,
        mesh=mesh,
        in_specs=(
            rows, none, columns, columns, columns, columns, columns, none, none, none, none, none, none,
            P("tp", None), P("dp", None), rows,
        ),
        out_specs=(
            rows, rows, none, both, both, both, both, both, none, none, none, none, none, none, P("tp", "dp"),
        ),
        check_vma=False,
    )
```

```python
import functools

import jax
import jax.numpy as jnp
from jax import lax
from jax.experimental import pallas as pl
from jax.experimental.pallas import tpu as pltpu
from jax.sharding import PartitionSpec as P

EPSILON = 1e-05
HIGHEST = lax.Precision.HIGHEST
F32 = jnp.float32
BF16 = jnp.bfloat16
CHUNK = 128
LANES = 128
CONTRACT_FIRST = (((0,), (0,)), ((), ()))
CONTRACT_LAST = (((1,), (1,)), ((), ()))


def dot(a, b, dims=(((1,), (0,)), ((), ()))):
    return lax.dot_general(a, b, dims, preferred_element_type=F32)


def two_parts(v):
    high = v.astype(BF16)
    return jnp.concatenate([high, (v - high.astype(F32)).astype(BF16)], axis=1)


def prepare_chunk(width, x, bc, raw_dt, pos, prm_ref, head_ref, expand_ref, ext):
    rows = CHUNK
    ext[8:, :width] = x.astype(F32)
    ext[8:, width:] = bc.astype(F32)
    pre = prm_ref[3:4, :] * ext[8:, :] + prm_ref[4:5, :]
    for back in (1, 2, 3):
        here = (pos >= back).astype(F32)
        pre = pre + prm_ref[3 - back : 4 - back, :] * (ext[8 - back : 8 - back + rows, :] * here)
    sig = jax.nn.sigmoid(pre)
    act = pre * sig
    xc = act[:, :width]
    state_size = (act.shape[1] - width) // 2
    b_rows = act[:, width : width + state_size].astype(BF16)
    c_rows = act[:, width + state_size :].astype(BF16)
    raw = raw_dt.astype(F32) + head_ref[0:1, :]
    dt = jnp.maximum(raw, 0.0) + jnp.log1p(jnp.exp(-jnp.abs(raw)))
    log_decay = -dt * head_ref[1:2, :]
    t_idx = lax.broadcasted_iota(jnp.int32, (rows, rows), 0)
    s_idx = lax.broadcasted_iota(jnp.int32, (rows, rows), 1)
    lower = (s_idx <= t_idx).astype(F32)
    cum = lax.dot_general(
        lower, log_decay, (((1,), (0,)), ((), ())), precision=HIGHEST, preferred_element_type=F32
    )
    same = (s_idx <= t_idx) & (s_idx >= t_idx - pos)
    scores = jnp.where(same, dot(c_rows, b_rows, CONTRACT_LAST), 0.0)
    t_col = lax.broadcasted_iota(jnp.int32, (rows, 1), 0)
    pos_last = pos[rows - 1 : rows, :]
    cum_last = cum[rows - 1 : rows, :]
    inward = jnp.exp(cum) * (pos > t_col).astype(F32)
    tail = jnp.exp(cum_last - cum) * (t_col >= rows - 1 - pos_last).astype(F32)
    carried = jnp.exp(cum_last) * (pos_last >= rows).astype(F32)
    wide = dot(
        two_parts(jnp.concatenate([dt, inward, tail, jnp.broadcast_to(carried, (8, LANES))], axis=0)),
        expand_ref[...],
    )
    return dict(
        pre=pre,
        sig=sig,
        xc=xc,
        b=b_rows,
        c=c_rows,
        raw=raw,
        log_decay=log_decay,
        cum=cum,
        cum_t=cum.T,
        same=same,
        scores=scores,
        t_idx=t_idx,
        s_idx=s_idx,
        dt_w=wide[:rows],
        in_w=wide[rows : 2 * rows],
        tail_w=wide[2 * rows : 3 * rows],
        carried_w=wide[3 * rows : 3 * rows + 1],
    )


def decay_of(k, head):
    return jnp.exp(jnp.minimum(k["cum"][:, head : head + 1] - k["cum_t"][head : head + 1, :], 0.0))


def halves(pair):
    lane = lax.broadcasted_iota(jnp.int32, pair.shape, 1)
    zero = jnp.zeros_like(pair)
    return jnp.concatenate(
        [jnp.where(lane < LANES // 2, pair, zero), jnp.where(lane < LANES // 2, zero, pair)], axis=0
    )


def forward_chunk(
    width, at, zx_ref, bcdt_ref, pos_ref, prm_ref, head_ref, expand_ref, mixed_ref, g_ref, sum_ref, state_ref, ext,
    state,
):
    if isinstance(at, int):
        rows = slice(at * CHUNK, (at + 1) * CHUNK)
    else:
        rows = pl.ds(pl.multiple_of(at * CHUNK, CHUNK), CHUNK)
    ext[:8, :] = ext[CHUNK:, :]
    k = prepare_chunk(
        width,
        zx_ref[rows, width:],
        bcdt_ref[rows, : 2 * LANES],
        bcdt_ref[rows, 2 * LANES :],
        pos_ref[rows, :],
        prm_ref,
        head_ref,
        expand_ref,
        ext,
    )
    stepped = (k["xc"] * k["dt_w"]).astype(BF16)
    held = state[...]
    held_low = held.astype(BF16)
    state_ref[at] = held_low
    reached = dot(k["c"], held_low) * k["in_w"] + prm_ref[6:7, :width] * k["xc"]
    weighted = (stepped.astype(F32) * k["tail_w"]).astype(BF16)
    state[...] = k["carried_w"] * held + dot(k["b"], weighted, CONTRACT_FIRST)
    for pair in range(width // LANES):
        lanes = slice(pair * LANES, (pair + 1) * LANES)
        mixing = jnp.concatenate(
            [
                (decay_of(k, 2 * pair) * k["scores"]).astype(BF16),
                (decay_of(k, 2 * pair + 1) * k["scores"]).astype(BF16),
            ],
            axis=1,
        )
        mixed_ref[rows, lanes] = dot(mixing, halves(stepped[:, lanes])) + reached[:, lanes]
    z = zx_ref[rows, :width].astype(F32)
    g = mixed_ref[rows, :] * (z * jax.nn.sigmoid(z))
    g_ref[rows, :] = g
    total = jnp.sum(g * g, axis=1, keepdims=True)
    sum_ref[:, rows] = jnp.broadcast_to(total, (CHUNK, LANES)).T[:8, :]


def forward_kernel(
    width, zx_ref, bcdt_ref, pos_ref, prm_ref, head_ref, expand_ref, mixed_ref, g_ref, sum_ref, state_ref, ext, state
):
    @pl.when(pl.program_id(0) == 0)
    def _():
        state[...] = jnp.zeros_like(state)
        ext[...] = jnp.zeros_like(ext)

    forward_chunk(
        width, 0, zx_ref, bcdt_ref, pos_ref, prm_ref, head_ref, expand_ref, mixed_ref, g_ref, sum_ref, state_ref, ext,
        state,
    )


def backward_chunk(
    width, tokens, halo_x, halo_bc, held, x_ref, bcdt_ref, pos_ref, prm_ref, head_ref, expand_ref, mixed_ref,
    dy_ref, grad_x_ref, grad_bcdt_ref, grad_t_ref, small_ref, ext, d_state, later, later_pos,
):
    rows = CHUNK
    ext[:8, :width] = halo_x.astype(F32)[8:, :]
    ext[:8, width:] = halo_bc.astype(F32)[8:, :]
    pos = pos_ref[tokens, :]
    k = prepare_chunk(
        width,
        x_ref[tokens, :],
        bcdt_ref[tokens, : 2 * LANES],
        bcdt_ref[tokens, 2 * LANES :],
        pos,
        prm_ref,
        head_ref,
        expand_ref,
        ext,
    )
    xc = k["xc"]
    skip = prm_ref[6:7, :width]
    y = mixed_ref[tokens, :] - skip * xc
    dy_low = dy_ref[tokens, :]
    dy = dy_low.astype(F32)
    small_ref[6:7, :width] += jnp.sum(dy * xc, axis=0, keepdims=True)

    stepped = (xc * k["dt_w"]).astype(BF16)
    d_held = d_state[...]
    d_held_low = d_held.astype(BF16)
    held_low = held
    weighted = (stepped.astype(F32) * k["tail_w"]).astype(BF16)
    dy_in = (dy * k["in_w"]).astype(BF16)
    from_state = dot(k["b"], d_held_low) * k["tail_w"]
    dc = dot(dy_in, held_low, CONTRACT_LAST)
    db = dot(weighted, d_held_low, CONTRACT_LAST)
    d_state[...] = k["carried_w"] * d_held + dot(k["c"], dy_in, CONTRACT_FIRST)
    d_scores = jnp.zeros((rows, rows), F32)
    d_stepped = []
    for pair in range(width // LANES):
        lanes = slice(pair * LANES, (pair + 1) * LANES)
        decay_a = decay_of(k, 2 * pair)
        decay_b = decay_of(k, 2 * pair + 1)
        mixing = jnp.concatenate(
            [(decay_a * k["scores"]).astype(BF16), (decay_b * k["scores"]).astype(BF16)], axis=0
        )
        d_mixing = dot(dy_low[:, lanes], halves(stepped[:, lanes]), CONTRACT_LAST)
        d_scores = d_scores + decay_a * d_mixing[:, :rows] + decay_b * d_mixing[:, rows:]
        d_stepped.append(dot(mixing, halves(dy_low[:, lanes]), CONTRACT_FIRST))
    d_stepped = jnp.concatenate(d_stepped, axis=1) + from_state
    d_scores = jnp.where(k["same"], d_scores, 0.0).astype(BF16)
    dc = dc + dot(d_scores, k["b"])
    db = db + dot(d_scores, k["c"], CONTRACT_FIRST)
    dxc = skip * dy + d_stepped * k["dt_w"]

    stepped_f = stepped.astype(F32)
    tail_term = jnp.sum(stepped_f * from_state, axis=0, keepdims=True) + k["carried_w"] * jnp.sum(
        held_low.astype(F32) * d_held, axis=0, keepdims=True
    )
    gathered = two_parts(
        jnp.concatenate([dy * y - stepped_f * d_stepped, jnp.broadcast_to(tail_term, (8, width))], axis=0)
    )
    expand = expand_ref[:LANES, :]
    narrow = dot(gathered[:, :width], expand, CONTRACT_LAST) + dot(gathered[:, width:], expand, CONTRACT_LAST)
    d_cum = narrow[:rows]
    d_dt = dot((d_stepped * xc).astype(BF16), expand, CONTRACT_LAST)
    upper = (k["s_idx"] >= k["t_idx"]).astype(F32)
    d_decay = (
        lax.dot_general(
            upper, d_cum, (((1,), (0,)), ((), ())), precision=HIGHEST, preferred_element_type=F32
        )
        + narrow[rows : rows + 1]
    )
    d_raw = (d_dt - d_decay * head_ref[1:2, :]) * jax.nn.sigmoid(k["raw"])
    small_ref[7:8, :LANES] += jnp.sum(d_raw, axis=0, keepdims=True)
    small_ref[7:8, LANES : 2 * LANES] += jnp.sum(d_decay * k["log_decay"], axis=0, keepdims=True)
    grad_bcdt_ref[tokens, 2 * LANES :] = d_raw.astype(BF16)

    pre, sig = k["pre"], k["sig"]
    d_pre = jnp.concatenate([dxc, db, dc], axis=1) * (sig * (1.0 + pre * (1.0 - sig)))
    small_ref[4:5, :] += jnp.sum(d_pre, axis=0, keepdims=True)
    later[:rows, :] = d_pre
    later_pos[:rows, :] = jnp.broadcast_to(pos, (rows, LANES))
    x_own = ext[8:, :]
    d_in = prm_ref[3:4, :] * d_pre
    small_ref[3:4, :] += jnp.sum(d_pre * x_own, axis=0, keepdims=True)
    for back in (1, 2, 3):
        there = (later_pos[back : back + rows, 0:1] >= back).astype(F32)
        reaching = later[back : back + rows, :] * there
        small_ref[3 - back : 4 - back, :] += jnp.sum(reaching * x_own, axis=0, keepdims=True)
        d_in = d_in + prm_ref[3 - back : 4 - back, :] * reaching
    grad_x_ref[tokens, :] = d_in[:, :width].astype(BF16)
    grad_bcdt_ref[tokens, : 2 * LANES] = d_in[:, width:].astype(BF16)
    later[rows:, :] = later[:8, :]
    later_pos[rows:, :] = later_pos[:8, :]
    if grad_t_ref is not None:
        grad_t_ref[:width, tokens] = d_in[:, :width].T.astype(BF16)


def backward_start(small_ref, d_state, later, later_pos):
    d_state[...] = jnp.zeros_like(d_state)
    later[...] = jnp.zeros_like(later)
    later_pos[...] = jnp.zeros_like(later_pos)
    small_ref[...] = jnp.zeros_like(small_ref)


def backward_kernel(
    width, x_ref, bcdt_ref, halo_x_ref, halo_bc_ref, pos_ref, prm_ref, head_ref,
    expand_ref, mixed_ref, state_ref, dy_ref, grad_x_ref, grad_bcdt_ref, small_ref, ext, d_state,
    later, later_pos,
):
    @pl.when(pl.program_id(0) == 0)
    def _():
        backward_start(small_ref, d_state, later, later_pos)

    backward_chunk(
        width, slice(0, CHUNK), halo_x_ref[...], halo_bc_ref[:, : 2 * LANES], state_ref[0], x_ref, bcdt_ref, pos_ref,
        prm_ref, head_ref, expand_ref, mixed_ref, dy_ref, grad_x_ref, grad_bcdt_ref, None, small_ref,
        ext, d_state, later, later_pos,
    )


def mixer_forward(width, zx, bcdt, pos, prm, head_prm, expand):
    rows = zx.shape[0]
    chunks = rows // CHUNK

    def tokens(columns):
        return pl.BlockSpec((CHUNK, columns), lambda i: (i, 0))

    def whole(array):
        return pl.BlockSpec(array.shape, lambda i: (0, 0))

    return pl.pallas_call(
        functools.partial(forward_kernel, width),
        out_shape=(
            jax.ShapeDtypeStruct((rows, width), F32),
            jax.ShapeDtypeStruct((rows, width), F32),
            jax.ShapeDtypeStruct((8, rows), F32),
            jax.ShapeDtypeStruct((chunks, LANES, width), BF16),
        ),
        grid=(chunks,),
        in_specs=[tokens(2 * width), tokens(3 * LANES), tokens(1), whole(prm), whole(head_prm), whole(expand)],
        out_specs=(
            tokens(width),
            tokens(width),
            pl.BlockSpec((8, CHUNK), lambda i: (0, i)),
            pl.BlockSpec((1, LANES, width), lambda i: (i, 0, 0)),
        ),
        scratch_shapes=[
            pltpu.VMEM((CHUNK + 8, width + 2 * LANES), F32),
            pltpu.VMEM((LANES, width), F32),
        ],
        compiler_params=pltpu.CompilerParams(
            dimension_semantics=("arbitrary",), vmem_limit_bytes=40 * 1024 * 1024
        ),
    )(zx, bcdt, pos, prm, head_prm, expand)


def mixer_backward(width, zx, bcdt, pos, prm, head_prm, expand, mixed, states, dy):
    rows = zx.shape[0]
    chunks = rows // CHUNK

    def tokens(columns):
        return pl.BlockSpec((CHUNK, columns), lambda i: (chunks - 1 - i, 0))

    def before(columns, place):
        return pl.BlockSpec(
            (16, columns), lambda i: (jnp.maximum((chunks - 1 - i) * (CHUNK // 16) - 1, 0), place)
        )

    def whole(array):
        return pl.BlockSpec(array.shape, lambda i: (0, 0))

    return pl.pallas_call(
        functools.partial(backward_kernel, width),
        out_shape=(
            jax.ShapeDtypeStruct((rows, width), BF16),
            jax.ShapeDtypeStruct((rows, 3 * LANES), BF16),
            jax.ShapeDtypeStruct((8, width + 2 * LANES), F32),
        ),
        grid=(chunks,),
        in_specs=[
            pl.BlockSpec((CHUNK, width), lambda i: (chunks - 1 - i, 1)),
            tokens(3 * LANES),
            before(width, 1),
            before(3 * LANES, 0),
            tokens(1),
            whole(prm),
            whole(head_prm),
            whole(expand),
            tokens(width),
            pl.BlockSpec((1, LANES, width), lambda i: (chunks - 1 - i, 0, 0)),
            tokens(width),
        ],
        out_specs=(
            tokens(width),
            tokens(3 * LANES),
            pl.BlockSpec((8, width + 2 * LANES), lambda i: (0, 0)),
        ),
        scratch_shapes=[
            pltpu.VMEM((CHUNK + 8, width + 2 * LANES), F32),
            pltpu.VMEM((LANES, width), F32),
            pltpu.VMEM((CHUNK + 8, width + 2 * LANES), F32),
            pltpu.VMEM((CHUNK + 8, LANES), jnp.int32),
        ],
        compiler_params=pltpu.CompilerParams(
            dimension_semantics=("arbitrary",), vmem_limit_bytes=48 * 1024 * 1024
        ),
        cost_estimate=pl.CostEstimate(flops=rows * width * 2048, bytes_accessed=rows * width * 20, transcendentals=0),
    )(zx, bcdt, zx, bcdt, pos, prm, head_prm, expand, mixed, states, dy)


MESH = pl.DeviceIdType.MESH


def tp_places():
    me = lax.axis_index("tp")
    return me, me + 1 - 2 * lax.rem(me, 2), lax.rem(me + 2, 4), 3 - me


def greet(peers):
    barrier = pltpu.get_barrier_semaphore()
    for peer in peers:
        pl.semaphore_signal(barrier, inc=1, device_id=peer, device_id_type=MESH)
    pl.semaphore_wait(barrier, len(peers))


def send(src, dst, send_sem, recv_sem, peer):
    return pltpu.make_async_remote_copy(
        src_ref=src, dst_ref=dst, send_sem=send_sem, recv_sem=recv_sem, device_id=peer, device_id_type=MESH
    )


class Gather:
    def __init__(self, whole, rows, send_sems, recv_sems, own=None):
        me, side, up, _ = tp_places()
        half = rows // 2

        def part(place, which):
            return whole.at[pl.ds(pl.multiple_of(place * rows + which * half, half), half)]

        def one(n, place, which, peer):
            return send(part(place, which), part(place, which), send_sems.at[n], recv_sems.at[n], {"tp": peer})

        def quarter(n, which, late, peer):
            start = pl.multiple_of(me * rows + which * half + late * (half // 2), half // 2)
            piece = whole.at[pl.ds(start, half // 2)]
            return send(piece, piece, send_sems.at[n], recv_sems.at[n], {"tp": peer})

        self.side_first, self.up_first = one(0, me, 0, side), one(1, me, 1, up)
        self.side_then = [quarter(2, 1, 0, side), quarter(3, 1, 1, side)]
        self.up_then = [quarter(4, 0, 0, up), quarter(5, 0, 1, up)]
        self.pass_up, self.pass_side = one(6, side, 0, up), one(7, up, 1, side)

    def start(self):
        for copy in (self.side_first, self.up_first, self.side_then[0], self.up_then[0]):
            copy.start()

    def start_rest(self):
        self.side_then[1].start()
        self.up_then[1].start()

    def forward(self):
        self.side_first.wait_recv()
        self.pass_up.start()
        self.up_first.wait_recv()
        self.pass_side.start()

    def neighbours(self):
        for copy in self.side_then + self.up_then:
            copy.wait_recv()

    def finish(self):
        self.pass_up.wait_recv()
        self.pass_side.wait_recv()

    def end(self):
        for copy in [self.side_first, self.up_first, self.pass_up, self.pass_side] + self.side_then + self.up_then:
            copy.wait_send()


def set_up(width, heads, inner, taps_ref, flat_ref, lens_ref, prm, head, expand, pos):
    rank = lax.axis_index("tp")
    channels = taps_ref.shape[1]
    own = pl.ds(pl.multiple_of(rank * width, LANES), width)
    own_gain = pl.ds(pl.multiple_of(channels + rank * width, LANES), width)
    prm[...] = jnp.zeros_like(prm)
    prm[0:4, :width] = taps_ref[:, own]
    prm[0:4, width:] = taps_ref[:, inner:]
    prm[4:5, :width] = flat_ref[:, own]
    prm[4:5, width:] = flat_ref[:, inner:channels]
    prm[5:6, :width] = flat_ref[:, own_gain]
    lane = lax.broadcasted_iota(jnp.int32, (LANES, LANES), 1)
    pick = ((lax.broadcasted_iota(jnp.int32, (LANES, LANES), 0) == lane + rank * heads) & (lane < heads)).astype(F32)
    start = channels + inner
    tiles = [jnp.broadcast_to(flat_ref[:, start + n * LANES : start + (n + 1) * LANES], (8, LANES)) for n in range(3)]
    tiles[1] = jnp.exp(tiles[1])
    picked = lax.dot_general(
        jnp.concatenate(tiles, axis=0), pick, (((1,), (0,)), ((), ())), precision=HIGHEST, preferred_element_type=F32
    )
    head[...] = jnp.concatenate([picked[0:1], picked[8:9], jnp.zeros((6, LANES), F32)], axis=0)
    row = lax.broadcasted_iota(jnp.int32, (2 * LANES, width), 0)
    column = lax.broadcasted_iota(jnp.int32, (2 * LANES, width), 1)
    expand[...] = (lax.rem(row, LANES) == column // (width // heads)).astype(F32).astype(BF16)
    prm[6:7, :width] = dot(two_parts(picked[16:24]), expand[...])[0:1]
    starts = [jnp.int32(0)]
    for n in range(lens_ref.shape[1] - 1):
        starts.append(starts[-1] + lens_ref[0, n])

    def place(i, carry):
        token = lax.broadcasted_iota(jnp.int32, (CHUNK, 1), 0) + i * CHUNK
        begun = jnp.zeros((CHUNK, 1), jnp.int32)
        for first in starts[1:]:
            begun = jnp.where(token >= first, first, begun)
        pos[pl.ds(pl.multiple_of(i * CHUNK, CHUNK), CHUNK), :] = token - begun
        return carry

    lax.fori_loop(0, pos.shape[0] // CHUNK, place, 0)


def first_kernel(
    inner, heads, own_cols, x_ref, gain_ref, small_ref, taps_ref, flat_ref, lens_ref, wz_ref, wx_ref, w_out_ref, d_own_ref,
    u_out, zx_out, bcdt_out, wbc_out, mixed_out, g_out, yo_out, yo_t_out, state_out, d_out, dyo_out, coef_out, pos_out,
    prm_out, head_out, expand_out, cross_out,
    weights, w_out, u, zx, bcdt, wbc, mixed, g, yo, yo_t, states, d, dyo, coef, pos, prm, head, expand, ext, state, sums,
    acc, sems, sum_sems, load_sems, store_sems,
):
    rows, model = x_ref.shape
    total, width = mixed.shape
    chunks = total // CHUNK
    me, side, up, far = tp_places()
    dp = lax.axis_index("dp")
    parity = lax.rem(dp, 2)
    partner = {"dp": dp + 1 - 2 * parity}

    def block(place):
        return pl.ds(pl.multiple_of(place * rows, rows), rows)

    loads = [
        pltpu.make_async_copy(wz_ref, weights.at[:, :width], load_sems.at[0]),
        pltpu.make_async_copy(wx_ref, weights.at[:, width:], load_sems.at[1]),
        pltpu.make_async_copy(w_out_ref, w_out, load_sems.at[2]),
        pltpu.make_async_copy(d_own_ref, d.at[block(me)], load_sems.at[3]),
    ]
    for copy in loads:
        copy.start()
    stores = []

    def keep(source, target):
        copy = pltpu.make_async_copy(source, target, store_sems.at[len(stores)])
        copy.start()
        stores.append(copy)

    bc_own = pl.ds(pl.multiple_of(parity * LANES, LANES), LANES)
    wbc[pl.ds(pl.multiple_of(parity * LANES + me * own_cols, own_cols), own_cols), :] = small_ref[
        pl.ds(pl.multiple_of(parity * own_cols, own_cols), own_cols), :
    ]
    greet([{"tp": side}, {"tp": up}, {"tp": far}, partner])
    small_gather = Gather(wbc.at[bc_own], own_cols, sems.at[0], sems.at[1])
    small_gather.start()
    small_gather.start_rest()

    def norm(i, carry):
        piece = pl.ds(pl.multiple_of(i * 32, 32), 32)
        x = x_ref[piece, :].astype(F32)
        scale = lax.rsqrt(jnp.mean(x * x, axis=-1, keepdims=True) + EPSILON)
        u[pl.ds(pl.multiple_of(me * rows + i * 32, 32), 32), :] = (x * scale * gain_ref[...]).astype(BF16)
        return carry

    lax.fori_loop(0, rows // 32, norm, 0)
    small_gather.forward()
    gather = Gather(u, rows, sems.at[2], sems.at[3])
    gather.start()
    gather.start_rest()
    wbc[2 * LANES :, :] = jnp.zeros((LANES, model), BF16)
    wbc[2 * LANES : 2 * LANES + heads, :] = small_ref[2 * own_cols :, :]
    set_up(width, heads, inner, taps_ref, flat_ref, lens_ref, prm, head, expand, pos)
    keep(pos, pos_out)
    keep(prm, prm_out)
    keep(head, head_out)
    keep(expand, expand_out)
    loads[0].wait()
    loads[1].wait()

    def project(place):
        piece = block(place)

        def tile(n, carry):
            columns = pl.ds(pl.multiple_of(n * 512, 512), 512)
            zx[piece, columns] = dot(u[piece, :], weights[:, columns]).astype(BF16)
            return carry

        lax.fori_loop(0, 2 * width // 512, tile, 0)

    def project_small(place):
        bcdt[block(place), :] = dot(u[block(place), :], wbc[...], CONTRACT_LAST).astype(BF16)

    project(me)
    small_gather.neighbours()
    small_gather.finish()
    trade = send(wbc.at[bc_own], wbc.at[bc_own], sems.at[6, 0], sems.at[6, 1], partner)
    trade.start()
    gather.forward()
    loads[3].wait()
    d_gather = Gather(d, rows, sems.at[4], sems.at[5])
    d_gather.start()
    trade.wait()
    keep(wbc, wbc_out)
    project_small(me)
    gather.neighbours()
    project(side)
    project(up)
    project_small(side)
    project_small(up)
    gather.finish()
    keep(u, u_out)
    project(far)
    project_small(far)
    keep(zx, zx_out)
    keep(bcdt, bcdt_out)

    state[...] = jnp.zeros_like(state)
    ext[...] = jnp.zeros_like(ext)

    def chunk(i, carry):
        forward_chunk(
            width, i, zx, bcdt, pos, prm, head, expand, mixed, g, sums.at[0], states, ext, state
        )
        return carry

    lax.fori_loop(0, chunks, chunk, 0)

    copies = [
        send(sums.at[0], sums.at[2 + n], sum_sems.at[0, n], sum_sems.at[1, n], {"tp": peer})
        for n, peer in enumerate((side, up, far))
    ]
    for copy in copies:
        copy.start()
    d_gather.start_rest()
    keep(mixed, mixed_out)
    keep(g, g_out)
    keep(states, state_out)
    loads[2].wait()

    def back_to_heads(place):
        piece = block(place)
        acc[...] = jnp.zeros_like(acc)

        def tile(n, carry):
            columns = pl.ds(pl.multiple_of(n * 256, 256), 256)
            low = dot(d[piece, :], w_out[columns, :], CONTRACT_LAST).astype(BF16)
            dyo[piece, columns] = low
            both = low.astype(F32) * prm[5:6, columns] * g[piece, columns]
            acc[...] += both[:, :LANES] + both[:, LANES:]
            return carry

        lax.fori_loop(0, width // 256, tile, 0)
        column = jnp.sum(acc[...], axis=1, keepdims=True)
        sums[1, :, piece] = jnp.broadcast_to(column, (rows, LANES)).T[:8, :]
        keep(dyo.at[piece], dyo_out.at[piece])

    d_gather.forward()
    back_to_heads(me)
    for copy in copies:
        copy.wait()

    def gate(i, carry):
        piece = pl.ds(pl.multiple_of(i * CHUNK, CHUNK), CHUNK)
        squares = sums[0, :, piece] + sums[2, :, piece] + sums[3, :, piece] + sums[4, :, piece]
        scale = lax.rsqrt(squares / inner + EPSILON)
        columns = jnp.concatenate([scale, jnp.zeros((LANES - 8, LANES), F32)], axis=0).T
        coef[piece, :] = columns
        gated = g[piece, :] * columns[:, 0:1] * prm[5:6, :width]
        yo[piece, :] = gated.astype(BF16)
        yo_t[:, piece] = gated.T.astype(BF16)
        return carry

    lax.fori_loop(0, chunks, gate, 0)
    keep(coef, coef_out)
    keep(yo, yo_out)
    keep(yo_t, yo_t_out)
    d_gather.neighbours()
    back_to_heads(side)
    back_to_heads(up)
    d_gather.finish()
    keep(d, d_out)
    back_to_heads(far)
    keep(sums.at[1], cross_out)
    small_gather.end()
    gather.end()
    d_gather.end()
    for copy in stores:
        copy.wait()


def first_part(inner, heads, own_cols, x_in, gain, small, taps, flat, lens, w_z, w_x, w_out, d_out):
    rows, model = x_in.shape
    total = 4 * rows
    width = w_z.shape[1]
    chunks = total // CHUNK
    vmem = pl.BlockSpec(memory_space=pltpu.VMEM)
    anywhere = pl.BlockSpec(memory_space=pl.ANY)
    results = [
        ((total, model), BF16),
        ((total, 2 * width), BF16),
        ((total, 3 * LANES), BF16),
        ((3 * LANES, model), BF16),
        ((total, width), F32),
        ((total, width), F32),
        ((total, width), BF16),
        ((width, total), BF16),
        ((chunks, LANES, width), BF16),
        ((total, model), BF16),
        ((total, width), BF16),
        ((total, LANES), F32),
        ((total, 1), jnp.int32),
        ((8, width + 2 * LANES), F32),
        ((8, LANES), F32),
        ((2 * LANES, width), BF16),
    ]
    cross = jax.ShapeDtypeStruct((8, total), F32)
    return pl.pallas_call(
        functools.partial(first_kernel, inner, heads, own_cols),
        out_shape=[jax.ShapeDtypeStruct(*result) for result in results] + [cross],
        in_specs=[vmem] * 5 + [pl.BlockSpec(memory_space=pltpu.SMEM)] + [anywhere] * 4,
        out_specs=[anywhere] * (len(results) + 1),
        scratch_shapes=[pltpu.VMEM((model, 2 * width), BF16), pltpu.VMEM((width, model), BF16)]
        + [pltpu.VMEM(*result) for result in results]
        + [
            pltpu.VMEM((CHUNK + 8, width + 2 * LANES), F32),
            pltpu.VMEM((LANES, width), F32),
            pltpu.VMEM((5, 8, total), F32),
            pltpu.VMEM((rows, LANES), F32),
            pltpu.SemaphoreType.DMA((7, 8)),
            pltpu.SemaphoreType.DMA((2, 3)),
            pltpu.SemaphoreType.DMA((4,)),
            pltpu.SemaphoreType.DMA((24,)),
        ],
        compiler_params=pltpu.CompilerParams(
            collective_id=0, has_side_effects=True, vmem_limit_bytes=60 * 1024 * 1024
        ),
    )(x_in, gain, small, taps, flat, lens, w_z, w_x, w_out, d_out)


def add_into(target, other):
    rows = target.shape[0]
    tile = max(t for t in range(16, 257, 16) if rows % t == 0)

    def one(i, carry):
        piece = pl.ds(pl.multiple_of(i * tile, tile), tile)
        target[piece, :] = (target[piece, :].astype(F32) + other[piece, :].astype(F32)).astype(BF16)
        return carry

    lax.fori_loop(0, rows // tile, one, 0)


def line_order(count):
    low, high, out = 0, count - 1, []
    while low <= high:
        out += [high, low] if low < high else [low]
        low, high = low + 1, high - 1
    return out


class PairSum:
    def __init__(self, parts, pair, sems):
        dp = lax.axis_index("dp")
        self.parity = lax.rem(dp, 2)
        self.partner = {"dp": dp + 1 - 2 * self.parity}
        self.parts, self.pair, self.sems, self.swaps = parts, pair, sems, {}

    def theirs(self, z):
        return 2 * z + 1 - self.parity

    def ours(self, z):
        return 2 * z + self.parity

    def swap(self, z):
        copy = send(
            self.parts.at[self.theirs(z)], self.pair.at[z], self.sems.at[0, z], self.sems.at[1, z], self.partner
        )
        copy.start()
        self.swaps[z] = copy

    def merge(self, z):
        self.swaps[z].wait()
        add_into(self.parts.at[self.ours(z)], self.pair.at[z])


class LineSum:
    def __init__(self, parts, at, right, left, right_sems, left_sems):
        dp = lax.axis_index("dp")
        self.dp = dp
        self.count = lax.axis_size("dp") // 2
        self.z = dp // 2
        self.parts, self.at = parts, at
        self.lines = {1: (right, right_sems), -1: (left, left_sems)}

    def peers(self):
        n = 2 * self.count
        return [{"dp": lax.rem(self.dp + 2, n)}, {"dp": lax.rem(self.dp + n - 2, n)}]

    def away(self, way):
        return self.z if way == 1 else self.count - 1 - self.z

    def copies(self, way, step):
        line, line_sems = self.lines[way]
        far = self.count - step + self.away(way)
        z = far if way == 1 else self.count - 1 - far
        chunk = self.parts.at[self.at(z)]
        return lambda piece: self.piece(chunk, line, line_sems, step, piece, {"dp": self.dp + 2 * way})

    def piece(self, chunk, line, line_sems, step, piece, peer):
        half = chunk.shape[0] // 2
        rows = pl.ds(piece * half, half)
        copy = send(
            chunk.at[rows], line.at[step - 1, rows], line_sems.at[0, step - 1, piece], line_sems.at[1, step - 1, piece],
            peer,
        )
        return chunk.at[rows], copy

    def add_arrived(self, way, step, piece, target):
        line, line_sems = self.lines[way]
        chunk = self.parts.at[self.at(self.z)]
        self.piece(chunk, line, line_sems, step, piece, self.peers()[0])[1].wait_recv()
        half = chunk.shape[0] // 2
        add_into(target, line.at[step - 1, pl.ds(piece * half, half)])

    def lead(self, *steps):
        for way in (1, -1):

            @pl.when(self.away(way) == 0)
            def _():
                for step in steps:
                    for piece in range(2):
                        self.copies(way, step)(piece)[1].start()

    def relay(self, step, piece):
        for way in (1, -1):
            away = self.away(way)

            @pl.when((away >= 1) & (away <= min(step - 1, self.count - 2)))
            def _():
                chunk, copy = self.copies(way, step)(piece)
                self.add_arrived(way, step - 1, piece, chunk)
                copy.start()

    def finish(self):
        total = self.parts.at[self.at(self.z)]
        half = total.shape[0] // 2
        for piece in range(2):
            for way in (1, -1):

                @pl.when(self.away(way) >= 1)
                def _():
                    self.add_arrived(way, self.count - 1, piece, total.at[pl.ds(piece * half, half)])

        return total

    def end(self):
        for way in (1, -1):
            away = self.away(way)
            for step in range(1, self.count):

                @pl.when(away <= min(step - 1, self.count - 2))
                def _():
                    for piece in range(2):
                        self.copies(way, step)(piece)[1].wait_send()


class PlaneSum:
    def __init__(self, away, to_side, to_up, in_half, in_side, in_up, sems):
        _, side, up, _ = tp_places()
        side, up = {"tp": side}, {"tp": up}
        rows = to_side.shape[0]
        half = rows // 2
        self.to_side, self.to_up, self.in_half, self.half = to_side, to_up, in_half, half
        self.in_side, self.in_up = in_side, in_up
        low, high = pl.ds(0, half), pl.ds(half, half)

        def one(n, source, target, peer):
            return send(source, target, sems.at[0, n], sems.at[1, n], peer)

        self.away_side = one(0, away.at[low], in_half.at[0], side)
        self.away_up = one(1, away.at[high], in_half.at[1], up)
        self.side_low = one(2, to_side.at[low], in_side.at[low], side)
        self.side_high = one(3, to_side.at[high], in_side.at[high], side)
        self.up_low = one(4, to_up.at[low], in_up.at[low], up)
        self.up_high = one(5, to_up.at[high], in_up.at[high], up)
        self.low, self.high = low, high

    def start_far(self):
        self.away_side.start()
        self.away_up.start()

    def start_side(self):
        self.side_low.start()

    def start_up(self):
        self.up_high.start()

    def pass_on(self):
        self.away_side.wait_recv()
        add_into(self.to_up.at[self.low], self.in_half.at[0])
        self.up_low.start()
        self.away_up.wait_recv()
        add_into(self.to_side.at[self.high], self.in_half.at[1])
        self.side_high.start()

    def finish(self):
        for copy in (self.side_low, self.up_high, self.side_high, self.up_low):
            copy.wait_recv()

    def end(self):
        for copy in (self.away_side, self.away_up, self.side_low, self.side_high, self.up_low, self.up_high):
            copy.wait_send()


def plane_scratch(rows, model):
    half = rows // 2
    return [
        pltpu.VMEM((rows, model), BF16),
        pltpu.VMEM((rows, model), BF16),
        pltpu.VMEM((rows, model), BF16),
        pltpu.VMEM((2, half, model), BF16),
        pltpu.VMEM((rows, model), BF16),
        pltpu.VMEM((rows, model), BF16),
        pltpu.SemaphoreType.DMA((2, 6)),
    ]


def pair_scratch(dp_count, shape):
    return [
        pltpu.VMEM((dp_count // 2,) + shape, BF16),
        pltpu.SemaphoreType.DMA((2, dp_count // 2)),
    ]


def line_scratch(dp_count, shape):
    steps = dp_count // 2 - 1
    return [
        pltpu.VMEM((steps,) + shape, BF16),
        pltpu.VMEM((steps,) + shape, BF16),
        pltpu.SemaphoreType.DMA((2, steps, 2)),
        pltpu.SemaphoreType.DMA((2, steps, 2)),
    ]


class Copies:
    def __init__(self, sems):
        self.sems, self.started = sems, []

    def start(self, source, target):
        copy = pltpu.make_async_copy(source, target, self.sems.at[len(self.started)])
        copy.start()
        self.started.append(copy)
        return copy


def product_chunk(left_t, right, chunk, target, tile):
    columns = pl.ds(pl.multiple_of(chunk * target.shape[1], target.shape[1]), target.shape[1])

    def one(i, carry):
        piece = pl.ds(pl.multiple_of(i * tile, tile), tile)
        target[piece, :] = dot(left_t[piece, :], right[:, columns]).astype(BF16)
        return carry

    lax.fori_loop(0, target.shape[0] // tile, one, 0)


def second_kernel(
    inner, x_ref, cross_ref, yo_ref, yo_t_ref, d_ref, w_out_ref, dyo_ref, g_ref, mixed_ref, zx_ref, coef_ref, prm_ref,
    u_ref, block_out, gw_out, dz_out, dy_out, gz_out, gain_out,
    yo, yo_t, d, w_out, dyo, g, mixed, z, coef, own, gz, parts, pair, pair_sems, gz_pair, gz_pair_sems,
    right, left, right_sems, left_sems,
    away, to_side, to_up, in_half, in_side, in_up, plane_sems, cross, cross_sems, load_sems, store_sems,
):
    rows, model = x_ref.shape
    total, width = yo.shape
    taken = parts.shape[1]
    me, side, up, far = tp_places()
    loads, stores = Copies(load_sems), Copies(store_sems)
    load_yo = loads.start(yo_ref, yo)
    load_w = loads.start(w_out_ref, w_out)
    cores = PairSum(parts, pair, pair_sems)
    gz_cores = PairSum(gz, gz_pair, gz_pair_sems)
    line = LineSum(parts, cores.ours, right, left, right_sems, left_sems)
    plane = PlaneSum(away, to_side, to_up, in_half, in_side, in_up, plane_sems)
    greet([{"tp": side}, {"tp": up}, {"tp": far}, cores.partner] + line.peers())
    crossing = [
        send(cross_ref, cross.at[n], cross_sems.at[0, n], cross_sems.at[1, n], {"tp": peer})
        for n, peer in enumerate((side, up, far))
    ]
    for copy in crossing:
        copy.start()

    def out_block(place, target):
        piece = pl.ds(pl.multiple_of(place * rows, rows), rows)

        def tile(n, carry):
            columns = pl.ds(pl.multiple_of(n * 512, 512), 512)
            target[:, columns] = dot(yo[piece, :], w_out[:, columns]).astype(target.dtype)
            return carry

        lax.fori_loop(0, model // 512, tile, 0)

    load_yo.wait()
    load_w.wait()
    load_yo_t = loads.start(yo_t_ref, yo_t)
    load_d = loads.start(d_ref, d)
    out_block(far, away)
    plane.start_far()
    load_yo_t.wait()
    load_d.wait()
    rest = [
        loads.start(dyo_ref, dyo),
        loads.start(g_ref, g),
        loads.start(mixed_ref, mixed),
        loads.start(zx_ref.at[:, :width], z),
        loads.start(coef_ref, coef),
    ]
    order = line_order(line.count)

    def products(z_chunk):
        product_chunk(yo_t, d, cores.theirs(z_chunk), parts.at[cores.theirs(z_chunk)], taken // 2)
        cores.swap(z_chunk)
        product_chunk(yo_t, d, cores.ours(z_chunk), parts.at[cores.ours(z_chunk)], taken // 2)

    for z_chunk in order[:2]:
        products(z_chunk)
    for z_chunk in order[:2]:
        cores.merge(z_chunk)
    line.lead(1)
    for z_chunk in order[2:]:
        products(z_chunk)

    def left_over(chunk, carry):
        columns = pl.ds(pl.multiple_of(chunk * parts.shape[2], parts.shape[2]), parts.shape[2])
        gz[chunk, width:, :] = dot(yo_t[taken:, :], d[:, columns]).astype(BF16)
        return carry

    for z_chunk in order[2:]:
        cores.merge(z_chunk)
    line.lead(*range(2, line.count))
    out_block(side, to_side)
    plane.start_side()
    out_block(up, to_up)
    plane.start_up()
    line.relay(2, 0)
    plane.pass_on()
    lax.fori_loop(0, parts.shape[0], left_over, 0)
    load_u = loads.start(u_ref, d)
    out_block(me, own)
    line.relay(2, 1)
    for copy in rest:
        copy.wait()
    for copy in crossing:
        copy.wait()
    gain_out[...] = jnp.zeros_like(gain_out)

    def gate_back(i, carry):
        piece = pl.ds(pl.multiple_of(i * CHUNK, CHUNK), CHUNK)
        crossed = cross_ref[:, piece] + cross[0, :, piece] + cross[1, :, piece] + cross[2, :, piece]
        crossed = jnp.concatenate([crossed, jnp.zeros((LANES - 8, LANES), F32)], axis=0).T[:, 0:1]
        scale = coef[piece, 0:1]
        back = scale * scale * scale * (crossed / inner)
        z_piece = z[piece, :].astype(F32)
        sig = jax.nn.sigmoid(z_piece)
        dyo_piece = dyo[piece, :].astype(F32)
        g_piece = g[piece, :]
        scaled = scale * dyo_piece
        dg = scaled * prm_ref[5:6, :width] - g_piece * back
        gain_out[0:1, :] += jnp.sum(scaled * g_piece, axis=0, keepdims=True)
        dz = dg * mixed[piece, :] * (sig * (1.0 + z_piece * (1.0 - sig)))
        yo[piece, :] = dz.astype(BF16)
        yo_t[:, piece] = dz.T.astype(BF16)
        dyo[piece, :] = (dg * (z_piece * sig)).astype(BF16)
        return carry

    chunks = total // CHUNK
    lax.fori_loop(0, chunks, gate_back, 0)
    stores.start(yo, dz_out)
    stores.start(dyo, dy_out)
    for step in range(3, line.count):
        line.relay(step, 0)
    load_u.wait()

    def gate_product(chunk):
        product_chunk(yo_t, d, chunk, gz.at[chunk, :width], width // 2)

    for z_chunk in order:
        gate_product(gz_cores.theirs(z_chunk))
        gz_cores.swap(z_chunk)
    for step in range(3, line.count):
        line.relay(step, 1)
    for z_chunk in order:
        gate_product(gz_cores.ours(z_chunk))
        gz_cores.merge(z_chunk)
        stores.start(gz.at[gz_cores.ours(z_chunk)], gz_out.at[z_chunk])
    sum_ref = line.finish()
    gw_out[...] = sum_ref[...]
    plane.finish()

    def add_own(i, carry):
        piece = pl.ds(pl.multiple_of(i * 32, 32), 32)
        total_out = own[piece, :] + in_side[piece, :].astype(F32) + in_up[piece, :].astype(F32)
        block_out[piece, :] = (x_ref[piece, :].astype(F32) + total_out).astype(BF16)
        return carry

    lax.fori_loop(0, rows // 32, add_own, 0)
    line.end()
    plane.end()
    for copy in stores.started:
        copy.wait()


def second_part(inner, x_in, cross, yo, yo_t, d, w_out, dyo, g, mixed, zx, coef, prm, u):
    rows, model = x_in.shape
    total, width = yo.shape
    dp_count = lax.axis_size("dp")
    cut = model // dp_count
    kept = width // 8
    vmem = pl.BlockSpec(memory_space=pltpu.VMEM)
    anywhere = pl.BlockSpec(memory_space=pl.ANY)
    return pl.pallas_call(
        functools.partial(second_kernel, inner),
        out_shape=(
            jax.ShapeDtypeStruct((rows, model), BF16),
            jax.ShapeDtypeStruct((width - kept, cut), BF16),
            jax.ShapeDtypeStruct((total, width), BF16),
            jax.ShapeDtypeStruct((total, width), BF16),
            jax.ShapeDtypeStruct((dp_count // 2, width + kept, cut), BF16),
            jax.ShapeDtypeStruct((8, width), F32),
        ),
        in_specs=[vmem] * 2 + [anywhere] * 9 + [vmem, anywhere],
        out_specs=(vmem, vmem, anywhere, anywhere, anywhere, vmem),
        scratch_shapes=[
            pltpu.VMEM((total, width), BF16),
            pltpu.VMEM((width, total), BF16),
            pltpu.VMEM((total, model), BF16),
            pltpu.VMEM((width, model), BF16),
            pltpu.VMEM((total, width), BF16),
            pltpu.VMEM((total, width), F32),
            pltpu.VMEM((total, width), F32),
            pltpu.VMEM((total, width), BF16),
            pltpu.VMEM((total, LANES), F32),
            pltpu.VMEM((rows, model), F32),
            pltpu.VMEM((dp_count, width + kept, cut), BF16),
            pltpu.VMEM((dp_count, width - kept, cut), BF16),
        ]
        + pair_scratch(dp_count, (width - kept, cut))
        + pair_scratch(dp_count, (width + kept, cut))
        + line_scratch(dp_count, (width - kept, cut))
        + plane_scratch(rows, model)
        + [
            pltpu.VMEM((3, 8, total), F32),
            pltpu.SemaphoreType.DMA((2, 3)),
            pltpu.SemaphoreType.DMA((10,)),
            pltpu.SemaphoreType.DMA((2 + dp_count // 2,)),
        ],
        compiler_params=pltpu.CompilerParams(
            collective_id=1, has_side_effects=True, vmem_limit_bytes=60 * 1024 * 1024
        ),
    )(x_in, cross, yo, yo_t, d, w_out, dyo, g, mixed, zx, coef, prm, u)


def third_kernel(
    own_cols, heads, zx_ref, bcdt_ref, pos_ref, prm_ref, head_ref, expand_ref, mixed_ref, state_ref, dy_ref,
    u_ref, gz_ref,
    gw_z, dx_out, dbcdt_out, gl_out, small_out,
    x, bcdt, mixed, states, dy, u, dx, dbcdt, dx_t, gl, bc_in, ext, d_state, later, later_pos,
    pair, pair_sems, parts, right, left, right_sems, left_sems, bc_sems, load_sems, store_sems,
):
    total, width = mixed.shape
    chunks = total // CHUNK
    me, side, up, far = tp_places()
    loads, stores = Copies(load_sems), Copies(store_sems)
    load_parts = loads.start(gz_ref, parts)
    cores = PairSum(gl, pair, pair_sems)
    line = LineSum(parts, lambda z: z, right, left, right_sems, left_sems)
    order = line_order(line.count)
    halves_of_loads = []
    for first in (total // 2, 0):
        piece = pl.ds(first, total // 2)
        pieces = pl.ds(first // CHUNK, chunks // 2)
        halves_of_loads.append(
            [
                loads.start(zx_ref.at[piece, width:], x.at[piece]),
                loads.start(bcdt_ref.at[piece], bcdt.at[piece]),
                loads.start(mixed_ref.at[piece], mixed.at[piece]),
                loads.start(state_ref.at[pieces], states.at[pieces]),
                loads.start(dy_ref.at[piece], dy.at[piece]),
            ]
        )
    load_u = loads.start(u_ref, u)
    greet([{"tp": side}, {"tp": up}, {"tp": far}, cores.partner] + line.peers())
    backward_start(small_out, d_state, later, later_pos)
    load_parts.wait()
    line.lead(*range(1, line.count))
    for copies in halves_of_loads:
        for copy in copies:
            copy.wait()
    hooks = {3: (2, 0), 5: (2, 1), 7: (3, 0), chunks: (3, 1)}

    def chunk(i, carry):
        at = chunks - 1 - i
        tokens = pl.ds(pl.multiple_of(at * CHUNK, CHUNK), CHUNK)
        halo = pl.ds(pl.multiple_of(lax.rem(at * CHUNK + total - 16, total), 16), 16)
        backward_chunk(
            width, tokens, x[halo, :], bcdt[halo, : 2 * LANES], states[at], x, bcdt, pos_ref, prm_ref, head_ref,
            expand_ref, mixed, dy, dx, dbcdt, dx_t, small_out, ext, d_state, later, later_pos,
        )
        for when, turn in hooks.items():

            @pl.when(i == when - 1)
            def _():
                line.relay(*turn)

        return carry

    lax.fori_loop(0, chunks, chunk, 0)
    stores.start(dx, dx_out)
    stores.start(dbcdt, dbcdt_out)

    pick_row = lax.broadcasted_iota(jnp.int32, (2 * own_cols, 2 * LANES), 0)
    pick_col = lax.broadcasted_iota(jnp.int32, (2 * own_cols, 2 * LANES), 1)

    def columns_of(place):
        wanted = jnp.where(pick_row < own_cols, pick_row, pick_row - own_cols + LANES) + place * own_cols
        pick = (pick_col == wanted).astype(F32).astype(BF16)
        return dot(pick, dbcdt[:, : 2 * LANES], CONTRACT_LAST)

    copies = []
    for n, peer in enumerate((side, up, far)):
        bc_in[n] = columns_of(peer).astype(BF16)
        copies.append(send(bc_in.at[n], bc_in.at[3 + n], bc_sems.at[0, n], bc_sems.at[1, n], {"tp": peer}))
        copies[-1].start()
    own_bc = columns_of(me)
    dx_t[width:, :] = jnp.zeros((LANES, total), BF16)
    dx_t[width + 2 * own_cols : width + 2 * own_cols + heads, :] = dbcdt[:, 2 * LANES :].astype(F32).T[:heads, :].astype(
        BF16
    )
    load_u.wait()

    def x_product(chunk):
        product_chunk(dx_t, u, chunk, gl.at[chunk, :width], width // 2)

    def bc_product(chunk):
        columns = pl.ds(pl.multiple_of(chunk * gl.shape[2], gl.shape[2]), gl.shape[2])
        gl[chunk, width:, :] = dot(dx_t[width:, :], u[:, columns]).astype(BF16)

    for z_chunk in order[:2]:
        x_product(cores.theirs(z_chunk))
    for copy in copies:
        copy.wait()
    for n in range(3):
        own_bc = own_bc + bc_in[3 + n].astype(F32)
    dx_t[width : width + 2 * own_cols, :] = own_bc.astype(BF16)
    for z_chunk in order:
        if z_chunk not in order[:2]:
            x_product(cores.theirs(z_chunk))
        bc_product(cores.theirs(z_chunk))
        cores.swap(z_chunk)
    for z_chunk in order:
        x_product(cores.ours(z_chunk))
        bc_product(cores.ours(z_chunk))
        cores.merge(z_chunk)
        stores.start(gl.at[cores.ours(z_chunk)], gl_out.at[z_chunk])
    sum_ref = line.finish()

    gw_z[...] = sum_ref[...]
    line.end()
    for copy in stores.started:
        copy.wait()


def third_part(own_cols, heads, zx, bcdt, pos, prm, head_prm, expand, mixed, states, dy, u, gz):
    total, width = mixed.shape
    model = u.shape[1]
    dp_count = lax.axis_size("dp")
    cut = model // dp_count
    vmem = pl.BlockSpec(memory_space=pltpu.VMEM)
    anywhere = pl.BlockSpec(memory_space=pl.ANY)
    return pl.pallas_call(
        functools.partial(third_kernel, own_cols, heads),
        out_shape=(
            jax.ShapeDtypeStruct(gz.shape[1:], BF16),
            jax.ShapeDtypeStruct((total, width), BF16),
            jax.ShapeDtypeStruct((total, 3 * LANES), BF16),
            jax.ShapeDtypeStruct((dp_count // 2, width + LANES, cut), BF16),
            jax.ShapeDtypeStruct((8, width + 2 * LANES), F32),
        ),
        in_specs=[anywhere] * 2 + [vmem] * 4 + [anywhere] * 5,
        out_specs=(vmem, anywhere, anywhere, anywhere, vmem),
        scratch_shapes=[
            pltpu.VMEM((total, width), BF16),
            pltpu.VMEM(bcdt.shape, BF16),
            pltpu.VMEM((total, width), F32),
            pltpu.VMEM(states.shape, BF16),
            pltpu.VMEM((total, width), BF16),
            pltpu.VMEM((total, model), BF16),
            pltpu.VMEM((total, width), BF16),
            pltpu.VMEM((total, 3 * LANES), BF16),
            pltpu.VMEM((width + LANES, total), BF16),
            pltpu.VMEM((dp_count, width + LANES, cut), BF16),
            pltpu.VMEM((6, 2 * own_cols, total), BF16),
            pltpu.VMEM((CHUNK + 8, width + 2 * LANES), F32),
            pltpu.VMEM((LANES, width), F32),
            pltpu.VMEM((CHUNK + 8, width + 2 * LANES), F32),
            pltpu.VMEM((CHUNK + 8, LANES), jnp.int32),
        ]
        + pair_scratch(dp_count, (width + LANES, cut))
        + [pltpu.VMEM(gz.shape, BF16)]
        + line_scratch(dp_count, gz.shape[1:])
        + [pltpu.SemaphoreType.DMA((2, 3)), pltpu.SemaphoreType.DMA((12,)), pltpu.SemaphoreType.DMA((2 + dp_count // 2,))],
        compiler_params=pltpu.CompilerParams(
            collective_id=2, has_side_effects=True, vmem_limit_bytes=60 * 1024 * 1024
        ),
    )(zx, bcdt, pos, prm, head_prm, expand, mixed, states, dy, u, gz)


def fourth_kernel(
    heads, x_ref, d_own_ref, gain_ref, small_ref, gain_sum_ref, expand_ref, dz_ref, dx_ref, dbcdt_ref, wz_ref, wx_ref,
    wbc_ref, u_ref, gl_ref,
    gw_x, grad_x, sums,
    dz, dx, dbcdt, wz, wx, wbc, u, own, gain_part, packed, over_z, parts,
    right, left, right_sems, left_sems,
    away, to_side, to_up, in_half, in_side, in_up, plane_sems, z_sems, tp_sems, load_sems,
):
    rows, model = x_ref.shape
    width = dz.shape[1]
    me, side, up, far = tp_places()
    dp_count = 2 * parts.shape[0]
    loads = Copies(load_sems)
    weights = [loads.start(wz_ref, wz), loads.start(wx_ref, wx), loads.start(wbc_ref, wbc)]
    loads_of = {}

    def load_block(name, place):
        piece = pl.ds(pl.multiple_of(place * rows, rows), rows)
        loads_of[name] = [
            loads.start(source.at[piece], target.at[piece])
            for source, target in ((dz_ref, dz), (dx_ref, dx), (dbcdt_ref, dbcdt), (u_ref, u))
        ]

    load_block("far", far)
    load_parts = loads.start(gl_ref, parts)
    line = LineSum(parts, lambda z: z, right, left, right_sems, left_sems)
    plane = PlaneSum(away, to_side, to_up, in_half, in_side, in_up, plane_sems)
    partner = {"dp": line.dp + 1 - 2 * lax.rem(line.dp, 2)}
    others = [{"dp": lax.rem(line.dp + 2 * n, dp_count)} for n in range(1, dp_count // 2)]
    greet([{"tp": side}, {"tp": up}, {"tp": far}, partner] + others)
    load_parts.wait()
    line.lead(*range(1, line.count - 1))
    for name, place in (("side", side), ("up", up), ("me", me)):
        load_block(name, place)
    gain_part[...] = jnp.zeros_like(gain_part)

    def du_block(name, place, target):
        for copy in loads_of[name]:
            copy.wait()
        piece = pl.ds(pl.multiple_of(place * rows, rows), rows)

        def tile(n, carry):
            columns = pl.ds(pl.multiple_of(n * 512, 512), 512)
            du = (
                dot(dz[piece, :], wz[columns, :], CONTRACT_LAST)
                + dot(dx[piece, :], wx[columns, :], CONTRACT_LAST)
                + dot(dbcdt[piece, :], wbc[:, columns])
            )
            target[:, columns] = du.astype(target.dtype)
            gain_part[0:1, columns] += jnp.sum(du * u[piece, columns].astype(F32), axis=0, keepdims=True)
            return carry

        lax.fori_loop(0, model // 512, tile, 0)

    for copy in weights:
        copy.wait()
    du_block("far", far, away)
    plane.start_far()
    du_block("side", side, to_side)
    plane.start_side()
    line.relay(2, 0)
    du_block("up", up, to_up)
    plane.start_up()
    line.relay(2, 1)
    plane.pass_on()
    du_block("me", me, own)
    for step in range(3, line.count):
        line.relay(step, 0)

    wide = width + 2 * LANES
    shift = (
        lax.broadcasted_iota(jnp.int32, (LANES, LANES), 1)
        == lax.broadcasted_iota(jnp.int32, (LANES, LANES), 0) + me * heads
    ).astype(F32)
    shift = jnp.where(lax.broadcasted_iota(jnp.int32, (LANES, LANES), 0) < heads, shift, 0.0)
    skip_rows = two_parts(jnp.broadcast_to(small_ref[6:7, :width], (8, width)))
    expand = expand_ref[:LANES, :]
    per_head = dot(skip_rows[:, :width], expand, CONTRACT_LAST) + dot(skip_rows[:, width:], expand, CONTRACT_LAST)
    tiles = jnp.concatenate([small_ref[:, :LANES], small_ref[:, LANES : 2 * LANES], per_head], axis=0)
    placed = lax.dot_general(
        tiles, shift, (((1,), (0,)), ((), ())), precision=HIGHEST, preferred_element_type=F32
    )
    packed[0, :, :wide] = small_ref[...]
    packed[0, 5:6, :width] = gain_sum_ref[0:1, :]
    packed[0, 6:7, width : width + LANES] = placed[16:17]
    packed[0, 7:8, :LANES] = placed[7:8]
    packed[0, 7:8, LANES : 2 * LANES] = placed[15:16]
    packed[0, :, wide:] = jnp.concatenate([gain_part[0:1, :] / gain_ref[...], jnp.zeros((7, model), F32)], axis=0)
    trade = send(packed.at[0], packed.at[1], z_sems.at[0, 0], z_sems.at[1, 0], partner)
    trade.start()
    trade.wait()
    over_z[0] = packed[0] + packed[1]
    copies = [
        send(over_z.at[0], over_z.at[n], z_sems.at[0, n], z_sems.at[1, n], others[n - 1])
        for n in range(1, dp_count // 2)
    ]
    for copy in copies:
        copy.start()
    line.lead(line.count - 1)
    for step in range(3, line.count):
        line.relay(step, 1)
    for copy in copies:
        copy.wait()
    everything = over_z[0]
    for n in range(1, dp_count // 2):
        everything = everything + over_z[n]
    sums[me] = everything
    copies = [
        send(sums.at[me], sums.at[me], tp_sems.at[0, n], tp_sems.at[1, n], {"tp": peer})
        for n, peer in enumerate((side, up, far))
    ]
    for copy in copies:
        copy.start()
    plane.finish()

    def norm_back(i, carry):
        piece = pl.ds(pl.multiple_of(i * 32, 32), 32)
        x = x_ref[piece, :].astype(F32)
        r_in = lax.rsqrt(jnp.mean(x * x, axis=-1, keepdims=True) + EPSILON)
        du = own[piece, :] + in_side[piece, :].astype(F32) + in_up[piece, :].astype(F32)
        e_in = du * gain_ref[...]
        back = r_in * r_in * r_in * jnp.mean(e_in * x, axis=-1, keepdims=True)
        grad_x[piece, :] = d_own_ref[piece, :].astype(F32) + r_in * e_in - x * back
        return carry

    lax.fori_loop(0, rows // 32, norm_back, 0)
    for copy in copies:
        copy.wait()
    sum_ref = line.finish()

    gw_x[...] = sum_ref[...]
    line.end()
    plane.end()


def fourth_part(heads, x_in, d_out, gain, small, gain_sum, expand, dz, dx, dbcdt, w_z, w_x, wbc, u, gl):
    rows, model = x_in.shape
    total, width = dz.shape
    dp_count = lax.axis_size("dp")
    cut = model // dp_count
    wide = width + 2 * LANES + model
    vmem = pl.BlockSpec(memory_space=pltpu.VMEM)
    anywhere = pl.BlockSpec(memory_space=pl.ANY)
    return pl.pallas_call(
        functools.partial(fourth_kernel, heads),
        out_shape=(
            jax.ShapeDtypeStruct(gl.shape[1:], BF16),
            jax.ShapeDtypeStruct((rows, model), F32),
            jax.ShapeDtypeStruct((4, 8, wide), F32),
        ),
        in_specs=[vmem] * 6 + [anywhere] * 8,
        out_specs=(vmem,) * 3,
        scratch_shapes=[
            pltpu.VMEM((total, width), BF16),
            pltpu.VMEM((total, width), BF16),
            pltpu.VMEM((total, 3 * LANES), BF16),
            pltpu.VMEM((model, width), BF16),
            pltpu.VMEM((model, width), BF16),
            pltpu.VMEM((3 * LANES, model), BF16),
            pltpu.VMEM((total, model), BF16),
            pltpu.VMEM((rows, model), F32),
            pltpu.VMEM((8, model), F32),
            pltpu.VMEM((2, 8, wide), F32),
            pltpu.VMEM((dp_count // 2, 8, wide), F32),
            pltpu.VMEM(gl.shape, BF16),
        ]
        + line_scratch(dp_count, gl.shape[1:])
        + plane_scratch(rows, model)
        + [
            pltpu.SemaphoreType.DMA((2, dp_count // 2)),
            pltpu.SemaphoreType.DMA((2, 3)),
            pltpu.SemaphoreType.DMA((20,)),
        ],
        compiler_params=pltpu.CompilerParams(
            collective_id=3, has_side_effects=True, vmem_limit_bytes=60 * 1024 * 1024
        ),
    )(x_in, d_out, gain, small, gain_sum, expand, dz, dx, dbcdt, w_z, w_x, wbc, u, gl)


def results_kernel(
    own_cols, heads, block_ref, grad_x_ref, first_ref, z_ref, x_ref, sums_ref,
    block_out, grad_x, gw_z, gw_x, gw_b, gw_c, gw_dt, gw_out, conv_w, conv_b, gate, norm, dt_bias, a_log, skip,
    held_block, held_grad_x, first, z, x, load_sems, sems,
):
    loads, copies = Copies(load_sems), Copies(sems)
    for source, target in ((first_ref, first), (z_ref, z), (x_ref, x), (grad_x_ref, held_grad_x), (block_ref, held_block)):
        loads.start(source, target)
    load_first, load_z, load_x, load_grad_x, load_block = loads.started
    taken = first.shape[0]
    width = gw_z.shape[1]
    count = sums_ref.shape[0]
    inner = gate.shape[1]
    wide = width + 2 * LANES

    def over_tp(rows, columns):
        total = sums_ref[0, rows, columns]
        for n in range(1, count):
            total = total + sums_ref[n, rows, columns]
        return total

    for n in range(count):
        own = slice(n * width, (n + 1) * width)
        conv_w[:, own] = sums_ref[n, 0:4, :width]
        conv_b[:, own] = sums_ref[n, 4:5, :width]
        gate[:, own] = sums_ref[n, 5:6, :width]
    conv_w[:, inner:] = over_tp(slice(0, 4), slice(width, wide))
    conv_b[:, inner:] = over_tp(slice(4, 5), slice(width, wide))
    norm[...] = over_tp(slice(0, 1), slice(wide, None))
    total_heads = dt_bias.shape[1]
    dt_bias[...] = over_tp(slice(7, 8), slice(0, LANES))[:, :total_heads]
    a_log[...] = over_tp(slice(7, 8), slice(LANES, 2 * LANES))[:, :total_heads]
    skip[...] = over_tp(slice(6, 7), slice(width, width + LANES))[:, :total_heads]
    load_grad_x.wait()
    copies.start(held_grad_x, grad_x)
    load_block.wait()
    copies.start(held_block, block_out)
    load_first.wait()
    gw_out[:taken, :] = first[...].astype(F32)
    load_z.wait()
    gw_out[taken:, :] = z[width:, :].astype(F32)

    def turn(source, target):
        def one(i, carry):
            piece = pl.ds(pl.multiple_of(i * CHUNK, CHUNK), CHUNK)
            target[:, piece] = source[piece, :].T.astype(F32)
            return carry

        lax.fori_loop(0, width // CHUNK, one, 0)

    turn(z, gw_z)
    load_x.wait()
    turn(x, gw_x)
    gw_b[...] = x[width : width + own_cols, :].astype(F32)
    gw_c[...] = x[width + own_cols : width + 2 * own_cols, :].astype(F32)
    gw_dt[...] = x[width + 2 * own_cols : width + 2 * own_cols + heads, :].astype(F32)
    for copy in copies.started:
        copy.wait()


def results_part(own_cols, heads, block_out, grad_x, first, gw_z, gw_x, sums):
    cut = first.shape[1]
    count = sums.shape[0]
    width = gw_x.shape[0] - LANES
    inner = width * count
    model = grad_x.shape[1]
    vmem = pl.BlockSpec(memory_space=pltpu.VMEM)
    anywhere = pl.BlockSpec(memory_space=pl.ANY)
    shapes = [
        (cut, width),
        (cut, width),
        (own_cols, cut),
        (own_cols, cut),
        (heads, cut),
        (width, cut),
        (4, inner + 2 * LANES),
        (1, inner + 2 * LANES),
        (1, inner),
        (1, model),
        (1, heads * count),
        (1, heads * count),
        (1, heads * count),
    ]
    return pl.pallas_call(
        functools.partial(results_kernel, own_cols, heads),
        out_shape=[
            jax.ShapeDtypeStruct(block_out.shape, BF16),
            jax.ShapeDtypeStruct(grad_x.shape, F32),
        ]
        + [jax.ShapeDtypeStruct(shape, F32) for shape in shapes],
        in_specs=[anywhere] * 5 + [vmem],
        out_specs=[anywhere] * 2 + [vmem] * len(shapes),
        scratch_shapes=[pltpu.VMEM(large.shape, large.dtype) for large in (block_out, grad_x, first, gw_z, gw_x)]
        + [pltpu.SemaphoreType.DMA((5,)), pltpu.SemaphoreType.DMA((2,))],
        compiler_params=pltpu.CompilerParams(vmem_limit_bytes=60 * 1024 * 1024),
    )(block_out, grad_x, first, gw_z, gw_x, sums)


def in_norm_scale(values):
    return lax.rsqrt(jnp.mean(values * values, axis=-1, keepdims=True) + EPSILON)


def body(
    x_in, norm_gain, w_z, w_x, w_b, w_c, w_dt, conv_w, conv_b, dt_bias, a_log, d_skip, gate_gain, w_out,
    doc_lens, d_out,
):
    tp_count = lax.axis_size("tp")
    in_planes = tp_count == 4 and lax.axis_size("dp") == 8
    rank = lax.axis_index("tp")
    dev_rows, model = x_in.shape
    rows = dev_rows * tp_count
    inner = gate_gain.shape[0]
    width = w_z.shape[1]
    heads = w_dt.shape[1]
    state_size = (conv_w.shape[0] - inner) // 2
    head_size = width // heads
    own_cols = w_b.shape[1]

    x_float = x_in.astype(F32)
    r_in = in_norm_scale(x_float)
    small_weights = jnp.concatenate([w_b, w_c, w_dt], axis=1).T
    if in_planes:
        lanes = jnp.zeros((LANES - d_skip.shape[0],), F32)
        flat = jnp.concatenate([conv_b, gate_gain, dt_bias, lanes, a_log, lanes, d_skip, lanes])[None, :]
        (
            gathered, zx, bcdt, w_bcdt, mixed, g, yo, yo_t, states, grad_gathered, dyo, coef, pos, prm, head_prm, expand,
            cross,
        ) = first_part(
            inner, heads, own_cols, x_in, norm_gain[None, :], small_weights, conv_w.T, flat, doc_lens, w_z, w_x, w_out,
            d_out,
        )
        gain_own = prm[5, :width]
    else:
        normed = (x_float * r_in * norm_gain[None, :]).astype(BF16)
        gathered = lax.all_gather(normed, "tp", axis=0, tiled=True)
        w_bc = lax.all_gather(small_weights[: 2 * own_cols], "tp", axis=0).reshape(tp_count, 2, own_cols, model)
        w_bcdt = jnp.concatenate(
            [
                jnp.swapaxes(w_bc, 0, 1).reshape(2 * state_size, model),
                small_weights[2 * own_cols :],
                jnp.zeros((LANES - heads, model), BF16),
            ],
            axis=0,
        )
        zx = dot(gathered, jnp.concatenate([w_z, w_x], axis=1)).astype(BF16)
        bcdt = dot(gathered, w_bcdt, CONTRACT_LAST).astype(BF16)
        lengths = doc_lens[0]
        doc_starts = jnp.cumsum(lengths) - lengths
        positions = jnp.arange(rows, dtype=jnp.int32)
        started = jnp.where(positions[:, None] >= doc_starts[None, :], doc_starts[None, :], 0)
        pos = (positions - jnp.max(started, axis=1))[:, None]

        def own(array, count):
            return lax.dynamic_slice_in_dim(array, rank * count, count, axis=0)

        taps = jnp.concatenate([own(conv_w[:inner], width), conv_w[inner:]], axis=0).T
        bias = jnp.concatenate([own(conv_b[:inner], width), conv_b[inner:]])
        pad_bc = jnp.zeros((2 * state_size,), F32)
        gain_own = own(gate_gain, width)
        skip_own = jnp.repeat(own(d_skip, heads), head_size)
        prm = jnp.concatenate(
            [
                taps,
                bias[None],
                jnp.concatenate([gain_own, pad_bc])[None],
                jnp.concatenate([skip_own, pad_bc])[None],
                jnp.zeros((1, width + 2 * state_size), F32),
            ],
            axis=0,
        )
        pad_heads = jnp.zeros((LANES - heads,), F32)
        head_prm = jnp.concatenate(
            [
                jnp.concatenate([own(dt_bias, heads), pad_heads])[None],
                jnp.concatenate([jnp.exp(own(a_log, heads)), pad_heads])[None],
                jnp.zeros((6, LANES), F32),
            ],
            axis=0,
        )
        expand = (
            (jnp.arange(2 * LANES) % LANES)[:, None] == (jnp.arange(width) // head_size)[None, :]
        ).astype(BF16)
        mixed, g, g_sum, states = mixer_forward(width, zx, bcdt, pos, prm, head_prm, expand)
        grad_gathered = lax.all_gather(d_out, "tp", axis=0, tiled=True)
        dyo = dot(grad_gathered, w_out, CONTRACT_LAST).astype(BF16)
        eg_sum = jnp.sum(dyo.astype(F32) * gain_own[None, :] * g, axis=1)
        g_total, eg_total = lax.psum((g_sum[0], eg_sum), "tp")
        r_gate = lax.rsqrt(g_total / inner + EPSILON)
        zeros = jnp.zeros_like(r_gate)
        coef = jnp.stack([r_gate] + [zeros] * 7 + [r_gate**3 * (eg_total / inner)] + [zeros] * (LANES - 9), axis=1)
        yo = (g * r_gate[:, None] * gain_own[None, :]).astype(BF16)

    if in_planes:
        block_out, gw_first, dz, dy, gz, gain_sum = second_part(
            inner, x_in, cross, yo, yo_t, grad_gathered, w_out, dyo, g, mixed, zx, coef, prm, gathered
        )
        gw_z, grad_xs, grad_bcdt, gl, small = third_part(
            own_cols, heads, zx, bcdt, pos, prm, head_prm, expand, mixed, states, dy, gathered, gz
        )
        gw_x, grad_x, sums = fourth_part(
            heads, x_in, d_out, norm_gain[None, :], small, gain_sum, expand, dz, grad_xs, grad_bcdt, w_z, w_x, w_bcdt,
            gathered, gl
        )
        (
            block_out, grad_x, gw_z, gw_x, gw_b, gw_c, gw_dt, gw_out, g_conv_w, g_conv_b, g_gate, g_norm, g_dt_bias,
            g_a_log, g_skip
        ) = results_part(
            own_cols, heads, block_out, grad_x, gw_first, gw_z, gw_x, sums
        )
        return (
            block_out, grad_x, g_norm[0], gw_z, gw_x, gw_b.T, gw_c.T, gw_dt.T, g_conv_w.T, g_conv_b[0], g_dt_bias[0],
            g_a_log[0], g_skip[0], g_gate[0], gw_out
        )
    else:

        def scatter_dp(partial):
            return lax.psum_scatter(partial.astype(BF16), "dp", scatter_dimension=0, tiled=True).astype(F32)

        def scatter_tp(array):
            return lax.psum_scatter(array.astype(BF16), "tp", scatter_dimension=0, tiled=True).astype(F32)

        grad_w_out = scatter_dp(dot(grad_gathered, yo, CONTRACT_FIRST)).T
        z = zx[:, :width].astype(F32)
        sig_z = jax.nn.sigmoid(z)
        dg = coef[:, 0:1] * (dyo.astype(F32) * gain_own[None, :]) - g * coef[:, 8:9]
        dz = (dg * mixed * (sig_z * (1.0 + z * (1.0 - sig_z)))).astype(BF16)
        dy = (dg * (z * sig_z)).astype(BF16)
        gain_sum = jnp.sum(dyo.astype(F32) * g * coef[:, 0:1], axis=0)
        grad_w_z = scatter_dp(dot(gathered, dz, CONTRACT_FIRST))
        block_out = (x_float + scatter_tp(dot(yo, w_out))).astype(BF16)
        grad_xs, grad_bcdt, small = mixer_backward(
            width, zx, bcdt, pos, prm, head_prm, expand, mixed, states, dy
        )
        small = small.at[5, :width].set(gain_sum)
        d_bc = grad_bcdt[:, : 2 * state_size]
        by_owner = jnp.moveaxis(d_bc.reshape(rows, 2, tp_count, own_cols), 2, 0)
        by_owner = by_owner.reshape(tp_count, rows, 2 * own_cols)
        d_bc_own = lax.psum_scatter(by_owner.astype(F32), "tp", scatter_dimension=0, tiled=False)
        d_rest = jnp.concatenate(
            [
                d_bc_own.astype(BF16),
                grad_bcdt[:, 2 * state_size : 2 * state_size + heads],
                jnp.zeros((rows, (-2 * own_cols - heads) % LANES), BF16),
            ],
            axis=1,
        )
        grad_w_x = scatter_dp(dot(gathered, grad_xs, CONTRACT_FIRST))
        grad_rest = scatter_dp(dot(gathered, d_rest, CONTRACT_FIRST))
        du_part = (
            dot(dz, w_z, CONTRACT_LAST) + dot(grad_xs, w_x, CONTRACT_LAST) + dot(grad_bcdt, w_bcdt)
        )
        gain_part = jnp.sum(du_part * gathered.astype(F32), axis=0) / norm_gain
        du = scatter_tp(du_part)
        e_in = du * norm_gain[None, :]
        grad_x = d_out.astype(F32) + r_in * e_in - x_float * (
            r_in**3 * jnp.mean(e_in * x_float, axis=-1, keepdims=True)
        )
        sums = lax.all_gather(lax.psum(small, "dp"), "tp")
        grad_norm_gain = lax.psum(gain_part, ("dp", "tp"))

    channels = jnp.swapaxes(sums[:, :7, :width], 0, 1).reshape(7, inner)
    shared = jnp.sum(sums[:, :5, width : width + 2 * state_size], axis=0)
    grad_conv = jnp.concatenate([channels[:5], shared], axis=1)
    return (
        block_out,
        grad_x,
        grad_norm_gain,
        grad_w_z,
        grad_w_x,
        grad_rest[:, :own_cols],
        grad_rest[:, own_cols : 2 * own_cols],
        grad_rest[:, 2 * own_cols : 2 * own_cols + heads],
        grad_conv[:4].T,
        grad_conv[4],
        sums[:, 7, :heads].reshape(-1),
        sums[:, 7, LANES : LANES + heads].reshape(-1),
        channels[6].reshape(heads * tp_count, head_size).sum(axis=1),
        channels[5],
        grad_w_out,
    )


def solution(mesh):
    rows = P(("dp", "tp"), None)
    columns = P(None, "tp")
    both = P("dp", "tp")
    none = P()
    return jax.shard_map(
        body,
        mesh=mesh,
        in_specs=(
            rows, none, columns, columns, columns, columns, columns, none, none, none, none, none, none,
            P("tp", None), P("dp", None), rows,
        ),
        out_specs=(
            rows, rows, none, both, both, both, both, both, none, none, none, none, none, none, P("tp", "dp"),
        ),
        check_vma=False,
    )
```

```python
import functools

import jax
import jax.numpy as jnp
from jax import lax
from jax.experimental import pallas as pl
from jax.experimental.pallas import tpu as pltpu
from jax.sharding import PartitionSpec as P

EPSILON = 1e-05
HIGHEST = lax.Precision.HIGHEST
F32 = jnp.float32
BF16 = jnp.bfloat16
CHUNK = 128
LANES = 128
CONTRACT_FIRST = (((0,), (0,)), ((), ()))
CONTRACT_LAST = (((1,), (1,)), ((), ()))


def dot(a, b, dims=(((1,), (0,)), ((), ()))):
    return lax.dot_general(a, b, dims, preferred_element_type=F32)


def two_parts(v):
    high = v.astype(BF16)
    return jnp.concatenate([high, (v - high.astype(F32)).astype(BF16)], axis=1)


def convolve(width, x, bc, pos, prm_ref, ext):
    ext[8:, :width] = x.astype(F32)
    ext[8:, width:] = bc.astype(F32)
    pre = prm_ref[3:4, :] * ext[8:, :] + prm_ref[4:5, :]
    for back in (1, 2, 3):
        here = (pos >= back).astype(F32)
        pre = pre + prm_ref[3 - back : 4 - back, :] * (ext[8 - back : 8 - back + CHUNK, :] * here)
    return pre


def prepare_chunk(width, pre, raw_dt, pos, head_ref, expand_ref):
    rows = CHUNK
    sig = jax.nn.sigmoid(pre)
    act = pre * sig
    xc = act[:, :width]
    state_size = (act.shape[1] - width) // 2
    b_rows = act[:, width : width + state_size].astype(BF16)
    c_rows = act[:, width + state_size :].astype(BF16)
    raw = raw_dt.astype(F32) + head_ref[0:1, :]
    dt = jnp.maximum(raw, 0.0) + jnp.log1p(jnp.exp(-jnp.abs(raw)))
    log_decay = -dt * head_ref[1:2, :]
    t_idx = lax.broadcasted_iota(jnp.int32, (rows, rows), 0)
    s_idx = lax.broadcasted_iota(jnp.int32, (rows, rows), 1)
    lower = (s_idx <= t_idx).astype(F32)
    cum = lax.dot_general(
        lower, log_decay, (((1,), (0,)), ((), ())), precision=HIGHEST, preferred_element_type=F32
    )
    same = (s_idx <= t_idx) & (s_idx >= t_idx - pos)
    scores = jnp.where(same, dot(c_rows, b_rows, CONTRACT_LAST), 0.0)
    t_col = lax.broadcasted_iota(jnp.int32, (rows, 1), 0)
    pos_last = pos[rows - 1 : rows, :]
    cum_last = cum[rows - 1 : rows, :]
    inward = jnp.exp(cum) * (pos > t_col).astype(F32)
    tail = jnp.exp(cum_last - cum) * (t_col >= rows - 1 - pos_last).astype(F32)
    carried = jnp.exp(cum_last) * (pos_last >= rows).astype(F32)
    wide = dot(
        two_parts(jnp.concatenate([dt, inward, tail, jnp.broadcast_to(carried, (8, LANES))], axis=0)),
        expand_ref[...],
    )
    return dict(
        sig=sig,
        xc=xc,
        b=b_rows,
        c=c_rows,
        raw=raw,
        log_decay=log_decay,
        cum=cum,
        cum_t=cum.T,
        same=same,
        scores=scores,
        t_idx=t_idx,
        s_idx=s_idx,
        dt_w=wide[:rows],
        in_w=wide[rows : 2 * rows],
        tail_w=wide[2 * rows : 3 * rows],
        carried_w=wide[3 * rows : 3 * rows + 1],
    )


def decay_of(k, head):
    return jnp.exp(jnp.minimum(k["cum"][:, head : head + 1] - k["cum_t"][head : head + 1, :], 0.0))


def halves(pair):
    lane = lax.broadcasted_iota(jnp.int32, pair.shape, 1)
    zero = jnp.zeros_like(pair)
    return jnp.concatenate(
        [jnp.where(lane < LANES // 2, pair, zero), jnp.where(lane < LANES // 2, zero, pair)], axis=0
    )


def forward_chunk(
    width, at, zx_ref, bcdt_ref, pos_ref, prm_ref, head_ref, expand_ref, mixed_ref, g_ref, sum_ref, state_ref,
    pre_ref, ext, state,
):
    if isinstance(at, int):
        rows = slice(at * CHUNK, (at + 1) * CHUNK)
    else:
        rows = pl.ds(pl.multiple_of(at * CHUNK, CHUNK), CHUNK)
    ext[:8, :] = ext[CHUNK:, :]
    pos = pos_ref[rows, :]
    pre = convolve(width, zx_ref[rows, width:], bcdt_ref[rows, : 2 * LANES], pos, prm_ref, ext)
    pre_ref[rows, :] = pre
    k = prepare_chunk(width, pre, bcdt_ref[rows, 2 * LANES :], pos, head_ref, expand_ref)
    stepped = (k["xc"] * k["dt_w"]).astype(BF16)
    held = state[...]
    held_low = held.astype(BF16)
    state_ref[at] = held_low
    reached = dot(k["c"], held_low) * k["in_w"] + prm_ref[6:7, :width] * k["xc"]
    weighted = (stepped.astype(F32) * k["tail_w"]).astype(BF16)
    state[...] = k["carried_w"] * held + dot(k["b"], weighted, CONTRACT_FIRST)
    for pair in range(width // LANES):
        lanes = slice(pair * LANES, (pair + 1) * LANES)
        mixing = jnp.concatenate(
            [
                (decay_of(k, 2 * pair) * k["scores"]).astype(BF16),
                (decay_of(k, 2 * pair + 1) * k["scores"]).astype(BF16),
            ],
            axis=1,
        )
        mixed_ref[rows, lanes] = dot(mixing, halves(stepped[:, lanes])) + reached[:, lanes]
    z = zx_ref[rows, :width].astype(F32)
    g = mixed_ref[rows, :] * (z * jax.nn.sigmoid(z))
    g_ref[rows, :] = g
    total = jnp.sum(g * g, axis=1, keepdims=True)
    sum_ref[:, rows] = jnp.broadcast_to(total, (CHUNK, LANES)).T[:8, :]


def forward_kernel(
    width, zx_ref, bcdt_ref, pos_ref, prm_ref, head_ref, expand_ref, mixed_ref, g_ref, sum_ref, state_ref,
    pre_ref, ext, state,
):
    @pl.when(pl.program_id(0) == 0)
    def _():
        state[...] = jnp.zeros_like(state)
        ext[...] = jnp.zeros_like(ext)

    forward_chunk(
        width, 0, zx_ref, bcdt_ref, pos_ref, prm_ref, head_ref, expand_ref, mixed_ref, g_ref, sum_ref, state_ref,
        pre_ref, ext, state,
    )


def backward_chunk(
    width, tokens, held, pre_ref, x_ref, bcdt_ref, pos_ref, prm_ref, head_ref, expand_ref, mixed_ref,
    dy_ref, grad_x_ref, grad_bcdt_ref, grad_t_ref, small_ref, d_state, later, later_pos,
):
    rows = CHUNK
    pos = pos_ref[tokens, :]
    pre = pre_ref[tokens, :]
    k = prepare_chunk(width, pre, bcdt_ref[tokens, 2 * LANES :], pos, head_ref, expand_ref)
    xc = k["xc"]
    skip = prm_ref[6:7, :width]
    y = mixed_ref[tokens, :] - skip * xc
    dy_low = dy_ref[tokens, :]
    dy = dy_low.astype(F32)
    small_ref[6:7, :width] += jnp.sum(dy * xc, axis=0, keepdims=True)

    stepped = (xc * k["dt_w"]).astype(BF16)
    d_held = d_state[...]
    d_held_low = d_held.astype(BF16)
    held_low = held
    weighted = (stepped.astype(F32) * k["tail_w"]).astype(BF16)
    dy_in = (dy * k["in_w"]).astype(BF16)
    from_state = dot(k["b"], d_held_low) * k["tail_w"]
    dc = dot(dy_in, held_low, CONTRACT_LAST)
    db = dot(weighted, d_held_low, CONTRACT_LAST)
    d_state[...] = k["carried_w"] * d_held + dot(k["c"], dy_in, CONTRACT_FIRST)
    d_scores = jnp.zeros((rows, rows), F32)
    d_stepped = []
    for pair in range(width // LANES):
        lanes = slice(pair * LANES, (pair + 1) * LANES)
        decay_a = decay_of(k, 2 * pair)
        decay_b = decay_of(k, 2 * pair + 1)
        mixing = jnp.concatenate(
            [(decay_a * k["scores"]).astype(BF16), (decay_b * k["scores"]).astype(BF16)], axis=0
        )
        d_mixing = dot(dy_low[:, lanes], halves(stepped[:, lanes]), CONTRACT_LAST)
        d_scores = d_scores + decay_a * d_mixing[:, :rows] + decay_b * d_mixing[:, rows:]
        d_stepped.append(dot(mixing, halves(dy_low[:, lanes]), CONTRACT_FIRST))
    d_stepped = jnp.concatenate(d_stepped, axis=1) + from_state
    d_scores = jnp.where(k["same"], d_scores, 0.0).astype(BF16)
    dc = dc + dot(d_scores, k["b"])
    db = db + dot(d_scores, k["c"], CONTRACT_FIRST)
    dxc = skip * dy + d_stepped * k["dt_w"]

    stepped_f = stepped.astype(F32)
    tail_term = jnp.sum(stepped_f * from_state, axis=0, keepdims=True) + k["carried_w"] * jnp.sum(
        held_low.astype(F32) * d_held, axis=0, keepdims=True
    )
    gathered = two_parts(
        jnp.concatenate([dy * y - stepped_f * d_stepped, jnp.broadcast_to(tail_term, (8, width))], axis=0)
    )
    expand = expand_ref[:LANES, :]
    narrow = dot(gathered[:, :width], expand, CONTRACT_LAST) + dot(gathered[:, width:], expand, CONTRACT_LAST)
    d_cum = narrow[:rows]
    d_dt = dot((d_stepped * xc).astype(BF16), expand, CONTRACT_LAST)
    upper = (k["s_idx"] >= k["t_idx"]).astype(F32)
    d_decay = (
        lax.dot_general(
            upper, d_cum, (((1,), (0,)), ((), ())), precision=HIGHEST, preferred_element_type=F32
        )
        + narrow[rows : rows + 1]
    )
    d_raw = (d_dt - d_decay * head_ref[1:2, :]) * jax.nn.sigmoid(k["raw"])
    small_ref[7:8, :LANES] += jnp.sum(d_raw, axis=0, keepdims=True)
    small_ref[7:8, LANES : 2 * LANES] += jnp.sum(d_decay * k["log_decay"], axis=0, keepdims=True)
    grad_bcdt_ref[tokens, 2 * LANES :] = d_raw.astype(BF16)

    sig = k["sig"]
    d_pre = jnp.concatenate([dxc, db, dc], axis=1) * (sig * (1.0 + pre * (1.0 - sig)))
    small_ref[4:5, :] += jnp.sum(d_pre, axis=0, keepdims=True)
    later[:rows, :] = d_pre
    later_pos[:rows, :] = jnp.broadcast_to(pos, (rows, LANES))
    x_own = jnp.concatenate([x_ref[tokens, :], bcdt_ref[tokens, : 2 * LANES]], axis=1).astype(F32)
    d_in = prm_ref[3:4, :] * d_pre
    small_ref[3:4, :] += jnp.sum(d_pre * x_own, axis=0, keepdims=True)
    for back in (1, 2, 3):
        there = (later_pos[back : back + rows, :] >= back).astype(F32)
        reaching = later[back : back + rows, :] * jnp.concatenate([there] * (later.shape[1] // LANES), axis=1)
        small_ref[3 - back : 4 - back, :] += jnp.sum(reaching * x_own, axis=0, keepdims=True)
        d_in = d_in + prm_ref[3 - back : 4 - back, :] * reaching
    grad_x_ref[tokens, :] = d_in[:, :width].astype(BF16)
    grad_bcdt_ref[tokens, : 2 * LANES] = d_in[:, width:].astype(BF16)
    later[rows:, :] = later[:8, :]
    later_pos[rows:, :] = later_pos[:8, :]
    if grad_t_ref is not None:
        grad_t_ref[:width, tokens] = d_in[:, :width].T.astype(BF16)


def backward_start(small_ref, d_state, later, later_pos):
    d_state[...] = jnp.zeros_like(d_state)
    later[...] = jnp.zeros_like(later)
    later_pos[...] = jnp.zeros_like(later_pos)
    small_ref[...] = jnp.zeros_like(small_ref)


def backward_kernel(
    width, pre_ref, x_ref, bcdt_ref, pos_ref, prm_ref, head_ref, expand_ref, mixed_ref, state_ref, dy_ref, grad_x_ref,
    grad_bcdt_ref, small_ref, d_state, later, later_pos,
):
    @pl.when(pl.program_id(0) == 0)
    def _():
        backward_start(small_ref, d_state, later, later_pos)

    backward_chunk(
        width, slice(0, CHUNK), state_ref[0], pre_ref, x_ref, bcdt_ref, pos_ref, prm_ref, head_ref, expand_ref, mixed_ref,
        dy_ref, grad_x_ref, grad_bcdt_ref, None, small_ref, d_state, later, later_pos,
    )


def mixer_forward(width, zx, bcdt, pos, prm, head_prm, expand):
    rows = zx.shape[0]
    chunks = rows // CHUNK

    def tokens(columns):
        return pl.BlockSpec((CHUNK, columns), lambda i: (i, 0))

    def whole(array):
        return pl.BlockSpec(array.shape, lambda i: (0, 0))

    return pl.pallas_call(
        functools.partial(forward_kernel, width),
        out_shape=(
            jax.ShapeDtypeStruct((rows, width), F32),
            jax.ShapeDtypeStruct((rows, width), F32),
            jax.ShapeDtypeStruct((8, rows), F32),
            jax.ShapeDtypeStruct((chunks, LANES, width), BF16),
            jax.ShapeDtypeStruct((rows, width + 2 * LANES), F32),
        ),
        grid=(chunks,),
        in_specs=[tokens(2 * width), tokens(3 * LANES), tokens(1), whole(prm), whole(head_prm), whole(expand)],
        out_specs=(
            tokens(width),
            tokens(width),
            pl.BlockSpec((8, CHUNK), lambda i: (0, i)),
            pl.BlockSpec((1, LANES, width), lambda i: (i, 0, 0)),
            tokens(width + 2 * LANES),
        ),
        scratch_shapes=[
            pltpu.VMEM((CHUNK + 8, width + 2 * LANES), F32),
            pltpu.VMEM((LANES, width), F32),
        ],
        compiler_params=pltpu.CompilerParams(
            dimension_semantics=("arbitrary",), vmem_limit_bytes=40 * 1024 * 1024
        ),
    )(zx, bcdt, pos, prm, head_prm, expand)


def mixer_backward(width, pre, zx, bcdt, pos, prm, head_prm, expand, mixed, states, dy):
    rows = zx.shape[0]
    chunks = rows // CHUNK

    def tokens(columns):
        return pl.BlockSpec((CHUNK, columns), lambda i: (chunks - 1 - i, 0))

    def whole(array):
        return pl.BlockSpec(array.shape, lambda i: (0, 0))

    return pl.pallas_call(
        functools.partial(backward_kernel, width),
        out_shape=(
            jax.ShapeDtypeStruct((rows, width), BF16),
            jax.ShapeDtypeStruct((rows, 3 * LANES), BF16),
            jax.ShapeDtypeStruct((8, width + 2 * LANES), F32),
        ),
        grid=(chunks,),
        in_specs=[
            tokens(width + 2 * LANES),
            pl.BlockSpec((CHUNK, width), lambda i: (chunks - 1 - i, 1)),
            tokens(3 * LANES),
            tokens(1),
            whole(prm),
            whole(head_prm),
            whole(expand),
            tokens(width),
            pl.BlockSpec((1, LANES, width), lambda i: (chunks - 1 - i, 0, 0)),
            tokens(width),
        ],
        out_specs=(
            tokens(width),
            tokens(3 * LANES),
            pl.BlockSpec((8, width + 2 * LANES), lambda i: (0, 0)),
        ),
        scratch_shapes=[
            pltpu.VMEM((LANES, width), F32),
            pltpu.VMEM((CHUNK + 8, width + 2 * LANES), F32),
            pltpu.VMEM((CHUNK + 8, LANES), jnp.int32),
        ],
        compiler_params=pltpu.CompilerParams(
            dimension_semantics=("arbitrary",), vmem_limit_bytes=48 * 1024 * 1024
        ),
        cost_estimate=pl.CostEstimate(flops=rows * width * 2048, bytes_accessed=rows * width * 20, transcendentals=0),
    )(pre, zx, bcdt, pos, prm, head_prm, expand, mixed, states, dy)


MESH = pl.DeviceIdType.MESH


def tp_places():
    me = lax.axis_index("tp")
    return me, me + 1 - 2 * lax.rem(me, 2), lax.rem(me + 2, 4), 3 - me


def greet(peers):
    barrier = pltpu.get_barrier_semaphore()
    for peer in peers:
        pl.semaphore_signal(barrier, inc=1, device_id=peer, device_id_type=MESH)
    pl.semaphore_wait(barrier, len(peers))


def send(src, dst, send_sem, recv_sem, peer):
    return pltpu.make_async_remote_copy(
        src_ref=src, dst_ref=dst, send_sem=send_sem, recv_sem=recv_sem, device_id=peer, device_id_type=MESH
    )


class Gather:
    def __init__(self, whole, rows, send_sems, recv_sems, own=None):
        me, side, up, _ = tp_places()
        half = rows // 2

        def part(place, which):
            return whole.at[pl.ds(pl.multiple_of(place * rows + which * half, half), half)]

        def one(n, place, which, peer):
            return send(part(place, which), part(place, which), send_sems.at[n], recv_sems.at[n], {"tp": peer})

        def quarter(n, which, late, peer):
            start = pl.multiple_of(me * rows + which * half + late * (half // 2), half // 2)
            piece = whole.at[pl.ds(start, half // 2)]
            return send(piece, piece, send_sems.at[n], recv_sems.at[n], {"tp": peer})

        self.side_first, self.up_first = one(0, me, 0, side), one(1, me, 1, up)
        self.side_then = [quarter(2, 1, 0, side), quarter(3, 1, 1, side)]
        self.up_then = [quarter(4, 0, 0, up), quarter(5, 0, 1, up)]
        self.pass_up, self.pass_side = one(6, side, 0, up), one(7, up, 1, side)

    def start(self):
        for copy in (self.side_first, self.up_first, self.side_then[0], self.up_then[0]):
            copy.start()

    def start_rest(self):
        self.side_then[1].start()
        self.up_then[1].start()

    def forward(self):
        self.side_first.wait_recv()
        self.pass_up.start()
        self.up_first.wait_recv()
        self.pass_side.start()

    def neighbours(self):
        for copy in self.side_then + self.up_then:
            copy.wait_recv()

    def finish(self):
        self.pass_up.wait_recv()
        self.pass_side.wait_recv()

    def end(self):
        for copy in [self.side_first, self.up_first, self.pass_up, self.pass_side] + self.side_then + self.up_then:
            copy.wait_send()


def set_up(width, heads, inner, taps_ref, flat_ref, lens_ref, prm, head, expand, pos):
    rank = lax.axis_index("tp")
    channels = taps_ref.shape[1]
    own = pl.ds(pl.multiple_of(rank * width, LANES), width)
    own_gain = pl.ds(pl.multiple_of(channels + rank * width, LANES), width)
    prm[...] = jnp.zeros_like(prm)
    prm[0:4, :width] = taps_ref[:, own]
    prm[0:4, width:] = taps_ref[:, inner:]
    prm[4:5, :width] = flat_ref[:, own]
    prm[4:5, width:] = flat_ref[:, inner:channels]
    prm[5:6, :width] = flat_ref[:, own_gain]
    lane = lax.broadcasted_iota(jnp.int32, (LANES, LANES), 1)
    pick = ((lax.broadcasted_iota(jnp.int32, (LANES, LANES), 0) == lane + rank * heads) & (lane < heads)).astype(F32)
    start = channels + inner
    tiles = [jnp.broadcast_to(flat_ref[:, start + n * LANES : start + (n + 1) * LANES], (8, LANES)) for n in range(3)]
    tiles[1] = jnp.exp(tiles[1])
    picked = lax.dot_general(
        jnp.concatenate(tiles, axis=0), pick, (((1,), (0,)), ((), ())), precision=HIGHEST, preferred_element_type=F32
    )
    head[...] = jnp.concatenate([picked[0:1], picked[8:9], jnp.zeros((6, LANES), F32)], axis=0)
    row = lax.broadcasted_iota(jnp.int32, (2 * LANES, width), 0)
    column = lax.broadcasted_iota(jnp.int32, (2 * LANES, width), 1)
    expand[...] = (lax.rem(row, LANES) == column // (width // heads)).astype(F32).astype(BF16)
    prm[6:7, :width] = dot(two_parts(picked[16:24]), expand[...])[0:1]
    starts = [jnp.int32(0)]
    for n in range(lens_ref.shape[1] - 1):
        starts.append(starts[-1] + lens_ref[0, n])

    def place(i, carry):
        token = lax.broadcasted_iota(jnp.int32, (CHUNK, 1), 0) + i * CHUNK
        begun = jnp.zeros((CHUNK, 1), jnp.int32)
        for first in starts[1:]:
            begun = jnp.where(token >= first, first, begun)
        pos[pl.ds(pl.multiple_of(i * CHUNK, CHUNK), CHUNK), :] = token - begun
        return carry

    lax.fori_loop(0, pos.shape[0] // CHUNK, place, 0)


def first_kernel(
    inner, heads, own_cols, x_ref, gain_ref, small_ref, taps_ref, flat_ref, lens_ref, wz_ref, wx_ref, w_out_ref, d_own_ref,
    u_out, zx_out, bcdt_out, wbc_out, mixed_out, g_out, yo_out, yo_t_out, state_out, d_out, dyo_out, coef_out, pos_out,
    prm_out, head_out, expand_out, pre_out, cross_out,
    weights, w_out, u, zx, bcdt, wbc, mixed, g, yo, yo_t, states, d, dyo, coef, pos, prm, head, expand, pre, ext, state, sums,
    acc, sems, sum_sems, load_sems, store_sems,
):
    rows, model = x_ref.shape
    total, width = mixed.shape
    chunks = total // CHUNK
    me, side, up, far = tp_places()
    dp = lax.axis_index("dp")
    parity = lax.rem(dp, 2)
    partner = {"dp": dp + 1 - 2 * parity}

    def block(place):
        return pl.ds(pl.multiple_of(place * rows, rows), rows)

    loads = [
        pltpu.make_async_copy(wz_ref, weights.at[:, :width], load_sems.at[0]),
        pltpu.make_async_copy(wx_ref, weights.at[:, width:], load_sems.at[1]),
        pltpu.make_async_copy(w_out_ref, w_out, load_sems.at[2]),
        pltpu.make_async_copy(d_own_ref, d.at[block(me)], load_sems.at[3]),
    ]
    for copy in loads:
        copy.start()
    stores = []

    def keep(source, target):
        copy = pltpu.make_async_copy(source, target, store_sems.at[len(stores)])
        copy.start()
        stores.append(copy)

    bc_own = pl.ds(pl.multiple_of(parity * LANES, LANES), LANES)
    wbc[pl.ds(pl.multiple_of(parity * LANES + me * own_cols, own_cols), own_cols), :] = small_ref[
        pl.ds(pl.multiple_of(parity * own_cols, own_cols), own_cols), :
    ]
    greet([{"tp": side}, {"tp": up}, {"tp": far}, partner])
    small_gather = Gather(wbc.at[bc_own], own_cols, sems.at[0], sems.at[1])
    small_gather.start()
    small_gather.start_rest()

    def norm(i, carry):
        piece = pl.ds(pl.multiple_of(i * 32, 32), 32)
        x = x_ref[piece, :].astype(F32)
        scale = lax.rsqrt(jnp.mean(x * x, axis=-1, keepdims=True) + EPSILON)
        u[pl.ds(pl.multiple_of(me * rows + i * 32, 32), 32), :] = (x * scale * gain_ref[...]).astype(BF16)
        return carry

    lax.fori_loop(0, rows // 32, norm, 0)
    small_gather.forward()
    gather = Gather(u, rows, sems.at[2], sems.at[3])
    gather.start()
    gather.start_rest()
    wbc[2 * LANES :, :] = jnp.zeros((LANES, model), BF16)
    wbc[2 * LANES : 2 * LANES + heads, :] = small_ref[2 * own_cols :, :]
    set_up(width, heads, inner, taps_ref, flat_ref, lens_ref, prm, head, expand, pos)
    keep(pos, pos_out)
    keep(prm, prm_out)
    keep(head, head_out)
    keep(expand, expand_out)
    loads[0].wait()
    loads[1].wait()

    def project(place):
        piece = block(place)

        def tile(n, carry):
            columns = pl.ds(pl.multiple_of(n * 512, 512), 512)
            zx[piece, columns] = dot(u[piece, :], weights[:, columns]).astype(BF16)
            return carry

        lax.fori_loop(0, 2 * width // 512, tile, 0)

    def project_small(place):
        bcdt[block(place), :] = dot(u[block(place), :], wbc[...], CONTRACT_LAST).astype(BF16)

    project(me)
    small_gather.neighbours()
    small_gather.finish()
    trade = send(wbc.at[bc_own], wbc.at[bc_own], sems.at[6, 0], sems.at[6, 1], partner)
    trade.start()
    gather.forward()
    loads[3].wait()
    d_gather = Gather(d, rows, sems.at[4], sems.at[5])
    d_gather.start()
    trade.wait()
    keep(wbc, wbc_out)
    project_small(me)
    gather.neighbours()
    project(side)
    project(up)
    project_small(side)
    project_small(up)
    gather.finish()
    keep(u, u_out)
    project(far)
    project_small(far)
    keep(zx, zx_out)
    keep(bcdt, bcdt_out)

    state[...] = jnp.zeros_like(state)
    ext[...] = jnp.zeros_like(ext)

    def chunk(i, carry):
        forward_chunk(
            width, i, zx, bcdt, pos, prm, head, expand, mixed, g, sums.at[0], states, pre, ext, state
        )
        return carry

    lax.fori_loop(0, chunks, chunk, 0)

    copies = [
        send(sums.at[0], sums.at[2 + n], sum_sems.at[0, n], sum_sems.at[1, n], {"tp": peer})
        for n, peer in enumerate((side, up, far))
    ]
    for copy in copies:
        copy.start()
    d_gather.start_rest()
    keep(mixed, mixed_out)
    keep(g, g_out)
    keep(states, state_out)
    keep(pre, pre_out)
    loads[2].wait()

    def back_to_heads(place):
        piece = block(place)
        acc[...] = jnp.zeros_like(acc)

        def tile(n, carry):
            columns = pl.ds(pl.multiple_of(n * 256, 256), 256)
            low = dot(d[piece, :], w_out[columns, :], CONTRACT_LAST).astype(BF16)
            dyo[piece, columns] = low
            both = low.astype(F32) * prm[5:6, columns] * g[piece, columns]
            acc[...] += both[:, :LANES] + both[:, LANES:]
            return carry

        lax.fori_loop(0, width // 256, tile, 0)
        column = jnp.sum(acc[...], axis=1, keepdims=True)
        sums[1, :, piece] = jnp.broadcast_to(column, (rows, LANES)).T[:8, :]
        keep(dyo.at[piece], dyo_out.at[piece])

    d_gather.forward()
    back_to_heads(me)
    for copy in copies:
        copy.wait()

    def gate(i, carry):
        piece = pl.ds(pl.multiple_of(i * CHUNK, CHUNK), CHUNK)
        squares = sums[0, :, piece] + sums[2, :, piece] + sums[3, :, piece] + sums[4, :, piece]
        scale = lax.rsqrt(squares / inner + EPSILON)
        columns = jnp.concatenate([scale, jnp.zeros((LANES - 8, LANES), F32)], axis=0).T
        coef[piece, :] = columns
        gated = g[piece, :] * columns[:, 0:1] * prm[5:6, :width]
        yo[piece, :] = gated.astype(BF16)
        yo_t[:, piece] = gated.T.astype(BF16)
        return carry

    lax.fori_loop(0, chunks, gate, 0)
    keep(coef, coef_out)
    keep(yo, yo_out)
    keep(yo_t, yo_t_out)
    d_gather.neighbours()
    back_to_heads(side)
    back_to_heads(up)
    d_gather.finish()
    keep(d, d_out)
    back_to_heads(far)
    keep(sums.at[1], cross_out)
    small_gather.end()
    gather.end()
    d_gather.end()
    for copy in stores:
        copy.wait()


def first_part(inner, heads, own_cols, x_in, gain, small, taps, flat, lens, w_z, w_x, w_out, d_out):
    rows, model = x_in.shape
    total = 4 * rows
    width = w_z.shape[1]
    chunks = total // CHUNK
    vmem = pl.BlockSpec(memory_space=pltpu.VMEM)
    anywhere = pl.BlockSpec(memory_space=pl.ANY)
    results = [
        ((total, model), BF16),
        ((total, 2 * width), BF16),
        ((total, 3 * LANES), BF16),
        ((3 * LANES, model), BF16),
        ((total, width), F32),
        ((total, width), F32),
        ((total, width), BF16),
        ((width, total), BF16),
        ((chunks, LANES, width), BF16),
        ((total, model), BF16),
        ((total, width), BF16),
        ((total, LANES), F32),
        ((total, 1), jnp.int32),
        ((8, width + 2 * LANES), F32),
        ((8, LANES), F32),
        ((2 * LANES, width), BF16),
        ((total, width + 2 * LANES), F32),
    ]
    cross = jax.ShapeDtypeStruct((8, total), F32)
    return pl.pallas_call(
        functools.partial(first_kernel, inner, heads, own_cols),
        out_shape=[jax.ShapeDtypeStruct(*result) for result in results] + [cross],
        in_specs=[vmem] * 5 + [pl.BlockSpec(memory_space=pltpu.SMEM)] + [anywhere] * 4,
        out_specs=[anywhere] * (len(results) + 1),
        scratch_shapes=[pltpu.VMEM((model, 2 * width), BF16), pltpu.VMEM((width, model), BF16)]
        + [pltpu.VMEM(*result) for result in results]
        + [
            pltpu.VMEM((CHUNK + 8, width + 2 * LANES), F32),
            pltpu.VMEM((LANES, width), F32),
            pltpu.VMEM((5, 8, total), F32),
            pltpu.VMEM((rows, LANES), F32),
            pltpu.SemaphoreType.DMA((7, 8)),
            pltpu.SemaphoreType.DMA((2, 3)),
            pltpu.SemaphoreType.DMA((4,)),
            pltpu.SemaphoreType.DMA((24,)),
        ],
        compiler_params=pltpu.CompilerParams(
            collective_id=0, has_side_effects=True, vmem_limit_bytes=60 * 1024 * 1024
        ),
    )(x_in, gain, small, taps, flat, lens, w_z, w_x, w_out, d_out)


def add_into(target, other):
    rows = target.shape[0]
    tile = max(t for t in range(16, 257, 16) if rows % t == 0)

    def one(i, carry):
        piece = pl.ds(pl.multiple_of(i * tile, tile), tile)
        target[piece, :] = (target[piece, :].astype(F32) + other[piece, :].astype(F32)).astype(BF16)
        return carry

    lax.fori_loop(0, rows // tile, one, 0)


def line_order(count):
    low, high, out = 0, count - 1, []
    while low <= high:
        out += [high, low] if low < high else [low]
        low, high = low + 1, high - 1
    return out


class PairSum:
    def __init__(self, parts, pair, sems):
        dp = lax.axis_index("dp")
        self.parity = lax.rem(dp, 2)
        self.partner = {"dp": dp + 1 - 2 * self.parity}
        self.parts, self.pair, self.sems = parts, pair, sems

    def theirs(self, z):
        return 2 * z + 1 - self.parity

    def ours(self, z):
        return 2 * z + self.parity

    def copy(self, z):
        return send(
            self.parts.at[self.theirs(z)], self.pair.at[z], self.sems.at[0, z], self.sems.at[1, z], self.partner
        )

    def swap(self, z):
        self.copy(z).start()

    def merge(self, z):
        self.copy(z).wait()
        add_into(self.parts.at[self.ours(z)], self.pair.at[z])


class LineSum:
    def __init__(self, parts, at, right, left, right_sems, left_sems):
        dp = lax.axis_index("dp")
        self.dp = dp
        self.count = lax.axis_size("dp") // 2
        self.z = dp // 2
        self.parts, self.at = parts, at
        self.lines = {1: (right, right_sems), -1: (left, left_sems)}

    def peers(self):
        n = 2 * self.count
        return [{"dp": lax.rem(self.dp + 2, n)}, {"dp": lax.rem(self.dp + n - 2, n)}]

    def away(self, way):
        return self.z if way == 1 else self.count - 1 - self.z

    def copies(self, way, step):
        line, line_sems = self.lines[way]
        far = self.count - step + self.away(way)
        z = far if way == 1 else self.count - 1 - far
        chunk = self.parts.at[self.at(z)]
        return lambda piece: self.piece(chunk, line, line_sems, step, piece, {"dp": self.dp + 2 * way})

    def piece(self, chunk, line, line_sems, step, piece, peer):
        half = chunk.shape[0] // 2
        rows = pl.ds(piece * half, half)
        copy = send(
            chunk.at[rows], line.at[step - 1, rows], line_sems.at[0, step - 1, piece], line_sems.at[1, step - 1, piece],
            peer,
        )
        return chunk.at[rows], copy

    def add_arrived(self, way, step, piece, target):
        line, line_sems = self.lines[way]
        chunk = self.parts.at[self.at(self.z)]
        self.piece(chunk, line, line_sems, step, piece, self.peers()[0])[1].wait_recv()
        half = chunk.shape[0] // 2
        add_into(target, line.at[step - 1, pl.ds(piece * half, half)])

    def lead(self, *steps):
        for way in (1, -1):

            @pl.when(self.away(way) == 0)
            def _():
                for step in steps:
                    for piece in range(2):
                        self.copies(way, step)(piece)[1].start()

    def relay(self, step, piece):
        for way in (1, -1):
            away = self.away(way)

            @pl.when((away >= 1) & (away <= min(step - 1, self.count - 2)))
            def _():
                chunk, copy = self.copies(way, step)(piece)
                self.add_arrived(way, step - 1, piece, chunk)
                copy.start()

    def finish(self):
        total = self.parts.at[self.at(self.z)]
        half = total.shape[0] // 2
        for piece in range(2):
            for way in (1, -1):

                @pl.when(self.away(way) >= 1)
                def _():
                    self.add_arrived(way, self.count - 1, piece, total.at[pl.ds(piece * half, half)])

        return total

    def end(self):
        for way in (1, -1):
            away = self.away(way)
            for step in range(1, self.count):

                @pl.when(away <= min(step - 1, self.count - 2))
                def _():
                    for piece in range(2):
                        self.copies(way, step)(piece)[1].wait_send()


class PlaneSum:
    def __init__(self, away, to_side, to_up, in_far, in_side, in_up, sems):
        _, side, up, _ = tp_places()
        peers = ({"tp": side}, {"tp": up})
        self.to, self.in_far, self.into = (to_side, to_up), in_far, (in_side, in_up)

        def one(kind, n, source, target, peer):
            return send(source.at[n], target.at[n], sems.at[0, kind, n], sems.at[1, kind, n], peer)

        self.one, self.peers, self.away = one, peers, away
        self.far = [one(0, n, away, in_far, peers[n % 2]) for n in range(4)]
        self.near = [[one(1 + w, n, self.to[w], self.into[w], peers[w]) for n in range(4)] for w in range(2)]

    def start_far(self, n, odd):
        self.one(0, n, self.away, self.in_far, self.peers[odd]).start()

    def start_near(self, way, n, odd):
        if odd == way:
            self.one(1 + way, n, self.to[way], self.into[way], self.peers[way]).start()

    def pass_on(self):
        for n in range(4):
            way = 1 - n % 2
            self.far[n].wait_recv()
            add_into(self.to[way].at[n], self.in_far.at[n])
            self.near[way][n].start()

    def finish(self):
        for copy in self.near[0] + self.near[1]:
            copy.wait_recv()

    def received(self, piece):
        side, up = (jnp.concatenate([into[n, piece, :] for n in range(4)], axis=1) for into in self.into)
        return side.astype(F32) + up.astype(F32)

    def end(self):
        for copy in self.far + self.near[0] + self.near[1]:
            copy.wait_send()


def plane_scratch(rows, model):
    return [pltpu.VMEM((4, rows, model // 4), BF16) for _ in range(6)] + [pltpu.SemaphoreType.DMA((2, 3, 4))]


def pair_scratch(dp_count, shape):
    return [
        pltpu.VMEM((dp_count // 2,) + shape, BF16),
        pltpu.SemaphoreType.DMA((2, dp_count // 2)),
    ]


def line_scratch(dp_count, shape):
    steps = dp_count // 2 - 1
    return [
        pltpu.VMEM((steps,) + shape, BF16),
        pltpu.VMEM((steps,) + shape, BF16),
        pltpu.SemaphoreType.DMA((2, steps, 2)),
        pltpu.SemaphoreType.DMA((2, steps, 2)),
    ]


class Copies:
    def __init__(self, sems):
        self.sems, self.started = sems, []

    def start(self, source, target):
        copy = pltpu.make_async_copy(source, target, self.sems.at[len(self.started)])
        copy.start()
        self.started.append(copy)
        return copy


def product_chunk(left_t, right, chunk, target, tile):
    columns = pl.ds(pl.multiple_of(chunk * target.shape[1], target.shape[1]), target.shape[1])

    def one(i, carry):
        piece = pl.ds(pl.multiple_of(i * tile, tile), tile)
        target[piece, :] = dot(left_t[piece, :], right[:, columns]).astype(BF16)
        return carry

    lax.fori_loop(0, target.shape[0] // tile, one, 0)


def second_kernel(
    inner, x_ref, cross_ref, yo_ref, yo_t_ref, d_ref, w_out_ref, dyo_ref, g_ref, mixed_ref, zx_ref, coef_ref, prm_ref,
    u_ref, block_out, gw_out, dz_out, dy_out, gz_out, gain_out,
    yo, yo_t, d, w_out, dyo, g, mixed, z, coef, own, gz, parts, pair, pair_sems, gz_pair, gz_pair_sems,
    right, left, right_sems, left_sems,
    away, to_side, to_up, in_far, in_side, in_up, plane_sems, cross, cross_sems, load_sems, store_sems,
):
    rows, model = x_ref.shape
    total, width = yo.shape
    taken = parts.shape[1]
    me, side, up, far = tp_places()
    loads, stores = Copies(load_sems), Copies(store_sems)
    load_yo = loads.start(yo_ref, yo)
    load_w = loads.start(w_out_ref, w_out)
    cores = PairSum(parts, pair, pair_sems)
    gz_cores = PairSum(gz, gz_pair, gz_pair_sems)
    line = LineSum(parts, cores.ours, right, left, right_sems, left_sems)
    plane = PlaneSum(away, to_side, to_up, in_far, in_side, in_up, plane_sems)
    greet([{"tp": side}, {"tp": up}, {"tp": far}, cores.partner] + line.peers())
    crossing = [
        send(cross_ref, cross.at[n], cross_sems.at[0, n], cross_sems.at[1, n], {"tp": peer})
        for n, peer in enumerate((side, up, far))
    ]
    for copy in crossing:
        copy.start()

    quarter = model // 4

    def out_block(place, target, started=None):
        piece = pl.ds(pl.multiple_of(place * rows, rows), rows)

        def two(m, carry):
            for odd in range(2):
                n = 2 * m + odd
                columns = pl.ds(pl.multiple_of(n * quarter, quarter), quarter)
                value = dot(yo[piece, :], w_out[:, columns])
                if started is None:
                    target[:, columns] = value
                else:
                    target[n] = value.astype(BF16)
                    started(n, odd)
            return carry

        lax.fori_loop(0, 2, two, 0)

    load_yo.wait()
    load_w.wait()
    load_yo_t = loads.start(yo_t_ref, yo_t)
    load_d = loads.start(d_ref, d)
    out_block(far, away, plane.start_far)
    load_yo_t.wait()
    load_d.wait()
    rest = [
        loads.start(dyo_ref, dyo),
        loads.start(g_ref, g),
        loads.start(mixed_ref, mixed),
        loads.start(zx_ref.at[:, :width], z),
        loads.start(coef_ref, coef),
    ]
    order = line_order(line.count)

    def products(first, step):
        def one(i, carry):
            z_chunk = first + step * i
            product_chunk(yo_t, d, cores.theirs(z_chunk), parts.at[cores.theirs(z_chunk)], taken // 2)
            cores.swap(z_chunk)
            product_chunk(yo_t, d, cores.ours(z_chunk), parts.at[cores.ours(z_chunk)], taken // 2)
            return carry

        lax.fori_loop(0, 2, one, 0)

    products(order[0], order[1] - order[0])
    for z_chunk in order[:2]:
        cores.merge(z_chunk)
    line.lead(1)
    products(order[2], order[3] - order[2])

    def left_over(chunk, carry):
        columns = pl.ds(pl.multiple_of(chunk * parts.shape[2], parts.shape[2]), parts.shape[2])
        gz[chunk, width:, :] = dot(yo_t[taken:, :], d[:, columns]).astype(BF16)
        return carry

    for z_chunk in order[2:]:
        cores.merge(z_chunk)
    line.lead(*range(2, line.count))
    out_block(side, to_side, functools.partial(plane.start_near, 0))
    out_block(up, to_up, functools.partial(plane.start_near, 1))
    line.relay(2, 0)
    plane.pass_on()
    lax.fori_loop(0, parts.shape[0], left_over, 0)
    load_u = loads.start(u_ref, d)
    out_block(me, own)
    line.relay(2, 1)
    for copy in rest:
        copy.wait()
    for copy in crossing:
        copy.wait()
    gain_out[...] = jnp.zeros_like(gain_out)

    def gate_back(i, carry):
        piece = pl.ds(pl.multiple_of(i * CHUNK, CHUNK), CHUNK)
        crossed = cross_ref[:, piece] + cross[0, :, piece] + cross[1, :, piece] + cross[2, :, piece]
        crossed = jnp.concatenate([crossed, jnp.zeros((LANES - 8, LANES), F32)], axis=0).T[:, 0:1]
        scale = coef[piece, 0:1]
        back = scale * scale * scale * (crossed / inner)
        z_piece = z[piece, :].astype(F32)
        sig = jax.nn.sigmoid(z_piece)
        dyo_piece = dyo[piece, :].astype(F32)
        g_piece = g[piece, :]
        scaled = scale * dyo_piece
        dg = scaled * prm_ref[5:6, :width] - g_piece * back
        gain_out[0:1, :] += jnp.sum(scaled * g_piece, axis=0, keepdims=True)
        dz = dg * mixed[piece, :] * (sig * (1.0 + z_piece * (1.0 - sig)))
        yo[piece, :] = dz.astype(BF16)
        yo_t[:, piece] = dz.T.astype(BF16)
        dyo[piece, :] = (dg * (z_piece * sig)).astype(BF16)
        return carry

    chunks = total // CHUNK
    lax.fori_loop(0, chunks, gate_back, 0)
    stores.start(yo, dz_out)
    stores.start(dyo, dy_out)
    for step in range(3, line.count):
        line.relay(step, 0)
    load_u.wait()

    def gate_product(chunk):
        product_chunk(yo_t, d, chunk, gz.at[chunk, :width], width // 2)

    def theirs(z_chunk, carry):
        gate_product(gz_cores.theirs(z_chunk))
        gz_cores.swap(z_chunk)
        return carry

    lax.fori_loop(0, line.count, theirs, 0)
    for step in range(3, line.count):
        line.relay(step, 1)

    def ours(z_chunk, carry):
        gate_product(gz_cores.ours(z_chunk))
        return carry

    lax.fori_loop(0, line.count, ours, 0)
    for z_chunk in range(line.count):
        gz_cores.merge(z_chunk)
        stores.start(gz.at[gz_cores.ours(z_chunk)], gz_out.at[z_chunk])
    sum_ref = line.finish()
    gw_out[...] = sum_ref[...]
    plane.finish()

    def add_own(i, carry):
        piece = pl.ds(pl.multiple_of(i * 32, 32), 32)
        total_out = own[piece, :] + plane.received(piece)
        block_out[piece, :] = (x_ref[piece, :].astype(F32) + total_out).astype(BF16)
        return carry

    lax.fori_loop(0, rows // 32, add_own, 0)
    line.end()
    plane.end()
    for copy in stores.started:
        copy.wait()


def second_part(inner, x_in, cross, yo, yo_t, d, w_out, dyo, g, mixed, zx, coef, prm, u):
    rows, model = x_in.shape
    total, width = yo.shape
    dp_count = lax.axis_size("dp")
    cut = model // dp_count
    kept = width // 8
    vmem = pl.BlockSpec(memory_space=pltpu.VMEM)
    anywhere = pl.BlockSpec(memory_space=pl.ANY)
    return pl.pallas_call(
        functools.partial(second_kernel, inner),
        out_shape=(
            jax.ShapeDtypeStruct((rows, model), BF16),
            jax.ShapeDtypeStruct((width - kept, cut), BF16),
            jax.ShapeDtypeStruct((total, width), BF16),
            jax.ShapeDtypeStruct((total, width), BF16),
            jax.ShapeDtypeStruct((dp_count // 2, width + kept, cut), BF16),
            jax.ShapeDtypeStruct((8, width), F32),
        ),
        in_specs=[vmem] * 2 + [anywhere] * 9 + [vmem, anywhere],
        out_specs=(vmem, vmem, anywhere, anywhere, anywhere, vmem),
        scratch_shapes=[
            pltpu.VMEM((total, width), BF16),
            pltpu.VMEM((width, total), BF16),
            pltpu.VMEM((total, model), BF16),
            pltpu.VMEM((width, model), BF16),
            pltpu.VMEM((total, width), BF16),
            pltpu.VMEM((total, width), F32),
            pltpu.VMEM((total, width), F32),
            pltpu.VMEM((total, width), BF16),
            pltpu.VMEM((total, LANES), F32),
            pltpu.VMEM((rows, model), F32),
            pltpu.VMEM((dp_count, width + kept, cut), BF16),
            pltpu.VMEM((dp_count, width - kept, cut), BF16),
        ]
        + pair_scratch(dp_count, (width - kept, cut))
        + pair_scratch(dp_count, (width + kept, cut))
        + line_scratch(dp_count, (width - kept, cut))
        + plane_scratch(rows, model)
        + [
            pltpu.VMEM((3, 8, total), F32),
            pltpu.SemaphoreType.DMA((2, 3)),
            pltpu.SemaphoreType.DMA((10,)),
            pltpu.SemaphoreType.DMA((2 + dp_count // 2,)),
        ],
        compiler_params=pltpu.CompilerParams(
            collective_id=1, has_side_effects=True, vmem_limit_bytes=60 * 1024 * 1024
        ),
    )(x_in, cross, yo, yo_t, d, w_out, dyo, g, mixed, zx, coef, prm, u)


def third_kernel(
    own_cols, heads, zx_ref, bcdt_ref, pos_ref, prm_ref, head_ref, expand_ref, mixed_ref, state_ref, dy_ref,
    pre_ref, u_ref, gz_ref,
    gw_z, dx_out, dbcdt_out, gl_out, small_out,
    x, bcdt, mixed, states, dy, pre, u, dx, dbcdt, dx_t, gl, bc_in, d_state, later, later_pos,
    pair, pair_sems, parts, right, left, right_sems, left_sems, bc_sems, load_sems, store_sems,
):
    total, width = mixed.shape
    chunks = total // CHUNK
    me, side, up, far = tp_places()
    loads, stores = Copies(load_sems), Copies(store_sems)
    load_parts = loads.start(gz_ref, parts)
    cores = PairSum(gl, pair, pair_sems)
    line = LineSum(parts, lambda z: z, right, left, right_sems, left_sems)
    halves_of_loads = []
    for first in (total // 2, 0):
        piece = pl.ds(first, total // 2)
        pieces = pl.ds(first // CHUNK, chunks // 2)
        halves_of_loads.append(
            [
                loads.start(zx_ref.at[piece, width:], x.at[piece]),
                loads.start(bcdt_ref.at[piece], bcdt.at[piece]),
                loads.start(mixed_ref.at[piece], mixed.at[piece]),
                loads.start(state_ref.at[pieces], states.at[pieces]),
                loads.start(dy_ref.at[piece], dy.at[piece]),
                loads.start(pre_ref.at[piece], pre.at[piece]),
            ]
        )
    load_u = loads.start(u_ref, u)
    greet([{"tp": side}, {"tp": up}, {"tp": far}, cores.partner] + line.peers())
    backward_start(small_out, d_state, later, later_pos)
    load_parts.wait()
    line.lead(*range(1, line.count))
    for copy in halves_of_loads[0]:
        copy.wait()
    hooks = {3: (2, 0), 5: (2, 1), 7: (3, 0), chunks: (3, 1)}

    def chunk(i, carry):
        at = chunks - 1 - i
        tokens = pl.ds(pl.multiple_of(at * CHUNK, CHUNK), CHUNK)

        @pl.when(i == chunks // 2)
        def _():
            for copy in halves_of_loads[1]:
                copy.wait()

        backward_chunk(
            width, tokens, states[at], pre, x, bcdt, pos_ref, prm_ref, head_ref, expand_ref, mixed, dy, dx, dbcdt, dx_t,
            small_out, d_state, later, later_pos,
        )
        for when, turn in hooks.items():

            @pl.when(i == when - 1)
            def _():
                line.relay(*turn)

        return carry

    lax.fori_loop(0, chunks, chunk, 0)
    stores.start(dx, dx_out)
    stores.start(dbcdt, dbcdt_out)

    pick_row = lax.broadcasted_iota(jnp.int32, (2 * own_cols, 2 * LANES), 0)
    pick_col = lax.broadcasted_iota(jnp.int32, (2 * own_cols, 2 * LANES), 1)

    def columns_of(place):
        wanted = jnp.where(pick_row < own_cols, pick_row, pick_row - own_cols + LANES) + place * own_cols
        pick = (pick_col == wanted).astype(F32).astype(BF16)
        return dot(pick, dbcdt[:, : 2 * LANES], CONTRACT_LAST)

    copies = []
    for n, peer in enumerate((side, up, far)):
        bc_in[n] = columns_of(peer).astype(BF16)
        copies.append(send(bc_in.at[n], bc_in.at[3 + n], bc_sems.at[0, n], bc_sems.at[1, n], {"tp": peer}))
        copies[-1].start()
    own_bc = columns_of(me)
    dx_t[width:, :] = jnp.zeros((LANES, total), BF16)
    dx_t[width + 2 * own_cols : width + 2 * own_cols + heads, :] = dbcdt[:, 2 * LANES :].astype(F32).T[:heads, :].astype(
        BF16
    )
    load_u.wait()

    def x_product(chunk):
        product_chunk(dx_t, u, chunk, gl.at[chunk, :width], width // 2)

    def bc_product(chunk):
        columns = pl.ds(pl.multiple_of(chunk * gl.shape[2], gl.shape[2]), gl.shape[2])
        gl[chunk, width:, :] = dot(dx_t[width:, :], u[:, columns]).astype(BF16)

    def their_x(z_chunk, carry):
        x_product(cores.theirs(z_chunk))
        return carry

    def their_bc(z_chunk, carry):
        bc_product(cores.theirs(z_chunk))
        cores.swap(z_chunk)
        return carry

    def ours(z_chunk, carry):
        x_product(cores.ours(z_chunk))
        bc_product(cores.ours(z_chunk))
        return carry

    lax.fori_loop(0, line.count, their_x, 0)
    for copy in copies:
        copy.wait()
    for n in range(3):
        own_bc = own_bc + bc_in[3 + n].astype(F32)
    dx_t[width : width + 2 * own_cols, :] = own_bc.astype(BF16)
    lax.fori_loop(0, line.count, their_bc, 0)
    lax.fori_loop(0, line.count, ours, 0)
    for z_chunk in range(line.count):
        cores.merge(z_chunk)
        stores.start(gl.at[cores.ours(z_chunk)], gl_out.at[z_chunk])
    sum_ref = line.finish()

    gw_z[...] = sum_ref[...]
    line.end()
    for copy in stores.started:
        copy.wait()


def third_part(own_cols, heads, zx, bcdt, pos, prm, head_prm, expand, mixed, states, dy, pre, u, gz):
    total, width = mixed.shape
    model = u.shape[1]
    dp_count = lax.axis_size("dp")
    cut = model // dp_count
    vmem = pl.BlockSpec(memory_space=pltpu.VMEM)
    anywhere = pl.BlockSpec(memory_space=pl.ANY)
    return pl.pallas_call(
        functools.partial(third_kernel, own_cols, heads),
        out_shape=(
            jax.ShapeDtypeStruct(gz.shape[1:], BF16),
            jax.ShapeDtypeStruct((total, width), BF16),
            jax.ShapeDtypeStruct((total, 3 * LANES), BF16),
            jax.ShapeDtypeStruct((dp_count // 2, width + LANES, cut), BF16),
            jax.ShapeDtypeStruct((8, width + 2 * LANES), F32),
        ),
        in_specs=[anywhere] * 2 + [vmem] * 4 + [anywhere] * 6,
        out_specs=(vmem, anywhere, anywhere, anywhere, vmem),
        scratch_shapes=[
            pltpu.VMEM((total, width), BF16),
            pltpu.VMEM(bcdt.shape, BF16),
            pltpu.VMEM((total, width), F32),
            pltpu.VMEM(states.shape, BF16),
            pltpu.VMEM((total, width), BF16),
            pltpu.VMEM((total, width + 2 * LANES), F32),
            pltpu.VMEM((total, model), BF16),
            pltpu.VMEM((total, width), BF16),
            pltpu.VMEM((total, 3 * LANES), BF16),
            pltpu.VMEM((width + LANES, total), BF16),
            pltpu.VMEM((dp_count, width + LANES, cut), BF16),
            pltpu.VMEM((6, 2 * own_cols, total), BF16),
            pltpu.VMEM((LANES, width), F32),
            pltpu.VMEM((CHUNK + 8, width + 2 * LANES), F32),
            pltpu.VMEM((CHUNK + 8, LANES), jnp.int32),
        ]
        + pair_scratch(dp_count, (width + LANES, cut))
        + [pltpu.VMEM(gz.shape, BF16)]
        + line_scratch(dp_count, gz.shape[1:])
        + [pltpu.SemaphoreType.DMA((2, 3)), pltpu.SemaphoreType.DMA((14,)), pltpu.SemaphoreType.DMA((2 + dp_count // 2,))],
        compiler_params=pltpu.CompilerParams(
            collective_id=2, has_side_effects=True, vmem_limit_bytes=60 * 1024 * 1024
        ),
    )(zx, bcdt, pos, prm, head_prm, expand, mixed, states, dy, pre, u, gz)


def fourth_kernel(
    heads, x_ref, d_own_ref, gain_ref, small_ref, gain_sum_ref, expand_ref, dz_ref, dx_ref, dbcdt_ref, wz_ref, wx_ref,
    wbc_ref, u_ref, gl_ref,
    gw_x, grad_x, sums,
    dz, dx, dbcdt, wz, wx, wbc, u, own, gain_part, packed, over_z, parts,
    right, left, right_sems, left_sems,
    away, to_side, to_up, in_far, in_side, in_up, plane_sems, z_sems, tp_sems, load_sems,
):
    rows, model = x_ref.shape
    width = dz.shape[1]
    me, side, up, far = tp_places()
    dp_count = 2 * parts.shape[0]
    loads = Copies(load_sems)
    weights = [loads.start(wz_ref, wz), loads.start(wx_ref, wx), loads.start(wbc_ref, wbc)]
    loads_of = {}

    def load_block(name, place):
        piece = pl.ds(pl.multiple_of(place * rows, rows), rows)
        loads_of[name] = [
            loads.start(source.at[piece], target.at[piece])
            for source, target in ((dz_ref, dz), (dx_ref, dx), (dbcdt_ref, dbcdt), (u_ref, u))
        ]

    load_block("far", far)
    load_parts = loads.start(gl_ref, parts)
    line = LineSum(parts, lambda z: z, right, left, right_sems, left_sems)
    plane = PlaneSum(away, to_side, to_up, in_far, in_side, in_up, plane_sems)
    partner = {"dp": line.dp + 1 - 2 * lax.rem(line.dp, 2)}
    others = [{"dp": lax.rem(line.dp + 2 * n, dp_count)} for n in range(1, dp_count // 2)]
    greet([{"tp": side}, {"tp": up}, {"tp": far}, partner] + others)
    load_parts.wait()
    line.lead(*range(1, line.count - 1))
    for name, place in (("side", side), ("up", up), ("me", me)):
        load_block(name, place)
    gain_part[...] = jnp.zeros_like(gain_part)

    quarter = model // 4

    def du_block(name, place, target, started=None):
        for copy in loads_of[name]:
            copy.wait()
        piece = pl.ds(pl.multiple_of(place * rows, rows), rows)

        def two(m, carry):
            for odd in range(2):
                n = 2 * m + odd
                columns = pl.ds(pl.multiple_of(n * quarter, quarter), quarter)
                du = (
                    dot(dz[piece, :], wz[columns, :], CONTRACT_LAST)
                    + dot(dx[piece, :], wx[columns, :], CONTRACT_LAST)
                    + dot(dbcdt[piece, :], wbc[:, columns])
                )
                if started is None:
                    target[:, columns] = du
                else:
                    target[n] = du.astype(BF16)
                    started(n, odd)
                gain_part[pl.ds(n, 1), :] += jnp.sum(du * u[piece, columns].astype(F32), axis=0, keepdims=True)
            return carry

        lax.fori_loop(0, 2, two, 0)

    for copy in weights:
        copy.wait()
    du_block("far", far, away, plane.start_far)
    du_block("side", side, to_side, functools.partial(plane.start_near, 0))
    line.relay(2, 0)
    du_block("up", up, to_up, functools.partial(plane.start_near, 1))
    line.relay(2, 1)
    du_block("me", me, own)

    wide = width + 2 * LANES
    shift = (
        lax.broadcasted_iota(jnp.int32, (LANES, LANES), 1)
        == lax.broadcasted_iota(jnp.int32, (LANES, LANES), 0) + me * heads
    ).astype(F32)
    shift = jnp.where(lax.broadcasted_iota(jnp.int32, (LANES, LANES), 0) < heads, shift, 0.0)
    skip_rows = two_parts(jnp.broadcast_to(small_ref[6:7, :width], (8, width)))
    expand = expand_ref[:LANES, :]
    per_head = dot(skip_rows[:, :width], expand, CONTRACT_LAST) + dot(skip_rows[:, width:], expand, CONTRACT_LAST)
    tiles = jnp.concatenate([small_ref[:, :LANES], small_ref[:, LANES : 2 * LANES], per_head], axis=0)
    placed = lax.dot_general(
        tiles, shift, (((1,), (0,)), ((), ())), precision=HIGHEST, preferred_element_type=F32
    )
    packed[0, :, :wide] = small_ref[...]
    packed[0, 5:6, :width] = gain_sum_ref[0:1, :]
    packed[0, 6:7, width : width + LANES] = placed[16:17]
    packed[0, 7:8, :LANES] = placed[7:8]
    packed[0, 7:8, LANES : 2 * LANES] = placed[15:16]
    packed[0, :, wide:] = jnp.zeros((8, quarter), F32)
    for n in range(4):
        packed[0, n : n + 1, wide:] = gain_part[n : n + 1, :] / gain_ref[:, n * quarter : (n + 1) * quarter]
    trade = send(packed.at[0], packed.at[1], z_sems.at[0, 0], z_sems.at[1, 0], partner)
    trade.start()
    plane.pass_on()
    trade.wait()
    over_z[0] = packed[0] + packed[1]
    copies = [
        send(over_z.at[0], over_z.at[n], z_sems.at[0, n], z_sems.at[1, n], others[n - 1])
        for n in range(1, dp_count // 2)
    ]
    for copy in copies:
        copy.start()
    line.lead(line.count - 1)
    for step in range(3, line.count):
        line.relay(step, 0)
        line.relay(step, 1)
    for copy in copies:
        copy.wait()
    everything = over_z[0]
    for n in range(1, dp_count // 2):
        everything = everything + over_z[n]
    sums[me] = everything
    copies = [
        send(sums.at[me], sums.at[me], tp_sems.at[0, n], tp_sems.at[1, n], {"tp": peer})
        for n, peer in enumerate((side, up, far))
    ]
    for copy in copies:
        copy.start()
    plane.finish()

    def norm_back(i, carry):
        piece = pl.ds(pl.multiple_of(i * 32, 32), 32)
        x = x_ref[piece, :].astype(F32)
        r_in = lax.rsqrt(jnp.mean(x * x, axis=-1, keepdims=True) + EPSILON)
        du = own[piece, :] + plane.received(piece)
        e_in = du * gain_ref[...]
        back = r_in * r_in * r_in * jnp.mean(e_in * x, axis=-1, keepdims=True)
        grad_x[piece, :] = d_own_ref[piece, :].astype(F32) + r_in * e_in - x * back
        return carry

    lax.fori_loop(0, rows // 32, norm_back, 0)
    for copy in copies:
        copy.wait()
    sum_ref = line.finish()

    gw_x[...] = sum_ref[...]
    line.end()
    plane.end()


def fourth_part(heads, x_in, d_out, gain, small, gain_sum, expand, dz, dx, dbcdt, w_z, w_x, wbc, u, gl):
    rows, model = x_in.shape
    total, width = dz.shape
    dp_count = lax.axis_size("dp")
    cut = model // dp_count
    wide = width + 2 * LANES + model // 4
    vmem = pl.BlockSpec(memory_space=pltpu.VMEM)
    anywhere = pl.BlockSpec(memory_space=pl.ANY)
    return pl.pallas_call(
        functools.partial(fourth_kernel, heads),
        out_shape=(
            jax.ShapeDtypeStruct(gl.shape[1:], BF16),
            jax.ShapeDtypeStruct((rows, model), F32),
            jax.ShapeDtypeStruct((4, 8, wide), F32),
        ),
        in_specs=[vmem] * 6 + [anywhere] * 8,
        out_specs=(vmem,) * 3,
        scratch_shapes=[
            pltpu.VMEM((total, width), BF16),
            pltpu.VMEM((total, width), BF16),
            pltpu.VMEM((total, 3 * LANES), BF16),
            pltpu.VMEM((model, width), BF16),
            pltpu.VMEM((model, width), BF16),
            pltpu.VMEM((3 * LANES, model), BF16),
            pltpu.VMEM((total, model), BF16),
            pltpu.VMEM((rows, model), F32),
            pltpu.VMEM((8, model // 4), F32),
            pltpu.VMEM((2, 8, wide), F32),
            pltpu.VMEM((dp_count // 2, 8, wide), F32),
            pltpu.VMEM(gl.shape, BF16),
        ]
        + line_scratch(dp_count, gl.shape[1:])
        + plane_scratch(rows, model)
        + [
            pltpu.SemaphoreType.DMA((2, dp_count // 2)),
            pltpu.SemaphoreType.DMA((2, 3)),
            pltpu.SemaphoreType.DMA((20,)),
        ],
        compiler_params=pltpu.CompilerParams(
            collective_id=3, has_side_effects=True, vmem_limit_bytes=60 * 1024 * 1024
        ),
    )(x_in, d_out, gain, small, gain_sum, expand, dz, dx, dbcdt, w_z, w_x, wbc, u, gl)


def results_kernel(
    own_cols, heads, block_ref, grad_x_ref, first_ref, z_ref, x_ref, sums_ref,
    block_out, grad_x, gw_z, gw_x, gw_b, gw_c, gw_dt, gw_out, conv_w, conv_b, gate, norm, dt_bias, a_log, skip,
    held_block, held_grad_x, first, z, x, held_z, held_x, held_out, load_sems, sems,
):
    loads, copies = Copies(load_sems), Copies(sems)
    for source, target in ((first_ref, first), (z_ref, z), (x_ref, x), (grad_x_ref, held_grad_x), (block_ref, held_block)):
        loads.start(source, target)
    load_first, load_z, load_x, load_grad_x, load_block = loads.started
    taken = first.shape[0]
    width = gw_z.shape[1]
    count = sums_ref.shape[0]
    inner = gate.shape[1]
    wide = width + 2 * LANES

    def over_tp(rows, columns):
        total = sums_ref[0, rows, columns]
        for n in range(1, count):
            total = total + sums_ref[n, rows, columns]
        return total

    for n in range(count):
        own = slice(n * width, (n + 1) * width)
        conv_w[:, own] = sums_ref[n, 0:4, :width]
        conv_b[:, own] = sums_ref[n, 4:5, :width]
        gate[:, own] = sums_ref[n, 5:6, :width]
    conv_w[:, inner:] = over_tp(slice(0, 4), slice(width, wide))
    conv_b[:, inner:] = over_tp(slice(4, 5), slice(width, wide))
    quarter = norm.shape[1] // 4
    for n in range(4):
        norm[:, n * quarter : (n + 1) * quarter] = over_tp(slice(n, n + 1), slice(wide, None))
    total_heads = dt_bias.shape[1]
    dt_bias[...] = over_tp(slice(7, 8), slice(0, LANES))[:, :total_heads]
    a_log[...] = over_tp(slice(7, 8), slice(LANES, 2 * LANES))[:, :total_heads]
    skip[...] = over_tp(slice(6, 7), slice(width, width + LANES))[:, :total_heads]
    load_grad_x.wait()
    copies.start(held_grad_x, grad_x)
    load_block.wait()
    copies.start(held_block, block_out)

    def turn(source, held, target):
        def one(i, carry):
            piece = pl.ds(pl.multiple_of(i * CHUNK, CHUNK), CHUNK)
            held[:, piece] = source[piece, :].T.astype(F32)
            return carry

        lax.fori_loop(0, width // CHUNK, one, 0)
        copies.start(held, target)

    load_first.wait()
    load_z.wait()
    held_out[:taken, :] = first[...].astype(F32)
    held_out[taken:, :] = z[width:, :].astype(F32)
    copies.start(held_out, gw_out)
    turn(z, held_z, gw_z)
    load_x.wait()
    turn(x, held_x, gw_x)
    gw_b[...] = x[width : width + own_cols, :].astype(F32)
    gw_c[...] = x[width + own_cols : width + 2 * own_cols, :].astype(F32)
    gw_dt[...] = x[width + 2 * own_cols : width + 2 * own_cols + heads, :].astype(F32)
    for copy in copies.started:
        copy.wait()


def results_part(own_cols, heads, block_out, grad_x, first, gw_z, gw_x, sums):
    cut = first.shape[1]
    count = sums.shape[0]
    width = gw_x.shape[0] - LANES
    inner = width * count
    model = grad_x.shape[1]
    vmem = pl.BlockSpec(memory_space=pltpu.VMEM)
    anywhere = pl.BlockSpec(memory_space=pl.ANY)
    shapes = [
        (cut, width),
        (cut, width),
        (own_cols, cut),
        (own_cols, cut),
        (heads, cut),
        (width, cut),
        (4, inner + 2 * LANES),
        (1, inner + 2 * LANES),
        (1, inner),
        (1, model),
        (1, heads * count),
        (1, heads * count),
        (1, heads * count),
    ]
    return pl.pallas_call(
        functools.partial(results_kernel, own_cols, heads),
        out_shape=[
            jax.ShapeDtypeStruct(block_out.shape, BF16),
            jax.ShapeDtypeStruct(grad_x.shape, F32),
        ]
        + [jax.ShapeDtypeStruct(shape, F32) for shape in shapes],
        in_specs=[anywhere] * 5 + [vmem],
        out_specs=[anywhere] * 4 + [vmem] * 3 + [anywhere] + [vmem] * 7,
        scratch_shapes=[pltpu.VMEM(large.shape, large.dtype) for large in (block_out, grad_x, first, gw_z, gw_x)]
        + [pltpu.VMEM((cut, width), F32), pltpu.VMEM((cut, width), F32), pltpu.VMEM((width, cut), F32)]
        + [pltpu.SemaphoreType.DMA((5,)), pltpu.SemaphoreType.DMA((5,))],
        compiler_params=pltpu.CompilerParams(vmem_limit_bytes=60 * 1024 * 1024),
    )(block_out, grad_x, first, gw_z, gw_x, sums)


def in_norm_scale(values):
    return lax.rsqrt(jnp.mean(values * values, axis=-1, keepdims=True) + EPSILON)


def body(
    x_in, norm_gain, w_z, w_x, w_b, w_c, w_dt, conv_w, conv_b, dt_bias, a_log, d_skip, gate_gain, w_out,
    doc_lens, d_out,
):
    tp_count = lax.axis_size("tp")
    in_planes = tp_count == 4 and lax.axis_size("dp") == 8
    rank = lax.axis_index("tp")
    dev_rows, model = x_in.shape
    rows = dev_rows * tp_count
    inner = gate_gain.shape[0]
    width = w_z.shape[1]
    heads = w_dt.shape[1]
    state_size = (conv_w.shape[0] - inner) // 2
    head_size = width // heads
    own_cols = w_b.shape[1]

    x_float = x_in.astype(F32)
    r_in = in_norm_scale(x_float)
    small_weights = jnp.concatenate([w_b, w_c, w_dt], axis=1).T
    if in_planes:
        lanes = jnp.zeros((LANES - d_skip.shape[0],), F32)
        flat = jnp.concatenate([conv_b, gate_gain, dt_bias, lanes, a_log, lanes, d_skip, lanes])[None, :]
        (
            gathered, zx, bcdt, w_bcdt, mixed, g, yo, yo_t, states, grad_gathered, dyo, coef, pos, prm, head_prm, expand,
            pre, cross,
        ) = first_part(
            inner, heads, own_cols, x_in, norm_gain[None, :], small_weights, conv_w.T, flat, doc_lens, w_z, w_x, w_out,
            d_out,
        )
        gain_own = prm[5, :width]
    else:
        normed = (x_float * r_in * norm_gain[None, :]).astype(BF16)
        gathered = lax.all_gather(normed, "tp", axis=0, tiled=True)
        w_bc = lax.all_gather(small_weights[: 2 * own_cols], "tp", axis=0).reshape(tp_count, 2, own_cols, model)
        w_bcdt = jnp.concatenate(
            [
                jnp.swapaxes(w_bc, 0, 1).reshape(2 * state_size, model),
                small_weights[2 * own_cols :],
                jnp.zeros((LANES - heads, model), BF16),
            ],
            axis=0,
        )
        zx = dot(gathered, jnp.concatenate([w_z, w_x], axis=1)).astype(BF16)
        bcdt = dot(gathered, w_bcdt, CONTRACT_LAST).astype(BF16)
        lengths = doc_lens[0]
        doc_starts = jnp.cumsum(lengths) - lengths
        positions = jnp.arange(rows, dtype=jnp.int32)
        started = jnp.where(positions[:, None] >= doc_starts[None, :], doc_starts[None, :], 0)
        pos = (positions - jnp.max(started, axis=1))[:, None]

        def own(array, count):
            return lax.dynamic_slice_in_dim(array, rank * count, count, axis=0)

        taps = jnp.concatenate([own(conv_w[:inner], width), conv_w[inner:]], axis=0).T
        bias = jnp.concatenate([own(conv_b[:inner], width), conv_b[inner:]])
        pad_bc = jnp.zeros((2 * state_size,), F32)
        gain_own = own(gate_gain, width)
        skip_own = jnp.repeat(own(d_skip, heads), head_size)
        prm = jnp.concatenate(
            [
                taps,
                bias[None],
                jnp.concatenate([gain_own, pad_bc])[None],
                jnp.concatenate([skip_own, pad_bc])[None],
                jnp.zeros((1, width + 2 * state_size), F32),
            ],
            axis=0,
        )
        pad_heads = jnp.zeros((LANES - heads,), F32)
        head_prm = jnp.concatenate(
            [
                jnp.concatenate([own(dt_bias, heads), pad_heads])[None],
                jnp.concatenate([jnp.exp(own(a_log, heads)), pad_heads])[None],
                jnp.zeros((6, LANES), F32),
            ],
            axis=0,
        )
        expand = (
            (jnp.arange(2 * LANES) % LANES)[:, None] == (jnp.arange(width) // head_size)[None, :]
        ).astype(BF16)
        mixed, g, g_sum, states, pre = mixer_forward(width, zx, bcdt, pos, prm, head_prm, expand)
        grad_gathered = lax.all_gather(d_out, "tp", axis=0, tiled=True)
        dyo = dot(grad_gathered, w_out, CONTRACT_LAST).astype(BF16)
        eg_sum = jnp.sum(dyo.astype(F32) * gain_own[None, :] * g, axis=1)
        g_total, eg_total = lax.psum((g_sum[0], eg_sum), "tp")
        r_gate = lax.rsqrt(g_total / inner + EPSILON)
        zeros = jnp.zeros_like(r_gate)
        coef = jnp.stack([r_gate] + [zeros] * 7 + [r_gate**3 * (eg_total / inner)] + [zeros] * (LANES - 9), axis=1)
        yo = (g * r_gate[:, None] * gain_own[None, :]).astype(BF16)

    if in_planes:
        block_out, gw_first, dz, dy, gz, gain_sum = second_part(
            inner, x_in, cross, yo, yo_t, grad_gathered, w_out, dyo, g, mixed, zx, coef, prm, gathered
        )
        gw_z, grad_xs, grad_bcdt, gl, small = third_part(
            own_cols, heads, zx, bcdt, pos, prm, head_prm, expand, mixed, states, dy, pre, gathered, gz
        )
        gw_x, grad_x, sums = fourth_part(
            heads, x_in, d_out, norm_gain[None, :], small, gain_sum, expand, dz, grad_xs, grad_bcdt, w_z, w_x, w_bcdt,
            gathered, gl
        )
        (
            block_out, grad_x, gw_z, gw_x, gw_b, gw_c, gw_dt, gw_out, g_conv_w, g_conv_b, g_gate, g_norm, g_dt_bias,
            g_a_log, g_skip
        ) = results_part(
            own_cols, heads, block_out, grad_x, gw_first, gw_z, gw_x, sums
        )
        return (
            block_out, grad_x, g_norm[0], gw_z, gw_x, gw_b.T, gw_c.T, gw_dt.T, g_conv_w.T, g_conv_b[0], g_dt_bias[0],
            g_a_log[0], g_skip[0], g_gate[0], gw_out
        )
    else:

        def scatter_dp(partial):
            return lax.psum_scatter(partial.astype(BF16), "dp", scatter_dimension=0, tiled=True).astype(F32)

        def scatter_tp(array):
            return lax.psum_scatter(array.astype(BF16), "tp", scatter_dimension=0, tiled=True).astype(F32)

        grad_w_out = scatter_dp(dot(grad_gathered, yo, CONTRACT_FIRST)).T
        z = zx[:, :width].astype(F32)
        sig_z = jax.nn.sigmoid(z)
        dg = coef[:, 0:1] * (dyo.astype(F32) * gain_own[None, :]) - g * coef[:, 8:9]
        dz = (dg * mixed * (sig_z * (1.0 + z * (1.0 - sig_z)))).astype(BF16)
        dy = (dg * (z * sig_z)).astype(BF16)
        gain_sum = jnp.sum(dyo.astype(F32) * g * coef[:, 0:1], axis=0)
        grad_w_z = scatter_dp(dot(gathered, dz, CONTRACT_FIRST))
        block_out = (x_float + scatter_tp(dot(yo, w_out))).astype(BF16)
        grad_xs, grad_bcdt, small = mixer_backward(
            width, pre, zx, bcdt, pos, prm, head_prm, expand, mixed, states, dy
        )
        small = small.at[5, :width].set(gain_sum)
        d_bc = grad_bcdt[:, : 2 * state_size]
        by_owner = jnp.moveaxis(d_bc.reshape(rows, 2, tp_count, own_cols), 2, 0)
        by_owner = by_owner.reshape(tp_count, rows, 2 * own_cols)
        d_bc_own = lax.psum_scatter(by_owner.astype(F32), "tp", scatter_dimension=0, tiled=False)
        d_rest = jnp.concatenate(
            [
                d_bc_own.astype(BF16),
                grad_bcdt[:, 2 * state_size : 2 * state_size + heads],
                jnp.zeros((rows, (-2 * own_cols - heads) % LANES), BF16),
            ],
            axis=1,
        )
        grad_w_x = scatter_dp(dot(gathered, grad_xs, CONTRACT_FIRST))
        grad_rest = scatter_dp(dot(gathered, d_rest, CONTRACT_FIRST))
        du_part = (
            dot(dz, w_z, CONTRACT_LAST) + dot(grad_xs, w_x, CONTRACT_LAST) + dot(grad_bcdt, w_bcdt)
        )
        gain_part = jnp.sum(du_part * gathered.astype(F32), axis=0) / norm_gain
        du = scatter_tp(du_part)
        e_in = du * norm_gain[None, :]
        grad_x = d_out.astype(F32) + r_in * e_in - x_float * (
            r_in**3 * jnp.mean(e_in * x_float, axis=-1, keepdims=True)
        )
        sums = lax.all_gather(lax.psum(small, "dp"), "tp")
        grad_norm_gain = lax.psum(gain_part, ("dp", "tp"))

    channels = jnp.swapaxes(sums[:, :7, :width], 0, 1).reshape(7, inner)
    shared = jnp.sum(sums[:, :5, width : width + 2 * state_size], axis=0)
    grad_conv = jnp.concatenate([channels[:5], shared], axis=1)
    return (
        block_out,
        grad_x,
        grad_norm_gain,
        grad_w_z,
        grad_w_x,
        grad_rest[:, :own_cols],
        grad_rest[:, own_cols : 2 * own_cols],
        grad_rest[:, 2 * own_cols : 2 * own_cols + heads],
        grad_conv[:4].T,
        grad_conv[4],
        sums[:, 7, :heads].reshape(-1),
        sums[:, 7, LANES : LANES + heads].reshape(-1),
        channels[6].reshape(heads * tp_count, head_size).sum(axis=1),
        channels[5],
        grad_w_out,
    )


def solution(mesh):
    rows = P(("dp", "tp"), None)
    columns = P(None, "tp")
    both = P("dp", "tp")
    none = P()
    return jax.shard_map(
        body,
        mesh=mesh,
        in_specs=(
            rows, none, columns, columns, columns, columns, columns, none, none, none, none, none, none,
            P("tp", None), P("dp", None), rows,
        ),
        out_specs=(
            rows, rows, none, both, both, both, both, both, none, none, none, none, none, none, P("tp", "dp"),
        ),
        check_vma=False,
    )
```

```python
import functools

import jax
import jax.numpy as jnp
from jax import lax
from jax.experimental import pallas as pl
from jax.experimental.pallas import tpu as pltpu
from jax.sharding import PartitionSpec as P

EPSILON = 1e-05
HIGHEST = lax.Precision.HIGHEST
F32 = jnp.float32
BF16 = jnp.bfloat16
CHUNK = 128
LANES = 128
CONTRACT_FIRST = (((0,), (0,)), ((), ()))
CONTRACT_LAST = (((1,), (1,)), ((), ()))


def dot(a, b, dims=(((1,), (0,)), ((), ()))):
    return lax.dot_general(a, b, dims, preferred_element_type=F32)


def two_parts(v):
    high = v.astype(BF16)
    return jnp.concatenate([high, (v - high.astype(F32)).astype(BF16)], axis=1)


def convolve(width, x, bc, pos, prm_ref, ext):
    ext[8:, :width] = x.astype(F32)
    ext[8:, width:] = bc.astype(F32)
    pre = prm_ref[3:4, :] * ext[8:, :] + prm_ref[4:5, :]
    for back in (1, 2, 3):
        here = (pos >= back).astype(F32)
        pre = pre + prm_ref[3 - back : 4 - back, :] * (ext[8 - back : 8 - back + CHUNK, :] * here)
    return pre


def prepare_chunk(width, pre, raw_dt, pos, head_ref, expand_ref):
    rows = CHUNK
    sig = jax.nn.sigmoid(pre)
    act = pre * sig
    xc = act[:, :width]
    state_size = (act.shape[1] - width) // 2
    b_rows = act[:, width : width + state_size].astype(BF16)
    c_rows = act[:, width + state_size :].astype(BF16)
    raw = raw_dt.astype(F32) + head_ref[0:1, :]
    dt = jnp.maximum(raw, 0.0) + jnp.log1p(jnp.exp(-jnp.abs(raw)))
    log_decay = -dt * head_ref[1:2, :]
    t_idx = lax.broadcasted_iota(jnp.int32, (rows, rows), 0)
    s_idx = lax.broadcasted_iota(jnp.int32, (rows, rows), 1)
    lower = (s_idx <= t_idx).astype(F32)
    cum = lax.dot_general(
        lower, log_decay, (((1,), (0,)), ((), ())), precision=HIGHEST, preferred_element_type=F32
    )
    same = (s_idx <= t_idx) & (s_idx >= t_idx - pos)
    scores = jnp.where(same, dot(c_rows, b_rows, CONTRACT_LAST), 0.0)
    t_col = lax.broadcasted_iota(jnp.int32, (rows, 1), 0)
    pos_last = pos[rows - 1 : rows, :]
    cum_last = cum[rows - 1 : rows, :]
    inward = jnp.exp(cum) * (pos > t_col).astype(F32)
    tail = jnp.exp(cum_last - cum) * (t_col >= rows - 1 - pos_last).astype(F32)
    carried = jnp.exp(cum_last) * (pos_last >= rows).astype(F32)
    wide = dot(
        two_parts(jnp.concatenate([dt, inward, tail, jnp.broadcast_to(carried, (8, LANES))], axis=0)),
        expand_ref[...],
    )
    return dict(
        sig=sig,
        xc=xc,
        b=b_rows,
        c=c_rows,
        raw=raw,
        log_decay=log_decay,
        cum=cum,
        cum_t=cum.T,
        same=same,
        scores=scores,
        t_idx=t_idx,
        s_idx=s_idx,
        dt_w=wide[:rows],
        in_w=wide[rows : 2 * rows],
        tail_w=wide[2 * rows : 3 * rows],
        carried_w=wide[3 * rows : 3 * rows + 1],
    )


def decay_of(k, head):
    return jnp.exp(jnp.minimum(k["cum"][:, head : head + 1] - k["cum_t"][head : head + 1, :], 0.0))


def halves(pair):
    lane = lax.broadcasted_iota(jnp.int32, pair.shape, 1)
    zero = jnp.zeros_like(pair)
    return jnp.concatenate(
        [jnp.where(lane < LANES // 2, pair, zero), jnp.where(lane < LANES // 2, zero, pair)], axis=0
    )


def forward_chunk(
    width, at, zx_ref, bcdt_ref, pos_ref, prm_ref, head_ref, expand_ref, mixed_ref, g_ref, sum_ref, state_ref,
    pre_ref, ext, state,
):
    if isinstance(at, int):
        rows = slice(at * CHUNK, (at + 1) * CHUNK)
    else:
        rows = pl.ds(pl.multiple_of(at * CHUNK, CHUNK), CHUNK)
    ext[:8, :] = ext[CHUNK:, :]
    pos = pos_ref[rows, :]
    pre = convolve(width, zx_ref[rows, width:], bcdt_ref[rows, : 2 * LANES], pos, prm_ref, ext)
    pre_ref[rows, :] = pre
    k = prepare_chunk(width, pre, bcdt_ref[rows, 2 * LANES :], pos, head_ref, expand_ref)
    stepped = (k["xc"] * k["dt_w"]).astype(BF16)
    held = state[...]
    held_low = held.astype(BF16)
    state_ref[at] = held_low
    reached = dot(k["c"], held_low) * k["in_w"] + prm_ref[6:7, :width] * k["xc"]
    weighted = (stepped.astype(F32) * k["tail_w"]).astype(BF16)
    state[...] = k["carried_w"] * held + dot(k["b"], weighted, CONTRACT_FIRST)
    for pair in range(width // LANES):
        lanes = slice(pair * LANES, (pair + 1) * LANES)
        mixing = jnp.concatenate(
            [
                (decay_of(k, 2 * pair) * k["scores"]).astype(BF16),
                (decay_of(k, 2 * pair + 1) * k["scores"]).astype(BF16),
            ],
            axis=1,
        )
        mixed_ref[rows, lanes] = dot(mixing, halves(stepped[:, lanes])) + reached[:, lanes]
    z = zx_ref[rows, :width].astype(F32)
    g = mixed_ref[rows, :] * (z * jax.nn.sigmoid(z))
    g_ref[rows, :] = g
    total = jnp.sum(g * g, axis=1, keepdims=True)
    sum_ref[:, rows] = jnp.broadcast_to(total, (CHUNK, LANES)).T[:8, :]


def forward_kernel(
    width, zx_ref, bcdt_ref, pos_ref, prm_ref, head_ref, expand_ref, mixed_ref, g_ref, sum_ref, state_ref,
    pre_ref, ext, state,
):
    @pl.when(pl.program_id(0) == 0)
    def _():
        state[...] = jnp.zeros_like(state)
        ext[...] = jnp.zeros_like(ext)

    forward_chunk(
        width, 0, zx_ref, bcdt_ref, pos_ref, prm_ref, head_ref, expand_ref, mixed_ref, g_ref, sum_ref, state_ref,
        pre_ref, ext, state,
    )


def backward_chunk(
    width, tokens, held, pre_ref, x_ref, bcdt_ref, pos_ref, prm_ref, head_ref, expand_ref, mixed_ref,
    dy_ref, grad_x_ref, grad_bcdt_ref, grad_t_ref, small_ref, d_state, later, later_pos,
):
    rows = CHUNK
    pos = pos_ref[tokens, :]
    pre = pre_ref[tokens, :]
    k = prepare_chunk(width, pre, bcdt_ref[tokens, 2 * LANES :], pos, head_ref, expand_ref)
    xc = k["xc"]
    skip = prm_ref[6:7, :width]
    y = mixed_ref[tokens, :] - skip * xc
    dy_low = dy_ref[tokens, :]
    dy = dy_low.astype(F32)
    small_ref[6:7, :width] += jnp.sum(dy * xc, axis=0, keepdims=True)

    stepped = (xc * k["dt_w"]).astype(BF16)
    d_held = d_state[...]
    d_held_low = d_held.astype(BF16)
    held_low = held
    weighted = (stepped.astype(F32) * k["tail_w"]).astype(BF16)
    dy_in = (dy * k["in_w"]).astype(BF16)
    from_state = dot(k["b"], d_held_low) * k["tail_w"]
    dc = dot(dy_in, held_low, CONTRACT_LAST)
    db = dot(weighted, d_held_low, CONTRACT_LAST)
    d_state[...] = k["carried_w"] * d_held + dot(k["c"], dy_in, CONTRACT_FIRST)
    d_scores = jnp.zeros((rows, rows), F32)
    d_stepped = []
    for pair in range(width // LANES):
        lanes = slice(pair * LANES, (pair + 1) * LANES)
        decay_a = decay_of(k, 2 * pair)
        decay_b = decay_of(k, 2 * pair + 1)
        mixing = jnp.concatenate(
            [(decay_a * k["scores"]).astype(BF16), (decay_b * k["scores"]).astype(BF16)], axis=0
        )
        d_mixing = dot(dy_low[:, lanes], halves(stepped[:, lanes]), CONTRACT_LAST)
        d_scores = d_scores + decay_a * d_mixing[:, :rows] + decay_b * d_mixing[:, rows:]
        d_stepped.append(dot(mixing, halves(dy_low[:, lanes]), CONTRACT_FIRST))
    d_stepped = jnp.concatenate(d_stepped, axis=1) + from_state
    d_scores = jnp.where(k["same"], d_scores, 0.0).astype(BF16)
    dc = dc + dot(d_scores, k["b"])
    db = db + dot(d_scores, k["c"], CONTRACT_FIRST)
    dxc = skip * dy + d_stepped * k["dt_w"]

    stepped_f = stepped.astype(F32)
    tail_term = jnp.sum(stepped_f * from_state, axis=0, keepdims=True) + k["carried_w"] * jnp.sum(
        held_low.astype(F32) * d_held, axis=0, keepdims=True
    )
    gathered = two_parts(
        jnp.concatenate([dy * y - stepped_f * d_stepped, jnp.broadcast_to(tail_term, (8, width))], axis=0)
    )
    expand = expand_ref[:LANES, :]
    narrow = dot(gathered[:, :width], expand, CONTRACT_LAST) + dot(gathered[:, width:], expand, CONTRACT_LAST)
    d_cum = narrow[:rows]
    d_dt = dot((d_stepped * xc).astype(BF16), expand, CONTRACT_LAST)
    upper = (k["s_idx"] >= k["t_idx"]).astype(F32)
    d_decay = (
        lax.dot_general(
            upper, d_cum, (((1,), (0,)), ((), ())), precision=HIGHEST, preferred_element_type=F32
        )
        + narrow[rows : rows + 1]
    )
    d_raw = (d_dt - d_decay * head_ref[1:2, :]) * jax.nn.sigmoid(k["raw"])
    small_ref[7:8, :LANES] += jnp.sum(d_raw, axis=0, keepdims=True)
    small_ref[7:8, LANES : 2 * LANES] += jnp.sum(d_decay * k["log_decay"], axis=0, keepdims=True)
    grad_bcdt_ref[tokens, 2 * LANES :] = d_raw.astype(BF16)

    sig = k["sig"]
    d_pre = jnp.concatenate([dxc, db, dc], axis=1) * (sig * (1.0 + pre * (1.0 - sig)))
    small_ref[4:5, :] += jnp.sum(d_pre, axis=0, keepdims=True)
    later[:rows, :] = d_pre
    later_pos[:rows, :] = jnp.broadcast_to(pos, (rows, LANES))
    x_own = jnp.concatenate([x_ref[tokens, :], bcdt_ref[tokens, : 2 * LANES]], axis=1).astype(F32)
    d_in = prm_ref[3:4, :] * d_pre
    small_ref[3:4, :] += jnp.sum(d_pre * x_own, axis=0, keepdims=True)
    for back in (1, 2, 3):
        there = (later_pos[back : back + rows, :] >= back).astype(F32)
        reaching = later[back : back + rows, :] * jnp.concatenate([there] * (later.shape[1] // LANES), axis=1)
        small_ref[3 - back : 4 - back, :] += jnp.sum(reaching * x_own, axis=0, keepdims=True)
        d_in = d_in + prm_ref[3 - back : 4 - back, :] * reaching
    grad_x_ref[tokens, :] = d_in[:, :width].astype(BF16)
    grad_bcdt_ref[tokens, : 2 * LANES] = d_in[:, width:].astype(BF16)
    later[rows:, :] = later[:8, :]
    later_pos[rows:, :] = later_pos[:8, :]
    if grad_t_ref is not None:
        grad_t_ref[:width, tokens] = d_in[:, :width].T.astype(BF16)


def backward_start(small_ref, d_state, later, later_pos):
    d_state[...] = jnp.zeros_like(d_state)
    later[...] = jnp.zeros_like(later)
    later_pos[...] = jnp.zeros_like(later_pos)
    small_ref[...] = jnp.zeros_like(small_ref)


def backward_kernel(
    width, pre_ref, x_ref, bcdt_ref, pos_ref, prm_ref, head_ref, expand_ref, mixed_ref, state_ref, dy_ref, grad_x_ref,
    grad_bcdt_ref, small_ref, d_state, later, later_pos,
):
    @pl.when(pl.program_id(0) == 0)
    def _():
        backward_start(small_ref, d_state, later, later_pos)

    backward_chunk(
        width, slice(0, CHUNK), state_ref[0], pre_ref, x_ref, bcdt_ref, pos_ref, prm_ref, head_ref, expand_ref, mixed_ref,
        dy_ref, grad_x_ref, grad_bcdt_ref, None, small_ref, d_state, later, later_pos,
    )


def mixer_forward(width, zx, bcdt, pos, prm, head_prm, expand):
    rows = zx.shape[0]
    chunks = rows // CHUNK

    def tokens(columns):
        return pl.BlockSpec((CHUNK, columns), lambda i: (i, 0))

    def whole(array):
        return pl.BlockSpec(array.shape, lambda i: (0, 0))

    return pl.pallas_call(
        functools.partial(forward_kernel, width),
        out_shape=(
            jax.ShapeDtypeStruct((rows, width), F32),
            jax.ShapeDtypeStruct((rows, width), F32),
            jax.ShapeDtypeStruct((8, rows), F32),
            jax.ShapeDtypeStruct((chunks, LANES, width), BF16),
            jax.ShapeDtypeStruct((rows, width + 2 * LANES), F32),
        ),
        grid=(chunks,),
        in_specs=[tokens(2 * width), tokens(3 * LANES), tokens(1), whole(prm), whole(head_prm), whole(expand)],
        out_specs=(
            tokens(width),
            tokens(width),
            pl.BlockSpec((8, CHUNK), lambda i: (0, i)),
            pl.BlockSpec((1, LANES, width), lambda i: (i, 0, 0)),
            tokens(width + 2 * LANES),
        ),
        scratch_shapes=[
            pltpu.VMEM((CHUNK + 8, width + 2 * LANES), F32),
            pltpu.VMEM((LANES, width), F32),
        ],
        compiler_params=pltpu.CompilerParams(
            dimension_semantics=("arbitrary",), vmem_limit_bytes=40 * 1024 * 1024
        ),
    )(zx, bcdt, pos, prm, head_prm, expand)


def mixer_backward(width, pre, zx, bcdt, pos, prm, head_prm, expand, mixed, states, dy):
    rows = zx.shape[0]
    chunks = rows // CHUNK

    def tokens(columns):
        return pl.BlockSpec((CHUNK, columns), lambda i: (chunks - 1 - i, 0))

    def whole(array):
        return pl.BlockSpec(array.shape, lambda i: (0, 0))

    return pl.pallas_call(
        functools.partial(backward_kernel, width),
        out_shape=(
            jax.ShapeDtypeStruct((rows, width), BF16),
            jax.ShapeDtypeStruct((rows, 3 * LANES), BF16),
            jax.ShapeDtypeStruct((8, width + 2 * LANES), F32),
        ),
        grid=(chunks,),
        in_specs=[
            tokens(width + 2 * LANES),
            pl.BlockSpec((CHUNK, width), lambda i: (chunks - 1 - i, 1)),
            tokens(3 * LANES),
            tokens(1),
            whole(prm),
            whole(head_prm),
            whole(expand),
            tokens(width),
            pl.BlockSpec((1, LANES, width), lambda i: (chunks - 1 - i, 0, 0)),
            tokens(width),
        ],
        out_specs=(
            tokens(width),
            tokens(3 * LANES),
            pl.BlockSpec((8, width + 2 * LANES), lambda i: (0, 0)),
        ),
        scratch_shapes=[
            pltpu.VMEM((LANES, width), F32),
            pltpu.VMEM((CHUNK + 8, width + 2 * LANES), F32),
            pltpu.VMEM((CHUNK + 8, LANES), jnp.int32),
        ],
        compiler_params=pltpu.CompilerParams(
            dimension_semantics=("arbitrary",), vmem_limit_bytes=48 * 1024 * 1024
        ),
        cost_estimate=pl.CostEstimate(flops=rows * width * 2048, bytes_accessed=rows * width * 20, transcendentals=0),
    )(pre, zx, bcdt, pos, prm, head_prm, expand, mixed, states, dy)


MESH = pl.DeviceIdType.MESH


def tp_places():
    me = lax.axis_index("tp")
    return me, me + 1 - 2 * lax.rem(me, 2), lax.rem(me + 2, 4), 3 - me


def greet(peers):
    barrier = pltpu.get_barrier_semaphore()
    for peer in peers:
        pl.semaphore_signal(barrier, inc=1, device_id=peer, device_id_type=MESH)
    pl.semaphore_wait(barrier, len(peers))


def send(src, dst, send_sem, recv_sem, peer):
    return pltpu.make_async_remote_copy(
        src_ref=src, dst_ref=dst, send_sem=send_sem, recv_sem=recv_sem, device_id=peer, device_id_type=MESH
    )


class Gather:
    def __init__(self, whole, rows, send_sems, recv_sems, own=None):
        me, side, up, _ = tp_places()
        half = rows // 2

        def part(place, which):
            return whole.at[pl.ds(pl.multiple_of(place * rows + which * half, half), half)]

        def one(n, place, which, peer):
            return send(part(place, which), part(place, which), send_sems.at[n], recv_sems.at[n], {"tp": peer})

        def quarter(n, which, late, peer):
            start = pl.multiple_of(me * rows + which * half + late * (half // 2), half // 2)
            piece = whole.at[pl.ds(start, half // 2)]
            return send(piece, piece, send_sems.at[n], recv_sems.at[n], {"tp": peer})

        self.side_first, self.up_first = one(0, me, 0, side), one(1, me, 1, up)
        self.side_then = [quarter(2, 1, 0, side), quarter(3, 1, 1, side)]
        self.up_then = [quarter(4, 0, 0, up), quarter(5, 0, 1, up)]
        self.pass_up, self.pass_side = one(6, side, 0, up), one(7, up, 1, side)

    def start(self):
        for copy in (self.side_first, self.up_first, self.side_then[0], self.up_then[0]):
            copy.start()

    def start_rest(self):
        self.side_then[1].start()
        self.up_then[1].start()

    def forward(self):
        self.side_first.wait_recv()
        self.pass_up.start()
        self.up_first.wait_recv()
        self.pass_side.start()

    def neighbours(self):
        for copy in self.side_then + self.up_then:
            copy.wait_recv()

    def finish(self):
        self.pass_up.wait_recv()
        self.pass_side.wait_recv()

    def end(self):
        for copy in [self.side_first, self.up_first, self.pass_up, self.pass_side] + self.side_then + self.up_then:
            copy.wait_send()


def set_up(width, heads, inner, taps_ref, flat_ref, lens_ref, prm, head, expand, pos):
    rank = lax.axis_index("tp")
    channels = taps_ref.shape[1]
    own = pl.ds(pl.multiple_of(rank * width, LANES), width)
    own_gain = pl.ds(pl.multiple_of(channels + rank * width, LANES), width)
    prm[...] = jnp.zeros_like(prm)
    prm[0:4, :width] = taps_ref[:, own]
    prm[0:4, width:] = taps_ref[:, inner:]
    prm[4:5, :width] = flat_ref[:, own]
    prm[4:5, width:] = flat_ref[:, inner:channels]
    prm[5:6, :width] = flat_ref[:, own_gain]
    lane = lax.broadcasted_iota(jnp.int32, (LANES, LANES), 1)
    pick = ((lax.broadcasted_iota(jnp.int32, (LANES, LANES), 0) == lane + rank * heads) & (lane < heads)).astype(F32)
    start = channels + inner
    tiles = [jnp.broadcast_to(flat_ref[:, start + n * LANES : start + (n + 1) * LANES], (8, LANES)) for n in range(3)]
    tiles[1] = jnp.exp(tiles[1])
    picked = lax.dot_general(
        jnp.concatenate(tiles, axis=0), pick, (((1,), (0,)), ((), ())), precision=HIGHEST, preferred_element_type=F32
    )
    head[...] = jnp.concatenate([picked[0:1], picked[8:9], jnp.zeros((6, LANES), F32)], axis=0)
    row = lax.broadcasted_iota(jnp.int32, (2 * LANES, width), 0)
    column = lax.broadcasted_iota(jnp.int32, (2 * LANES, width), 1)
    expand[...] = (lax.rem(row, LANES) == column // (width // heads)).astype(F32).astype(BF16)
    prm[6:7, :width] = dot(two_parts(picked[16:24]), expand[...])[0:1]
    starts = [jnp.int32(0)]
    for n in range(lens_ref.shape[1] - 1):
        starts.append(starts[-1] + lens_ref[0, n])

    def place(i, carry):
        token = lax.broadcasted_iota(jnp.int32, (CHUNK, 1), 0) + i * CHUNK
        begun = jnp.zeros((CHUNK, 1), jnp.int32)
        for first in starts[1:]:
            begun = jnp.where(token >= first, first, begun)
        pos[pl.ds(pl.multiple_of(i * CHUNK, CHUNK), CHUNK), :] = token - begun
        return carry

    lax.fori_loop(0, pos.shape[0] // CHUNK, place, 0)


def first_kernel(
    inner, heads, own_cols, x_ref, gain_ref, wb_ref, wc_ref, wdt_ref, taps_ref, flat_ref, lens_ref, wz_ref, wx_ref, w_out_ref, d_own_ref,
    u_out, zx_out, bcdt_out, wbc_out, mixed_out, g_out, yo_out, yo_t_out, state_out, d_out, dyo_out, coef_out, pos_out,
    prm_out, head_out, expand_out, pre_out, cross_out, branch_out,
    weights, w_out, u, zx, bcdt, wbc, mixed, g, yo, yo_t, states, d, dyo, coef, pos, prm, head, expand, pre, ext, state, sums,
    acc, sems, sum_sems, load_sems, store_sems,
):
    rows, model = x_ref.shape
    total, width = mixed.shape
    chunks = total // CHUNK
    me, side, up, far = tp_places()
    dp = lax.axis_index("dp")
    parity = lax.rem(dp, 2)
    partner = {"dp": dp + 1 - 2 * parity}

    def block(place):
        return pl.ds(pl.multiple_of(place * rows, rows), rows)

    loads = [
        pltpu.make_async_copy(wz_ref, weights.at[:, :width], load_sems.at[0]),
        pltpu.make_async_copy(wx_ref, weights.at[:, width:], load_sems.at[1]),
        pltpu.make_async_copy(w_out_ref, w_out, load_sems.at[2]),
        pltpu.make_async_copy(d_own_ref, d.at[block(me)], load_sems.at[3]),
    ]
    for copy in loads:
        copy.start()
    stores = []

    def keep(source, target):
        copy = pltpu.make_async_copy(source, target, store_sems.at[len(stores)])
        copy.start()
        stores.append(copy)

    bc_own = pl.ds(pl.multiple_of(parity * LANES, LANES), LANES)
    wbc[pl.ds(pl.multiple_of(parity * LANES + me * own_cols, own_cols), own_cols), :] = jnp.where(
        parity == 0, wb_ref[...], wc_ref[...]
    )
    greet([{"tp": side}, {"tp": up}, {"tp": far}, partner])
    small_gather = Gather(wbc.at[bc_own], own_cols, sems.at[0], sems.at[1])
    small_gather.start()
    small_gather.start_rest()

    def norm(i, carry):
        piece = pl.ds(pl.multiple_of(i * 32, 32), 32)
        x = x_ref[piece, :].astype(F32)
        scale = lax.rsqrt(jnp.mean(x * x, axis=-1, keepdims=True) + EPSILON)
        u[pl.ds(pl.multiple_of(me * rows + i * 32, 32), 32), :] = (x * scale * gain_ref[...]).astype(BF16)
        return carry

    lax.fori_loop(0, rows // 32, norm, 0)
    small_gather.forward()
    gather = Gather(u, rows, sems.at[2], sems.at[3])
    gather.start()
    gather.start_rest()
    wbc[2 * LANES :, :] = jnp.zeros((LANES, model), BF16)
    wbc[2 * LANES : 2 * LANES + heads, :] = wdt_ref[...]
    set_up(width, heads, inner, taps_ref, flat_ref, lens_ref, prm, head, expand, pos)
    keep(pos, pos_out)
    keep(prm, prm_out)
    keep(head, head_out)
    keep(expand, expand_out)
    loads[0].wait()
    loads[1].wait()

    def project(place):
        piece = block(place)

        def tile(n, carry):
            columns = pl.ds(pl.multiple_of(n * 512, 512), 512)
            zx[piece, columns] = dot(u[piece, :], weights[:, columns]).astype(BF16)
            return carry

        lax.fori_loop(0, 2 * width // 512, tile, 0)

    def project_small(place):
        bcdt[block(place), :] = dot(u[block(place), :], wbc[...], CONTRACT_LAST).astype(BF16)

    project(me)
    small_gather.neighbours()
    small_gather.finish()
    trade = send(wbc.at[bc_own], wbc.at[bc_own], sems.at[6, 0], sems.at[6, 1], partner)
    trade.start()
    gather.forward()
    loads[3].wait()
    d_gather = Gather(d, rows, sems.at[4], sems.at[5])
    d_gather.start()
    trade.wait()
    keep(wbc, wbc_out)
    project_small(me)
    gather.neighbours()
    project(side)
    project(up)
    project_small(side)
    project_small(up)
    gather.finish()
    keep(u, u_out)
    project(far)
    project_small(far)
    keep(zx, zx_out)
    keep(bcdt, bcdt_out)

    state[...] = jnp.zeros_like(state)
    ext[...] = jnp.zeros_like(ext)

    def chunk(i, carry):
        forward_chunk(
            width, i, zx, bcdt, pos, prm, head, expand, mixed, g, sums.at[0], states, pre, ext, state
        )
        return carry

    lax.fori_loop(0, chunks, chunk, 0)

    copies = [
        send(sums.at[0], sums.at[2 + n], sum_sems.at[0, n], sum_sems.at[1, n], {"tp": peer})
        for n, peer in enumerate((side, up, far))
    ]
    for copy in copies:
        copy.start()
    d_gather.start_rest()
    keep(mixed, mixed_out)
    keep(g, g_out)
    keep(states, state_out)
    keep(pre, pre_out)
    loads[2].wait()

    def back_to_heads(place):
        piece = block(place)
        acc[...] = jnp.zeros_like(acc)

        def tile(n, carry):
            columns = pl.ds(pl.multiple_of(n * 256, 256), 256)
            low = dot(d[piece, :], w_out[columns, :], CONTRACT_LAST).astype(BF16)
            dyo[piece, columns] = low
            both = low.astype(F32) * prm[5:6, columns] * g[piece, columns]
            acc[...] += both[:, :LANES] + both[:, LANES:]
            return carry

        lax.fori_loop(0, width // 256, tile, 0)
        column = jnp.sum(acc[...], axis=1, keepdims=True)
        sums[1, :, piece] = jnp.broadcast_to(column, (rows, LANES)).T[:8, :]
        keep(dyo.at[piece], dyo_out.at[piece])

    d_gather.forward()
    back_to_heads(me)
    for copy in copies:
        copy.wait()

    def gate(i, carry):
        piece = pl.ds(pl.multiple_of(i * CHUNK, CHUNK), CHUNK)
        squares = sums[0, :, piece] + sums[2, :, piece] + sums[3, :, piece] + sums[4, :, piece]
        scale = lax.rsqrt(squares / inner + EPSILON)
        columns = jnp.concatenate([scale, jnp.zeros((LANES - 8, LANES), F32)], axis=0).T
        coef[piece, :] = columns
        gated = g[piece, :] * columns[:, 0:1] * prm[5:6, :width]
        yo[piece, :] = gated.astype(BF16)
        yo_t[:, piece] = gated.T.astype(BF16)
        return carry

    lax.fori_loop(0, chunks, gate, 0)
    keep(coef, coef_out)
    keep(yo, yo_out)
    keep(yo_t, yo_t_out)
    branch = weights.at[:total, :]

    def out_block(place):
        piece = block(place)

        def tile(n, carry):
            columns = pl.ds(pl.multiple_of(n * 512, 512), 512)
            branch[piece, columns] = dot(yo[piece, :], w_out[:, columns]).astype(BF16)
            return carry

        lax.fori_loop(0, model // 512, tile, 0)
        keep(branch.at[piece], branch_out.at[piece])

    out_block(far)
    out_block(side)
    d_gather.neighbours()
    back_to_heads(side)
    back_to_heads(up)
    out_block(up)
    out_block(me)
    d_gather.finish()
    keep(d, d_out)
    back_to_heads(far)
    keep(sums.at[1], cross_out)
    small_gather.end()
    gather.end()
    d_gather.end()
    for copy in stores:
        copy.wait()


def first_part(inner, heads, own_cols, x_in, gain, w_b, w_c, w_dt, taps, flat, lens, w_z, w_x, w_out, d_out):
    rows, model = x_in.shape
    total = 4 * rows
    width = w_z.shape[1]
    chunks = total // CHUNK
    vmem = pl.BlockSpec(memory_space=pltpu.VMEM)
    anywhere = pl.BlockSpec(memory_space=pl.ANY)
    results = [
        ((total, model), BF16),
        ((total, 2 * width), BF16),
        ((total, 3 * LANES), BF16),
        ((3 * LANES, model), BF16),
        ((total, width), F32),
        ((total, width), F32),
        ((total, width), BF16),
        ((width, total), BF16),
        ((chunks, LANES, width), BF16),
        ((total, model), BF16),
        ((total, width), BF16),
        ((total, LANES), F32),
        ((total, 1), jnp.int32),
        ((8, width + 2 * LANES), F32),
        ((8, LANES), F32),
        ((2 * LANES, width), BF16),
        ((total, width + 2 * LANES), F32),
    ]
    cross = [jax.ShapeDtypeStruct((8, total), F32), jax.ShapeDtypeStruct((total, model), BF16)]
    return pl.pallas_call(
        functools.partial(first_kernel, inner, heads, own_cols),
        out_shape=[jax.ShapeDtypeStruct(*result) for result in results] + cross,
        in_specs=[vmem] * 7 + [pl.BlockSpec(memory_space=pltpu.SMEM)] + [anywhere] * 4,
        out_specs=[anywhere] * (len(results) + 2),
        scratch_shapes=[pltpu.VMEM((model, 2 * width), BF16), pltpu.VMEM((width, model), BF16)]
        + [pltpu.VMEM(*result) for result in results]
        + [
            pltpu.VMEM((CHUNK + 8, width + 2 * LANES), F32),
            pltpu.VMEM((LANES, width), F32),
            pltpu.VMEM((5, 8, total), F32),
            pltpu.VMEM((rows, LANES), F32),
            pltpu.SemaphoreType.DMA((7, 8)),
            pltpu.SemaphoreType.DMA((2, 3)),
            pltpu.SemaphoreType.DMA((4,)),
            pltpu.SemaphoreType.DMA((30,)),
        ],
        compiler_params=pltpu.CompilerParams(
            collective_id=0, has_side_effects=True, vmem_limit_bytes=60 * 1024 * 1024
        ),
    )(x_in, gain, w_b, w_c, w_dt, taps, flat, lens, w_z, w_x, w_out, d_out)


def add_into(target, other):
    rows = target.shape[0]
    tile = max(t for t in range(16, 257, 16) if rows % t == 0)

    def one(i, carry):
        piece = pl.ds(pl.multiple_of(i * tile, tile), tile)
        target[piece, :] = (target[piece, :].astype(F32) + other[piece, :].astype(F32)).astype(BF16)
        return carry

    lax.fori_loop(0, rows // tile, one, 0)


def line_order(count):
    low, high, out = 0, count - 1, []
    while low <= high:
        out += [high, low] if low < high else [low]
        low, high = low + 1, high - 1
    return out


class PairSum:
    def __init__(self, parts, pair, sems):
        dp = lax.axis_index("dp")
        self.parity = lax.rem(dp, 2)
        self.partner = {"dp": dp + 1 - 2 * self.parity}
        self.parts, self.pair, self.sems = parts, pair, sems

    def theirs(self, z):
        return 2 * z + 1 - self.parity

    def ours(self, z):
        return 2 * z + self.parity

    def copy(self, z):
        return send(
            self.parts.at[self.theirs(z)], self.pair.at[z], self.sems.at[0, z], self.sems.at[1, z], self.partner
        )

    def swap(self, z):
        self.copy(z).start()

    def merge(self, z):
        self.copy(z).wait()
        add_into(self.parts.at[self.ours(z)], self.pair.at[z])


class LineSum:
    def __init__(self, parts, at, right, left, right_sems, left_sems):
        dp = lax.axis_index("dp")
        self.dp = dp
        self.count = lax.axis_size("dp") // 2
        self.z = dp // 2
        self.parts, self.at = parts, at
        self.lines = {1: (right, right_sems), -1: (left, left_sems)}

    def peers(self):
        n = 2 * self.count
        return [{"dp": lax.rem(self.dp + 2, n)}, {"dp": lax.rem(self.dp + n - 2, n)}]

    def away(self, way):
        return self.z if way == 1 else self.count - 1 - self.z

    def copies(self, way, step):
        line, line_sems = self.lines[way]
        far = self.count - step + self.away(way)
        z = far if way == 1 else self.count - 1 - far
        chunk = self.parts.at[self.at(z)]
        return lambda piece: self.piece(chunk, line, line_sems, step, piece, {"dp": self.dp + 2 * way})

    def piece(self, chunk, line, line_sems, step, piece, peer):
        half = chunk.shape[0] // 2
        rows = pl.ds(piece * half, half)
        copy = send(
            chunk.at[rows], line.at[step - 1, rows], line_sems.at[0, step - 1, piece], line_sems.at[1, step - 1, piece],
            peer,
        )
        return chunk.at[rows], copy

    def add_arrived(self, way, step, piece, target):
        line, line_sems = self.lines[way]
        chunk = self.parts.at[self.at(self.z)]
        self.piece(chunk, line, line_sems, step, piece, self.peers()[0])[1].wait_recv()
        half = chunk.shape[0] // 2
        add_into(target, line.at[step - 1, pl.ds(piece * half, half)])

    def lead(self, *steps):
        for way in (1, -1):

            @pl.when(self.away(way) == 0)
            def _():
                for step in steps:
                    for piece in range(2):
                        self.copies(way, step)(piece)[1].start()

    def relay(self, step, piece):
        for way in (1, -1):
            away = self.away(way)

            @pl.when((away >= 1) & (away <= min(step - 1, self.count - 2)))
            def _():
                chunk, copy = self.copies(way, step)(piece)
                self.add_arrived(way, step - 1, piece, chunk)
                copy.start()

    def finish(self):
        total = self.parts.at[self.at(self.z)]
        half = total.shape[0] // 2
        for piece in range(2):
            for way in (1, -1):

                @pl.when(self.away(way) >= 1)
                def _():
                    self.add_arrived(way, self.count - 1, piece, total.at[pl.ds(piece * half, half)])

        return total

    def end(self):
        for way in (1, -1):
            away = self.away(way)
            for step in range(1, self.count):

                @pl.when(away <= min(step - 1, self.count - 2))
                def _():
                    for piece in range(2):
                        self.copies(way, step)(piece)[1].wait_send()


class PlaneSum:
    def __init__(self, away, to_side, to_up, in_far, in_side, in_up, sems):
        _, side, up, _ = tp_places()
        peers = ({"tp": side}, {"tp": up})
        self.to, self.in_far, self.into = (to_side, to_up), in_far, (in_side, in_up)

        def one(kind, n, source, target, peer):
            return send(source.at[n], target.at[n], sems.at[0, kind, n], sems.at[1, kind, n], peer)

        self.one, self.peers, self.away = one, peers, away
        self.far = [one(0, n, away, in_far, peers[n % 2]) for n in range(4)]
        self.near = [[one(1 + w, n, self.to[w], self.into[w], peers[w]) for n in range(4)] for w in range(2)]

    def start_far(self, n, odd):
        self.one(0, n, self.away, self.in_far, self.peers[odd]).start()

    def start_near(self, way, n, odd):
        if odd == way:
            self.one(1 + way, n, self.to[way], self.into[way], self.peers[way]).start()

    def pass_on(self):
        for n in range(4):
            way = 1 - n % 2
            self.far[n].wait_recv()
            add_into(self.to[way].at[n], self.in_far.at[n])
            self.near[way][n].start()

    def finish(self):
        for copy in self.near[0] + self.near[1]:
            copy.wait_recv()

    def received(self, piece):
        side, up = (jnp.concatenate([into[n, piece, :] for n in range(4)], axis=1) for into in self.into)
        return side.astype(F32) + up.astype(F32)

    def end(self):
        for copy in self.far + self.near[0] + self.near[1]:
            copy.wait_send()


def plane_scratch(rows, model):
    return [pltpu.VMEM((4, rows, model // 4), BF16) for _ in range(6)] + [pltpu.SemaphoreType.DMA((2, 3, 4))]


def pair_scratch(dp_count, shape):
    return [
        pltpu.VMEM((dp_count // 2,) + shape, BF16),
        pltpu.SemaphoreType.DMA((2, dp_count // 2)),
    ]


def line_scratch(dp_count, shape):
    steps = dp_count // 2 - 1
    return [
        pltpu.VMEM((steps,) + shape, BF16),
        pltpu.VMEM((steps,) + shape, BF16),
        pltpu.SemaphoreType.DMA((2, steps, 2)),
        pltpu.SemaphoreType.DMA((2, steps, 2)),
    ]


class Copies:
    def __init__(self, sems):
        self.sems, self.started = sems, []

    def start(self, source, target):
        copy = pltpu.make_async_copy(source, target, self.sems.at[len(self.started)])
        copy.start()
        self.started.append(copy)
        return copy


def product_chunk(left_t, right, chunk, target, tile):
    columns = pl.ds(pl.multiple_of(chunk * target.shape[1], target.shape[1]), target.shape[1])

    def one(i, carry):
        piece = pl.ds(pl.multiple_of(i * tile, tile), tile)
        target[piece, :] = dot(left_t[piece, :], right[:, columns]).astype(BF16)
        return carry

    lax.fori_loop(0, target.shape[0] // tile, one, 0)


def second_kernel(
    inner, x_ref, cross_ref, branch_ref, yo_t_ref, d_ref, dyo_ref, g_ref, mixed_ref, zx_ref, coef_ref, prm_ref,
    u_ref, block_out, gw_out, dz_out, dy_out, gz_out, gain_out,
    dz, yo_t, d, dyo, g, mixed, z, coef, own, gz, parts, pair, pair_sems, gz_pair, gz_pair_sems,
    right, left, right_sems, left_sems,
    away, to_side, to_up, in_far, in_side, in_up, plane_sems, cross, cross_sems, load_sems, store_sems,
):
    rows, model = x_ref.shape
    total, width = dz.shape
    taken = parts.shape[1]
    me, side, up, far = tp_places()
    loads, stores = Copies(load_sems), Copies(store_sems)
    quarter = model // 4

    def load_block(place, target):
        piece = pl.ds(pl.multiple_of(place * rows, rows), rows)
        return [
            loads.start(branch_ref.at[piece, n * quarter : (n + 1) * quarter], target.at[n]) for n in range(4)
        ]

    load_far = load_block(far, away)
    load_yo_t = loads.start(yo_t_ref, yo_t)
    load_d = loads.start(d_ref, d)
    cores = PairSum(parts, pair, pair_sems)
    gz_cores = PairSum(gz, gz_pair, gz_pair_sems)
    line = LineSum(parts, cores.ours, right, left, right_sems, left_sems)
    plane = PlaneSum(away, to_side, to_up, in_far, in_side, in_up, plane_sems)
    greet([{"tp": side}, {"tp": up}, {"tp": far}, cores.partner] + line.peers())
    crossing = [
        send(cross_ref, cross.at[n], cross_sems.at[0, n], cross_sems.at[1, n], {"tp": peer})
        for n, peer in enumerate((side, up, far))
    ]
    for copy in crossing:
        copy.start()

    for n, copy in enumerate(load_far):
        copy.wait()
        plane.start_far(n, n % 2)
    load_yo_t.wait()
    load_d.wait()
    load_side, load_up = load_block(side, to_side), load_block(up, to_up)
    load_own = loads.start(branch_ref.at[pl.ds(pl.multiple_of(me * rows, rows), rows)], own)
    rest = [
        loads.start(dyo_ref, dyo),
        loads.start(g_ref, g),
        loads.start(mixed_ref, mixed),
        loads.start(zx_ref.at[:, :width], z),
        loads.start(coef_ref, coef),
    ]
    order = line_order(line.count)

    def products(first, step):
        def one(i, carry):
            z_chunk = first + step * i
            product_chunk(yo_t, d, cores.theirs(z_chunk), parts.at[cores.theirs(z_chunk)], taken // 2)
            cores.swap(z_chunk)
            product_chunk(yo_t, d, cores.ours(z_chunk), parts.at[cores.ours(z_chunk)], taken // 2)
            return carry

        lax.fori_loop(0, 2, one, 0)

    products(order[0], order[1] - order[0])
    for z_chunk in order[:2]:
        cores.merge(z_chunk)
    line.lead(1)
    products(order[2], order[3] - order[2])

    def left_over(chunk, carry):
        columns = pl.ds(pl.multiple_of(chunk * parts.shape[2], parts.shape[2]), parts.shape[2])
        gz[chunk, width:, :] = dot(yo_t[taken:, :], d[:, columns]).astype(BF16)
        return carry

    for z_chunk in order[2:]:
        cores.merge(z_chunk)
    line.lead(*range(2, line.count))
    for copy in load_side + load_up:
        copy.wait()
    for n in range(4):
        plane.start_near(n % 2, n, n % 2)
    line.relay(2, 0)
    plane.pass_on()
    lax.fori_loop(0, parts.shape[0], left_over, 0)
    load_u = loads.start(u_ref, d)
    load_own.wait()
    line.relay(2, 1)
    for copy in rest:
        copy.wait()
    for copy in crossing:
        copy.wait()
    gain_out[...] = jnp.zeros_like(gain_out)

    def gate_back(i, carry):
        piece = pl.ds(pl.multiple_of(i * CHUNK, CHUNK), CHUNK)
        crossed = cross_ref[:, piece] + cross[0, :, piece] + cross[1, :, piece] + cross[2, :, piece]
        crossed = jnp.concatenate([crossed, jnp.zeros((LANES - 8, LANES), F32)], axis=0).T[:, 0:1]
        scale = coef[piece, 0:1]
        back = scale * scale * scale * (crossed / inner)
        z_piece = z[piece, :].astype(F32)
        sig = jax.nn.sigmoid(z_piece)
        dyo_piece = dyo[piece, :].astype(F32)
        g_piece = g[piece, :]
        scaled = scale * dyo_piece
        dg = scaled * prm_ref[5:6, :width] - g_piece * back
        gain_out[0:1, :] += jnp.sum(scaled * g_piece, axis=0, keepdims=True)
        d_z = dg * mixed[piece, :] * (sig * (1.0 + z_piece * (1.0 - sig)))
        dz[piece, :] = d_z.astype(BF16)
        yo_t[:, piece] = d_z.T.astype(BF16)
        dyo[piece, :] = (dg * (z_piece * sig)).astype(BF16)
        return carry

    chunks = total // CHUNK
    lax.fori_loop(0, chunks, gate_back, 0)
    stores.start(dz, dz_out)
    stores.start(dyo, dy_out)
    for step in range(3, line.count):
        line.relay(step, 0)
    load_u.wait()

    def gate_product(chunk):
        product_chunk(yo_t, d, chunk, gz.at[chunk, :width], width // 2)

    def theirs(z_chunk, carry):
        gate_product(gz_cores.theirs(z_chunk))
        gz_cores.swap(z_chunk)
        return carry

    lax.fori_loop(0, line.count, theirs, 0)
    for step in range(3, line.count):
        line.relay(step, 1)

    def ours(z_chunk, carry):
        gate_product(gz_cores.ours(z_chunk))
        return carry

    lax.fori_loop(0, line.count, ours, 0)
    for z_chunk in range(line.count):
        gz_cores.merge(z_chunk)
        stores.start(gz.at[gz_cores.ours(z_chunk)], gz_out.at[z_chunk])
    sum_ref = line.finish()
    gw_out[...] = sum_ref[...]
    plane.finish()

    def add_own(i, carry):
        piece = pl.ds(pl.multiple_of(i * 32, 32), 32)
        total_out = own[piece, :].astype(F32) + plane.received(piece)
        block_out[piece, :] = (x_ref[piece, :].astype(F32) + total_out).astype(BF16)
        return carry

    lax.fori_loop(0, rows // 32, add_own, 0)
    line.end()
    plane.end()
    for copy in stores.started:
        copy.wait()


def second_part(inner, x_in, cross, branch, yo_t, d, dyo, g, mixed, zx, coef, prm, u):
    rows, model = x_in.shape
    width, total = yo_t.shape
    dp_count = lax.axis_size("dp")
    cut = model // dp_count
    kept = width // 8
    vmem = pl.BlockSpec(memory_space=pltpu.VMEM)
    anywhere = pl.BlockSpec(memory_space=pl.ANY)
    return pl.pallas_call(
        functools.partial(second_kernel, inner),
        out_shape=(
            jax.ShapeDtypeStruct((rows, model), BF16),
            jax.ShapeDtypeStruct((width - kept, cut), BF16),
            jax.ShapeDtypeStruct((total, width), BF16),
            jax.ShapeDtypeStruct((total, width), BF16),
            jax.ShapeDtypeStruct((dp_count // 2, width + kept, cut), BF16),
            jax.ShapeDtypeStruct((8, width), F32),
        ),
        in_specs=[vmem] * 2 + [anywhere] * 8 + [vmem, anywhere],
        out_specs=(vmem, vmem, anywhere, anywhere, anywhere, vmem),
        scratch_shapes=[
            pltpu.VMEM((total, width), BF16),
            pltpu.VMEM((width, total), BF16),
            pltpu.VMEM((total, model), BF16),
            pltpu.VMEM((total, width), BF16),
            pltpu.VMEM((total, width), F32),
            pltpu.VMEM((total, width), F32),
            pltpu.VMEM((total, width), BF16),
            pltpu.VMEM((total, LANES), F32),
            pltpu.VMEM((rows, model), BF16),
            pltpu.VMEM((dp_count, width + kept, cut), BF16),
            pltpu.VMEM((dp_count, width - kept, cut), BF16),
        ]
        + pair_scratch(dp_count, (width - kept, cut))
        + pair_scratch(dp_count, (width + kept, cut))
        + line_scratch(dp_count, (width - kept, cut))
        + plane_scratch(rows, model)
        + [
            pltpu.VMEM((3, 8, total), F32),
            pltpu.SemaphoreType.DMA((2, 3)),
            pltpu.SemaphoreType.DMA((22,)),
            pltpu.SemaphoreType.DMA((2 + dp_count // 2,)),
        ],
        compiler_params=pltpu.CompilerParams(
            collective_id=1, has_side_effects=True, vmem_limit_bytes=60 * 1024 * 1024
        ),
    )(x_in, cross, branch, yo_t, d, dyo, g, mixed, zx, coef, prm, u)


def third_kernel(
    own_cols, heads, zx_ref, bcdt_ref, pos_ref, prm_ref, head_ref, expand_ref, mixed_ref, state_ref, dy_ref,
    pre_ref, u_ref, gz_ref,
    gw_z, dx_out, dbcdt_out, gl_out, small_out,
    x, bcdt, mixed, states, dy, pre, u, dx, dbcdt, dx_t, gl, bc_in, d_state, later, later_pos,
    pair, pair_sems, parts, right, left, right_sems, left_sems, bc_sems, load_sems, store_sems,
):
    total, width = mixed.shape
    chunks = total // CHUNK
    me, side, up, far = tp_places()
    loads, stores = Copies(load_sems), Copies(store_sems)
    load_parts = loads.start(gz_ref, parts)
    cores = PairSum(gl, pair, pair_sems)
    line = LineSum(parts, lambda z: z, right, left, right_sems, left_sems)
    halves_of_loads = []
    for first in (total // 2, 0):
        piece = pl.ds(first, total // 2)
        pieces = pl.ds(first // CHUNK, chunks // 2)
        halves_of_loads.append(
            [
                loads.start(zx_ref.at[piece, width:], x.at[piece]),
                loads.start(bcdt_ref.at[piece], bcdt.at[piece]),
                loads.start(mixed_ref.at[piece], mixed.at[piece]),
                loads.start(state_ref.at[pieces], states.at[pieces]),
                loads.start(dy_ref.at[piece], dy.at[piece]),
                loads.start(pre_ref.at[piece], pre.at[piece]),
            ]
        )
    load_u = loads.start(u_ref, u)
    greet([{"tp": side}, {"tp": up}, {"tp": far}, cores.partner] + line.peers())
    backward_start(small_out, d_state, later, later_pos)
    load_parts.wait()
    line.lead(*range(1, line.count))
    for copy in halves_of_loads[0]:
        copy.wait()
    hooks = {3: (2, 0), 5: (2, 1), 7: (3, 0), chunks: (3, 1)}

    def chunk(i, carry):
        at = chunks - 1 - i
        tokens = pl.ds(pl.multiple_of(at * CHUNK, CHUNK), CHUNK)

        @pl.when(i == chunks // 2)
        def _():
            for copy in halves_of_loads[1]:
                copy.wait()

        backward_chunk(
            width, tokens, states[at], pre, x, bcdt, pos_ref, prm_ref, head_ref, expand_ref, mixed, dy, dx, dbcdt, dx_t,
            small_out, d_state, later, later_pos,
        )
        for when, turn in hooks.items():

            @pl.when(i == when - 1)
            def _():
                line.relay(*turn)

        return carry

    lax.fori_loop(0, chunks, chunk, 0)
    stores.start(dx, dx_out)
    stores.start(dbcdt, dbcdt_out)

    pick_row = lax.broadcasted_iota(jnp.int32, (2 * own_cols, 2 * LANES), 0)
    pick_col = lax.broadcasted_iota(jnp.int32, (2 * own_cols, 2 * LANES), 1)

    def columns_of(place):
        wanted = jnp.where(pick_row < own_cols, pick_row, pick_row - own_cols + LANES) + place * own_cols
        pick = (pick_col == wanted).astype(F32).astype(BF16)
        return dot(pick, dbcdt[:, : 2 * LANES], CONTRACT_LAST)

    copies = []
    for n, peer in enumerate((side, up, far)):
        bc_in[n] = columns_of(peer).astype(BF16)
        copies.append(send(bc_in.at[n], bc_in.at[3 + n], bc_sems.at[0, n], bc_sems.at[1, n], {"tp": peer}))
        copies[-1].start()
    own_bc = columns_of(me)
    dx_t[width:, :] = jnp.zeros((dx_t.shape[0] - width, total), BF16)
    dx_t[width + 2 * own_cols : width + 2 * own_cols + heads, :] = dbcdt[:, 2 * LANES :].astype(F32).T[:heads, :].astype(
        BF16
    )
    load_u.wait()

    def x_product(chunk):
        product_chunk(dx_t, u, chunk, gl.at[chunk, :width], width // 2)

    def bc_product(chunk):
        columns = pl.ds(pl.multiple_of(chunk * gl.shape[2], gl.shape[2]), gl.shape[2])
        gl[chunk, width:, :] = dot(dx_t[width:, :], u[:, columns]).astype(BF16)

    def their_x(z_chunk, carry):
        x_product(cores.theirs(z_chunk))
        return carry

    def their_bc(z_chunk, carry):
        bc_product(cores.theirs(z_chunk))
        cores.swap(z_chunk)
        return carry

    def ours(z_chunk, carry):
        x_product(cores.ours(z_chunk))
        bc_product(cores.ours(z_chunk))
        return carry

    lax.fori_loop(0, line.count, their_x, 0)
    for copy in copies:
        copy.wait()
    for n in range(3):
        own_bc = own_bc + bc_in[3 + n].astype(F32)
    dx_t[width : width + 2 * own_cols, :] = own_bc.astype(BF16)
    lax.fori_loop(0, line.count, their_bc, 0)
    lax.fori_loop(0, line.count, ours, 0)
    for z_chunk in range(line.count):
        cores.merge(z_chunk)
        stores.start(gl.at[cores.ours(z_chunk)], gl_out.at[z_chunk])
    sum_ref = line.finish()

    gw_z[...] = sum_ref[...]
    line.end()
    for copy in stores.started:
        copy.wait()


def third_part(own_cols, heads, zx, bcdt, pos, prm, head_prm, expand, mixed, states, dy, pre, u, gz):
    total, width = mixed.shape
    model = u.shape[1]
    dp_count = lax.axis_size("dp")
    cut = model // dp_count
    all_rows = width + -(-(2 * own_cols + heads) // 32) * 32
    vmem = pl.BlockSpec(memory_space=pltpu.VMEM)
    anywhere = pl.BlockSpec(memory_space=pl.ANY)
    return pl.pallas_call(
        functools.partial(third_kernel, own_cols, heads),
        out_shape=(
            jax.ShapeDtypeStruct(gz.shape[1:], BF16),
            jax.ShapeDtypeStruct((total, width), BF16),
            jax.ShapeDtypeStruct((total, 3 * LANES), BF16),
            jax.ShapeDtypeStruct((dp_count // 2, all_rows, cut), BF16),
            jax.ShapeDtypeStruct((8, width + 2 * LANES), F32),
        ),
        in_specs=[anywhere] * 2 + [vmem] * 4 + [anywhere] * 6,
        out_specs=(vmem, anywhere, anywhere, anywhere, vmem),
        scratch_shapes=[
            pltpu.VMEM((total, width), BF16),
            pltpu.VMEM(bcdt.shape, BF16),
            pltpu.VMEM((total, width), F32),
            pltpu.VMEM(states.shape, BF16),
            pltpu.VMEM((total, width), BF16),
            pltpu.VMEM((total, width + 2 * LANES), F32),
            pltpu.VMEM((total, model), BF16),
            pltpu.VMEM((total, width), BF16),
            pltpu.VMEM((total, 3 * LANES), BF16),
            pltpu.VMEM((all_rows, total), BF16),
            pltpu.VMEM((dp_count, all_rows, cut), BF16),
            pltpu.VMEM((6, 2 * own_cols, total), BF16),
            pltpu.VMEM((LANES, width), F32),
            pltpu.VMEM((CHUNK + 8, width + 2 * LANES), F32),
            pltpu.VMEM((CHUNK + 8, LANES), jnp.int32),
        ]
        + pair_scratch(dp_count, (all_rows, cut))
        + [pltpu.VMEM(gz.shape, BF16)]
        + line_scratch(dp_count, gz.shape[1:])
        + [pltpu.SemaphoreType.DMA((2, 3)), pltpu.SemaphoreType.DMA((14,)), pltpu.SemaphoreType.DMA((2 + dp_count // 2,))],
        compiler_params=pltpu.CompilerParams(
            collective_id=2, has_side_effects=True, vmem_limit_bytes=60 * 1024 * 1024
        ),
    )(zx, bcdt, pos, prm, head_prm, expand, mixed, states, dy, pre, u, gz)


def fourth_kernel(
    heads, x_ref, d_own_ref, gain_ref, small_ref, gain_sum_ref, expand_ref, dz_ref, dx_ref, dbcdt_ref, wz_ref, wx_ref,
    wbc_ref, u_ref, gl_ref,
    gw_x, grad_x, sums,
    dz, dx, dbcdt, wz, wx, wbc, u, own, gain_part, packed, over_z, parts,
    right, left, right_sems, left_sems,
    away, to_side, to_up, in_far, in_side, in_up, plane_sems, z_sems, tp_sems, load_sems,
):
    rows, model = x_ref.shape
    width = dz.shape[1]
    me, side, up, far = tp_places()
    dp_count = 2 * parts.shape[0]
    loads = Copies(load_sems)
    weights = [loads.start(wz_ref, wz), loads.start(wx_ref, wx), loads.start(wbc_ref, wbc)]
    loads_of = {}

    def load_block(name, place):
        piece = pl.ds(pl.multiple_of(place * rows, rows), rows)
        loads_of[name] = [
            loads.start(source.at[piece], target.at[piece])
            for source, target in ((dz_ref, dz), (dx_ref, dx), (dbcdt_ref, dbcdt), (u_ref, u))
        ]

    load_block("far", far)
    load_parts = loads.start(gl_ref, parts)
    line = LineSum(parts, lambda z: z, right, left, right_sems, left_sems)
    plane = PlaneSum(away, to_side, to_up, in_far, in_side, in_up, plane_sems)
    partner = {"dp": line.dp + 1 - 2 * lax.rem(line.dp, 2)}
    others = [{"dp": lax.rem(line.dp + 2 * n, dp_count)} for n in range(1, dp_count // 2)]
    greet([{"tp": side}, {"tp": up}, {"tp": far}, partner] + others)
    load_parts.wait()
    line.lead(*range(1, line.count - 1))
    for name, place in (("side", side), ("up", up), ("me", me)):
        load_block(name, place)
    gain_part[...] = jnp.zeros_like(gain_part)

    quarter = model // 4

    def du_block(name, place, target, started=None):
        for copy in loads_of[name]:
            copy.wait()
        piece = pl.ds(pl.multiple_of(place * rows, rows), rows)

        def two(m, carry):
            for odd in range(2):
                n = 2 * m + odd
                columns = pl.ds(pl.multiple_of(n * quarter, quarter), quarter)
                du = (
                    dot(dz[piece, :], wz[columns, :], CONTRACT_LAST)
                    + dot(dx[piece, :], wx[columns, :], CONTRACT_LAST)
                    + dot(dbcdt[piece, :], wbc[:, columns])
                )
                if started is None:
                    target[:, columns] = du
                else:
                    target[n] = du.astype(BF16)
                    started(n, odd)
                gain_part[pl.ds(n, 1), :] += jnp.sum(du * u[piece, columns].astype(F32), axis=0, keepdims=True)
            return carry

        lax.fori_loop(0, 2, two, 0)

    for copy in weights:
        copy.wait()
    du_block("far", far, away, plane.start_far)
    du_block("side", side, to_side, functools.partial(plane.start_near, 0))
    line.relay(2, 0)
    du_block("up", up, to_up, functools.partial(plane.start_near, 1))
    line.relay(2, 1)
    du_block("me", me, own)

    wide = width + 2 * LANES
    shift = (
        lax.broadcasted_iota(jnp.int32, (LANES, LANES), 1)
        == lax.broadcasted_iota(jnp.int32, (LANES, LANES), 0) + me * heads
    ).astype(F32)
    shift = jnp.where(lax.broadcasted_iota(jnp.int32, (LANES, LANES), 0) < heads, shift, 0.0)
    skip_rows = two_parts(jnp.broadcast_to(small_ref[6:7, :width], (8, width)))
    expand = expand_ref[:LANES, :]
    per_head = dot(skip_rows[:, :width], expand, CONTRACT_LAST) + dot(skip_rows[:, width:], expand, CONTRACT_LAST)
    tiles = jnp.concatenate([small_ref[:, :LANES], small_ref[:, LANES : 2 * LANES], per_head], axis=0)
    placed = lax.dot_general(
        tiles, shift, (((1,), (0,)), ((), ())), precision=HIGHEST, preferred_element_type=F32
    )
    packed[0, :, :wide] = small_ref[...]
    packed[0, 5:6, :width] = gain_sum_ref[0:1, :]
    packed[0, 6:7, width : width + LANES] = placed[16:17]
    packed[0, 7:8, :LANES] = placed[7:8]
    packed[0, 7:8, LANES : 2 * LANES] = placed[15:16]
    packed[0, :, wide:] = jnp.zeros((8, quarter), F32)
    for n in range(4):
        packed[0, n : n + 1, wide:] = gain_part[n : n + 1, :] / gain_ref[:, n * quarter : (n + 1) * quarter]
    trade = send(packed.at[0], packed.at[1], z_sems.at[0, 0], z_sems.at[1, 0], partner)
    trade.start()
    plane.pass_on()
    trade.wait()
    over_z[0] = packed[0] + packed[1]
    copies = [
        send(over_z.at[0], over_z.at[n], z_sems.at[0, n], z_sems.at[1, n], others[n - 1])
        for n in range(1, dp_count // 2)
    ]
    for copy in copies:
        copy.start()
    line.lead(line.count - 1)
    for step in range(3, line.count):
        line.relay(step, 0)
        line.relay(step, 1)
    for copy in copies:
        copy.wait()
    everything = over_z[0]
    for n in range(1, dp_count // 2):
        everything = everything + over_z[n]
    sums[me] = everything
    copies = [
        send(sums.at[me], sums.at[me], tp_sems.at[0, n], tp_sems.at[1, n], {"tp": peer})
        for n, peer in enumerate((side, up, far))
    ]
    for copy in copies:
        copy.start()
    plane.finish()

    def norm_back(i, carry):
        piece = pl.ds(pl.multiple_of(i * 32, 32), 32)
        x = x_ref[piece, :].astype(F32)
        r_in = lax.rsqrt(jnp.mean(x * x, axis=-1, keepdims=True) + EPSILON)
        du = own[piece, :] + plane.received(piece)
        e_in = du * gain_ref[...]
        back = r_in * r_in * r_in * jnp.mean(e_in * x, axis=-1, keepdims=True)
        grad_x[piece, :] = d_own_ref[piece, :].astype(F32) + r_in * e_in - x * back
        return carry

    lax.fori_loop(0, rows // 32, norm_back, 0)
    for copy in copies:
        copy.wait()
    sum_ref = line.finish()

    gw_x[...] = sum_ref[...]
    line.end()
    plane.end()


def fourth_part(heads, x_in, d_out, gain, small, gain_sum, expand, dz, dx, dbcdt, w_z, w_x, wbc, u, gl):
    rows, model = x_in.shape
    total, width = dz.shape
    dp_count = lax.axis_size("dp")
    cut = model // dp_count
    wide = width + 2 * LANES + model // 4
    vmem = pl.BlockSpec(memory_space=pltpu.VMEM)
    anywhere = pl.BlockSpec(memory_space=pl.ANY)
    return pl.pallas_call(
        functools.partial(fourth_kernel, heads),
        out_shape=(
            jax.ShapeDtypeStruct(gl.shape[1:], BF16),
            jax.ShapeDtypeStruct((rows, model), F32),
            jax.ShapeDtypeStruct((4, 8, wide), F32),
        ),
        in_specs=[vmem] * 6 + [anywhere] * 8,
        out_specs=(vmem,) * 3,
        scratch_shapes=[
            pltpu.VMEM((total, width), BF16),
            pltpu.VMEM((total, width), BF16),
            pltpu.VMEM((total, 3 * LANES), BF16),
            pltpu.VMEM((model, width), BF16),
            pltpu.VMEM((model, width), BF16),
            pltpu.VMEM((3 * LANES, model), BF16),
            pltpu.VMEM((total, model), BF16),
            pltpu.VMEM((rows, model), F32),
            pltpu.VMEM((8, model // 4), F32),
            pltpu.VMEM((2, 8, wide), F32),
            pltpu.VMEM((dp_count // 2, 8, wide), F32),
            pltpu.VMEM(gl.shape, BF16),
        ]
        + line_scratch(dp_count, gl.shape[1:])
        + plane_scratch(rows, model)
        + [
            pltpu.SemaphoreType.DMA((2, dp_count // 2)),
            pltpu.SemaphoreType.DMA((2, 3)),
            pltpu.SemaphoreType.DMA((20,)),
        ],
        compiler_params=pltpu.CompilerParams(
            collective_id=3, has_side_effects=True, vmem_limit_bytes=60 * 1024 * 1024
        ),
    )(x_in, d_out, gain, small, gain_sum, expand, dz, dx, dbcdt, w_z, w_x, wbc, u, gl)


def results_kernel(
    own_cols, heads, block_ref, grad_x_ref, first_ref, z_ref, x_ref, sums_ref,
    block_out, grad_x, gw_z, gw_x, gw_b, gw_c, gw_dt, gw_out, conv_w, conv_b, gate, norm, dt_bias, a_log, skip,
    held_block, held_grad_x, first, z, x, held_z, held_x, held_out, load_sems, sems,
):
    loads, copies = Copies(load_sems), Copies(sems)
    for source, target in ((first_ref, first), (z_ref, z), (x_ref, x), (grad_x_ref, held_grad_x), (block_ref, held_block)):
        loads.start(source, target)
    load_first, load_z, load_x, load_grad_x, load_block = loads.started
    taken = first.shape[0]
    width = gw_z.shape[1]
    count = sums_ref.shape[0]
    inner = gate.shape[1]
    wide = width + 2 * LANES

    def over_tp(rows, columns):
        total = sums_ref[0, rows, columns]
        for n in range(1, count):
            total = total + sums_ref[n, rows, columns]
        return total

    for n in range(count):
        own = slice(n * width, (n + 1) * width)
        conv_w[:, own] = sums_ref[n, 0:4, :width]
        conv_b[:, own] = sums_ref[n, 4:5, :width]
        gate[:, own] = sums_ref[n, 5:6, :width]
    conv_w[:, inner:] = over_tp(slice(0, 4), slice(width, wide))
    conv_b[:, inner:] = over_tp(slice(4, 5), slice(width, wide))
    quarter = norm.shape[1] // 4
    for n in range(4):
        norm[:, n * quarter : (n + 1) * quarter] = over_tp(slice(n, n + 1), slice(wide, None))
    total_heads = dt_bias.shape[1]
    dt_bias[...] = over_tp(slice(7, 8), slice(0, LANES))[:, :total_heads]
    a_log[...] = over_tp(slice(7, 8), slice(LANES, 2 * LANES))[:, :total_heads]
    skip[...] = over_tp(slice(6, 7), slice(width, width + LANES))[:, :total_heads]
    load_grad_x.wait()
    copies.start(held_grad_x, grad_x)
    load_block.wait()
    copies.start(held_block, block_out)

    def turn(source, held, target):
        def one(i, carry):
            piece = pl.ds(pl.multiple_of(i * CHUNK, CHUNK), CHUNK)
            held[:, piece] = source[piece, :].T.astype(F32)
            return carry

        lax.fori_loop(0, width // CHUNK, one, 0)
        copies.start(held, target)

    load_first.wait()
    load_z.wait()
    held_out[:taken, :] = first[...].astype(F32)
    held_out[taken:, :] = z[width:, :].astype(F32)
    copies.start(held_out, gw_out)
    turn(z, held_z, gw_z)
    load_x.wait()
    turn(x, held_x, gw_x)
    gw_b[...] = x[width : width + own_cols, :].astype(F32)
    gw_c[...] = x[width + own_cols : width + 2 * own_cols, :].astype(F32)
    gw_dt[...] = x[width + 2 * own_cols : width + 2 * own_cols + heads, :].astype(F32)
    for copy in copies.started:
        copy.wait()


def results_part(own_cols, heads, width, block_out, grad_x, first, gw_z, gw_x, sums):
    cut = first.shape[1]
    count = sums.shape[0]
    inner = width * count
    model = grad_x.shape[1]
    vmem = pl.BlockSpec(memory_space=pltpu.VMEM)
    anywhere = pl.BlockSpec(memory_space=pl.ANY)
    shapes = [
        (cut, width),
        (cut, width),
        (own_cols, cut),
        (own_cols, cut),
        (heads, cut),
        (width, cut),
        (4, inner + 2 * LANES),
        (1, inner + 2 * LANES),
        (1, inner),
        (1, model),
        (1, heads * count),
        (1, heads * count),
        (1, heads * count),
    ]
    return pl.pallas_call(
        functools.partial(results_kernel, own_cols, heads),
        out_shape=[
            jax.ShapeDtypeStruct(block_out.shape, BF16),
            jax.ShapeDtypeStruct(grad_x.shape, F32),
        ]
        + [jax.ShapeDtypeStruct(shape, F32) for shape in shapes],
        in_specs=[anywhere] * 5 + [vmem],
        out_specs=[anywhere] * 4 + [vmem] * 3 + [anywhere] + [vmem] * 7,
        scratch_shapes=[pltpu.VMEM(large.shape, large.dtype) for large in (block_out, grad_x, first, gw_z, gw_x)]
        + [pltpu.VMEM((cut, width), F32), pltpu.VMEM((cut, width), F32), pltpu.VMEM((width, cut), F32)]
        + [pltpu.SemaphoreType.DMA((5,)), pltpu.SemaphoreType.DMA((5,))],
        compiler_params=pltpu.CompilerParams(vmem_limit_bytes=60 * 1024 * 1024),
    )(block_out, grad_x, first, gw_z, gw_x, sums)


def in_norm_scale(values):
    return lax.rsqrt(jnp.mean(values * values, axis=-1, keepdims=True) + EPSILON)


def body(
    x_in, norm_gain, w_z, w_x, w_b, w_c, w_dt, conv_w, conv_b, dt_bias, a_log, d_skip, gate_gain, w_out,
    doc_lens, d_out,
):
    tp_count = lax.axis_size("tp")
    in_planes = tp_count == 4 and lax.axis_size("dp") == 8
    rank = lax.axis_index("tp")
    dev_rows, model = x_in.shape
    rows = dev_rows * tp_count
    inner = gate_gain.shape[0]
    width = w_z.shape[1]
    heads = w_dt.shape[1]
    state_size = (conv_w.shape[0] - inner) // 2
    head_size = width // heads
    own_cols = w_b.shape[1]

    x_float = x_in.astype(F32)
    r_in = in_norm_scale(x_float)
    small_weights = jnp.concatenate([w_b, w_c, w_dt], axis=1).T
    if in_planes:
        lanes = jnp.zeros((LANES - d_skip.shape[0],), F32)
        flat = jnp.concatenate([conv_b, gate_gain, dt_bias, lanes, a_log, lanes, d_skip, lanes])[None, :]
        (
            gathered, zx, bcdt, w_bcdt, mixed, g, yo, yo_t, states, grad_gathered, dyo, coef, pos, prm, head_prm, expand,
            pre, cross, branch,
        ) = first_part(
            inner, heads, own_cols, x_in, norm_gain[None, :], w_b.T, w_c.T, w_dt.T, conv_w.T, flat, doc_lens, w_z, w_x,
            w_out, d_out,
        )
        gain_own = prm[5, :width]
    else:
        normed = (x_float * r_in * norm_gain[None, :]).astype(BF16)
        gathered = lax.all_gather(normed, "tp", axis=0, tiled=True)
        w_bc = lax.all_gather(small_weights[: 2 * own_cols], "tp", axis=0).reshape(tp_count, 2, own_cols, model)
        w_bcdt = jnp.concatenate(
            [
                jnp.swapaxes(w_bc, 0, 1).reshape(2 * state_size, model),
                small_weights[2 * own_cols :],
                jnp.zeros((LANES - heads, model), BF16),
            ],
            axis=0,
        )
        zx = dot(gathered, jnp.concatenate([w_z, w_x], axis=1)).astype(BF16)
        bcdt = dot(gathered, w_bcdt, CONTRACT_LAST).astype(BF16)
        lengths = doc_lens[0]
        doc_starts = jnp.cumsum(lengths) - lengths
        positions = jnp.arange(rows, dtype=jnp.int32)
        started = jnp.where(positions[:, None] >= doc_starts[None, :], doc_starts[None, :], 0)
        pos = (positions - jnp.max(started, axis=1))[:, None]

        def own(array, count):
            return lax.dynamic_slice_in_dim(array, rank * count, count, axis=0)

        taps = jnp.concatenate([own(conv_w[:inner], width), conv_w[inner:]], axis=0).T
        bias = jnp.concatenate([own(conv_b[:inner], width), conv_b[inner:]])
        pad_bc = jnp.zeros((2 * state_size,), F32)
        gain_own = own(gate_gain, width)
        skip_own = jnp.repeat(own(d_skip, heads), head_size)
        prm = jnp.concatenate(
            [
                taps,
                bias[None],
                jnp.concatenate([gain_own, pad_bc])[None],
                jnp.concatenate([skip_own, pad_bc])[None],
                jnp.zeros((1, width + 2 * state_size), F32),
            ],
            axis=0,
        )
        pad_heads = jnp.zeros((LANES - heads,), F32)
        head_prm = jnp.concatenate(
            [
                jnp.concatenate([own(dt_bias, heads), pad_heads])[None],
                jnp.concatenate([jnp.exp(own(a_log, heads)), pad_heads])[None],
                jnp.zeros((6, LANES), F32),
            ],
            axis=0,
        )
        expand = (
            (jnp.arange(2 * LANES) % LANES)[:, None] == (jnp.arange(width) // head_size)[None, :]
        ).astype(BF16)
        mixed, g, g_sum, states, pre = mixer_forward(width, zx, bcdt, pos, prm, head_prm, expand)
        grad_gathered = lax.all_gather(d_out, "tp", axis=0, tiled=True)
        dyo = dot(grad_gathered, w_out, CONTRACT_LAST).astype(BF16)
        eg_sum = jnp.sum(dyo.astype(F32) * gain_own[None, :] * g, axis=1)
        g_total, eg_total = lax.psum((g_sum[0], eg_sum), "tp")
        r_gate = lax.rsqrt(g_total / inner + EPSILON)
        zeros = jnp.zeros_like(r_gate)
        coef = jnp.stack([r_gate] + [zeros] * 7 + [r_gate**3 * (eg_total / inner)] + [zeros] * (LANES - 9), axis=1)
        yo = (g * r_gate[:, None] * gain_own[None, :]).astype(BF16)

    if in_planes:
        block_out, gw_first, dz, dy, gz, gain_sum = second_part(
            inner, x_in, cross, branch, yo_t, grad_gathered, dyo, g, mixed, zx, coef, prm, gathered
        )
        gw_z, grad_xs, grad_bcdt, gl, small = third_part(
            own_cols, heads, zx, bcdt, pos, prm, head_prm, expand, mixed, states, dy, pre, gathered, gz
        )
        gw_x, grad_x, sums = fourth_part(
            heads, x_in, d_out, norm_gain[None, :], small, gain_sum, expand, dz, grad_xs, grad_bcdt, w_z, w_x, w_bcdt,
            gathered, gl
        )
        (
            block_out, grad_x, gw_z, gw_x, gw_b, gw_c, gw_dt, gw_out, g_conv_w, g_conv_b, g_gate, g_norm, g_dt_bias,
            g_a_log, g_skip
        ) = results_part(
            own_cols, heads, width, block_out, grad_x, gw_first, gw_z, gw_x, sums
        )
        return (
            block_out, grad_x, g_norm[0], gw_z, gw_x, gw_b.T, gw_c.T, gw_dt.T, g_conv_w.T, g_conv_b[0], g_dt_bias[0],
            g_a_log[0], g_skip[0], g_gate[0], gw_out
        )
    else:

        def scatter_dp(partial):
            return lax.psum_scatter(partial.astype(BF16), "dp", scatter_dimension=0, tiled=True).astype(F32)

        def scatter_tp(array):
            return lax.psum_scatter(array.astype(BF16), "tp", scatter_dimension=0, tiled=True).astype(F32)

        grad_w_out = scatter_dp(dot(grad_gathered, yo, CONTRACT_FIRST)).T
        z = zx[:, :width].astype(F32)
        sig_z = jax.nn.sigmoid(z)
        dg = coef[:, 0:1] * (dyo.astype(F32) * gain_own[None, :]) - g * coef[:, 8:9]
        dz = (dg * mixed * (sig_z * (1.0 + z * (1.0 - sig_z)))).astype(BF16)
        dy = (dg * (z * sig_z)).astype(BF16)
        gain_sum = jnp.sum(dyo.astype(F32) * g * coef[:, 0:1], axis=0)
        grad_w_z = scatter_dp(dot(gathered, dz, CONTRACT_FIRST))
        block_out = (x_float + scatter_tp(dot(yo, w_out))).astype(BF16)
        grad_xs, grad_bcdt, small = mixer_backward(
            width, pre, zx, bcdt, pos, prm, head_prm, expand, mixed, states, dy
        )
        small = small.at[5, :width].set(gain_sum)
        d_bc = grad_bcdt[:, : 2 * state_size]
        by_owner = jnp.moveaxis(d_bc.reshape(rows, 2, tp_count, own_cols), 2, 0)
        by_owner = by_owner.reshape(tp_count, rows, 2 * own_cols)
        d_bc_own = lax.psum_scatter(by_owner.astype(F32), "tp", scatter_dimension=0, tiled=False)
        d_rest = jnp.concatenate(
            [
                d_bc_own.astype(BF16),
                grad_bcdt[:, 2 * state_size : 2 * state_size + heads],
                jnp.zeros((rows, (-2 * own_cols - heads) % LANES), BF16),
            ],
            axis=1,
        )
        grad_w_x = scatter_dp(dot(gathered, grad_xs, CONTRACT_FIRST))
        grad_rest = scatter_dp(dot(gathered, d_rest, CONTRACT_FIRST))
        du_part = (
            dot(dz, w_z, CONTRACT_LAST) + dot(grad_xs, w_x, CONTRACT_LAST) + dot(grad_bcdt, w_bcdt)
        )
        gain_part = jnp.sum(du_part * gathered.astype(F32), axis=0) / norm_gain
        du = scatter_tp(du_part)
        e_in = du * norm_gain[None, :]
        grad_x = d_out.astype(F32) + r_in * e_in - x_float * (
            r_in**3 * jnp.mean(e_in * x_float, axis=-1, keepdims=True)
        )
        sums = lax.all_gather(lax.psum(small, "dp"), "tp")
        grad_norm_gain = lax.psum(gain_part, ("dp", "tp"))

    channels = jnp.swapaxes(sums[:, :7, :width], 0, 1).reshape(7, inner)
    shared = jnp.sum(sums[:, :5, width : width + 2 * state_size], axis=0)
    grad_conv = jnp.concatenate([channels[:5], shared], axis=1)
    return (
        block_out,
        grad_x,
        grad_norm_gain,
        grad_w_z,
        grad_w_x,
        grad_rest[:, :own_cols],
        grad_rest[:, own_cols : 2 * own_cols],
        grad_rest[:, 2 * own_cols : 2 * own_cols + heads],
        grad_conv[:4].T,
        grad_conv[4],
        sums[:, 7, :heads].reshape(-1),
        sums[:, 7, LANES : LANES + heads].reshape(-1),
        channels[6].reshape(heads * tp_count, head_size).sum(axis=1),
        channels[5],
        grad_w_out,
    )


def solution(mesh):
    rows = P(("dp", "tp"), None)
    columns = P(None, "tp")
    both = P("dp", "tp")
    none = P()
    return jax.shard_map(
        body,
        mesh=mesh,
        in_specs=(
            rows, none, columns, columns, columns, columns, columns, none, none, none, none, none, none,
            P("tp", None), P("dp", None), rows,
        ),
        out_specs=(
            rows, rows, none, both, both, both, both, both, none, none, none, none, none, none, P("tp", "dp"),
        ),
        check_vma=False,
    )
```

```python
import functools

import jax
import jax.numpy as jnp
from jax import lax
from jax.experimental import pallas as pl
from jax.experimental.pallas import tpu as pltpu
from jax.sharding import PartitionSpec as P

EPSILON = 1e-05
HIGHEST = lax.Precision.HIGHEST
F32 = jnp.float32
BF16 = jnp.bfloat16
CHUNK = 128
LANES = 128
CONTRACT_FIRST = (((0,), (0,)), ((), ()))
CONTRACT_LAST = (((1,), (1,)), ((), ()))


def dot(a, b, dims=(((1,), (0,)), ((), ()))):
    return lax.dot_general(a, b, dims, preferred_element_type=F32)


def two_parts(v):
    high = v.astype(BF16)
    return jnp.concatenate([high, (v - high.astype(F32)).astype(BF16)], axis=1)


def convolve(width, x, bc, pos, prm_ref, ext):
    ext[8:, :width] = x.astype(F32)
    ext[8:, width:] = bc.astype(F32)
    pre = prm_ref[3:4, :] * ext[8:, :] + prm_ref[4:5, :]
    for back in (1, 2, 3):
        here = (pos >= back).astype(F32)
        pre = pre + prm_ref[3 - back : 4 - back, :] * (ext[8 - back : 8 - back + CHUNK, :] * here)
    return pre


def prepare_chunk(width, pre, raw_dt, pos, head_ref, expand_ref):
    rows = CHUNK
    sig = jax.nn.sigmoid(pre)
    act = pre * sig
    xc = act[:, :width]
    state_size = (act.shape[1] - width) // 2
    b_rows = act[:, width : width + state_size].astype(BF16)
    c_rows = act[:, width + state_size :].astype(BF16)
    raw = raw_dt.astype(F32) + head_ref[0:1, :]
    dt = jnp.maximum(raw, 0.0) + jnp.log1p(jnp.exp(-jnp.abs(raw)))
    log_decay = -dt * head_ref[1:2, :]
    t_idx = lax.broadcasted_iota(jnp.int32, (rows, rows), 0)
    s_idx = lax.broadcasted_iota(jnp.int32, (rows, rows), 1)
    lower = (s_idx <= t_idx).astype(F32)
    cum = lax.dot_general(
        lower, log_decay, (((1,), (0,)), ((), ())), precision=HIGHEST, preferred_element_type=F32
    )
    same = (s_idx <= t_idx) & (s_idx >= t_idx - pos)
    scores = jnp.where(same, dot(c_rows, b_rows, CONTRACT_LAST), 0.0)
    t_col = lax.broadcasted_iota(jnp.int32, (rows, 1), 0)
    pos_last = pos[rows - 1 : rows, :]
    cum_last = cum[rows - 1 : rows, :]
    inward = jnp.exp(cum) * (pos > t_col).astype(F32)
    tail = jnp.exp(cum_last - cum) * (t_col >= rows - 1 - pos_last).astype(F32)
    carried = jnp.exp(cum_last) * (pos_last >= rows).astype(F32)
    wide = dot(
        two_parts(jnp.concatenate([dt, inward, tail, jnp.broadcast_to(carried, (8, LANES))], axis=0)),
        expand_ref[...],
    )
    return dict(
        sig=sig,
        xc=xc,
        b=b_rows,
        c=c_rows,
        raw=raw,
        log_decay=log_decay,
        cum=cum,
        cum_t=cum.T,
        same=same,
        scores=scores,
        t_idx=t_idx,
        s_idx=s_idx,
        dt_w=wide[:rows],
        in_w=wide[rows : 2 * rows],
        tail_w=wide[2 * rows : 3 * rows],
        carried_w=wide[3 * rows : 3 * rows + 1],
    )


def decay_of(k, head):
    return jnp.exp(jnp.minimum(k["cum"][:, head : head + 1] - k["cum_t"][head : head + 1, :], 0.0))


def halves(pair):
    lane = lax.broadcasted_iota(jnp.int32, pair.shape, 1)
    zero = jnp.zeros_like(pair)
    return jnp.concatenate(
        [jnp.where(lane < LANES // 2, pair, zero), jnp.where(lane < LANES // 2, zero, pair)], axis=0
    )


def forward_chunk(
    width, at, zx_ref, bcdt_ref, pos_ref, prm_ref, head_ref, expand_ref, mixed_ref, g_ref, sum_ref, state_ref,
    pre_ref, ext, state,
):
    if isinstance(at, int):
        rows = slice(at * CHUNK, (at + 1) * CHUNK)
    else:
        rows = pl.ds(pl.multiple_of(at * CHUNK, CHUNK), CHUNK)
    ext[:8, :] = ext[CHUNK:, :]
    pos = pos_ref[rows, :]
    pre = convolve(width, zx_ref[rows, width:], bcdt_ref[rows, : 2 * LANES], pos, prm_ref, ext)
    pre_ref[rows, :] = pre
    k = prepare_chunk(width, pre, bcdt_ref[rows, 2 * LANES :], pos, head_ref, expand_ref)
    stepped = (k["xc"] * k["dt_w"]).astype(BF16)
    held = state[...]
    held_low = held.astype(BF16)
    state_ref[at] = held_low
    reached = dot(k["c"], held_low) * k["in_w"] + prm_ref[6:7, :width] * k["xc"]
    weighted = (stepped.astype(F32) * k["tail_w"]).astype(BF16)
    state[...] = k["carried_w"] * held + dot(k["b"], weighted, CONTRACT_FIRST)
    for pair in range(width // LANES):
        lanes = slice(pair * LANES, (pair + 1) * LANES)
        mixing = jnp.concatenate(
            [
                (decay_of(k, 2 * pair) * k["scores"]).astype(BF16),
                (decay_of(k, 2 * pair + 1) * k["scores"]).astype(BF16),
            ],
            axis=1,
        )
        mixed_ref[rows, lanes] = dot(mixing, halves(stepped[:, lanes])) + reached[:, lanes]
    z = zx_ref[rows, :width].astype(F32)
    g = mixed_ref[rows, :] * (z * jax.nn.sigmoid(z))
    g_ref[rows, :] = g
    total = jnp.sum(g * g, axis=1, keepdims=True)
    sum_ref[:, rows] = jnp.broadcast_to(total, (CHUNK, LANES)).T[:8, :]


def forward_kernel(
    width, zx_ref, bcdt_ref, pos_ref, prm_ref, head_ref, expand_ref, mixed_ref, g_ref, sum_ref, state_ref,
    pre_ref, ext, state,
):
    @pl.when(pl.program_id(0) == 0)
    def _():
        state[...] = jnp.zeros_like(state)
        ext[...] = jnp.zeros_like(ext)

    forward_chunk(
        width, 0, zx_ref, bcdt_ref, pos_ref, prm_ref, head_ref, expand_ref, mixed_ref, g_ref, sum_ref, state_ref,
        pre_ref, ext, state,
    )


def backward_chunk(
    width, tokens, held, pre_ref, x_ref, bcdt_ref, pos_ref, prm_ref, head_ref, expand_ref, mixed_ref,
    dy_ref, grad_x_ref, grad_bcdt_ref, grad_t_ref, small_ref, d_state, later, later_pos,
):
    rows = CHUNK
    pos = pos_ref[tokens, :]
    pre = pre_ref[tokens, :]
    k = prepare_chunk(width, pre, bcdt_ref[tokens, 2 * LANES :], pos, head_ref, expand_ref)
    xc = k["xc"]
    skip = prm_ref[6:7, :width]
    y = mixed_ref[tokens, :] - skip * xc
    dy_low = dy_ref[tokens, :]
    dy = dy_low.astype(F32)
    small_ref[6:7, :width] += jnp.sum(dy * xc, axis=0, keepdims=True)

    stepped = (xc * k["dt_w"]).astype(BF16)
    d_held = d_state[...]
    d_held_low = d_held.astype(BF16)
    held_low = held
    weighted = (stepped.astype(F32) * k["tail_w"]).astype(BF16)
    dy_in = (dy * k["in_w"]).astype(BF16)
    from_state = dot(k["b"], d_held_low) * k["tail_w"]
    dc = dot(dy_in, held_low, CONTRACT_LAST)
    db = dot(weighted, d_held_low, CONTRACT_LAST)
    d_state[...] = k["carried_w"] * d_held + dot(k["c"], dy_in, CONTRACT_FIRST)
    d_scores = jnp.zeros((rows, rows), F32)
    d_stepped = []
    for pair in range(width // LANES):
        lanes = slice(pair * LANES, (pair + 1) * LANES)
        decay_a = decay_of(k, 2 * pair)
        decay_b = decay_of(k, 2 * pair + 1)
        mixing = jnp.concatenate(
            [(decay_a * k["scores"]).astype(BF16), (decay_b * k["scores"]).astype(BF16)], axis=0
        )
        d_mixing = dot(dy_low[:, lanes], halves(stepped[:, lanes]), CONTRACT_LAST)
        d_scores = d_scores + decay_a * d_mixing[:, :rows] + decay_b * d_mixing[:, rows:]
        d_stepped.append(dot(mixing, halves(dy_low[:, lanes]), CONTRACT_FIRST))
    d_stepped = jnp.concatenate(d_stepped, axis=1) + from_state
    d_scores = jnp.where(k["same"], d_scores, 0.0).astype(BF16)
    dc = dc + dot(d_scores, k["b"])
    db = db + dot(d_scores, k["c"], CONTRACT_FIRST)
    dxc = skip * dy + d_stepped * k["dt_w"]

    stepped_f = stepped.astype(F32)
    tail_term = jnp.sum(stepped_f * from_state, axis=0, keepdims=True) + k["carried_w"] * jnp.sum(
        held_low.astype(F32) * d_held, axis=0, keepdims=True
    )
    gathered = two_parts(
        jnp.concatenate([dy * y - stepped_f * d_stepped, jnp.broadcast_to(tail_term, (8, width))], axis=0)
    )
    expand = expand_ref[:LANES, :]
    narrow = dot(gathered[:, :width], expand, CONTRACT_LAST) + dot(gathered[:, width:], expand, CONTRACT_LAST)
    d_cum = narrow[:rows]
    d_dt = dot((d_stepped * xc).astype(BF16), expand, CONTRACT_LAST)
    upper = (k["s_idx"] >= k["t_idx"]).astype(F32)
    d_decay = (
        lax.dot_general(
            upper, d_cum, (((1,), (0,)), ((), ())), precision=HIGHEST, preferred_element_type=F32
        )
        + narrow[rows : rows + 1]
    )
    d_raw = (d_dt - d_decay * head_ref[1:2, :]) * jax.nn.sigmoid(k["raw"])
    small_ref[7:8, :LANES] += jnp.sum(d_raw, axis=0, keepdims=True)
    small_ref[7:8, LANES : 2 * LANES] += jnp.sum(d_decay * k["log_decay"], axis=0, keepdims=True)
    grad_bcdt_ref[tokens, 2 * LANES :] = d_raw.astype(BF16)

    sig = k["sig"]
    d_pre = jnp.concatenate([dxc, db, dc], axis=1) * (sig * (1.0 + pre * (1.0 - sig)))
    small_ref[4:5, :] += jnp.sum(d_pre, axis=0, keepdims=True)
    later[:rows, :] = d_pre
    later_pos[:rows, :] = jnp.broadcast_to(pos, (rows, LANES))
    x_own = jnp.concatenate([x_ref[tokens, :], bcdt_ref[tokens, : 2 * LANES]], axis=1).astype(F32)
    d_in = prm_ref[3:4, :] * d_pre
    small_ref[3:4, :] += jnp.sum(d_pre * x_own, axis=0, keepdims=True)
    for back in (1, 2, 3):
        there = (later_pos[back : back + rows, :] >= back).astype(F32)
        reaching = later[back : back + rows, :] * jnp.concatenate([there] * (later.shape[1] // LANES), axis=1)
        small_ref[3 - back : 4 - back, :] += jnp.sum(reaching * x_own, axis=0, keepdims=True)
        d_in = d_in + prm_ref[3 - back : 4 - back, :] * reaching
    grad_x_ref[tokens, :] = d_in[:, :width].astype(BF16)
    grad_bcdt_ref[tokens, : 2 * LANES] = d_in[:, width:].astype(BF16)
    later[rows:, :] = later[:8, :]
    later_pos[rows:, :] = later_pos[:8, :]
    if grad_t_ref is not None:
        grad_t_ref[:width, tokens] = d_in[:, :width].T.astype(BF16)


def backward_start(small_ref, d_state, later, later_pos):
    d_state[...] = jnp.zeros_like(d_state)
    later[...] = jnp.zeros_like(later)
    later_pos[...] = jnp.zeros_like(later_pos)
    small_ref[...] = jnp.zeros_like(small_ref)


def backward_kernel(
    width, pre_ref, x_ref, bcdt_ref, pos_ref, prm_ref, head_ref, expand_ref, mixed_ref, state_ref, dy_ref, grad_x_ref,
    grad_bcdt_ref, small_ref, d_state, later, later_pos,
):
    @pl.when(pl.program_id(0) == 0)
    def _():
        backward_start(small_ref, d_state, later, later_pos)

    backward_chunk(
        width, slice(0, CHUNK), state_ref[0], pre_ref, x_ref, bcdt_ref, pos_ref, prm_ref, head_ref, expand_ref, mixed_ref,
        dy_ref, grad_x_ref, grad_bcdt_ref, None, small_ref, d_state, later, later_pos,
    )


def mixer_forward(width, zx, bcdt, pos, prm, head_prm, expand):
    rows = zx.shape[0]
    chunks = rows // CHUNK

    def tokens(columns):
        return pl.BlockSpec((CHUNK, columns), lambda i: (i, 0))

    def whole(array):
        return pl.BlockSpec(array.shape, lambda i: (0, 0))

    return pl.pallas_call(
        functools.partial(forward_kernel, width),
        out_shape=(
            jax.ShapeDtypeStruct((rows, width), F32),
            jax.ShapeDtypeStruct((rows, width), F32),
            jax.ShapeDtypeStruct((8, rows), F32),
            jax.ShapeDtypeStruct((chunks, LANES, width), BF16),
            jax.ShapeDtypeStruct((rows, width + 2 * LANES), F32),
        ),
        grid=(chunks,),
        in_specs=[tokens(2 * width), tokens(3 * LANES), tokens(1), whole(prm), whole(head_prm), whole(expand)],
        out_specs=(
            tokens(width),
            tokens(width),
            pl.BlockSpec((8, CHUNK), lambda i: (0, i)),
            pl.BlockSpec((1, LANES, width), lambda i: (i, 0, 0)),
            tokens(width + 2 * LANES),
        ),
        scratch_shapes=[
            pltpu.VMEM((CHUNK + 8, width + 2 * LANES), F32),
            pltpu.VMEM((LANES, width), F32),
        ],
        compiler_params=pltpu.CompilerParams(
            dimension_semantics=("arbitrary",), vmem_limit_bytes=40 * 1024 * 1024
        ),
    )(zx, bcdt, pos, prm, head_prm, expand)


def mixer_backward(width, pre, zx, bcdt, pos, prm, head_prm, expand, mixed, states, dy):
    rows = zx.shape[0]
    chunks = rows // CHUNK

    def tokens(columns):
        return pl.BlockSpec((CHUNK, columns), lambda i: (chunks - 1 - i, 0))

    def whole(array):
        return pl.BlockSpec(array.shape, lambda i: (0, 0))

    return pl.pallas_call(
        functools.partial(backward_kernel, width),
        out_shape=(
            jax.ShapeDtypeStruct((rows, width), BF16),
            jax.ShapeDtypeStruct((rows, 3 * LANES), BF16),
            jax.ShapeDtypeStruct((8, width + 2 * LANES), F32),
        ),
        grid=(chunks,),
        in_specs=[
            tokens(width + 2 * LANES),
            pl.BlockSpec((CHUNK, width), lambda i: (chunks - 1 - i, 1)),
            tokens(3 * LANES),
            tokens(1),
            whole(prm),
            whole(head_prm),
            whole(expand),
            tokens(width),
            pl.BlockSpec((1, LANES, width), lambda i: (chunks - 1 - i, 0, 0)),
            tokens(width),
        ],
        out_specs=(
            tokens(width),
            tokens(3 * LANES),
            pl.BlockSpec((8, width + 2 * LANES), lambda i: (0, 0)),
        ),
        scratch_shapes=[
            pltpu.VMEM((LANES, width), F32),
            pltpu.VMEM((CHUNK + 8, width + 2 * LANES), F32),
            pltpu.VMEM((CHUNK + 8, LANES), jnp.int32),
        ],
        compiler_params=pltpu.CompilerParams(
            dimension_semantics=("arbitrary",), vmem_limit_bytes=48 * 1024 * 1024
        ),
        cost_estimate=pl.CostEstimate(flops=rows * width * 2048, bytes_accessed=rows * width * 20, transcendentals=0),
    )(pre, zx, bcdt, pos, prm, head_prm, expand, mixed, states, dy)


MESH = pl.DeviceIdType.MESH


def tp_places():
    me = lax.axis_index("tp")
    return me, me + 1 - 2 * lax.rem(me, 2), lax.rem(me + 2, 4), 3 - me


def greet(peers):
    barrier = pltpu.get_barrier_semaphore()
    for peer in peers:
        pl.semaphore_signal(barrier, inc=1, device_id=peer, device_id_type=MESH)
    pl.semaphore_wait(barrier, len(peers))


def send(src, dst, send_sem, recv_sem, peer):
    return pltpu.make_async_remote_copy(
        src_ref=src, dst_ref=dst, send_sem=send_sem, recv_sem=recv_sem, device_id=peer, device_id_type=MESH
    )


class Gather:
    def __init__(self, whole, rows, send_sems, recv_sems, own=None):
        me, side, up, _ = tp_places()
        half = rows // 2

        def part(place, which):
            return whole.at[pl.ds(pl.multiple_of(place * rows + which * half, half), half)]

        def one(n, place, which, peer):
            return send(part(place, which), part(place, which), send_sems.at[n], recv_sems.at[n], {"tp": peer})

        def quarter(n, which, late, peer):
            start = pl.multiple_of(me * rows + which * half + late * (half // 2), half // 2)
            piece = whole.at[pl.ds(start, half // 2)]
            return send(piece, piece, send_sems.at[n], recv_sems.at[n], {"tp": peer})

        self.side_first, self.up_first = one(0, me, 0, side), one(1, me, 1, up)
        self.side_then = [quarter(2, 1, 0, side), quarter(3, 1, 1, side)]
        self.up_then = [quarter(4, 0, 0, up), quarter(5, 0, 1, up)]
        self.pass_up, self.pass_side = one(6, side, 0, up), one(7, up, 1, side)

    def start(self):
        for copy in (self.side_first, self.up_first, self.side_then[0], self.up_then[0]):
            copy.start()

    def start_rest(self):
        self.side_then[1].start()
        self.up_then[1].start()

    def forward(self):
        self.side_first.wait_recv()
        self.pass_up.start()
        self.up_first.wait_recv()
        self.pass_side.start()

    def neighbours(self):
        for copy in self.side_then + self.up_then:
            copy.wait_recv()

    def finish(self):
        self.pass_up.wait_recv()
        self.pass_side.wait_recv()

    def end(self):
        for copy in [self.side_first, self.up_first, self.pass_up, self.pass_side] + self.side_then + self.up_then:
            copy.wait_send()


def set_up(width, heads, inner, taps_ref, flat_ref, lens_ref, prm, head, expand, pos):
    rank = lax.axis_index("tp")
    channels = taps_ref.shape[1]
    own = pl.ds(pl.multiple_of(rank * width, LANES), width)
    own_gain = pl.ds(pl.multiple_of(channels + rank * width, LANES), width)
    prm[...] = jnp.zeros_like(prm)
    prm[0:4, :width] = taps_ref[:, own]
    prm[0:4, width:] = taps_ref[:, inner:]
    prm[4:5, :width] = flat_ref[:, own]
    prm[4:5, width:] = flat_ref[:, inner:channels]
    prm[5:6, :width] = flat_ref[:, own_gain]
    lane = lax.broadcasted_iota(jnp.int32, (LANES, LANES), 1)
    pick = ((lax.broadcasted_iota(jnp.int32, (LANES, LANES), 0) == lane + rank * heads) & (lane < heads)).astype(F32)
    start = channels + inner
    tiles = [jnp.broadcast_to(flat_ref[:, start + n * LANES : start + (n + 1) * LANES], (8, LANES)) for n in range(3)]
    tiles[1] = jnp.exp(tiles[1])
    picked = lax.dot_general(
        jnp.concatenate(tiles, axis=0), pick, (((1,), (0,)), ((), ())), precision=HIGHEST, preferred_element_type=F32
    )
    head[...] = jnp.concatenate([picked[0:1], picked[8:9], jnp.zeros((6, LANES), F32)], axis=0)
    row = lax.broadcasted_iota(jnp.int32, (2 * LANES, width), 0)
    column = lax.broadcasted_iota(jnp.int32, (2 * LANES, width), 1)
    expand[...] = (lax.rem(row, LANES) == column // (width // heads)).astype(F32).astype(BF16)
    prm[6:7, :width] = dot(two_parts(picked[16:24]), expand[...])[0:1]
    starts = [jnp.int32(0)]
    for n in range(lens_ref.shape[1] - 1):
        starts.append(starts[-1] + lens_ref[0, n])

    def place(i, carry):
        token = lax.broadcasted_iota(jnp.int32, (CHUNK, 1), 0) + i * CHUNK
        begun = jnp.zeros((CHUNK, 1), jnp.int32)
        for first in starts[1:]:
            begun = jnp.where(token >= first, first, begun)
        pos[pl.ds(pl.multiple_of(i * CHUNK, CHUNK), CHUNK), :] = token - begun
        return carry

    lax.fori_loop(0, pos.shape[0] // CHUNK, place, 0)


def first_kernel(
    inner, heads, own_cols, x_ref, gain_ref, wb_ref, wc_ref, wdt_ref, taps_ref, flat_ref, lens_ref, wz_ref, wx_ref, w_out_ref, d_own_ref,
    u_out, zx_out, bcdt_out, wbc_out, mixed_out, g_out, yo_out, yo_t_out, state_out, d_out, dyo_out, coef_out, pos_out,
    prm_out, head_out, expand_out, pre_out, cross_out, branch_out,
    weights, w_out, u, zx, bcdt, wbc, mixed, g, yo, yo_t, states, d, dyo, coef, pos, prm, head, expand, pre, ext, state, sums,
    acc, sems, sum_sems, load_sems, store_sems,
):
    rows, model = x_ref.shape
    total, width = mixed.shape
    chunks = total // CHUNK
    me, side, up, far = tp_places()
    dp = lax.axis_index("dp")
    parity = lax.rem(dp, 2)
    partner = {"dp": dp + 1 - 2 * parity}

    def block(place):
        return pl.ds(pl.multiple_of(place * rows, rows), rows)

    loads = [
        pltpu.make_async_copy(wz_ref, weights.at[:, :width], load_sems.at[0]),
        pltpu.make_async_copy(wx_ref, weights.at[:, width:], load_sems.at[1]),
        pltpu.make_async_copy(w_out_ref, w_out, load_sems.at[2]),
        pltpu.make_async_copy(d_own_ref, d.at[block(me)], load_sems.at[3]),
    ]
    for copy in loads:
        copy.start()
    stores = []

    def keep(source, target):
        copy = pltpu.make_async_copy(source, target, store_sems.at[len(stores)])
        copy.start()
        stores.append(copy)

    bc_own = pl.ds(pl.multiple_of(parity * LANES, LANES), LANES)
    wbc[pl.ds(pl.multiple_of(parity * LANES + me * own_cols, own_cols), own_cols), :] = jnp.where(
        parity == 0, wb_ref[...], wc_ref[...]
    )
    greet([{"tp": side}, {"tp": up}, {"tp": far}, partner])
    small_gather = Gather(wbc.at[bc_own], own_cols, sems.at[0], sems.at[1])
    small_gather.start()
    small_gather.start_rest()

    def norm(i, carry):
        piece = pl.ds(pl.multiple_of(i * 32, 32), 32)
        x = x_ref[piece, :].astype(F32)
        scale = lax.rsqrt(jnp.mean(x * x, axis=-1, keepdims=True) + EPSILON)
        u[pl.ds(pl.multiple_of(me * rows + i * 32, 32), 32), :] = (x * scale * gain_ref[...]).astype(BF16)
        return carry

    lax.fori_loop(0, rows // 32, norm, 0)
    small_gather.forward()
    gather = Gather(u, rows, sems.at[2], sems.at[3])
    gather.start()
    gather.start_rest()
    wbc[2 * LANES :, :] = jnp.zeros((LANES, model), BF16)
    wbc[2 * LANES : 2 * LANES + heads, :] = wdt_ref[...]
    set_up(width, heads, inner, taps_ref, flat_ref, lens_ref, prm, head, expand, pos)
    keep(pos, pos_out)
    keep(prm, prm_out)
    keep(head, head_out)
    keep(expand, expand_out)
    loads[0].wait()
    loads[1].wait()

    def project(place):
        piece = block(place)

        def tile(n, carry):
            columns = pl.ds(pl.multiple_of(n * 512, 512), 512)
            zx[piece, columns] = dot(u[piece, :], weights[:, columns]).astype(BF16)
            return carry

        lax.fori_loop(0, 2 * width // 512, tile, 0)

    def project_small(place):
        bcdt[block(place), :] = dot(u[block(place), :], wbc[...], CONTRACT_LAST).astype(BF16)

    project(me)
    small_gather.neighbours()
    small_gather.finish()
    trade = send(wbc.at[bc_own], wbc.at[bc_own], sems.at[6, 0], sems.at[6, 1], partner)
    trade.start()
    gather.forward()
    loads[3].wait()
    d_gather = Gather(d, rows, sems.at[4], sems.at[5])
    d_gather.start()
    trade.wait()
    keep(wbc, wbc_out)
    project_small(me)
    gather.neighbours()
    project(side)
    project(up)
    project_small(side)
    project_small(up)
    gather.finish()
    keep(u, u_out)
    project(far)
    project_small(far)
    keep(zx, zx_out)
    keep(bcdt, bcdt_out)

    state[...] = jnp.zeros_like(state)
    ext[...] = jnp.zeros_like(ext)

    def chunk(i, carry):
        forward_chunk(
            width, i, zx, bcdt, pos, prm, head, expand, mixed, g, sums.at[0], states, pre, ext, state
        )
        return carry

    lax.fori_loop(0, chunks, chunk, 0)

    copies = [
        send(sums.at[0], sums.at[2 + n], sum_sems.at[0, n], sum_sems.at[1, n], {"tp": peer})
        for n, peer in enumerate((side, up, far))
    ]
    for copy in copies:
        copy.start()
    d_gather.start_rest()
    keep(mixed, mixed_out)
    keep(g, g_out)
    keep(states, state_out)
    keep(pre, pre_out)
    loads[2].wait()

    def back_to_heads(place):
        piece = block(place)
        acc[...] = jnp.zeros_like(acc)

        def tile(n, carry):
            columns = pl.ds(pl.multiple_of(n * 256, 256), 256)
            low = dot(d[piece, :], w_out[columns, :], CONTRACT_LAST).astype(BF16)
            dyo[piece, columns] = low
            both = low.astype(F32) * prm[5:6, columns] * g[piece, columns]
            acc[...] += both[:, :LANES] + both[:, LANES:]
            return carry

        lax.fori_loop(0, width // 256, tile, 0)
        column = jnp.sum(acc[...], axis=1, keepdims=True)
        sums[1, :, piece] = jnp.broadcast_to(column, (rows, LANES)).T[:8, :]
        keep(dyo.at[piece], dyo_out.at[piece])

    d_gather.forward()
    back_to_heads(me)
    for copy in copies:
        copy.wait()

    def gate(i, carry):
        piece = pl.ds(pl.multiple_of(i * CHUNK, CHUNK), CHUNK)
        squares = sums[0, :, piece] + sums[2, :, piece] + sums[3, :, piece] + sums[4, :, piece]
        scale = lax.rsqrt(squares / inner + EPSILON)
        columns = jnp.concatenate([scale, jnp.zeros((LANES - 8, LANES), F32)], axis=0).T
        coef[piece, :] = columns
        gated = g[piece, :] * columns[:, 0:1] * prm[5:6, :width]
        yo[piece, :] = gated.astype(BF16)
        yo_t[:, piece] = gated.T.astype(BF16)
        return carry

    lax.fori_loop(0, chunks, gate, 0)
    keep(coef, coef_out)
    keep(yo, yo_out)
    keep(yo_t, yo_t_out)
    branch = weights.at[:total, :]

    def out_block(place):
        piece = block(place)

        def tile(n, carry):
            columns = pl.ds(pl.multiple_of(n * 512, 512), 512)
            branch[piece, columns] = dot(yo[piece, :], w_out[:, columns]).astype(BF16)
            return carry

        lax.fori_loop(0, model // 512, tile, 0)
        keep(branch.at[piece], branch_out.at[piece])

    out_block(far)
    out_block(side)
    d_gather.neighbours()
    back_to_heads(side)
    back_to_heads(up)
    out_block(up)
    out_block(me)
    d_gather.finish()
    keep(d, d_out)
    back_to_heads(far)
    keep(sums.at[1], cross_out)
    small_gather.end()
    gather.end()
    d_gather.end()
    for copy in stores:
        copy.wait()


def first_part(inner, heads, own_cols, x_in, gain, w_b, w_c, w_dt, taps, flat, lens, w_z, w_x, w_out, d_out):
    rows, model = x_in.shape
    total = 4 * rows
    width = w_z.shape[1]
    chunks = total // CHUNK
    vmem = pl.BlockSpec(memory_space=pltpu.VMEM)
    anywhere = pl.BlockSpec(memory_space=pl.ANY)
    results = [
        ((total, model), BF16),
        ((total, 2 * width), BF16),
        ((total, 3 * LANES), BF16),
        ((3 * LANES, model), BF16),
        ((total, width), F32),
        ((total, width), F32),
        ((total, width), BF16),
        ((width, total), BF16),
        ((chunks, LANES, width), BF16),
        ((total, model), BF16),
        ((total, width), BF16),
        ((total, LANES), F32),
        ((total, 1), jnp.int32),
        ((8, width + 2 * LANES), F32),
        ((8, LANES), F32),
        ((2 * LANES, width), BF16),
        ((total, width + 2 * LANES), F32),
    ]
    cross = [jax.ShapeDtypeStruct((8, total), F32), jax.ShapeDtypeStruct((total, model), BF16)]
    return pl.pallas_call(
        functools.partial(first_kernel, inner, heads, own_cols),
        out_shape=[jax.ShapeDtypeStruct(*result) for result in results] + cross,
        in_specs=[vmem] * 7 + [pl.BlockSpec(memory_space=pltpu.SMEM)] + [anywhere] * 4,
        out_specs=[anywhere] * (len(results) + 2),
        scratch_shapes=[pltpu.VMEM((model, 2 * width), BF16), pltpu.VMEM((width, model), BF16)]
        + [pltpu.VMEM(*result) for result in results]
        + [
            pltpu.VMEM((CHUNK + 8, width + 2 * LANES), F32),
            pltpu.VMEM((LANES, width), F32),
            pltpu.VMEM((5, 8, total), F32),
            pltpu.VMEM((rows, LANES), F32),
            pltpu.SemaphoreType.DMA((7, 8)),
            pltpu.SemaphoreType.DMA((2, 3)),
            pltpu.SemaphoreType.DMA((4,)),
            pltpu.SemaphoreType.DMA((30,)),
        ],
        compiler_params=pltpu.CompilerParams(
            collective_id=0, has_side_effects=True, vmem_limit_bytes=60 * 1024 * 1024
        ),
    )(x_in, gain, w_b, w_c, w_dt, taps, flat, lens, w_z, w_x, w_out, d_out)


def add_into(target, other):
    rows = target.shape[0]
    tile = max(t for t in range(16, 257, 16) if rows % t == 0)

    def one(i, carry):
        piece = pl.ds(pl.multiple_of(i * tile, tile), tile)
        target[piece, :] = (target[piece, :].astype(F32) + other[piece, :].astype(F32)).astype(BF16)
        return carry

    lax.fori_loop(0, rows // tile, one, 0)


def line_order(count):
    low, high, out = 0, count - 1, []
    while low <= high:
        out += [high, low] if low < high else [low]
        low, high = low + 1, high - 1
    return out


class PairSum:
    def __init__(self, parts, pair, sems):
        dp = lax.axis_index("dp")
        self.parity = lax.rem(dp, 2)
        self.partner = {"dp": dp + 1 - 2 * self.parity}
        self.parts, self.pair, self.sems = parts, pair, sems

    def theirs(self, z):
        return 2 * z + 1 - self.parity

    def ours(self, z):
        return 2 * z + self.parity

    def copy(self, z):
        return send(
            self.parts.at[self.theirs(z)], self.pair.at[z], self.sems.at[0, z], self.sems.at[1, z], self.partner
        )

    def swap(self, z):
        self.copy(z).start()

    def merge(self, z):
        self.copy(z).wait()
        add_into(self.parts.at[self.ours(z)], self.pair.at[z])


class LineSum:
    def __init__(self, parts, at, right, left, right_sems, left_sems):
        dp = lax.axis_index("dp")
        self.dp = dp
        self.count = lax.axis_size("dp") // 2
        self.z = dp // 2
        self.parts, self.at = parts, at
        self.lines = {1: (right, right_sems), -1: (left, left_sems)}

    def peers(self):
        n = 2 * self.count
        return [{"dp": lax.rem(self.dp + 2, n)}, {"dp": lax.rem(self.dp + n - 2, n)}]

    def away(self, way):
        return self.z if way == 1 else self.count - 1 - self.z

    def copies(self, way, step):
        line, line_sems = self.lines[way]
        far = self.count - step + self.away(way)
        z = far if way == 1 else self.count - 1 - far
        chunk = self.parts.at[self.at(z)]
        return lambda piece: self.piece(chunk, line, line_sems, step, piece, {"dp": self.dp + 2 * way})

    def piece(self, chunk, line, line_sems, step, piece, peer):
        half = chunk.shape[0] // 2
        rows = pl.ds(piece * half, half)
        copy = send(
            chunk.at[rows], line.at[step - 1, rows], line_sems.at[0, step - 1, piece], line_sems.at[1, step - 1, piece],
            peer,
        )
        return chunk.at[rows], copy

    def add_arrived(self, way, step, piece, target):
        line, line_sems = self.lines[way]
        chunk = self.parts.at[self.at(self.z)]
        self.piece(chunk, line, line_sems, step, piece, self.peers()[0])[1].wait_recv()
        half = chunk.shape[0] // 2
        add_into(target, line.at[step - 1, pl.ds(piece * half, half)])

    def lead(self, *steps):
        for way in (1, -1):

            @pl.when(self.away(way) == 0)
            def _():
                for step in steps:
                    for piece in range(2):
                        self.copies(way, step)(piece)[1].start()

    def relay(self, step, piece):
        for way in (1, -1):
            away = self.away(way)

            @pl.when((away >= 1) & (away <= min(step - 1, self.count - 2)))
            def _():
                chunk, copy = self.copies(way, step)(piece)
                self.add_arrived(way, step - 1, piece, chunk)
                copy.start()

    def finish(self):
        total = self.parts.at[self.at(self.z)]
        half = total.shape[0] // 2
        for piece in range(2):
            for way in (1, -1):

                @pl.when(self.away(way) >= 1)
                def _():
                    self.add_arrived(way, self.count - 1, piece, total.at[pl.ds(piece * half, half)])

        return total

    def end(self):
        for way in (1, -1):
            away = self.away(way)
            for step in range(1, self.count):

                @pl.when(away <= min(step - 1, self.count - 2))
                def _():
                    for piece in range(2):
                        self.copies(way, step)(piece)[1].wait_send()


class PlaneSum:
    def __init__(self, away, to_side, to_up, in_far, in_side, in_up, sems):
        _, side, up, _ = tp_places()
        peers = ({"tp": side}, {"tp": up})
        self.to, self.in_far, self.into = (to_side, to_up), in_far, (in_side, in_up)

        def one(kind, n, source, target, peer):
            return send(source.at[n], target.at[n], sems.at[0, kind, n], sems.at[1, kind, n], peer)

        self.one, self.peers, self.away = one, peers, away
        self.far = [one(0, n, away, in_far, peers[n % 2]) for n in range(4)]
        self.near = [[one(1 + w, n, self.to[w], self.into[w], peers[w]) for n in range(4)] for w in range(2)]

    def start_far(self, n, odd):
        self.one(0, n, self.away, self.in_far, self.peers[odd]).start()

    def start_near(self, way, n, odd):
        if odd == way:
            self.one(1 + way, n, self.to[way], self.into[way], self.peers[way]).start()

    def pass_on(self):
        for n in range(4):
            way = 1 - n % 2
            self.far[n].wait_recv()
            add_into(self.to[way].at[n], self.in_far.at[n])
            self.near[way][n].start()

    def finish(self):
        for copy in self.near[0] + self.near[1]:
            copy.wait_recv()

    def received(self, piece):
        side, up = (jnp.concatenate([into[n, piece, :] for n in range(4)], axis=1) for into in self.into)
        return side.astype(F32) + up.astype(F32)

    def end(self):
        for copy in self.far + self.near[0] + self.near[1]:
            copy.wait_send()


def plane_scratch(rows, model):
    return [pltpu.VMEM((4, rows, model // 4), BF16) for _ in range(6)] + [pltpu.SemaphoreType.DMA((2, 3, 4))]


def pair_scratch(dp_count, shape):
    return [
        pltpu.VMEM((dp_count // 2,) + shape, BF16),
        pltpu.SemaphoreType.DMA((2, dp_count // 2)),
    ]


def line_scratch(dp_count, shape):
    steps = dp_count // 2 - 1
    return [
        pltpu.VMEM((steps,) + shape, BF16),
        pltpu.VMEM((steps,) + shape, BF16),
        pltpu.SemaphoreType.DMA((2, steps, 2)),
        pltpu.SemaphoreType.DMA((2, steps, 2)),
    ]


class Copies:
    def __init__(self, sems):
        self.sems, self.started = sems, []

    def start(self, source, target):
        copy = pltpu.make_async_copy(source, target, self.sems.at[len(self.started)])
        copy.start()
        self.started.append(copy)
        return copy


def product_chunk(left_t, right, chunk, target, tile):
    columns = pl.ds(pl.multiple_of(chunk * target.shape[1], target.shape[1]), target.shape[1])

    def one(i, carry):
        piece = pl.ds(pl.multiple_of(i * tile, tile), tile)
        target[piece, :] = dot(left_t[piece, :], right[:, columns]).astype(BF16)
        return carry

    lax.fori_loop(0, target.shape[0] // tile, one, 0)


def second_kernel(
    inner, x_ref, cross_ref, branch_ref, yo_t_ref, d_ref, dyo_ref, g_ref, mixed_ref, zx_ref, coef_ref, prm_ref,
    u_ref, block_out, gw_out, dz_out, dy_out, gz_out, gain_out,
    dz, yo_t, d, dyo, g, mixed, z, coef, own, gz, parts, pair, pair_sems, gz_pair, gz_pair_sems,
    right, left, right_sems, left_sems,
    away, to_side, to_up, in_far, in_side, in_up, plane_sems, cross, cross_sems, load_sems, store_sems,
):
    rows, model = x_ref.shape
    total, width = dz.shape
    taken = parts.shape[1]
    me, side, up, far = tp_places()
    loads, stores = Copies(load_sems), Copies(store_sems)
    quarter = model // 4

    def load_block(place, target):
        piece = pl.ds(pl.multiple_of(place * rows, rows), rows)
        return [
            loads.start(branch_ref.at[piece, n * quarter : (n + 1) * quarter], target.at[n]) for n in range(4)
        ]

    load_far = load_block(far, away)
    load_yo_t = loads.start(yo_t_ref, yo_t)
    load_d = loads.start(d_ref, d)
    cores = PairSum(parts, pair, pair_sems)
    gz_cores = PairSum(gz, gz_pair, gz_pair_sems)
    line = LineSum(parts, cores.ours, right, left, right_sems, left_sems)
    plane = PlaneSum(away, to_side, to_up, in_far, in_side, in_up, plane_sems)
    greet([{"tp": side}, {"tp": up}, {"tp": far}, cores.partner] + line.peers())
    crossing = [
        send(cross_ref, cross.at[n], cross_sems.at[0, n], cross_sems.at[1, n], {"tp": peer})
        for n, peer in enumerate((side, up, far))
    ]
    for copy in crossing:
        copy.start()

    for n, copy in enumerate(load_far):
        copy.wait()
        plane.start_far(n, n % 2)
    load_yo_t.wait()
    load_d.wait()
    load_side, load_up = load_block(side, to_side), load_block(up, to_up)
    load_own = loads.start(branch_ref.at[pl.ds(pl.multiple_of(me * rows, rows), rows)], own)
    rest = [
        loads.start(dyo_ref, dyo),
        loads.start(g_ref, g),
        loads.start(mixed_ref, mixed),
        loads.start(zx_ref.at[:, :width], z),
        loads.start(coef_ref, coef),
    ]
    order = line_order(line.count)

    def products(first, step):
        def one(i, carry):
            z_chunk = first + step * i
            product_chunk(yo_t, d, cores.theirs(z_chunk), parts.at[cores.theirs(z_chunk)], taken // 2)
            cores.swap(z_chunk)
            product_chunk(yo_t, d, cores.ours(z_chunk), parts.at[cores.ours(z_chunk)], taken // 2)
            return carry

        lax.fori_loop(0, 2, one, 0)

    products(order[0], order[1] - order[0])
    for z_chunk in order[:2]:
        cores.merge(z_chunk)
    line.lead(1)
    products(order[2], order[3] - order[2])

    def left_over(chunk, carry):
        columns = pl.ds(pl.multiple_of(chunk * parts.shape[2], parts.shape[2]), parts.shape[2])
        gz[chunk, width:, :] = dot(yo_t[taken:, :], d[:, columns]).astype(BF16)
        return carry

    for z_chunk in order[2:]:
        cores.merge(z_chunk)
    line.lead(*range(2, line.count))
    for copy in load_side + load_up:
        copy.wait()
    for n in range(4):
        plane.start_near(n % 2, n, n % 2)
    line.relay(2, 0)
    plane.pass_on()
    lax.fori_loop(0, parts.shape[0], left_over, 0)
    load_u = loads.start(u_ref, d)
    load_own.wait()
    line.relay(2, 1)
    for copy in rest:
        copy.wait()
    for copy in crossing:
        copy.wait()
    gain_out[...] = jnp.zeros_like(gain_out)

    def gate_back(i, carry):
        piece = pl.ds(pl.multiple_of(i * CHUNK, CHUNK), CHUNK)
        crossed = cross_ref[:, piece] + cross[0, :, piece] + cross[1, :, piece] + cross[2, :, piece]
        crossed = jnp.concatenate([crossed, jnp.zeros((LANES - 8, LANES), F32)], axis=0).T[:, 0:1]
        scale = coef[piece, 0:1]
        back = scale * scale * scale * (crossed / inner)
        z_piece = z[piece, :].astype(F32)
        sig = jax.nn.sigmoid(z_piece)
        dyo_piece = dyo[piece, :].astype(F32)
        g_piece = g[piece, :]
        scaled = scale * dyo_piece
        dg = scaled * prm_ref[5:6, :width] - g_piece * back
        gain_out[0:1, :] += jnp.sum(scaled * g_piece, axis=0, keepdims=True)
        d_z = dg * mixed[piece, :] * (sig * (1.0 + z_piece * (1.0 - sig)))
        dz[piece, :] = d_z.astype(BF16)
        yo_t[:, piece] = d_z.T.astype(BF16)
        dyo[piece, :] = (dg * (z_piece * sig)).astype(BF16)
        return carry

    chunks = total // CHUNK
    lax.fori_loop(0, chunks, gate_back, 0)
    stores.start(dz, dz_out)
    stores.start(dyo, dy_out)
    for step in range(3, line.count):
        line.relay(step, 0)
    load_u.wait()

    def gate_product(chunk):
        product_chunk(yo_t, d, chunk, gz.at[chunk, :width], width // 2)

    def theirs(z_chunk, carry):
        gate_product(gz_cores.theirs(z_chunk))
        gz_cores.swap(z_chunk)
        return carry

    lax.fori_loop(0, line.count, theirs, 0)
    for step in range(3, line.count):
        line.relay(step, 1)

    def ours(z_chunk, carry):
        gate_product(gz_cores.ours(z_chunk))
        return carry

    lax.fori_loop(0, line.count, ours, 0)
    for z_chunk in range(line.count):
        gz_cores.merge(z_chunk)
        stores.start(gz.at[gz_cores.ours(z_chunk)], gz_out.at[z_chunk])
    sum_ref = line.finish()
    gw_out[...] = sum_ref[...]
    plane.finish()

    def add_own(i, carry):
        piece = pl.ds(pl.multiple_of(i * 32, 32), 32)
        total_out = own[piece, :].astype(F32) + plane.received(piece)
        block_out[piece, :] = (x_ref[piece, :].astype(F32) + total_out).astype(BF16)
        return carry

    lax.fori_loop(0, rows // 32, add_own, 0)
    line.end()
    plane.end()
    for copy in stores.started:
        copy.wait()


def second_part(inner, x_in, cross, branch, yo_t, d, dyo, g, mixed, zx, coef, prm, u):
    rows, model = x_in.shape
    width, total = yo_t.shape
    dp_count = lax.axis_size("dp")
    cut = model // dp_count
    kept = width // 8
    vmem = pl.BlockSpec(memory_space=pltpu.VMEM)
    anywhere = pl.BlockSpec(memory_space=pl.ANY)
    return pl.pallas_call(
        functools.partial(second_kernel, inner),
        out_shape=(
            jax.ShapeDtypeStruct((rows, model), BF16),
            jax.ShapeDtypeStruct((width - kept, cut), BF16),
            jax.ShapeDtypeStruct((total, width), BF16),
            jax.ShapeDtypeStruct((total, width), BF16),
            jax.ShapeDtypeStruct((dp_count // 2, width + kept, cut), BF16),
            jax.ShapeDtypeStruct((8, width), F32),
        ),
        in_specs=[vmem] * 2 + [anywhere] * 8 + [vmem, anywhere],
        out_specs=(vmem, vmem, anywhere, anywhere, anywhere, vmem),
        scratch_shapes=[
            pltpu.VMEM((total, width), BF16),
            pltpu.VMEM((width, total), BF16),
            pltpu.VMEM((total, model), BF16),
            pltpu.VMEM((total, width), BF16),
            pltpu.VMEM((total, width), F32),
            pltpu.VMEM((total, width), F32),
            pltpu.VMEM((total, width), BF16),
            pltpu.VMEM((total, LANES), F32),
            pltpu.VMEM((rows, model), BF16),
            pltpu.VMEM((dp_count, width + kept, cut), BF16),
            pltpu.VMEM((dp_count, width - kept, cut), BF16),
        ]
        + pair_scratch(dp_count, (width - kept, cut))
        + pair_scratch(dp_count, (width + kept, cut))
        + line_scratch(dp_count, (width - kept, cut))
        + plane_scratch(rows, model)
        + [
            pltpu.VMEM((3, 8, total), F32),
            pltpu.SemaphoreType.DMA((2, 3)),
            pltpu.SemaphoreType.DMA((22,)),
            pltpu.SemaphoreType.DMA((2 + dp_count // 2,)),
        ],
        compiler_params=pltpu.CompilerParams(
            collective_id=1, has_side_effects=True, vmem_limit_bytes=60 * 1024 * 1024
        ),
    )(x_in, cross, branch, yo_t, d, dyo, g, mixed, zx, coef, prm, u)


def third_kernel(
    own_cols, heads, zx_ref, bcdt_ref, pos_ref, prm_ref, head_ref, expand_ref, mixed_ref, state_ref, dy_ref,
    pre_ref, u_ref, gz_ref,
    gw_z, dx_out, dbcdt_out, gl_out, small_out,
    x, bcdt, mixed, states, dy, pre, u, dx, dbcdt, dx_t, gl, bc_in, d_state, later, later_pos,
    pair, pair_sems, parts, right, left, right_sems, left_sems, bc_sems, load_sems, store_sems,
):
    total, width = mixed.shape
    chunks = total // CHUNK
    me, side, up, far = tp_places()
    loads, stores = Copies(load_sems), Copies(store_sems)
    load_parts = loads.start(gz_ref, parts)
    cores = PairSum(gl, pair, pair_sems)
    line = LineSum(parts, lambda z: z, right, left, right_sems, left_sems)
    halves_of_loads = []
    for first in (total // 2, 0):
        piece = pl.ds(first, total // 2)
        pieces = pl.ds(first // CHUNK, chunks // 2)
        halves_of_loads.append(
            [
                loads.start(zx_ref.at[piece, width:], x.at[piece]),
                loads.start(bcdt_ref.at[piece], bcdt.at[piece]),
                loads.start(mixed_ref.at[piece], mixed.at[piece]),
                loads.start(state_ref.at[pieces], states.at[pieces]),
                loads.start(dy_ref.at[piece], dy.at[piece]),
                loads.start(pre_ref.at[piece], pre.at[piece]),
            ]
        )
    load_u = loads.start(u_ref, u)
    greet([{"tp": side}, {"tp": up}, {"tp": far}, cores.partner] + line.peers())
    backward_start(small_out, d_state, later, later_pos)
    load_parts.wait()
    line.lead(*range(1, line.count))
    for copy in halves_of_loads[0]:
        copy.wait()
    hooks = {3: (2, 0), 5: (2, 1), 7: (3, 0), chunks: (3, 1)}

    def chunk(i, carry):
        at = chunks - 1 - i
        tokens = pl.ds(pl.multiple_of(at * CHUNK, CHUNK), CHUNK)

        @pl.when(i == chunks // 2)
        def _():
            for copy in halves_of_loads[1]:
                copy.wait()

        backward_chunk(
            width, tokens, states[at], pre, x, bcdt, pos_ref, prm_ref, head_ref, expand_ref, mixed, dy, dx, dbcdt, dx_t,
            small_out, d_state, later, later_pos,
        )
        for when, turn in hooks.items():

            @pl.when(i == when - 1)
            def _():
                line.relay(*turn)

        return carry

    lax.fori_loop(0, chunks, chunk, 0)
    stores.start(dx, dx_out)
    stores.start(dbcdt, dbcdt_out)

    pick_row = lax.broadcasted_iota(jnp.int32, (2 * own_cols, 2 * LANES), 0)
    pick_col = lax.broadcasted_iota(jnp.int32, (2 * own_cols, 2 * LANES), 1)

    def columns_of(place):
        wanted = jnp.where(pick_row < own_cols, pick_row, pick_row - own_cols + LANES) + place * own_cols
        pick = (pick_col == wanted).astype(F32).astype(BF16)
        return dot(pick, dbcdt[:, : 2 * LANES], CONTRACT_LAST)

    copies = []
    for n, peer in enumerate((side, up, far)):
        bc_in[n] = columns_of(peer).astype(BF16)
        copies.append(send(bc_in.at[n], bc_in.at[3 + n], bc_sems.at[0, n], bc_sems.at[1, n], {"tp": peer}))
        copies[-1].start()
    own_bc = columns_of(me)
    dx_t[width:, :] = jnp.zeros((dx_t.shape[0] - width, total), BF16)
    dx_t[width + 2 * own_cols : width + 2 * own_cols + heads, :] = dbcdt[:, 2 * LANES :].astype(F32).T[:heads, :].astype(
        BF16
    )
    load_u.wait()

    def x_product(chunk):
        product_chunk(dx_t, u, chunk, gl.at[chunk, :width], width // 2)

    def bc_product(chunk):
        columns = pl.ds(pl.multiple_of(chunk * gl.shape[2], gl.shape[2]), gl.shape[2])
        gl[chunk, width:, :] = dot(dx_t[width:, :], u[:, columns]).astype(BF16)

    def their_x(z_chunk, carry):
        x_product(cores.theirs(z_chunk))
        return carry

    def their_bc(z_chunk, carry):
        bc_product(cores.theirs(z_chunk))
        cores.swap(z_chunk)
        return carry

    def ours(z_chunk, carry):
        x_product(cores.ours(z_chunk))
        bc_product(cores.ours(z_chunk))
        return carry

    lax.fori_loop(0, line.count, their_x, 0)
    for copy in copies:
        copy.wait()
    for n in range(3):
        own_bc = own_bc + bc_in[3 + n].astype(F32)
    dx_t[width : width + 2 * own_cols, :] = own_bc.astype(BF16)
    lax.fori_loop(0, line.count, their_bc, 0)
    lax.fori_loop(0, line.count, ours, 0)
    for z_chunk in range(line.count):
        cores.merge(z_chunk)
        stores.start(gl.at[cores.ours(z_chunk)], gl_out.at[z_chunk])
    sum_ref = line.finish()

    gw_z[...] = sum_ref[...]
    line.end()
    for copy in stores.started:
        copy.wait()


def third_part(own_cols, heads, zx, bcdt, pos, prm, head_prm, expand, mixed, states, dy, pre, u, gz):
    total, width = mixed.shape
    model = u.shape[1]
    dp_count = lax.axis_size("dp")
    cut = model // dp_count
    all_rows = width + -(-(2 * own_cols + heads) // 32) * 32
    vmem = pl.BlockSpec(memory_space=pltpu.VMEM)
    anywhere = pl.BlockSpec(memory_space=pl.ANY)
    return pl.pallas_call(
        functools.partial(third_kernel, own_cols, heads),
        out_shape=(
            jax.ShapeDtypeStruct(gz.shape[1:], BF16),
            jax.ShapeDtypeStruct((total, width), BF16),
            jax.ShapeDtypeStruct((total, 3 * LANES), BF16),
            jax.ShapeDtypeStruct((dp_count // 2, all_rows, cut), BF16),
            jax.ShapeDtypeStruct((8, width + 2 * LANES), F32),
        ),
        in_specs=[anywhere] * 2 + [vmem] * 4 + [anywhere] * 6,
        out_specs=(vmem, anywhere, anywhere, anywhere, vmem),
        scratch_shapes=[
            pltpu.VMEM((total, width), BF16),
            pltpu.VMEM(bcdt.shape, BF16),
            pltpu.VMEM((total, width), F32),
            pltpu.VMEM(states.shape, BF16),
            pltpu.VMEM((total, width), BF16),
            pltpu.VMEM((total, width + 2 * LANES), F32),
            pltpu.VMEM((total, model), BF16),
            pltpu.VMEM((total, width), BF16),
            pltpu.VMEM((total, 3 * LANES), BF16),
            pltpu.VMEM((all_rows, total), BF16),
            pltpu.VMEM((dp_count, all_rows, cut), BF16),
            pltpu.VMEM((6, 2 * own_cols, total), BF16),
            pltpu.VMEM((LANES, width), F32),
            pltpu.VMEM((CHUNK + 8, width + 2 * LANES), F32),
            pltpu.VMEM((CHUNK + 8, LANES), jnp.int32),
        ]
        + pair_scratch(dp_count, (all_rows, cut))
        + [pltpu.VMEM(gz.shape, BF16)]
        + line_scratch(dp_count, gz.shape[1:])
        + [pltpu.SemaphoreType.DMA((2, 3)), pltpu.SemaphoreType.DMA((14,)), pltpu.SemaphoreType.DMA((2 + dp_count // 2,))],
        compiler_params=pltpu.CompilerParams(
            collective_id=2, has_side_effects=True, vmem_limit_bytes=60 * 1024 * 1024
        ),
    )(zx, bcdt, pos, prm, head_prm, expand, mixed, states, dy, pre, u, gz)


def fourth_kernel(
    heads, x_ref, d_own_ref, gain_ref, small_ref, gain_sum_ref, expand_ref, dz_ref, dx_ref, dbcdt_ref, wz_ref, wx_ref,
    wbc_ref, u_ref, gl_ref,
    gw_x, grad_x, sums,
    dz, dx, dbcdt, wz, wx, wbc, u, own, gain_part, packed, over_z, parts,
    right, left, right_sems, left_sems,
    away, to_side, to_up, in_far, in_side, in_up, plane_sems, z_sems, tp_sems, load_sems,
):
    rows, model = x_ref.shape
    width = dz.shape[1]
    me, side, up, far = tp_places()
    dp_count = 2 * parts.shape[0]
    loads = Copies(load_sems)
    weights = [loads.start(wz_ref, wz), loads.start(wx_ref, wx), loads.start(wbc_ref, wbc)]
    loads_of = {}

    def load_block(name, place):
        piece = pl.ds(pl.multiple_of(place * rows, rows), rows)
        loads_of[name] = [
            loads.start(source.at[piece], target.at[piece])
            for source, target in ((dz_ref, dz), (dx_ref, dx), (dbcdt_ref, dbcdt), (u_ref, u))
        ]

    load_block("far", far)
    load_parts = loads.start(gl_ref, parts)
    line = LineSum(parts, lambda z: z, right, left, right_sems, left_sems)
    plane = PlaneSum(away, to_side, to_up, in_far, in_side, in_up, plane_sems)
    partner = {"dp": line.dp + 1 - 2 * lax.rem(line.dp, 2)}
    others = [{"dp": lax.rem(line.dp + 2 * n, dp_count)} for n in range(1, dp_count // 2)]
    greet([{"tp": side}, {"tp": up}, {"tp": far}, partner] + others)
    load_parts.wait()
    line.lead(*range(1, line.count - 1))
    for name, place in (("side", side), ("up", up), ("me", me)):
        load_block(name, place)
    gain_part[...] = jnp.zeros_like(gain_part)

    quarter = model // 4

    def du_block(name, place, target, started=None):
        for copy in loads_of[name]:
            copy.wait()
        piece = pl.ds(pl.multiple_of(place * rows, rows), rows)

        def two(m, carry):
            for odd in range(2):
                n = 2 * m + odd
                columns = pl.ds(pl.multiple_of(n * quarter, quarter), quarter)
                du = (
                    dot(dz[piece, :], wz[columns, :], CONTRACT_LAST)
                    + dot(dx[piece, :], wx[columns, :], CONTRACT_LAST)
                    + dot(dbcdt[piece, :], wbc[:, columns])
                )
                if started is None:
                    target[:, columns] = du
                else:
                    target[n] = du.astype(BF16)
                    started(n, odd)
                gain_part[pl.ds(n, 1), :] += jnp.sum(du * u[piece, columns].astype(F32), axis=0, keepdims=True)
            return carry

        lax.fori_loop(0, 2, two, 0)

    for copy in weights:
        copy.wait()
    du_block("far", far, away, plane.start_far)
    du_block("side", side, to_side, functools.partial(plane.start_near, 0))
    line.relay(2, 0)
    du_block("up", up, to_up, functools.partial(plane.start_near, 1))
    line.relay(2, 1)
    du_block("me", me, own)

    wide = width + 2 * LANES
    shift = (
        lax.broadcasted_iota(jnp.int32, (LANES, LANES), 1)
        == lax.broadcasted_iota(jnp.int32, (LANES, LANES), 0) + me * heads
    ).astype(F32)
    shift = jnp.where(lax.broadcasted_iota(jnp.int32, (LANES, LANES), 0) < heads, shift, 0.0)
    skip_rows = two_parts(jnp.broadcast_to(small_ref[6:7, :width], (8, width)))
    expand = expand_ref[:LANES, :]
    per_head = dot(skip_rows[:, :width], expand, CONTRACT_LAST) + dot(skip_rows[:, width:], expand, CONTRACT_LAST)
    tiles = jnp.concatenate([small_ref[:, :LANES], small_ref[:, LANES : 2 * LANES], per_head], axis=0)
    placed = lax.dot_general(
        tiles, shift, (((1,), (0,)), ((), ())), precision=HIGHEST, preferred_element_type=F32
    )
    packed[0, :, :wide] = small_ref[...]
    packed[0, 5:6, :width] = gain_sum_ref[0:1, :]
    packed[0, 6:7, width : width + LANES] = placed[16:17]
    packed[0, 7:8, :LANES] = placed[7:8]
    packed[0, 7:8, LANES : 2 * LANES] = placed[15:16]
    packed[0, :, wide:] = jnp.zeros((8, quarter), F32)
    for n in range(4):
        packed[0, n : n + 1, wide:] = gain_part[n : n + 1, :] / gain_ref[:, n * quarter : (n + 1) * quarter]
    trade = send(packed.at[0], packed.at[1], z_sems.at[0, 0], z_sems.at[1, 0], partner)
    trade.start()
    plane.pass_on()
    trade.wait()
    over_z[0] = packed[0] + packed[1]
    copies = [
        send(over_z.at[0], over_z.at[n], z_sems.at[0, n], z_sems.at[1, n], others[n - 1])
        for n in range(1, dp_count // 2)
    ]
    for copy in copies:
        copy.start()
    line.lead(line.count - 1)
    for step in range(3, line.count):
        line.relay(step, 0)
        line.relay(step, 1)
    for copy in copies:
        copy.wait()
    everything = over_z[0]
    for n in range(1, dp_count // 2):
        everything = everything + over_z[n]
    sums[me] = everything
    copies = [
        send(sums.at[me], sums.at[me], tp_sems.at[0, n], tp_sems.at[1, n], {"tp": peer})
        for n, peer in enumerate((side, up, far))
    ]
    for copy in copies:
        copy.start()
    plane.finish()

    def norm_back(i, carry):
        piece = pl.ds(pl.multiple_of(i * 32, 32), 32)
        x = x_ref[piece, :].astype(F32)
        r_in = lax.rsqrt(jnp.mean(x * x, axis=-1, keepdims=True) + EPSILON)
        du = own[piece, :] + plane.received(piece)
        e_in = du * gain_ref[...]
        back = r_in * r_in * r_in * jnp.mean(e_in * x, axis=-1, keepdims=True)
        grad_x[piece, :] = d_own_ref[piece, :].astype(F32) + r_in * e_in - x * back
        return carry

    lax.fori_loop(0, rows // 32, norm_back, 0)
    for copy in copies:
        copy.wait()
    sum_ref = line.finish()

    gw_x[...] = sum_ref[...]
    line.end()
    plane.end()


def fourth_part(heads, x_in, d_out, gain, small, gain_sum, expand, dz, dx, dbcdt, w_z, w_x, wbc, u, gl):
    rows, model = x_in.shape
    total, width = dz.shape
    dp_count = lax.axis_size("dp")
    cut = model // dp_count
    wide = width + 2 * LANES + model // 4
    vmem = pl.BlockSpec(memory_space=pltpu.VMEM)
    anywhere = pl.BlockSpec(memory_space=pl.ANY)
    return pl.pallas_call(
        functools.partial(fourth_kernel, heads),
        out_shape=(
            jax.ShapeDtypeStruct(gl.shape[1:], BF16),
            jax.ShapeDtypeStruct((rows, model), F32),
            jax.ShapeDtypeStruct((4, 8, wide), F32),
        ),
        in_specs=[vmem] * 6 + [anywhere] * 8,
        out_specs=(vmem,) * 3,
        scratch_shapes=[
            pltpu.VMEM((total, width), BF16),
            pltpu.VMEM((total, width), BF16),
            pltpu.VMEM((total, 3 * LANES), BF16),
            pltpu.VMEM((model, width), BF16),
            pltpu.VMEM((model, width), BF16),
            pltpu.VMEM((3 * LANES, model), BF16),
            pltpu.VMEM((total, model), BF16),
            pltpu.VMEM((rows, model), F32),
            pltpu.VMEM((8, model // 4), F32),
            pltpu.VMEM((2, 8, wide), F32),
            pltpu.VMEM((dp_count // 2, 8, wide), F32),
            pltpu.VMEM(gl.shape, BF16),
        ]
        + line_scratch(dp_count, gl.shape[1:])
        + plane_scratch(rows, model)
        + [
            pltpu.SemaphoreType.DMA((2, dp_count // 2)),
            pltpu.SemaphoreType.DMA((2, 3)),
            pltpu.SemaphoreType.DMA((20,)),
        ],
        compiler_params=pltpu.CompilerParams(
            collective_id=3, has_side_effects=True, vmem_limit_bytes=60 * 1024 * 1024
        ),
    )(x_in, d_out, gain, small, gain_sum, expand, dz, dx, dbcdt, w_z, w_x, wbc, u, gl)


def results_kernel(
    own_cols, heads, block_ref, grad_x_ref, first_ref, z_ref, x_ref, sums_ref,
    block_out, grad_x_out, gw_z_out, gw_x_out, gw_b_out, gw_c_out, gw_dt_out, gw_out_out, conv_w_out, conv_b_out, gate_out,
    norm_out, dt_bias_out, a_log_out, skip_out,
    block, grad_x, first, z, x, sums, gw_z, gw_x, gw_b, gw_c, gw_dt, gw_out, conv_w, conv_b, gate, norm, dt_bias, a_log,
    skip, load_sems, sems,
):
    loads, copies = Copies(load_sems), Copies(sems)
    for source, target in (
        (sums_ref, sums), (first_ref, first), (z_ref, z), (x_ref, x), (grad_x_ref, grad_x), (block_ref, block)
    ):
        loads.start(source, target)
    load_sums, load_first, load_z, load_x, load_grad_x, load_block = loads.started
    taken = first.shape[0]
    width = gw_z.shape[1]
    count = sums.shape[0]
    inner = gate.shape[1]
    wide = width + 2 * LANES

    def over_tp(rows, columns):
        total = sums[0, rows, columns]
        for n in range(1, count):
            total = total + sums[n, rows, columns]
        return total

    load_sums.wait()
    tiles = width // LANES
    for n in range(count):
        own = slice(n * width, (n + 1) * width)
        conv_w[:, own] = sums[n, 0:4, :width]
        gate[:, own] = sums[n, 5:6, :width]
        for tile in range(tiles):
            row = n * tiles + tile
            conv_b[row : row + 1, :] = sums[n, 4:5, tile * LANES : (tile + 1) * LANES]
    conv_w[:, inner:] = over_tp(slice(0, 4), slice(width, wide))
    for tile in range(2):
        row = count * tiles + tile
        conv_b[row : row + 1, :] = over_tp(slice(4, 5), slice(width + tile * LANES, width + (tile + 1) * LANES))
    quarter = norm.shape[1] // 4
    for n in range(4):
        norm[:, n * quarter : (n + 1) * quarter] = over_tp(slice(n, n + 1), slice(wide, None))
    total_heads = dt_bias.shape[1]
    dt_bias[...] = over_tp(slice(7, 8), slice(0, LANES))[:, :total_heads]
    a_log[...] = over_tp(slice(7, 8), slice(LANES, 2 * LANES))[:, :total_heads]
    skip[...] = over_tp(slice(6, 7), slice(width, width + LANES))[:, :total_heads]
    for source, target in (
        (conv_w, conv_w_out), (conv_b, conv_b_out), (gate, gate_out), (norm, norm_out), (dt_bias, dt_bias_out),
        (a_log, a_log_out), (skip, skip_out),
    ):
        copies.start(source, target)

    def turn(source, held, target):
        def one(i, carry):
            piece = pl.ds(pl.multiple_of(i * CHUNK, CHUNK), CHUNK)
            held[:, piece] = source[piece, :].T.astype(F32)
            return carry

        lax.fori_loop(0, width // CHUNK, one, 0)
        copies.start(held, target)

    load_first.wait()
    load_z.wait()
    gw_out[:taken, :] = first[...].astype(F32)
    gw_out[taken:, :] = z[width:, :].astype(F32)
    copies.start(gw_out, gw_out_out)
    load_grad_x.wait()
    copies.start(grad_x, grad_x_out)
    load_block.wait()
    copies.start(block, block_out)
    turn(z, gw_z, gw_z_out)
    load_x.wait()
    gw_b[...] = x[width : width + own_cols, :].astype(F32)
    gw_c[...] = x[width + own_cols : width + 2 * own_cols, :].astype(F32)
    gw_dt[...] = x[width + 2 * own_cols : width + 2 * own_cols + heads, :].astype(F32)
    for source, target in ((gw_b, gw_b_out), (gw_c, gw_c_out), (gw_dt, gw_dt_out)):
        copies.start(source, target)
    turn(x, gw_x, gw_x_out)
    for copy in copies.started:
        copy.wait()


def results_part(own_cols, heads, width, block_out, grad_x, first, gw_z, gw_x, sums):
    cut = first.shape[1]
    count = sums.shape[0]
    inner = width * count
    model = grad_x.shape[1]
    anywhere = pl.BlockSpec(memory_space=pl.ANY)
    shapes = [
        (cut, width),
        (cut, width),
        (own_cols, cut),
        (own_cols, cut),
        (heads, cut),
        (width, cut),
        (4, inner + 2 * LANES),
        (inner // LANES + 2, LANES),
        (1, inner),
        (1, model),
        (1, heads * count),
        (1, heads * count),
        (1, heads * count),
    ]
    sources = (block_out, grad_x, first, gw_z, gw_x, sums)
    return pl.pallas_call(
        functools.partial(results_kernel, own_cols, heads),
        out_shape=[jax.ShapeDtypeStruct(large.shape, large.dtype) for large in sources[:2]]
        + [jax.ShapeDtypeStruct(shape, F32) for shape in shapes],
        in_specs=[anywhere] * len(sources),
        out_specs=[anywhere] * (2 + len(shapes)),
        scratch_shapes=[pltpu.VMEM(large.shape, large.dtype) for large in sources]
        + [pltpu.VMEM(shape, F32) for shape in shapes]
        + [pltpu.SemaphoreType.DMA((len(sources),)), pltpu.SemaphoreType.DMA((2 + len(shapes),))],
        compiler_params=pltpu.CompilerParams(vmem_limit_bytes=60 * 1024 * 1024),
    )(*sources)


def in_norm_scale(values):
    return lax.rsqrt(jnp.mean(values * values, axis=-1, keepdims=True) + EPSILON)


def body(
    x_in, norm_gain, w_z, w_x, w_b, w_c, w_dt, conv_w, conv_b, dt_bias, a_log, d_skip, gate_gain, w_out,
    doc_lens, d_out,
):
    tp_count = lax.axis_size("tp")
    in_planes = tp_count == 4 and lax.axis_size("dp") == 8
    rank = lax.axis_index("tp")
    dev_rows, model = x_in.shape
    rows = dev_rows * tp_count
    inner = gate_gain.shape[0]
    width = w_z.shape[1]
    heads = w_dt.shape[1]
    state_size = (conv_w.shape[0] - inner) // 2
    head_size = width // heads
    own_cols = w_b.shape[1]

    x_float = x_in.astype(F32)
    r_in = in_norm_scale(x_float)
    small_weights = jnp.concatenate([w_b, w_c, w_dt], axis=1).T
    if in_planes:
        lanes = jnp.zeros((LANES - d_skip.shape[0],), F32)
        flat = jnp.concatenate([conv_b, gate_gain, dt_bias, lanes, a_log, lanes, d_skip, lanes])[None, :]
        (
            gathered, zx, bcdt, w_bcdt, mixed, g, yo, yo_t, states, grad_gathered, dyo, coef, pos, prm, head_prm, expand,
            pre, cross, branch,
        ) = first_part(
            inner, heads, own_cols, x_in, norm_gain[None, :], w_b.T, w_c.T, w_dt.T, conv_w.T, flat, doc_lens, w_z, w_x,
            w_out, d_out,
        )
        gain_own = prm[5, :width]
    else:
        normed = (x_float * r_in * norm_gain[None, :]).astype(BF16)
        gathered = lax.all_gather(normed, "tp", axis=0, tiled=True)
        w_bc = lax.all_gather(small_weights[: 2 * own_cols], "tp", axis=0).reshape(tp_count, 2, own_cols, model)
        w_bcdt = jnp.concatenate(
            [
                jnp.swapaxes(w_bc, 0, 1).reshape(2 * state_size, model),
                small_weights[2 * own_cols :],
                jnp.zeros((LANES - heads, model), BF16),
            ],
            axis=0,
        )
        zx = dot(gathered, jnp.concatenate([w_z, w_x], axis=1)).astype(BF16)
        bcdt = dot(gathered, w_bcdt, CONTRACT_LAST).astype(BF16)
        lengths = doc_lens[0]
        doc_starts = jnp.cumsum(lengths) - lengths
        positions = jnp.arange(rows, dtype=jnp.int32)
        started = jnp.where(positions[:, None] >= doc_starts[None, :], doc_starts[None, :], 0)
        pos = (positions - jnp.max(started, axis=1))[:, None]

        def own(array, count):
            return lax.dynamic_slice_in_dim(array, rank * count, count, axis=0)

        taps = jnp.concatenate([own(conv_w[:inner], width), conv_w[inner:]], axis=0).T
        bias = jnp.concatenate([own(conv_b[:inner], width), conv_b[inner:]])
        pad_bc = jnp.zeros((2 * state_size,), F32)
        gain_own = own(gate_gain, width)
        skip_own = jnp.repeat(own(d_skip, heads), head_size)
        prm = jnp.concatenate(
            [
                taps,
                bias[None],
                jnp.concatenate([gain_own, pad_bc])[None],
                jnp.concatenate([skip_own, pad_bc])[None],
                jnp.zeros((1, width + 2 * state_size), F32),
            ],
            axis=0,
        )
        pad_heads = jnp.zeros((LANES - heads,), F32)
        head_prm = jnp.concatenate(
            [
                jnp.concatenate([own(dt_bias, heads), pad_heads])[None],
                jnp.concatenate([jnp.exp(own(a_log, heads)), pad_heads])[None],
                jnp.zeros((6, LANES), F32),
            ],
            axis=0,
        )
        expand = (
            (jnp.arange(2 * LANES) % LANES)[:, None] == (jnp.arange(width) // head_size)[None, :]
        ).astype(BF16)
        mixed, g, g_sum, states, pre = mixer_forward(width, zx, bcdt, pos, prm, head_prm, expand)
        grad_gathered = lax.all_gather(d_out, "tp", axis=0, tiled=True)
        dyo = dot(grad_gathered, w_out, CONTRACT_LAST).astype(BF16)
        eg_sum = jnp.sum(dyo.astype(F32) * gain_own[None, :] * g, axis=1)
        g_total, eg_total = lax.psum((g_sum[0], eg_sum), "tp")
        r_gate = lax.rsqrt(g_total / inner + EPSILON)
        zeros = jnp.zeros_like(r_gate)
        coef = jnp.stack([r_gate] + [zeros] * 7 + [r_gate**3 * (eg_total / inner)] + [zeros] * (LANES - 9), axis=1)
        yo = (g * r_gate[:, None] * gain_own[None, :]).astype(BF16)

    if in_planes:
        block_out, gw_first, dz, dy, gz, gain_sum = second_part(
            inner, x_in, cross, branch, yo_t, grad_gathered, dyo, g, mixed, zx, coef, prm, gathered
        )
        gw_z, grad_xs, grad_bcdt, gl, small = third_part(
            own_cols, heads, zx, bcdt, pos, prm, head_prm, expand, mixed, states, dy, pre, gathered, gz
        )
        gw_x, grad_x, sums = fourth_part(
            heads, x_in, d_out, norm_gain[None, :], small, gain_sum, expand, dz, grad_xs, grad_bcdt, w_z, w_x, w_bcdt,
            gathered, gl
        )
        (
            block_out, grad_x, gw_z, gw_x, gw_b, gw_c, gw_dt, gw_out, g_conv_w, g_conv_b, g_gate, g_norm, g_dt_bias,
            g_a_log, g_skip
        ) = results_part(
            own_cols, heads, width, block_out, grad_x, gw_first, gw_z, gw_x, sums
        )
        return (
            block_out, grad_x, g_norm[0], gw_z, gw_x, gw_b.T, gw_c.T, gw_dt.T, g_conv_w.T, g_conv_b.reshape(-1), g_dt_bias[0],
            g_a_log[0], g_skip[0], g_gate[0], gw_out
        )
    else:

        def scatter_dp(partial):
            return lax.psum_scatter(partial.astype(BF16), "dp", scatter_dimension=0, tiled=True).astype(F32)

        def scatter_tp(array):
            return lax.psum_scatter(array.astype(BF16), "tp", scatter_dimension=0, tiled=True).astype(F32)

        grad_w_out = scatter_dp(dot(grad_gathered, yo, CONTRACT_FIRST)).T
        z = zx[:, :width].astype(F32)
        sig_z = jax.nn.sigmoid(z)
        dg = coef[:, 0:1] * (dyo.astype(F32) * gain_own[None, :]) - g * coef[:, 8:9]
        dz = (dg * mixed * (sig_z * (1.0 + z * (1.0 - sig_z)))).astype(BF16)
        dy = (dg * (z * sig_z)).astype(BF16)
        gain_sum = jnp.sum(dyo.astype(F32) * g * coef[:, 0:1], axis=0)
        grad_w_z = scatter_dp(dot(gathered, dz, CONTRACT_FIRST))
        block_out = (x_float + scatter_tp(dot(yo, w_out))).astype(BF16)
        grad_xs, grad_bcdt, small = mixer_backward(
            width, pre, zx, bcdt, pos, prm, head_prm, expand, mixed, states, dy
        )
        small = small.at[5, :width].set(gain_sum)
        d_bc = grad_bcdt[:, : 2 * state_size]
        by_owner = jnp.moveaxis(d_bc.reshape(rows, 2, tp_count, own_cols), 2, 0)
        by_owner = by_owner.reshape(tp_count, rows, 2 * own_cols)
        d_bc_own = lax.psum_scatter(by_owner.astype(F32), "tp", scatter_dimension=0, tiled=False)
        d_rest = jnp.concatenate(
            [
                d_bc_own.astype(BF16),
                grad_bcdt[:, 2 * state_size : 2 * state_size + heads],
                jnp.zeros((rows, (-2 * own_cols - heads) % LANES), BF16),
            ],
            axis=1,
        )
        grad_w_x = scatter_dp(dot(gathered, grad_xs, CONTRACT_FIRST))
        grad_rest = scatter_dp(dot(gathered, d_rest, CONTRACT_FIRST))
        du_part = (
            dot(dz, w_z, CONTRACT_LAST) + dot(grad_xs, w_x, CONTRACT_LAST) + dot(grad_bcdt, w_bcdt)
        )
        gain_part = jnp.sum(du_part * gathered.astype(F32), axis=0) / norm_gain
        du = scatter_tp(du_part)
        e_in = du * norm_gain[None, :]
        grad_x = d_out.astype(F32) + r_in * e_in - x_float * (
            r_in**3 * jnp.mean(e_in * x_float, axis=-1, keepdims=True)
        )
        sums = lax.all_gather(lax.psum(small, "dp"), "tp")
        grad_norm_gain = lax.psum(gain_part, ("dp", "tp"))

    channels = jnp.swapaxes(sums[:, :7, :width], 0, 1).reshape(7, inner)
    shared = jnp.sum(sums[:, :5, width : width + 2 * state_size], axis=0)
    grad_conv = jnp.concatenate([channels[:5], shared], axis=1)
    return (
        block_out,
        grad_x,
        grad_norm_gain,
        grad_w_z,
        grad_w_x,
        grad_rest[:, :own_cols],
        grad_rest[:, own_cols : 2 * own_cols],
        grad_rest[:, 2 * own_cols : 2 * own_cols + heads],
        grad_conv[:4].T,
        grad_conv[4],
        sums[:, 7, :heads].reshape(-1),
        sums[:, 7, LANES : LANES + heads].reshape(-1),
        channels[6].reshape(heads * tp_count, head_size).sum(axis=1),
        channels[5],
        grad_w_out,
    )


def solution(mesh):
    rows = P(("dp", "tp"), None)
    columns = P(None, "tp")
    both = P("dp", "tp")
    none = P()
    return jax.shard_map(
        body,
        mesh=mesh,
        in_specs=(
            rows, none, columns, columns, columns, columns, columns, none, none, none, none, none, none,
            P("tp", None), P("dp", None), rows,
        ),
        out_specs=(
            rows, rows, none, both, both, both, both, both, none, none, none, none, none, none, P("tp", "dp"),
        ),
        check_vma=False,
    )
```
